32 devices in a mesh: dp: 16 (over z, y, x), tensor: 2 (over core).
Axes of the slice: x: 2, y: 2, z: 4, core: 2. Of those that a mesh axis runs over, the one named last changes fastest.
Arguments:
- block_input: bfloat16 [16384, 1024], P('dp'), may hold values from -6 to 6
- segments: int32 [16384], P('dp'), may hold values from 0 to 4, as said below
- variates: int32 [16384], P('dp'), may hold values from 0 to 3
- time_ids: int32 [16384], P('dp'), may hold values from 0 to 511
- attn_gain: float32 [1024], replicated, may hold values from 0.25 to 1.75
- w_qkv: bfloat16 [1024, 3, 1024], P(None, None, 'tensor'), may hold values from -0.1875 to 0.1875
- head_bias: float32 [2, 16], P(None, 'tensor'), may hold values from -3 to 3
- w_out: bfloat16 [1024, 1024], P('tensor'), may hold values from -0.75 to 0.75
- ffn_gain: float32 [1024], replicated, may hold values from 0.25 to 1.75
- w_gate_up: bfloat16 [1024, 2, 4096], P(None, None, 'tensor'), may hold values from -0.1875 to 0.1875
- w_down: bfloat16 [4096, 1024], P('tensor'), may hold values from -0.09375 to 0.09375
- cotangent: bfloat16 [16384, 1024], P('dp'), may hold values from -6 to 6
Outputs:
- block_output: bfloat16 [16384, 1024], P('dp')
- input_grad: float32 [16384, 1024], P('dp')
- attn_gain_grad: float32 [1024], replicated
- w_qkv_grad: float32 [1024, 3, 1024], P(None, None, 'tensor')
- head_bias_grad: float32 [2, 16], P(None, 'tensor')
- w_out_grad: float32 [1024, 1024], P('tensor')
- ffn_gain_grad: float32 [1024], replicated
- w_gate_up_grad: float32 [1024, 2, 4096], P(None, None, 'tensor')
- w_down_grad: float32 [4096, 1024], P('tensor')
The draws below stay inside these ranges and needn't reach their ends.
Inputs may be any that keep to these rules, and one draw needn't show every extreme that they name: `segments`: each sequence of 1024 tokens holds 5 documents, numbered 0 to 4 in order of position; each holds 60 tokens or more and one holds exactly 60.
All inputs are finite; a program needn't handle non-finite values.
Results may differ from the reference program's by a relative error of at most 0.035.
Values may be sent and summed in bfloat16 or wider, within the bound.
A program may use at most 256 MiB of HBM per device.

```python
import math
from functools import partial
import jax
import jax.numpy as jnp
from jax import lax

D = 1024
HEADS = 16
HEAD_DIM = 64
FF = 4096
LEN = 1024
NDOC = 5
DOC_MIN = 60
VARIATES = 4
TIME_SPAN = 512
SEQS = 16
TOKENS = 16384
GROUPS = 2


def draw_segments(key, part):
    first_key = jax.random.fold_in(key, 11)
    second_key = jax.random.fold_in(key, 23)
    weights = jax.random.randint(first_key, (SEQS, NDOC), 1, 101)
    zero_slot = jax.random.randint(second_key, (SEQS, 1), 0, NDOC)
    weights = jnp.where(jnp.arange(NDOC)[None, :] == zero_slot, 0, weights)
    spare_tokens = LEN - NDOC * DOC_MIN
    running = jnp.cumsum(weights, axis=1)
    doc_ends = spare_tokens * running // running[:, -1:] + DOC_MIN * (jnp.arange(NDOC)[None, :] + 1)
    positions = jnp.arange(LEN)
    seg_ids = jnp.sum((positions[None, :, None] >= doc_ends[:, None, :]).astype(jnp.int32), axis=-1)
    return seg_ids.reshape(-1).astype(jnp.int32)


def touch_ends(entries, key, smallest, largest):
    dims = entries.shape
    index_at = [jax.random.randint(jax.random.fold_in(key, axis), (), 0, dims[axis]) for axis in range(len(dims))]
    entries = entries.at[tuple(index_at)].set(smallest)
    longest = dims.index(max(dims))
    index_at[longest] = (index_at[longest] + 1) % dims[longest]
    return entries.at[tuple(index_at)].set(largest)


def steps_of(key, extent, cuts, smallest, largest):
    loudness = 1.0
    for dim, parts in cuts:
        draws = jax.random.uniform(jax.random.fold_in(jax.random.fold_in(key, 6), dim), (parts,), jnp.float32, smallest / len(cuts), largest / len(cuts))
        loudness = loudness * jnp.repeat(jnp.exp(draws), extent[dim] // parts).reshape((-1,) + (1,) * (len(extent) - 1 - dim))
    return loudness


def bell_draw(key, extent, spread, reach, cuts=(), held_as=jnp.bfloat16):
    factor_of = steps_of(key, extent, cuts, -0.22, 0.18) if cuts else 1.0
    drawn = jax.random.normal(key, extent, jnp.float32) * spread * factor_of
    return jnp.minimum(jnp.maximum(drawn, -reach), reach).astype(held_as)


def setup_inputs(seed: int = 0) -> dict:
    keys = jax.random.split(jax.random.key(seed), 13)
    return {
        "block_input": bell_draw(keys[0], (TOKENS, D), 1.0, 6.0, ((0, 16),)),
        "segments": draw_segments(jax.random.fold_in(keys[12], 71), 0),
        "variates": touch_ends(jax.random.randint(keys[2], (TOKENS,), 0, VARIATES), jax.random.fold_in(keys[2], 1), 0, VARIATES - 1).astype(jnp.int32),
        "time_ids": touch_ends(jax.random.randint(keys[3], (TOKENS,), 0, TIME_SPAN), jax.random.fold_in(keys[3], 1), 0, TIME_SPAN - 1).astype(jnp.int32),
        "attn_gain": jnp.clip(1.0 + 0.15 * jax.random.normal(keys[4], (D,), jnp.float32), 0.25, 1.75),
        "w_qkv": bell_draw(keys[5], (D, 3, HEADS * HEAD_DIM), D ** -0.5, 0.1875, ((2, 2),)),
        "head_bias": bell_draw(keys[6], (2, HEADS), 1.0, 3.0, ((1, 2),), jnp.float32),
        "w_out": bell_draw(keys[7], (HEADS * HEAD_DIM, D), (D // 16) ** -0.5, 0.75, ((0, 2),)),
        "ffn_gain": jnp.clip(1.0 + 0.15 * jax.random.normal(keys[8], (D,), jnp.float32), 0.25, 1.75),
        "w_gate_up": bell_draw(keys[9], (D, 2, FF), D ** -0.5, 0.1875, ((2, 2),)),
        "w_down": bell_draw(keys[10], (FF, D), FF ** -0.5, 0.09375, ((0, 2),)),
        "cotangent": bell_draw(keys[11], (TOKENS, D), 1.0, 6.0, ((0, 16),)),
    }


EPSILON = 1e-05
MASKED = -1000000000.0

@jax.custom_vjp
def low(v):
    return lax.optimization_barrier(v.astype(jnp.bfloat16)).astype(jnp.float32)

@jax.custom_vjp
def low_back(v):
    return v

def low_keep(v):
    return (low(v), None)

def low_pass(kept, grad):
    return (grad,)

def back_keep(v):
    return (v, None)

def back_low(kept, grad):
    return (low(grad),)
low.defvjp(low_keep, low_pass)
low_back.defvjp(back_keep, back_low)

def rope_tables(time_ids, head_dim):
    half_dim = head_dim // 2
    freqs = jnp.exp(jnp.arange(half_dim, dtype=jnp.float32) * (-2.0 * math.log(10000.0) / head_dim))
    angles = time_ids.astype(jnp.float32)[:, None] * freqs[None, :]
    return (jnp.cos(angles)[:, None, :], jnp.sin(angles)[:, None, :])

def rotate(vectors, cosine, sine_part):
    half_dim = vectors.shape[-1] // 2
    first_half = vectors[..., :half_dim]
    second_half = vectors[..., half_dim:]
    return jnp.concatenate([first_half * cosine - second_half * sine_part, second_half * cosine + first_half * sine_part], axis=-1)

def layer_one(params, inputs):
    attn_gain, w_qkv, head_bias, w_out, ffn_gain, w_gate_up, w_down = params
    input_rows, seg_ids, var_ids, time_ids = inputs
    group_width = HEADS * HEAD_DIM // GROUPS
    hidden_width = FF // GROUPS
    highest = lax.Precision.HIGHEST
    attn_normed = low(input_rows * lax.rsqrt(lax.optimization_barrier(jnp.mean(input_rows * input_rows, axis=-1, keepdims=True)) + EPSILON) * attn_gain)
    shared_attn = low_back(jnp.broadcast_to(attn_normed, (GROUPS, LEN, D)))
    projected = jnp.einsum('gtd,dcgk->tcgk', shared_attn, w_qkv.reshape(D, 3, GROUPS, group_width), precision=highest)
    projected = low_back(projected.reshape(LEN, 3, HEADS, HEAD_DIM))
    cosine, sine_part = rope_tables(time_ids, HEAD_DIM)
    queries = low(rotate(projected[:, 0], cosine, sine_part))
    keys_rot = low(rotate(projected[:, 1], cosine, sine_part))
    values = low(projected[:, 2])
    same_var = var_ids[:, None] == var_ids[None, :]
    allowed = seg_ids[:, None] == seg_ids[None, :]
    scores = jnp.einsum('qhd,khd->hqk', queries, keys_rot, precision=highest) * HEAD_DIM ** (-0.5)
    scores = low_back(scores + jnp.where(same_var[None], head_bias[0][:, None, None], head_bias[1][:, None, None]))
    scores = jnp.where(allowed[None], scores, MASKED)
    row_max = lax.optimization_barrier(jnp.max(scores, axis=-1, keepdims=True))
    expanded = jnp.exp(scores - row_max)
    probs_low = low(expanded / lax.optimization_barrier(jnp.sum(expanded, axis=-1, keepdims=True)))
    attended = jnp.einsum('hqk,khd->qhd', probs_low, values, precision=highest).reshape(LEN, HEADS * HEAD_DIM)
    attended = low(low_back(attended))
    attn_parts = jnp.einsum('tgk,gkd->gtd', attended.reshape(LEN, GROUPS, group_width), w_out.reshape(GROUPS, group_width, D), precision=highest)
    attn_branch = low_back(lax.optimization_barrier(jnp.sum(low(attn_parts), axis=0)))
    mid_rows = input_rows + attn_branch
    ffn_normed = low(mid_rows * lax.rsqrt(lax.optimization_barrier(jnp.mean(mid_rows * mid_rows, axis=-1, keepdims=True)) + EPSILON) * ffn_gain)
    shared_ffn = low_back(jnp.broadcast_to(ffn_normed, (GROUPS, LEN, D)))
    gate_up = low_back(jnp.einsum('gtd,dcgf->tcgf', shared_ffn, w_gate_up.reshape(D, 2, GROUPS, hidden_width), precision=highest))
    hidden = low(jax.nn.silu(gate_up[:, 0]) * gate_up[:, 1])
    ffn_parts = jnp.einsum('tgf,gfd->gtd', hidden, w_down.reshape(GROUPS, hidden_width, D), precision=highest)
    return mid_rows + low_back(lax.optimization_barrier(jnp.sum(low(ffn_parts), axis=0)))

def reference(block_input, segments, variates, time_ids, attn_gain, w_qkv, head_bias, w_out, ffn_gain, w_gate_up, w_down, cotangent):
    params = (attn_gain.astype(jnp.float32), w_qkv.astype(jnp.float32), head_bias.astype(jnp.float32), w_out.astype(jnp.float32), ffn_gain.astype(jnp.float32), w_gate_up.astype(jnp.float32), w_down.astype(jnp.float32))
    integers = (segments.reshape(SEQS, LEN), variates.reshape(SEQS, LEN), time_ids.reshape(SEQS, LEN))

    def forward(all_rows, weights):
        step_fn = jax.checkpoint(partial(layer_one, weights))
        return lax.map(step_fn, (all_rows,) + integers)
    outputs, pullback = jax.vjp(forward, block_input.astype(jnp.float32).reshape(SEQS, LEN, D), params)
    input_grad, weight_grads = pullback(cotangent.astype(jnp.float32).reshape(SEQS, LEN, D))
    return (outputs.reshape(TOKENS, D).astype(jnp.bfloat16), input_grad.reshape(TOKENS, D), weight_grads[0], weight_grads[1], weight_grads[2], weight_grads[3], weight_grads[4], weight_grads[5], weight_grads[6])
```

```python
import functools
import math

import jax
import jax.numpy as jnp
from jax import lax
from jax.experimental import pallas as pl
from jax.experimental.pallas import tpu as pltpu
from jax.sharding import PartitionSpec as P

LEN = 1024
EPSILON = 1e-05
MASKED = -1000000000.0
BF = jnp.bfloat16
F32 = jnp.float32
MESH = pl.DeviceIdType.MESH
VMEM_LIMIT = 60 * 1024 * 1024
LANES = 128
HEAD = 64
VAR_COLS = 4
SEG_COL = 12
ONE_COL = 20


def dot_nn(a, b):
    return lax.dot_general(a, b, (((1,), (0,)), ((), ())), preferred_element_type=F32)


def dot_nt(a, b):
    return lax.dot_general(a, b, (((1,), (1,)), ((), ())), preferred_element_type=F32)


def dot_tn(a, b):
    return lax.dot_general(a, b, (((0,), (0,)), ((), ())), preferred_element_type=F32)


def whole_spec():
    return pl.BlockSpec(memory_space=pltpu.VMEM)


def split3(v):
    hi = v.astype(BF).astype(F32)
    mid = (v - hi).astype(BF).astype(F32)
    return hi, mid, v - hi - mid


def half_swap(u):
    lane = lax.broadcasted_iota(jnp.int32, u.shape, 1) % HEAD
    return jnp.where(lane < HEAD // 2, pltpu.roll(u, LANES - HEAD // 2, 1), pltpu.roll(u, HEAD // 2, 1))


def qkv_body(x_ref, gain_ref, w_ref, cos_ref, sin_ref, xn_ref, q_ref, k_ref, v_ref):
    x = x_ref[...].astype(F32)
    inv = lax.rsqrt(jnp.mean(x * x, axis=-1, keepdims=True) + EPSILON)
    xn = (x * inv * gain_ref[...]).astype(BF)
    xn_ref[...] = xn
    cosine = cos_ref[...]
    sine = sin_ref[...]
    for part, out, factor in ((0, q_ref, HEAD**-0.5), (1, k_ref, 1.0)):
        lin = dot_nn(xn, w_ref[part])
        for s in range(lin.shape[1] // LANES):
            u = lin[:, s * LANES : (s + 1) * LANES]
            rot = (u * cosine + half_swap(u) * sine).astype(BF)
            if factor != 1.0:
                rot = (rot.astype(F32) * factor).astype(BF)
            out[:, s * LANES : (s + 1) * LANES] = rot
    v_ref[...] = dot_nn(xn, w_ref[2]).astype(BF)


def qkv_call(x, gain, w, cosine, sine):
    rows, dim = x.shape
    width = w.shape[2]
    blk = min(256, rows)
    row = lambda cols: pl.BlockSpec((blk, cols), lambda i: (i, 0))
    return pl.pallas_call(
        qkv_body,
        grid=(rows // blk,),
        out_shape=[jax.ShapeDtypeStruct((rows, dim), BF)] + [jax.ShapeDtypeStruct((rows, width), BF)] * 3,
        in_specs=[
            row(dim),
            pl.BlockSpec((1, dim), lambda i: (0, 0)),
            pl.BlockSpec(w.shape, lambda i: (0, 0, 0)),
            row(LANES),
            row(LANES),
        ],
        out_specs=[row(dim), row(width), row(width), row(width)],
        compiler_params=pltpu.CompilerParams(vmem_limit_bytes=VMEM_LIMIT),
        name="qkv",
    )(x, gain, w, cosine, sine)


def attn_fwd_body(q_ref, k_ref, v_ref, base_ref, segq_ref, extk_ref, bias_ref, o_ref, o32_ref, extq_ref):
    rows = q_ref.shape[0]
    blk = 256
    lane = lax.broadcasted_iota(jnp.int32, (blk, LANES), 1)
    kx = jnp.concatenate([k_ref[...], extk_ref[...]], axis=1)
    ones = jnp.ones((rows, LANES), BF)
    vx = jnp.concatenate([v_ref[...], ones], axis=1)
    for i in range(rows // blk):
        sl = slice(i * blk, (i + 1) * blk)
        q = q_ref[sl, :].astype(F32)
        base = base_ref[sl, :]
        segq = segq_ref[sl, :]
        outs = []
        for h in range(2):
            ext = base * bias_ref[0, h : h + 1, :] + segq
            mine = (lane >= HEAD) if h else (lane < HEAD)
            qx = jnp.concatenate([jnp.where(mine, q, 0.0), ext], axis=1).astype(BF)
            s = dot_nt(qx, kx)
            top = jnp.max(s, axis=-1, keepdims=True)
            p = jnp.exp(s - top).astype(BF)
            ox = dot_nn(p, vx)
            total = ox[:, LANES:]
            outs.append(ox[:, :LANES] / total)
            lse = top + jnp.log(total)
            hi, mid, low = split3(lse)
            ext = jnp.where(
                lane == ONE_COL, -hi, jnp.where(lane == ONE_COL + 1, -mid, jnp.where(lane == ONE_COL + 2, -low, ext))
            )
            extq_ref[0, h, sl, :] = ext.astype(BF)
        o = jnp.where(lane < HEAD, outs[0], outs[1])
        o32_ref[sl, :] = o
        o_ref[sl, :] = o.astype(BF)


def attn_fwd_call(q, k, v, base, segq, extk, bias_rows):
    rows, width = q.shape
    pairs = width // LANES
    col = pl.BlockSpec((rows, LANES), lambda p: (0, p))
    full = pl.BlockSpec((rows, LANES), lambda p: (0, 0))
    return pl.pallas_call(
        attn_fwd_body,
        grid=(pairs,),
        out_shape=[
            jax.ShapeDtypeStruct((rows, width), BF),
            jax.ShapeDtypeStruct((rows, width), F32),
            jax.ShapeDtypeStruct((pairs, 2, rows, LANES), BF),
        ],
        in_specs=[col, col, col, full, full, full, pl.BlockSpec((1, 2, LANES), lambda p: (p, 0, 0))],
        out_specs=[col, col, pl.BlockSpec((1, 2, rows, LANES), lambda p: (p, 0, 0, 0))],
        compiler_params=pltpu.CompilerParams(vmem_limit_bytes=VMEM_LIMIT),
        name="attn_fwd",
    )(q, k, v, base, segq, extk, bias_rows)


def attn_bwd_body(
    q_ref, k_ref, v_ref, do_ref, o32_ref, extq_ref, extk_ref, oh_ref, cos_ref, sin_ref, dq_ref, dk_ref, dv_ref, gb_ref, dqt_ref
):
    rows = q_ref.shape[0]
    blk = 256
    lane = lax.broadcasted_iota(jnp.int32, (blk, LANES), 1)
    kx = jnp.concatenate([k_ref[...], extk_ref[...]], axis=1)
    kxt = kx.T
    lane_all = lax.broadcasted_iota(jnp.int32, (rows, LANES), 1)
    vx = jnp.concatenate([v_ref[...], jnp.where(lane_all < 3, 1.0, 0.0).astype(BF)], axis=1)
    dv = jnp.zeros((rows, LANES), F32)
    dk = jnp.zeros((rows, LANES), F32)
    for h in range(2):
        same = jnp.zeros((8, blk), F32)
        other = jnp.zeros((8, blk), F32)
        for i in range(rows // blk):
            sl = slice(i * blk, (i + 1) * blk)
            mine = (lane >= HEAD) if h else (lane < HEAD)
            q = jnp.where(mine, q_ref[sl, :].astype(F32), 0.0).astype(BF)
            do32 = jnp.where(mine, do_ref[sl, :].astype(F32), 0.0)
            do = do32.astype(BF)
            delta = jnp.sum(do32 * o32_ref[sl, :], axis=-1, keepdims=True)
            hi, mid, low = split3(delta)
            dext = jnp.where(lane == 0, -hi, jnp.where(lane == 1, -mid, jnp.where(lane == 2, -low, 0.0))).astype(BF)
            st = dot_nt(kx, jnp.concatenate([q, extq_ref[0, h, sl, :]], axis=1))
            pt = jnp.exp(st)
            dpt = dot_nt(vx, jnp.concatenate([do, dext], axis=1))
            dst = (pt * dpt).astype(BF)
            dv = dv + dot_nn(pt.astype(BF), do)
            dk = dk + dot_nn(dst, q)
            dqt = dot_nn(kxt, dst)
            dqt_ref[h * HEAD : (h + 1) * HEAD, sl] = dqt[h * HEAD : (h + 1) * HEAD, :]
            g = dqt[LANES : LANES + 8, :]
            oh = oh_ref[0, :, sl]
            same = same + g * oh
            other = other + g * oh_ref[1, :, sl]
        gb_ref[0, h, 0] = same
        gb_ref[0, h, 1] = other
    cosine = cos_ref[...]
    sine = sin_ref[...]
    dq = dqt_ref[...].T * HEAD**-0.5
    dq_ref[...] = (dq * cosine - half_swap(dq) * sine).astype(BF)
    dk_ref[...] = (dk * cosine - half_swap(dk) * sine).astype(BF)
    dv_ref[...] = dv.astype(BF)


def attn_bwd_call(q, k, v, do, o32, extq, extk, onehot, cosine, sine):
    rows, width = q.shape
    pairs = width // LANES
    col = pl.BlockSpec((rows, LANES), lambda p: (0, p))
    full = pl.BlockSpec((rows, LANES), lambda p: (0, 0))
    blk = 256
    return pl.pallas_call(
        attn_bwd_body,
        grid=(pairs,),
        out_shape=[jax.ShapeDtypeStruct((rows, width), BF)] * 3 + [jax.ShapeDtypeStruct((pairs, 2, 2, 8, blk), F32)],
        in_specs=[
            col, col, col, col, col,
            pl.BlockSpec((1, 2, rows, LANES), lambda p: (p, 0, 0, 0)),
            full,
            pl.BlockSpec((2, 8, rows), lambda p: (0, 0, 0)),
            full, full,
        ],
        out_specs=[col, col, col, pl.BlockSpec((1, 2, 2, 8, blk), lambda p: (p, 0, 0, 0, 0))],
        scratch_shapes=[pltpu.VMEM((LANES, rows), F32)],
        compiler_params=pltpu.CompilerParams(vmem_limit_bytes=VMEM_LIMIT),
        name="attn_bwd",
    )(q, k, v, do, o32, extq, extk, onehot, cosine, sine)


def partner_barrier():
    dp = lax.axis_index("dp")
    other = 1 - lax.axis_index("tensor")
    barrier = pltpu.get_barrier_semaphore()
    pl.semaphore_signal(barrier, inc=1, device_id=(dp, other), device_id_type=MESH)
    pl.semaphore_wait(barrier, 1)
    return (dp, other)


def send_rows(src, dst, sl, ssem, rsem, peer):
    return pltpu.make_async_remote_copy(
        src_ref=src.at[sl], dst_ref=dst.at[sl], send_sem=ssem, recv_sem=rsem, device_id=peer, device_id_type=MESH
    )


CHUNKS = 4


def attn_out_body(x_ref, o_ref, w_ref, gain_ref, mid_ref, xn_ref, mine, theirs, ssem, rsem):
    peer = partner_barrier()
    rows = x_ref.shape[0]
    blk = rows // CHUNKS
    copies = []
    for c in range(CHUNKS):
        sl = slice(c * blk, (c + 1) * blk)
        mine[sl, :] = dot_nn(o_ref[sl, :], w_ref[...]).astype(BF)
        copy = send_rows(mine, theirs, pl.ds(c * blk, blk), ssem.at[c], rsem.at[c], peer)
        copy.start()
        copies.append(copy)
    for c in range(CHUNKS):
        sl = slice(c * blk, (c + 1) * blk)
        copies[c].wait_recv()
        mid = x_ref[sl, :].astype(F32) + (mine[sl, :].astype(F32) + theirs[sl, :].astype(F32))
        inv = lax.rsqrt(jnp.mean(mid * mid, axis=-1, keepdims=True) + EPSILON)
        mid_ref[sl, :] = mid
        xn_ref[sl, :] = (mid * inv * gain_ref[...]).astype(BF)
    for c in range(CHUNKS):
        copies[c].wait_send()


def attn_out_call(x, o, w, gain):
    rows, dim = x.shape
    return pl.pallas_call(
        attn_out_body,
        out_shape=[jax.ShapeDtypeStruct((rows, dim), F32), jax.ShapeDtypeStruct((rows, dim), BF)],
        in_specs=[whole_spec()] * 4,
        out_specs=[whole_spec()] * 2,
        scratch_shapes=[
            pltpu.VMEM((rows, dim), BF),
            pltpu.VMEM((rows, dim), BF),
            pltpu.SemaphoreType.DMA((CHUNKS,)),
            pltpu.SemaphoreType.DMA((CHUNKS,)),
        ],
        compiler_params=pltpu.CompilerParams(collective_id=1, has_side_effects=True, vmem_limit_bytes=VMEM_LIMIT),
        name="attn_out",
    )(x, o, w, gain)


def ffn_body(xn_ref, ct_ref, wg_ref, wu_ref, wd_ref, out_ref, gx_ref, gd_ref, gg_ref, gu_ref, acc_o, acc_g, hid, dg, du):
    j = pl.program_id(0)
    rows = xn_ref.shape[0]
    blk = 256

    @pl.when(j == 0)
    def _():
        acc_o[...] = jnp.zeros_like(acc_o)
        acc_g[...] = jnp.zeros_like(acc_g)

    wg = wg_ref[...]
    wu = wu_ref[...]
    wd = wd_ref[...]
    for i in range(rows // blk):
        sl = slice(i * blk, (i + 1) * blk)
        xn = xn_ref[sl, :]
        gate = dot_nn(xn, wg)
        up = dot_nn(xn, wu)
        gh = dot_nt(ct_ref[sl, :], wd)
        sig = jax.nn.sigmoid(gate)
        silu = gate * sig
        hidden = (silu * up).astype(BF)
        dgate = (gh * up * sig * (1.0 + gate * (1.0 - sig))).astype(BF)
        dup = (gh * silu).astype(BF)
        hid[sl, :] = hidden
        dg[sl, :] = dgate
        du[sl, :] = dup
        acc_o[sl, :] += dot_nn(hidden, wd)
        acc_g[sl, :] += dot_nt(dgate, wg) + dot_nt(dup, wu)
    gd_ref[...] = dot_tn(hid[...], ct_ref[...]).astype(BF)
    gg_ref[...] = dot_tn(xn_ref[...], dg[...]).astype(BF)
    gu_ref[...] = dot_tn(xn_ref[...], du[...]).astype(BF)

    @pl.when(j == pl.num_programs(0) - 1)
    def _():
        out_ref[...] = acc_o[...].astype(BF)
        gx_ref[...] = acc_g[...].astype(BF)


def ffn_call(xn, ct, wg, wu, wd):
    rows, dim = xn.shape
    hidden = wd.shape[0]
    blk = 256
    full = pl.BlockSpec((rows, dim), lambda j: (0, 0))
    colw = pl.BlockSpec((dim, blk), lambda j: (0, j))
    roww = pl.BlockSpec((blk, dim), lambda j: (j, 0))
    return pl.pallas_call(
        ffn_body,
        grid=(hidden // blk,),
        out_shape=[
            jax.ShapeDtypeStruct((rows, dim), BF),
            jax.ShapeDtypeStruct((rows, dim), BF),
            jax.ShapeDtypeStruct((hidden, dim), BF),
            jax.ShapeDtypeStruct((dim, hidden), BF),
            jax.ShapeDtypeStruct((dim, hidden), BF),
        ],
        in_specs=[full, full, colw, colw, roww],
        out_specs=[full, full, roww, colw, colw],
        scratch_shapes=[pltpu.VMEM((rows, dim), F32)] * 2 + [pltpu.VMEM((rows, blk), BF)] * 3,
        compiler_params=pltpu.CompilerParams(vmem_limit_bytes=VMEM_LIMIT),
        name="ffn",
    )(xn, ct, wg, wu, wd)


def norm_back(rows_now, gain, grads):
    inv = lax.rsqrt(jnp.mean(rows_now * rows_now, axis=-1, keepdims=True) + EPSILON)
    scaled = grads * gain
    gain_grad = jnp.sum(grads * rows_now * inv, axis=0, keepdims=True)
    back = inv * scaled - rows_now * (inv * inv * inv) * jnp.mean(scaled * rows_now, axis=-1, keepdims=True)
    return back, gain_grad


def ffn_back_body(
    gx_ref, fo_ref, mid_ref, ct_ref, gain_ref, w_ref, at_ref,
    out_ref, gm_ref, do_ref, gw_ref, gg_ref, gx_in, fo_in, gb, ssem, rsem,
):
    peer = partner_barrier()
    rows = mid_ref.shape[0]
    blk = rows // CHUNKS
    copies = []
    for n, (src, dst) in enumerate(((gx_ref, gx_in), (fo_ref, fo_in))):
        for c in range(CHUNKS):
            at = n * CHUNKS + c
            copy = send_rows(src, dst, pl.ds(c * blk, blk), ssem.at[at], rsem.at[at], peer)
            copy.start()
            copies.append(copy)
    gain_sum = jnp.zeros((1, mid_ref.shape[1]), F32)
    for c in range(CHUNKS):
        sl = slice(c * blk, (c + 1) * blk)
        copies[c].wait_recv()
        grads = gx_ref[sl, :].astype(F32) + gx_in[sl, :].astype(F32)
        back, gain_grad = norm_back(mid_ref[sl, :], gain_ref[...], grads)
        gain_sum = gain_sum + gain_grad
        gm = ct_ref[sl, :].astype(F32) + back
        gm_ref[sl, :] = gm
        gb[sl, :] = gm.astype(BF)
        do_ref[sl, :] = dot_nt(gb[sl, :], w_ref[...]).astype(BF)
    gg_ref[...] = gain_sum
    gw_ref[...] = dot_tn(at_ref[...], gb[...]).astype(BF)
    for c in range(CHUNKS):
        sl = slice(c * blk, (c + 1) * blk)
        copies[CHUNKS + c].wait_recv()
        out_ref[sl, :] = (mid_ref[sl, :] + (fo_ref[sl, :].astype(F32) + fo_in[sl, :].astype(F32))).astype(BF)
    for copy in copies:
        copy.wait_send()


def ffn_back_call(gx, fo, mid, ct, gain, w, at):
    rows, dim = mid.shape
    width = w.shape[0]
    return pl.pallas_call(
        ffn_back_body,
        out_shape=[
            jax.ShapeDtypeStruct((rows, dim), BF),
            jax.ShapeDtypeStruct((rows, dim), F32),
            jax.ShapeDtypeStruct((rows, width), BF),
            jax.ShapeDtypeStruct((width, dim), BF),
            jax.ShapeDtypeStruct((1, dim), F32),
        ],
        in_specs=[whole_spec()] * 7,
        out_specs=[whole_spec()] * 5,
        scratch_shapes=[
            pltpu.VMEM((rows, dim), BF),
            pltpu.VMEM((rows, dim), BF),
            pltpu.VMEM((rows, dim), BF),
            pltpu.SemaphoreType.DMA((2 * CHUNKS,)),
            pltpu.SemaphoreType.DMA((2 * CHUNKS,)),
        ],
        compiler_params=pltpu.CompilerParams(collective_id=2, has_side_effects=True, vmem_limit_bytes=VMEM_LIMIT),
        name="ffn_back",
    )(gx, fo, mid, ct, gain, w, at)


def qkv_back_body(dq_ref, dk_ref, dv_ref, w_ref, xn_ref, x_ref, gain_ref, gm_ref, ig_ref, gw_ref, gg_ref, mine, theirs, ssem, rsem):
    peer = partner_barrier()
    rows = x_ref.shape[0]
    blk = rows // CHUNKS
    parts = (dq_ref, dk_ref, dv_ref)
    copies = []
    for c in range(CHUNKS):
        sl = slice(c * blk, (c + 1) * blk)
        total = dot_nt(dq_ref[sl, :], w_ref[0])
        total = total + dot_nt(dk_ref[sl, :], w_ref[1])
        total = total + dot_nt(dv_ref[sl, :], w_ref[2])
        mine[sl, :] = total.astype(BF)
        copy = send_rows(mine, theirs, pl.ds(c * blk, blk), ssem.at[c], rsem.at[c], peer)
        copy.start()
        copies.append(copy)
    for n in range(3):
        gw_ref[n] = dot_tn(xn_ref[...], parts[n][...]).astype(BF)
    gain_sum = jnp.zeros((1, x_ref.shape[1]), F32)
    for c in range(CHUNKS):
        sl = slice(c * blk, (c + 1) * blk)
        copies[c].wait_recv()
        grads = mine[sl, :].astype(F32) + theirs[sl, :].astype(F32)
        back, gain_grad = norm_back(x_ref[sl, :].astype(F32), gain_ref[...], grads)
        gain_sum = gain_sum + gain_grad
        ig_ref[sl, :] = gm_ref[sl, :] + back
    gg_ref[...] = gain_sum
    for copy in copies:
        copy.wait_send()


def qkv_back_call(dq, dk, dv, w, xn, x, gain, gm):
    rows, dim = x.shape
    return pl.pallas_call(
        qkv_back_body,
        out_shape=[
            jax.ShapeDtypeStruct((rows, dim), F32),
            jax.ShapeDtypeStruct(w.shape, BF),
            jax.ShapeDtypeStruct((1, dim), F32),
        ],
        in_specs=[whole_spec()] * 8,
        out_specs=[whole_spec()] * 3,
        scratch_shapes=[
            pltpu.VMEM((rows, dim), BF),
            pltpu.VMEM((rows, dim), BF),
            pltpu.SemaphoreType.DMA((CHUNKS,)),
            pltpu.SemaphoreType.DMA((CHUNKS,)),
        ],
        compiler_params=pltpu.CompilerParams(collective_id=3, has_side_effects=True, vmem_limit_bytes=VMEM_LIMIT),
        name="qkv_back",
    )(dq, dk, dv, w, xn, x, gain, gm)


def tables(time_ids):
    half = HEAD // 2
    freqs = jnp.exp(jnp.arange(half, dtype=F32) * (-2.0 * math.log(10000.0) / HEAD))
    angles = time_ids.astype(F32)[:, None] * freqs[None, :]
    cosine = jnp.cos(angles)
    sine = jnp.sin(angles)
    return jnp.tile(cosine, (1, 4)), jnp.tile(jnp.concatenate([-sine, sine], axis=1), (1, 2))


def mask_tables(segments, variates, head_bias):
    lane = jnp.arange(LANES)[None, :]
    var_here = (lane % VAR_COLS == variates[:, None]) & (lane < 3 * VAR_COLS)
    seg_here = (lane - SEG_COL == segments[:, None]) & (lane >= SEG_COL) & (lane < ONE_COL)
    seg_cols = (lane >= SEG_COL) & (lane < ONE_COL)
    ones = (lane >= ONE_COL) & (lane < ONE_COL + 3)
    base = jnp.where(var_here, 1.0, 0.0)
    segq = jnp.where(seg_cols & ~seg_here, MASKED, 0.0)
    extk = jnp.where(var_here | seg_here | ones, 1.0, 0.0).astype(BF)
    gap = head_bias[0] - head_bias[1]
    hi = lax.reduce_precision(gap, 8, 7)
    mid = lax.reduce_precision(gap - hi, 8, 7)
    low = gap - hi - mid
    kind = lane // VAR_COLS
    rows = jnp.where(kind == 0, hi[:, None], jnp.where(kind == 1, mid[:, None], jnp.where(kind == 2, low[:, None], 0.0)))
    match = jnp.arange(8)[:, None] == variates[None, :]
    valid = jnp.arange(8)[:, None] < VAR_COLS
    onehot = jnp.stack([jnp.where(match, 1.0, 0.0), jnp.where(valid & ~match, 1.0, 0.0)])
    return base, segq, extk, rows.reshape(-1, 2, LANES), onehot


def fast_local(
    block_input, segments, variates, time_ids, attn_gain, w_qkv, head_bias, w_out, ffn_gain, w_gate_up, w_down, cotangent
):
    w3 = jnp.transpose(w_qkv, (1, 0, 2))
    cosine, sine = tables(time_ids)
    base, segq, extk, bias_rows, onehot = mask_tables(segments, variates, head_bias)
    gain1 = attn_gain[None, :]
    gain2 = ffn_gain[None, :]
    xn, q, k, v = qkv_call(block_input, gain1, w3, cosine, sine)
    attended, o32, extq = attn_fwd_call(q, k, v, base, segq, extk, bias_rows)
    mid, xn2 = attn_out_call(block_input, attended, w_out, gain2)
    ffn_part, gx_part, g_down, g_gate, g_up = ffn_call(xn2, cotangent, w_gate_up[:, 0], w_gate_up[:, 1], w_down)
    block_output, grad_mid, do, g_out, g_gain2 = ffn_back_call(gx_part, ffn_part, mid, cotangent, gain2, w_out, attended)
    dq, dk, dv, gb = attn_bwd_call(q, k, v, do, o32, extq, extk, onehot, cosine, sine)
    input_grad, g_qkv, g_gain1 = qkv_back_call(dq, dk, dv, w3, xn, block_input, gain1, grad_mid)
    g_bias = jnp.sum(gb, axis=(3, 4)).reshape(-1, 2).T
    return block_output, input_grad, g_gain1[0], g_qkv, g_bias, g_out, g_gain2[0], g_gate, g_up, g_down


def rope_tables(time_ids, head_dim):
    half_dim = head_dim // 2
    freqs = jnp.exp(jnp.arange(half_dim, dtype=jnp.float32) * (-2.0 * math.log(10000.0) / head_dim))
    angles = time_ids.astype(jnp.float32)[:, None] * freqs[None, :]
    return (jnp.cos(angles)[:, None, :], jnp.sin(angles)[:, None, :])


def rotate(vectors, cosine, sine_part):
    half_dim = vectors.shape[-1] // 2
    first_half = vectors[..., :half_dim]
    second_half = vectors[..., half_dim:]
    return jnp.concatenate(
        [
            first_half * cosine - second_half * sine_part,
            second_half * cosine + first_half * sine_part,
        ],
        axis=-1,
    )


def rotate_back(grads, cosine, sine_part):
    half_dim = grads.shape[-1] // 2
    first_half = grads[..., :half_dim]
    second_half = grads[..., half_dim:]
    return jnp.concatenate(
        [
            first_half * cosine + second_half * sine_part,
            second_half * cosine - first_half * sine_part,
        ],
        axis=-1,
    )


def norm_rows(rows_now, gain):
    inverse = lax.rsqrt(jnp.mean(rows_now * rows_now, axis=-1, keepdims=True) + EPSILON)
    return (rows_now * inverse * gain, inverse)


def plain_norm_back(rows_now, inverse, gain, grads):
    scaled = grads * gain
    gain_grad = jnp.sum(grads * rows_now * inverse, axis=0)
    rows_grad = inverse * scaled - rows_now * (inverse * inverse * inverse) * jnp.mean(
        scaled * rows_now, axis=-1, keepdims=True
    )
    return (rows_grad, gain_grad)


def scores_of(queries, keys_rot, same_var, allowed, head_bias, score_scale):
    raw_scores = (
        jnp.einsum("sqhd,skhd->shqk", queries, keys_rot, preferred_element_type=jnp.float32)
        * score_scale
    )
    biased = raw_scores + jnp.where(
        same_var[:, None], head_bias[0][None, :, None, None], head_bias[1][None, :, None, None]
    )
    return jnp.where(allowed[:, None], biased, MASKED)


def plain_local(
    block_input,
    segments,
    variates,
    time_ids,
    attn_gain,
    w_qkv,
    head_bias,
    w_out,
    ffn_gain,
    w_gate_up,
    w_down,
    cotangent,
):
    row_count = block_input.shape[0]
    heads_here = head_bias.shape[1]
    head_dim = w_qkv.shape[2] // heads_here
    seq_count = row_count // LEN
    score_scale = head_dim ** (-0.5)
    input_rows = block_input.astype(jnp.float32)
    attn_normed, attn_inverse = norm_rows(input_rows, attn_gain)
    attn_normed_low = attn_normed.astype(jnp.bfloat16)
    projected = jnp.einsum(
        "td,dck->tck", attn_normed_low, w_qkv, preferred_element_type=jnp.float32
    )
    cosine, sine_part = rope_tables(time_ids, head_dim)
    head_shape = (row_count, heads_here, head_dim)
    seq_shape = (seq_count, LEN, heads_here, head_dim)
    queries = (
        rotate(projected[:, 0].reshape(head_shape), cosine, sine_part)
        .astype(jnp.bfloat16)
        .reshape(seq_shape)
    )
    keys_rot = (
        rotate(projected[:, 1].reshape(head_shape), cosine, sine_part)
        .astype(jnp.bfloat16)
        .reshape(seq_shape)
    )
    values = projected[:, 2].astype(jnp.bfloat16).reshape(seq_shape)
    seg_ids = segments.reshape(seq_count, LEN)
    var_ids = variates.reshape(seq_count, LEN)
    allowed = seg_ids[:, :, None] == seg_ids[:, None, :]
    same_var = var_ids[:, :, None] == var_ids[:, None, :]
    scores = scores_of(queries, keys_rot, same_var, allowed, head_bias, score_scale)
    row_max = jnp.max(scores, axis=-1, keepdims=True)
    exp_total = jnp.sum(jnp.exp(scores - row_max), axis=-1, keepdims=True)
    log_total = row_max + jnp.log(exp_total)
    probs_low = jnp.exp(scores - log_total).astype(jnp.bfloat16)
    attended = jnp.einsum("shqk,skhd->sqhd", probs_low, values, preferred_element_type=jnp.float32)
    attended = attended.reshape(row_count, heads_here * head_dim).astype(jnp.bfloat16)
    attn_branch = lax.psum(
        jnp.dot(attended, w_out, preferred_element_type=jnp.float32).astype(jnp.bfloat16), "tensor"
    ).astype(jnp.float32)
    mid_rows = input_rows + attn_branch
    ffn_normed, ffn_inverse = norm_rows(mid_rows, ffn_gain)
    ffn_normed_low = ffn_normed.astype(jnp.bfloat16)
    gate_up = jnp.einsum(
        "td,dcf->tcf", ffn_normed_low, w_gate_up, preferred_element_type=jnp.float32
    )
    gate_vals = gate_up[:, 0]
    up_vals = gate_up[:, 1]
    sigmoid_gate = jax.nn.sigmoid(gate_vals)
    silu_gate = gate_vals * sigmoid_gate
    hidden_low = (silu_gate * up_vals).astype(jnp.bfloat16)
    ffn_branch = lax.psum(
        jnp.dot(hidden_low, w_down, preferred_element_type=jnp.float32).astype(jnp.bfloat16),
        "tensor",
    ).astype(jnp.float32)
    block_output = (mid_rows + ffn_branch).astype(jnp.bfloat16)
    grad_down = jnp.einsum("tf,td->fd", hidden_low, cotangent, preferred_element_type=jnp.float32)
    grad_hidden = jnp.einsum("td,fd->tf", cotangent, w_down, preferred_element_type=jnp.float32)
    grad_gate = grad_hidden * up_vals * sigmoid_gate * (1.0 + gate_vals * (1.0 - sigmoid_gate))
    grad_up = grad_hidden * silu_gate
    grad_gate_up = jnp.stack([grad_gate, grad_up], axis=1).astype(jnp.bfloat16)
    grad_w_gate_up = jnp.einsum(
        "td,tcf->dcf", ffn_normed_low, grad_gate_up, preferred_element_type=jnp.float32
    )
    grad_ffn_normed = lax.psum(
        jnp.einsum(
            "tcf,dcf->td", grad_gate_up, w_gate_up, preferred_element_type=jnp.float32
        ).astype(jnp.bfloat16),
        "tensor",
    ).astype(jnp.float32)
    norm_grad_mid, grad_ffn_gain = plain_norm_back(mid_rows, ffn_inverse, ffn_gain, grad_ffn_normed)
    grad_mid = cotangent.astype(jnp.float32) + norm_grad_mid
    grad_branch = grad_mid.astype(jnp.bfloat16)
    grad_w_out = jnp.einsum("tk,td->kd", attended, grad_branch, preferred_element_type=jnp.float32)
    grad_attended = jnp.einsum("td,kd->tk", grad_branch, w_out, preferred_element_type=jnp.float32)
    grad_attended = grad_attended.astype(jnp.bfloat16).reshape(seq_shape)
    scores_again = scores_of(queries, keys_rot, same_var, allowed, head_bias, score_scale)
    probs_again = jnp.exp(scores_again - log_total)
    probs_again_low = probs_again.astype(jnp.bfloat16)
    grad_probs = jnp.einsum(
        "sqhd,skhd->shqk", grad_attended, values, preferred_element_type=jnp.float32
    )
    grad_values = jnp.einsum(
        "shqk,sqhd->skhd", probs_again_low, grad_attended, preferred_element_type=jnp.float32
    )
    grad_scores = probs_again * (
        grad_probs - jnp.sum(probs_again * grad_probs, axis=-1, keepdims=True)
    )
    grad_scores_low = grad_scores.astype(jnp.bfloat16)
    same_low = same_var.astype(jnp.bfloat16)
    other_low = jnp.logical_not(same_var).astype(jnp.bfloat16)
    grad_bias = jnp.stack(
        [
            jnp.einsum(
                "shqk,sqk->h", grad_scores_low, same_low, preferred_element_type=jnp.float32
            ),
            jnp.einsum(
                "shqk,sqk->h", grad_scores_low, other_low, preferred_element_type=jnp.float32
            ),
        ],
        axis=0,
    )
    grad_queries = (
        jnp.einsum("shqk,skhd->sqhd", grad_scores_low, keys_rot, preferred_element_type=jnp.float32)
        * score_scale
    )
    grad_keys = (
        jnp.einsum("shqk,sqhd->skhd", grad_scores_low, queries, preferred_element_type=jnp.float32)
        * score_scale
    )
    grad_query_lin = rotate_back(grad_queries.reshape(head_shape), cosine, sine_part).reshape(
        row_count, heads_here * head_dim
    )
    grad_key_lin = rotate_back(grad_keys.reshape(head_shape), cosine, sine_part).reshape(
        row_count, heads_here * head_dim
    )
    grad_value_lin = grad_values.reshape(row_count, heads_here * head_dim)
    grad_projected = jnp.stack([grad_query_lin, grad_key_lin, grad_value_lin], axis=1).astype(
        jnp.bfloat16
    )
    grad_w_qkv = jnp.einsum(
        "td,tck->dck", attn_normed_low, grad_projected, preferred_element_type=jnp.float32
    )
    grad_attn_normed = lax.psum(
        jnp.einsum("tck,dck->td", grad_projected, w_qkv, preferred_element_type=jnp.float32).astype(
            jnp.bfloat16
        ),
        "tensor",
    ).astype(jnp.float32)
    norm_grad_input, grad_attn_gain = plain_norm_back(
        input_rows, attn_inverse, attn_gain, grad_attn_normed
    )
    input_grad = grad_mid + norm_grad_input
    grad_attn_gain, grad_w_qkv, grad_bias, grad_w_out, grad_ffn_gain, grad_w_gate_up, grad_down = (
        lax.psum(
            (
                grad_attn_gain,
                grad_w_qkv,
                grad_bias,
                grad_w_out,
                grad_ffn_gain,
                grad_w_gate_up,
                grad_down,
            ),
            "dp",
        )
    )
    return (
        block_output,
        input_grad,
        grad_attn_gain,
        grad_w_qkv,
        grad_bias,
        grad_w_out,
        grad_ffn_gain,
        grad_w_gate_up,
        grad_down,
    )


def solution_local(*args):
    block_output, input_grad, g_gain1, g_qkv, g_bias, g_out, g_gain2, g_gate, g_up, g_down = fast_local(*args)
    g_gate, g_up, g_down = lax.psum((g_gate, g_up, g_down), "dp")
    g_qkv, g_out = lax.psum((g_qkv, g_out), "dp")
    g_gain1, g_bias, g_gain2 = lax.psum((g_gain1, g_bias, g_gain2), "dp")
    return (
        block_output,
        input_grad,
        g_gain1,
        jnp.transpose(g_qkv, (1, 0, 2)).astype(F32),
        g_bias,
        g_out.astype(F32),
        g_gain2,
        jnp.stack([g_gate, g_up], axis=1).astype(F32),
        g_down.astype(F32),
    )


def solution(mesh):
    placed = (
        P("dp", None), P("dp"), P("dp"), P("dp"), P(), P(None, None, "tensor"), P(None, "tensor"),
        P("tensor", None), P(), P(None, None, "tensor"), P("tensor", None), P("dp", None),
    )
    fast = mesh.shape["tensor"] == 2
    return jax.shard_map(
        solution_local if fast else plain_local,
        mesh=mesh,
        in_specs=placed,
        out_specs=(
            P("dp", None), P("dp", None), P(), P(None, None, "tensor"), P(None, "tensor"), P("tensor", None), P(),
            P(None, None, "tensor"), P("tensor", None),
        ),
        check_vma=False,
    )
```

```python
import functools
import math

import jax
import jax.numpy as jnp
from jax import lax
from jax.experimental import pallas as pl
from jax.experimental.pallas import tpu as pltpu
from jax.sharding import PartitionSpec as P

LEN = 1024
EPSILON = 1e-05
MASKED = -1000000000.0
BF = jnp.bfloat16
F32 = jnp.float32
MESH = pl.DeviceIdType.MESH
VMEM_LIMIT = 60 * 1024 * 1024
LANES = 128
HEAD = 64
VAR_COLS = 4
SEG_COL = 12
ONE_COL = 20
ROWS = 32
LAG = 2
HALF_ROWS = 512
GROUP_ROWS = 4 * HALF_ROWS
WIDE = 1024
SMALL = 8


def dot_nn(a, b):
    return lax.dot_general(a, b, (((1,), (0,)), ((), ())), preferred_element_type=F32)


def dot_nt(a, b):
    return lax.dot_general(a, b, (((1,), (1,)), ((), ())), preferred_element_type=F32)


def dot_tn(a, b):
    return lax.dot_general(a, b, (((0,), (0,)), ((), ())), preferred_element_type=F32)


def whole_spec():
    return pl.BlockSpec(memory_space=pltpu.VMEM)


def split3(v):
    hi = v.astype(BF).astype(F32)
    mid = (v - hi).astype(BF).astype(F32)
    return hi, mid, v - hi - mid


def half_swap(u):
    lane = lax.broadcasted_iota(jnp.int32, u.shape, 1) % HEAD
    return jnp.where(lane < HEAD // 2, pltpu.roll(u, LANES - HEAD // 2, 1), pltpu.roll(u, HEAD // 2, 1))


def qkv_body(x_ref, gain_ref, w_ref, cos_ref, sin_ref, xn_ref, q_ref, k_ref, v_ref):
    x = x_ref[...].astype(F32)
    inv = lax.rsqrt(jnp.mean(x * x, axis=-1, keepdims=True) + EPSILON)
    xn = (x * inv * gain_ref[...]).astype(BF)
    xn_ref[...] = xn
    cosine = cos_ref[...]
    sine = sin_ref[...]
    for part, out, factor in ((0, q_ref, HEAD**-0.5), (1, k_ref, 1.0)):
        lin = dot_nn(xn, w_ref[part])
        for s in range(lin.shape[1] // LANES):
            u = lin[:, s * LANES : (s + 1) * LANES]
            rot = (u * cosine + half_swap(u) * sine).astype(BF)
            if factor != 1.0:
                rot = (rot.astype(F32) * factor).astype(BF)
            out[:, s * LANES : (s + 1) * LANES] = rot
    v_ref[...] = dot_nn(xn, w_ref[2]).astype(BF)


def qkv_call(x, gain, w, cosine, sine):
    rows, dim = x.shape
    width = w.shape[2]
    blk = min(256, rows)
    row = lambda cols: pl.BlockSpec((blk, cols), lambda i: (i, 0))
    return pl.pallas_call(
        qkv_body,
        grid=(rows // blk,),
        out_shape=[jax.ShapeDtypeStruct((rows, dim), BF)] + [jax.ShapeDtypeStruct((rows, width), BF)] * 3,
        in_specs=[
            row(dim),
            pl.BlockSpec((1, dim), lambda i: (0, 0)),
            pl.BlockSpec(w.shape, lambda i: (0, 0, 0)),
            row(LANES),
            row(LANES),
        ],
        out_specs=[row(dim), row(width), row(width), row(width)],
        compiler_params=pltpu.CompilerParams(vmem_limit_bytes=VMEM_LIMIT),
        name="qkv",
    )(x, gain, w, cosine, sine)


def attn_fwd_body(q_ref, k_ref, v_ref, base_ref, segq_ref, extk_ref, bias_ref, o_ref, o32_ref, extq_ref):
    rows = q_ref.shape[0]
    blk = 256
    lane = lax.broadcasted_iota(jnp.int32, (blk, LANES), 1)
    kx = jnp.concatenate([k_ref[...], extk_ref[...]], axis=1)
    ones = jnp.ones((rows, LANES), BF)
    vx = jnp.concatenate([v_ref[...], ones], axis=1)
    for i in range(rows // blk):
        sl = slice(i * blk, (i + 1) * blk)
        q = q_ref[sl, :].astype(F32)
        base = base_ref[sl, :]
        segq = segq_ref[sl, :]
        outs = []
        for h in range(2):
            ext = base * bias_ref[0, h : h + 1, :] + segq
            mine = (lane >= HEAD) if h else (lane < HEAD)
            qx = jnp.concatenate([jnp.where(mine, q, 0.0), ext], axis=1).astype(BF)
            s = dot_nt(qx, kx)
            top = jnp.max(s, axis=-1, keepdims=True)
            p = jnp.exp(s - top).astype(BF)
            ox = dot_nn(p, vx)
            total = ox[:, LANES:]
            outs.append(ox[:, :LANES] / total)
            lse = top + jnp.log(total)
            hi, mid, low = split3(lse)
            ext = jnp.where(
                lane == ONE_COL, -hi, jnp.where(lane == ONE_COL + 1, -mid, jnp.where(lane == ONE_COL + 2, -low, ext))
            )
            extq_ref[0, h, sl, :] = ext.astype(BF)
        o = jnp.where(lane < HEAD, outs[0], outs[1])
        o32_ref[sl, :] = o
        o_ref[sl, :] = o.astype(BF)


def attn_fwd_call(q, k, v, base, segq, extk, bias_rows):
    rows, width = q.shape
    pairs = width // LANES
    col = pl.BlockSpec((rows, LANES), lambda p: (0, p))
    full = pl.BlockSpec((rows, LANES), lambda p: (0, 0))
    return pl.pallas_call(
        attn_fwd_body,
        grid=(pairs,),
        out_shape=[
            jax.ShapeDtypeStruct((rows, width), BF),
            jax.ShapeDtypeStruct((rows, width), F32),
            jax.ShapeDtypeStruct((pairs, 2, rows, LANES), BF),
        ],
        in_specs=[col, col, col, full, full, full, pl.BlockSpec((1, 2, LANES), lambda p: (p, 0, 0))],
        out_specs=[col, col, pl.BlockSpec((1, 2, rows, LANES), lambda p: (p, 0, 0, 0))],
        compiler_params=pltpu.CompilerParams(vmem_limit_bytes=VMEM_LIMIT),
        name="attn_fwd",
    )(q, k, v, base, segq, extk, bias_rows)


def attn_bwd_body(
    q_ref, k_ref, v_ref, do_ref, o32_ref, extq_ref, extk_ref, oh_ref, cos_ref, sin_ref, dq_ref, dk_ref, dv_ref, gb_ref, dqt_ref
):
    rows = q_ref.shape[0]
    blk = 256
    lane = lax.broadcasted_iota(jnp.int32, (blk, LANES), 1)
    kx = jnp.concatenate([k_ref[...], extk_ref[...]], axis=1)
    kxt = kx.T
    lane_all = lax.broadcasted_iota(jnp.int32, (rows, LANES), 1)
    vx = jnp.concatenate([v_ref[...], jnp.where(lane_all < 3, 1.0, 0.0).astype(BF)], axis=1)
    dv = jnp.zeros((rows, LANES), F32)
    dk = jnp.zeros((rows, LANES), F32)
    for h in range(2):
        same = jnp.zeros((8, blk), F32)
        other = jnp.zeros((8, blk), F32)
        for i in range(rows // blk):
            sl = slice(i * blk, (i + 1) * blk)
            mine = (lane >= HEAD) if h else (lane < HEAD)
            q = jnp.where(mine, q_ref[sl, :].astype(F32), 0.0).astype(BF)
            do32 = jnp.where(mine, do_ref[sl, :].astype(F32), 0.0)
            do = do32.astype(BF)
            delta = jnp.sum(do32 * o32_ref[sl, :], axis=-1, keepdims=True)
            hi, mid, low = split3(delta)
            dext = jnp.where(lane == 0, -hi, jnp.where(lane == 1, -mid, jnp.where(lane == 2, -low, 0.0))).astype(BF)
            st = dot_nt(kx, jnp.concatenate([q, extq_ref[0, h, sl, :]], axis=1))
            pt = jnp.exp(st)
            dpt = dot_nt(vx, jnp.concatenate([do, dext], axis=1))
            dst = (pt * dpt).astype(BF)
            dv = dv + dot_nn(pt.astype(BF), do)
            dk = dk + dot_nn(dst, q)
            dqt = dot_nn(kxt, dst)
            dqt_ref[h * HEAD : (h + 1) * HEAD, sl] = dqt[h * HEAD : (h + 1) * HEAD, :]
            g = dqt[LANES : LANES + 8, :]
            oh = oh_ref[0, :, sl]
            same = same + g * oh
            other = other + g * oh_ref[1, :, sl]
        gb_ref[0, h, 0] = same
        gb_ref[0, h, 1] = other
    cosine = cos_ref[...]
    sine = sin_ref[...]
    dq = dqt_ref[...].T * HEAD**-0.5
    dq_ref[...] = (dq * cosine - half_swap(dq) * sine).astype(BF)
    dk_ref[...] = (dk * cosine - half_swap(dk) * sine).astype(BF)
    dv_ref[...] = dv.astype(BF)


def attn_bwd_call(q, k, v, do, o32, extq, extk, onehot, cosine, sine):
    rows, width = q.shape
    pairs = width // LANES
    col = pl.BlockSpec((rows, LANES), lambda p: (0, p))
    full = pl.BlockSpec((rows, LANES), lambda p: (0, 0))
    blk = 256
    return pl.pallas_call(
        attn_bwd_body,
        grid=(pairs,),
        out_shape=[jax.ShapeDtypeStruct((rows, width), BF)] * 3 + [jax.ShapeDtypeStruct((pairs, 2, 2, 8, blk), F32)],
        in_specs=[
            col, col, col, col, col,
            pl.BlockSpec((1, 2, rows, LANES), lambda p: (p, 0, 0, 0)),
            full,
            pl.BlockSpec((2, 8, rows), lambda p: (0, 0, 0)),
            full, full,
        ],
        out_specs=[col, col, col, pl.BlockSpec((1, 2, 2, 8, blk), lambda p: (p, 0, 0, 0, 0))],
        scratch_shapes=[pltpu.VMEM((LANES, rows), F32)],
        compiler_params=pltpu.CompilerParams(vmem_limit_bytes=VMEM_LIMIT),
        name="attn_bwd",
    )(q, k, v, do, o32, extq, extk, onehot, cosine, sine)


def partner_barrier():
    dp = lax.axis_index("dp")
    other = 1 - lax.axis_index("tensor")
    barrier = pltpu.get_barrier_semaphore()
    pl.semaphore_signal(barrier, inc=1, device_id=(dp, other), device_id_type=MESH)
    pl.semaphore_wait(barrier, 1)
    return (dp, other)


def send_rows(src, dst, sl, ssem, rsem, peer):
    return pltpu.make_async_remote_copy(
        src_ref=src.at[sl], dst_ref=dst.at[sl], send_sem=ssem, recv_sem=rsem, device_id=peer, device_id_type=MESH
    )


CHUNKS = 4


def attn_out_body(x_ref, o_ref, w_ref, gain_ref, mid_ref, xn_ref, mine, theirs, ssem, rsem):
    peer = partner_barrier()
    rows = x_ref.shape[0]
    blk = rows // CHUNKS
    copies = []
    for c in range(CHUNKS):
        sl = slice(c * blk, (c + 1) * blk)
        mine[sl, :] = dot_nn(o_ref[sl, :], w_ref[...]).astype(BF)
        copy = send_rows(mine, theirs, pl.ds(c * blk, blk), ssem.at[c], rsem.at[c], peer)
        copy.start()
        copies.append(copy)
    for c in range(CHUNKS):
        sl = slice(c * blk, (c + 1) * blk)
        copies[c].wait_recv()
        mid = x_ref[sl, :].astype(F32) + (mine[sl, :].astype(F32) + theirs[sl, :].astype(F32))
        inv = lax.rsqrt(jnp.mean(mid * mid, axis=-1, keepdims=True) + EPSILON)
        mid_ref[sl, :] = mid
        xn_ref[sl, :] = (mid * inv * gain_ref[...]).astype(BF)
    for c in range(CHUNKS):
        copies[c].wait_send()


def attn_out_call(x, o, w, gain):
    rows, dim = x.shape
    return pl.pallas_call(
        attn_out_body,
        out_shape=[jax.ShapeDtypeStruct((rows, dim), F32), jax.ShapeDtypeStruct((rows, dim), BF)],
        in_specs=[whole_spec()] * 4,
        out_specs=[whole_spec()] * 2,
        scratch_shapes=[
            pltpu.VMEM((rows, dim), BF),
            pltpu.VMEM((rows, dim), BF),
            pltpu.SemaphoreType.DMA((CHUNKS,)),
            pltpu.SemaphoreType.DMA((CHUNKS,)),
        ],
        compiler_params=pltpu.CompilerParams(collective_id=1, has_side_effects=True, vmem_limit_bytes=VMEM_LIMIT),
        name="attn_out",
    )(x, o, w, gain)


def ffn_body(
    bits, xn_ref, ct_ref, wg_ref, wu_ref, wd_ref,
    out_ref, gx_ref, gd_ref, gk_ref, gs_ref, uk_ref, us_ref, acc_o, acc_g, hid, dg, du,
):
    j = pl.program_id(0)
    rows = xn_ref.shape[0]
    blk = 256

    @pl.when(j == 0)
    def _():
        acc_o[...] = jnp.zeros_like(acc_o)
        acc_g[...] = jnp.zeros_like(acc_g)

    wg = wg_ref[...]
    wu = wu_ref[...]
    wd = wd_ref[...]
    for i in range(rows // blk):
        sl = slice(i * blk, (i + 1) * blk)
        xn = xn_ref[sl, :]
        gate = dot_nn(xn, wg)
        up = dot_nn(xn, wu)
        gh = dot_nt(ct_ref[sl, :], wd)
        sig = jax.nn.sigmoid(gate)
        silu = gate * sig
        hidden = (silu * up).astype(BF)
        dgate = (gh * up * sig * (1.0 + gate * (1.0 - sig))).astype(BF)
        dup = (gh * silu).astype(BF)
        hid[sl, :] = hidden
        dg[sl, :] = dgate
        du[sl, :] = dup
        acc_o[sl, :] += dot_nn(hidden, wd)
        acc_g[sl, :] += dot_nt(dgate, wg) + dot_nt(dup, wu)
    gd_ref[0, 0] = dot_tn(hid[...], ct_ref[...]).astype(BF)
    for part, keep, send, bit in ((dg, gk_ref, gs_ref, bits[0]), (du, uk_ref, us_ref, bits[1])):
        grad = dot_tn(xn_ref[...], part[...]).astype(BF)

        @pl.when(bit == 0)
        def _():
            keep[0] = grad[:HALF_ROWS]
            send[0] = grad[HALF_ROWS:]

        @pl.when(bit == 1)
        def _():
            keep[0] = grad[HALF_ROWS:]
            send[0] = grad[:HALF_ROWS]

    @pl.when(j == pl.num_programs(0) - 1)
    def _():
        out_ref[...] = acc_o[...].astype(BF)
        gx_ref[...] = acc_g[...].astype(BF)


def ffn_call(xn, ct, wg, wu, wd, bits):
    rows, dim = xn.shape
    hidden = wd.shape[0]
    blk = 256
    full = pl.BlockSpec((rows, dim), lambda j, b: (0, 0))
    colw = pl.BlockSpec((dim, blk), lambda j, b: (0, j))
    roww = pl.BlockSpec((blk, dim), lambda j, b: (j, 0))
    grad = pl.BlockSpec((1, HALF_ROWS, blk), lambda j, b: (j // 4, 0, lax.rem(j, 4)))

    def down_at(j, b):
        group = j // 4
        half = lax.rem(j, 4) // 2
        bit = jnp.where(group == 0, b[0], b[1])
        return (jnp.where(half == bit, 0, 1), group, lax.rem(j, 2), 0)

    return pl.pallas_call(
        ffn_body,
        grid_spec=pltpu.PrefetchScalarGridSpec(
            num_scalar_prefetch=1,
            grid=(hidden // blk,),
            in_specs=[full, full, colw, colw, roww],
            out_specs=[full, full, pl.BlockSpec((1, 1, blk, dim), down_at), grad, grad, grad, grad],
            scratch_shapes=[pltpu.VMEM((rows, dim), F32)] * 2 + [pltpu.VMEM((rows, blk), BF)] * 3,
        ),
        out_shape=[
            jax.ShapeDtypeStruct((rows, dim), BF),
            jax.ShapeDtypeStruct((rows, dim), BF),
            jax.ShapeDtypeStruct((2, 2, HALF_ROWS, dim), BF),
        ]
        + [jax.ShapeDtypeStruct((2, HALF_ROWS, dim), BF)] * 4,
        compiler_params=pltpu.CompilerParams(vmem_limit_bytes=VMEM_LIMIT),
        name="ffn",
    )(bits, xn, ct, wg, wu, wd)


def pair_rows(w):
    dim, two, width = w.shape
    return jnp.transpose(w.reshape(dim, two, width // LANES, LANES), (0, 2, 1, 3)).reshape(-1, LANES)


def split_body(w_ref, wg_ref, wu_ref, wide):
    rows = wg_ref.shape[0]
    tiles = wg_ref.shape[1] // LANES
    wide[...] = w_ref[...].astype(F32)
    for c, out in ((0, wg_ref), (1, wu_ref)):
        for s in range(tiles):
            out[:, s * LANES : (s + 1) * LANES] = wide[pl.ds(2 * s + c, rows, stride=2 * tiles), :].astype(BF)


def split_call(w):
    dim, _, width = w.shape
    blk = 64
    flat = blk * 2 * width // LANES
    return pl.pallas_call(
        split_body,
        grid=(dim // blk,),
        out_shape=[jax.ShapeDtypeStruct((dim, width), BF)] * 2,
        in_specs=[pl.BlockSpec((flat, LANES), lambda i: (i, 0))],
        out_specs=[pl.BlockSpec((blk, width), lambda i: (i, 0))] * 2,
        scratch_shapes=[pltpu.VMEM((flat, LANES), F32)],
        compiler_params=pltpu.CompilerParams(vmem_limit_bytes=VMEM_LIMIT),
        name="split_gate_up",
    )(pair_rows(w))


def join_body(a_ref, b_ref, out_ref):
    rows = a_ref.shape[2]
    tiles = WIDE // LANES
    for f in range(2):
        for s in range(tiles):
            for c, src in ((0, a_ref), (1, b_ref)):
                at = (f * tiles + s) * 2 + c
                out_ref[pl.ds(at, rows, stride=4 * tiles), :] = src[0, f, :, s * LANES : (s + 1) * LANES].astype(F32)


def join_call(a, b):
    blk = 64
    tiles = 4 * WIDE // LANES
    half = pl.BlockSpec((1, 2, blk, WIDE), lambda i: (i // (HALF_ROWS // blk), 0, lax.rem(i, HALF_ROWS // blk), 0))
    flat = pl.pallas_call(
        join_body,
        grid=(2 * HALF_ROWS // blk,),
        out_shape=jax.ShapeDtypeStruct((2 * HALF_ROWS * tiles, LANES), F32),
        in_specs=[half, half],
        out_specs=pl.BlockSpec((blk * tiles, LANES), lambda i: (i, 0)),
        compiler_params=pltpu.CompilerParams(vmem_limit_bytes=VMEM_LIMIT),
        name="join_gate_up",
    )(a, b)
    split = flat.reshape(2 * HALF_ROWS, tiles // 2, 2, LANES)
    return jnp.transpose(split, (0, 2, 1, 3)).reshape(2 * HALF_ROWS, 2, 2 * WIDE)


def norm_back(rows_now, gain, grads):
    inv = lax.rsqrt(jnp.mean(rows_now * rows_now, axis=-1, keepdims=True) + EPSILON)
    scaled = grads * gain
    gain_grad = jnp.sum(grads * rows_now * inv, axis=0, keepdims=True)
    back = inv * scaled - rows_now * (inv * inv * inv) * jnp.mean(scaled * rows_now, axis=-1, keepdims=True)
    return back, gain_grad


def ffn_back_body(
    gx_ref, fo_ref, mid_ref, ct_ref, gain_ref, w_ref, out_ref, gm_ref, do_ref, gg_ref, gx_in, fo_in, ssem, rsem
):
    peer = partner_barrier()
    rows = mid_ref.shape[0]
    blk = rows // CHUNKS
    copies = []
    for n, (src, dst) in enumerate(((gx_ref, gx_in), (fo_ref, fo_in))):
        for c in range(CHUNKS):
            at = n * CHUNKS + c
            copy = send_rows(src, dst, pl.ds(c * blk, blk), ssem.at[at], rsem.at[at], peer)
            copy.start()
            copies.append(copy)
    gain_sum = jnp.zeros((1, mid_ref.shape[1]), F32)
    for c in range(CHUNKS):
        sl = slice(c * blk, (c + 1) * blk)
        copies[c].wait_recv()
        grads = gx_ref[sl, :].astype(F32) + gx_in[sl, :].astype(F32)
        back, gain_grad = norm_back(mid_ref[sl, :], gain_ref[...], grads)
        gain_sum = gain_sum + gain_grad
        gm = ct_ref[sl, :].astype(F32) + back
        gm_ref[sl, :] = gm
        do_ref[sl, :] = dot_nt(gm.astype(BF), w_ref[...]).astype(BF)
    gg_ref[...] = gain_sum
    for c in range(CHUNKS):
        sl = slice(c * blk, (c + 1) * blk)
        copies[CHUNKS + c].wait_recv()
        out_ref[sl, :] = (mid_ref[sl, :] + (fo_ref[sl, :].astype(F32) + fo_in[sl, :].astype(F32))).astype(BF)
    for copy in copies:
        copy.wait_send()


def ffn_back_call(gx, fo, mid, ct, gain, w):
    rows, dim = mid.shape
    width = w.shape[0]
    return pl.pallas_call(
        ffn_back_body,
        out_shape=[
            jax.ShapeDtypeStruct((rows, dim), BF),
            jax.ShapeDtypeStruct((rows, dim), F32),
            jax.ShapeDtypeStruct((rows, width), BF),
            jax.ShapeDtypeStruct((1, dim), F32),
        ],
        in_specs=[whole_spec()] * 6,
        out_specs=[whole_spec()] * 4,
        scratch_shapes=[
            pltpu.VMEM((rows, dim), BF),
            pltpu.VMEM((rows, dim), BF),
            pltpu.SemaphoreType.DMA((2 * CHUNKS,)),
            pltpu.SemaphoreType.DMA((2 * CHUNKS,)),
        ],
        compiler_params=pltpu.CompilerParams(collective_id=2, has_side_effects=True, vmem_limit_bytes=VMEM_LIMIT),
        name="ffn_back",
    )(gx, fo, mid, ct, gain, w)


def qkv_back_body(
    dq_ref, dk_ref, dv_ref, w_ref, xn_ref, x_ref, gain_ref, gm_ref, at_ref,
    ig_ref, qk_ref, vo_ref, gg_ref, mine, theirs, ssem, rsem,
):
    peer = partner_barrier()
    rows = x_ref.shape[0]
    blk = rows // CHUNKS
    width = dq_ref.shape[1]
    copies = []
    for c in range(CHUNKS):
        sl = slice(c * blk, (c + 1) * blk)
        total = dot_nt(dq_ref[sl, :], w_ref[0])
        total = total + dot_nt(dk_ref[sl, :], w_ref[1])
        total = total + dot_nt(dv_ref[sl, :], w_ref[2])
        mine[sl, :] = total.astype(BF)
        copy = send_rows(mine, theirs, pl.ds(c * blk, blk), ssem.at[c], rsem.at[c], peer)
        copy.start()
        copies.append(copy)
    qk_ref[:, :width] = dot_tn(xn_ref[...], dq_ref[...]).astype(BF)
    qk_ref[:, width:] = dot_tn(xn_ref[...], dk_ref[...]).astype(BF)
    grad_v = dot_tn(xn_ref[...], dv_ref[...]).astype(BF)
    vo_ref[:HALF_ROWS, :width] = grad_v[:HALF_ROWS]
    vo_ref[:HALF_ROWS, width:] = grad_v[HALF_ROWS:]
    vo_ref[HALF_ROWS:, :] = dot_tn(at_ref[...], gm_ref[...].astype(BF)).astype(BF)
    gain_sum = jnp.zeros((1, x_ref.shape[1]), F32)
    for c in range(CHUNKS):
        sl = slice(c * blk, (c + 1) * blk)
        copies[c].wait_recv()
        grads = mine[sl, :].astype(F32) + theirs[sl, :].astype(F32)
        back, gain_grad = norm_back(x_ref[sl, :].astype(F32), gain_ref[...], grads)
        gain_sum = gain_sum + gain_grad
        ig_ref[sl, :] = gm_ref[sl, :] + back
    gg_ref[...] = gain_sum
    for copy in copies:
        copy.wait_send()


def qkv_back_call(dq, dk, dv, w, xn, x, gain, gm, at):
    rows, dim = x.shape
    return pl.pallas_call(
        qkv_back_body,
        out_shape=[
            jax.ShapeDtypeStruct((rows, dim), F32),
            jax.ShapeDtypeStruct((dim, dim), BF),
            jax.ShapeDtypeStruct((dim, dim), BF),
            jax.ShapeDtypeStruct((1, dim), F32),
        ],
        in_specs=[whole_spec()] * 9,
        out_specs=[whole_spec()] * 4,
        scratch_shapes=[
            pltpu.VMEM((rows, dim), BF),
            pltpu.VMEM((rows, dim), BF),
            pltpu.SemaphoreType.DMA((CHUNKS,)),
            pltpu.SemaphoreType.DMA((CHUNKS,)),
        ],
        compiler_params=pltpu.CompilerParams(collective_id=3, has_side_effects=True, vmem_limit_bytes=VMEM_LIMIT),
        name="qkv_back",
    )(dq, dk, dv, w, xn, x, gain, gm, at)


def peers_of(dp):
    z = dp // 4
    y = (dp // 2) % 2
    x = dp % 2
    at = lambda zz, yy, xx: zz * 4 + yy * 2 + xx
    return z, y, x, at(z, y, 1 - x), at(z, 1 - y, x), at(z + 1 - 2 * (z % 2), y, x), at(3 - z, y, x)


def sum_body(
    gk, rg, uk, ru, dk, rda, rdb, qk, vo, small_in, out_a, out_b, small_out,
    L, S, Z, R, Y, F, sb, st, loc, s1s, s1r, sends, zr, rr, yr, ar, xr, lo, ss, sr,
):
    dp = lax.axis_index("dp")
    t = lax.axis_index("tensor")
    z, y, x, px, py, zn, mm = peers_of(dp)
    is_mid = (z == 1) | (z == 2)
    is_end = (z == 0) | (z == 3)
    mine = jnp.where(z == 2, WIDE // 2, 0)
    others = WIDE // 2 - mine
    n = GROUP_ROWS // ROWS
    first = (px, py)
    last = (py, px)
    outs = (out_a, out_b)
    owner = (x, y)

    def remote(src, dst, ssem, rsem, peer):
        return pltpu.make_async_remote_copy(
            src_ref=src, dst_ref=dst, send_sem=ssem, recv_sem=rsem, device_id=(peer, t), device_id_type=MESH
        )

    def loads(g, b):
        rows = pl.ds(b * HALF_ROWS, HALF_ROWS)
        if b < 2:
            srcs = ((gk, uk)[g].at[b], (rg, ru)[g].at[b])
        elif b == 2:
            srcs = (dk.at[0, g], (rda, rdb)[g].at[...])
        else:
            srcs = ((qk, vo)[g].at[pl.ds(pl.multiple_of(owner[g] * HALF_ROWS, HALF_ROWS), HALF_ROWS)],)
        return [
            pltpu.make_async_copy(src, (L, S)[k].at[g, rows], loc.at[g, b, k]) for k, src in enumerate(srcs)
        ]

    for b in range(4):
        for g in range(2):
            for copy in loads(g, b):
                copy.start()

    barrier = pltpu.get_barrier_semaphore()
    others_z = [lax.rem(z + k, 4) * 4 + y * 2 + x for k in range(1, 4)]
    for peer in [px, py] + others_z:
        pl.semaphore_signal(barrier, inc=1, device_id=(peer, t), device_id_type=MESH)
    pl.semaphore_wait(barrier, 5)

    def first_exchange(g):
        away = pl.ds(pl.multiple_of((1 - owner[g]) * HALF_ROWS, HALF_ROWS), HALF_ROWS)
        return remote(
            (qk, vo)[g].at[away], S.at[g, pl.ds(3 * HALF_ROWS, HALF_ROWS)], s1s.at[g], s1r.at[g], first[g]
        )

    small_x = remote(small_in, sb.at[0], ss.at[0], sr.at[0], px)
    small_y = remote(st.at[0], sb.at[1], ss.at[1], sr.at[1], py)
    small_z = [remote(st.at[1], sb.at[2 + z], ss.at[2 + k], sr.at[2 + z], others_z[k]) for k in range(3)]
    small_x.start()
    for g in range(2):
        first_exchange(g).start()

    def rows_of(i):
        return pl.ds(pl.multiple_of(i * ROWS, ROWS), ROWS)

    def cols_of(at):
        return pl.ds(pl.multiple_of(at, WIDE // 2), WIDE // 2)

    def z_copy(g, i):
        return remote(L.at[g, rows_of(i)], Z.at[g, rows_of(i)], sends.at[g, 0], zr.at[g, i], zn)

    def r_copy(g, i):
        return remote(L.at[g, rows_of(i), cols_of(others)], R.at[g, rows_of(i)], sends.at[g, 1], rr.at[g, i], mm)

    def y_copy(g, i):
        return remote(R.at[g, rows_of(i)], Y.at[g, rows_of(i)], sends.at[g, 2], yr.at[g, i], last[g])

    def a_copy(g, i, at):
        return remote(F.at[g, rows_of(i), cols_of(at)], F.at[g, rows_of(i), cols_of(at)], sends.at[g, 3], ar.at[g, i], mm)

    def o_copy(g, i):
        return remote(F.at[g, rows_of(i)], F.at[g, rows_of(i)], sends.at[g, 4], zr.at[g, i], zn)

    def x_copy(g, i):
        return remote(F.at[g, rows_of(i)], outs[g].at[owner[g], rows_of(i)], sends.at[g, 5], xr.at[g], first[g])

    def l_copy(g, i):
        return pltpu.make_async_copy(F.at[g, rows_of(i)], outs[g].at[owner[g], rows_of(i)], lo.at[g])

    def body(i, carry):
        @pl.when((i < n) & (lax.rem(i, n // 4) == 0))
        def _():
            for b in range(4):
                @pl.when(i == b * (n // 4))
                def _():
                    for g in range(2):
                        for copy in loads(g, b):
                            copy.wait()
                        if b == 3:
                            first_exchange(g).wait_recv()

        @pl.when(is_end & (i < n))
        def _():
            for g in range(2):
                r = rows_of(i)
                L[g, r, :] = (L[g, r, :].astype(F32) + S[g, r, :].astype(F32)).astype(BF)
                z_copy(g, i).start()

        @pl.when(is_mid)
        def _():
            j = i - 4 * LAG

            @pl.when((j >= 0) & (j < n))
            def _():
                for g in range(2):
                    a_copy(g, j, others).wait_recv()
                    o_copy(g, j).start()
                    x_copy(g, j).start()
                    l_copy(g, j).start()

            j3 = i - 3 * LAG

            @pl.when((j3 >= 0) & (j3 < n))
            def _():
                for g in range(2):
                    y_copy(g, j3).wait_recv()
                    r = rows_of(j3)
                    F[g, r, cols_of(mine)] = (R[g, r, :].astype(F32) + Y[g, r, :].astype(F32)).astype(BF)
                    a_copy(g, j3, mine).start()

            j2 = i - 2 * LAG

            @pl.when((j2 >= 0) & (j2 < n))
            def _():
                for g in range(2):
                    r_copy(g, j2).wait_recv()
                    r = rows_of(j2)
                    R[g, r, :] = (R[g, r, :].astype(F32) + L[g, r, cols_of(mine)].astype(F32)).astype(BF)
                    y_copy(g, j2).start()

            j1 = i - LAG

            @pl.when((j1 >= 0) & (j1 < n))
            def _():
                for g in range(2):
                    z_copy(g, j1).wait_recv()
                    r = rows_of(j1)
                    L[g, r, :] = (L[g, r, :].astype(F32) + S[g, r, :].astype(F32) + Z[g, r, :].astype(F32)).astype(BF)
                    r_copy(g, j1).start()

        @pl.when(is_end)
        def _():
            j = i - 5 * LAG

            @pl.when((j >= 0) & (j < n))
            def _():
                for g in range(2):
                    o_copy(g, j).wait_recv()
                    x_copy(g, j).start()
                    l_copy(g, j).start()

        @pl.when(i == n // 8)
        def _():
            small_x.wait_recv()
            st[0] = small_in[...] + sb[0]
            small_y.start()

        @pl.when(i == n // 4)
        def _():
            small_y.wait_recv()
            st[1] = st[0] + sb[1]
            for copy in small_z:
                copy.start()

        return carry

    lax.fori_loop(0, n + 5 * LAG, body, 0)

    for k in range(3):
        remote(st.at[1], sb.at[2 + lax.rem(z + k + 1, 4)], ss.at[2 + k], sr.at[2 + lax.rem(z + k + 1, 4)], others_z[k]).wait_recv()
    sb[2 + z] = st[1]
    small_out[...] = (sb[2] + sb[3]) + (sb[4] + sb[5])

    small_x.wait_send()
    small_y.wait_send()
    for copy in small_z:
        copy.wait_send()
    for g in range(2):
        first_exchange(g).wait_send()
        away = 1 - owner[g]

        @pl.when(is_end)
        def _():
            remote(L.at[g], Z.at[g], sends.at[g, 0], zr.at[g, 0], zn).wait_send()

        @pl.when(is_mid)
        def _():
            half = pl.ds(0, WIDE // 2)
            remote(R.at[g], Y.at[g], sends.at[g, 1], rr.at[g, 0], mm).wait_send()
            remote(R.at[g], Y.at[g], sends.at[g, 2], yr.at[g, 0], last[g]).wait_send()
            remote(R.at[g], Y.at[g], sends.at[g, 3], ar.at[g, 0], mm).wait_send()
            remote(F.at[g], F.at[g], sends.at[g, 4], zr.at[g, 0], zn).wait_send()

        whole = remote(F.at[g], outs[g].at[away], sends.at[g, 5], xr.at[g], first[g])
        whole.wait_send()
        whole.wait_recv()
        pltpu.make_async_copy(F.at[g], outs[g].at[owner[g]], lo.at[g]).wait()


def sum_call(gk, rg, uk, ru, dk, rda, rdb, qk, vo, small):
    any_spec = pl.BlockSpec(memory_space=pl.ANY)
    n = GROUP_ROWS // ROWS
    full = pltpu.VMEM((2, GROUP_ROWS, WIDE), BF)
    half = pltpu.VMEM((2, GROUP_ROWS, WIDE // 2), BF)
    dma = pltpu.SemaphoreType.DMA
    return pl.pallas_call(
        sum_body,
        out_shape=[jax.ShapeDtypeStruct((2, GROUP_ROWS, WIDE), BF)] * 2 + [jax.ShapeDtypeStruct((SMALL, WIDE), F32)],
        in_specs=[any_spec] * 9 + [whole_spec()],
        out_specs=[any_spec] * 2 + [whole_spec()],
        scratch_shapes=[
            full, full, full, half, half, full,
            pltpu.VMEM((6, SMALL, WIDE), F32),
            pltpu.VMEM((2, SMALL, WIDE), F32),
            dma((2, 4, 2)), dma((2,)), dma((2,)), dma((2, 6)),
            dma((2, n)), dma((2, n)), dma((2, n)), dma((2, n)),
            dma((2,)), dma((2,)), dma((5,)), dma((6,)),
        ],
        compiler_params=pltpu.CompilerParams(collective_id=4, has_side_effects=True, vmem_limit_bytes=VMEM_LIMIT),
        name="grad_sum",
    )(gk, rg, uk, ru, dk, rda, rdb, qk, vo, small)


def first_swap(sends, bit):
    pairs = [(d, d ^ bit) for d in range(16)]
    return [lax.ppermute(s, "dp", pairs) for s in sends]


def tables(time_ids):
    half = HEAD // 2
    freqs = jnp.exp(jnp.arange(half, dtype=F32) * (-2.0 * math.log(10000.0) / HEAD))
    angles = time_ids.astype(F32)[:, None] * freqs[None, :]
    cosine = jnp.cos(angles)
    sine = jnp.sin(angles)
    return jnp.tile(cosine, (1, 4)), jnp.tile(jnp.concatenate([-sine, sine], axis=1), (1, 2))


def mask_tables(segments, variates, head_bias):
    lane = jnp.arange(LANES)[None, :]
    var_here = (lane % VAR_COLS == variates[:, None]) & (lane < 3 * VAR_COLS)
    seg_here = (lane - SEG_COL == segments[:, None]) & (lane >= SEG_COL) & (lane < ONE_COL)
    seg_cols = (lane >= SEG_COL) & (lane < ONE_COL)
    ones = (lane >= ONE_COL) & (lane < ONE_COL + 3)
    base = jnp.where(var_here, 1.0, 0.0)
    segq = jnp.where(seg_cols & ~seg_here, MASKED, 0.0)
    extk = jnp.where(var_here | seg_here | ones, 1.0, 0.0).astype(BF)
    gap = head_bias[0] - head_bias[1]
    hi = lax.reduce_precision(gap, 8, 7)
    mid = lax.reduce_precision(gap - hi, 8, 7)
    low = gap - hi - mid
    kind = lane // VAR_COLS
    rows = jnp.where(kind == 0, hi[:, None], jnp.where(kind == 1, mid[:, None], jnp.where(kind == 2, low[:, None], 0.0)))
    match = jnp.arange(8)[:, None] == variates[None, :]
    valid = jnp.arange(8)[:, None] < VAR_COLS
    onehot = jnp.stack([jnp.where(match, 1.0, 0.0), jnp.where(valid & ~match, 1.0, 0.0)])
    return base, segq, extk, rows.reshape(-1, 2, LANES), onehot


def fast_local(
    block_input, segments, variates, time_ids, attn_gain, w_qkv, head_bias, w_out, ffn_gain, w_gate_up, w_down, cotangent
):
    dp = lax.axis_index("dp")
    bits = jnp.stack([dp % 2, (dp // 2) % 2]).astype(jnp.int32)
    w3 = jnp.transpose(w_qkv, (1, 0, 2))
    cosine, sine = tables(time_ids)
    base, segq, extk, bias_rows, onehot = mask_tables(segments, variates, head_bias)
    gain1 = attn_gain[None, :]
    gain2 = ffn_gain[None, :]
    wg, wu = split_call(w_gate_up)
    xn, q, k, v = qkv_call(block_input, gain1, w3, cosine, sine)
    attended, o32, extq = attn_fwd_call(q, k, v, base, segq, extk, bias_rows)
    mid, xn2 = attn_out_call(block_input, attended, w_out, gain2)
    ffn_part, gx_part, down, gk, gs, uk, us = ffn_call(xn2, cotangent, wg, wu, w_down, bits)
    rg, rda = first_swap([gs, down[1, 0]], 1)
    ru, rdb = first_swap([us, down[1, 1]], 2)
    block_output, grad_mid, do, g_gain2 = ffn_back_call(gx_part, ffn_part, mid, cotangent, gain2, w_out)
    dq, dk, dv, gb = attn_bwd_call(q, k, v, do, o32, extq, extk, onehot, cosine, sine)
    input_grad, qk, vo, g_gain1 = qkv_back_call(dq, dk, dv, w3, xn, block_input, gain1, grad_mid, attended)
    g_bias = jnp.sum(gb, axis=(3, 4)).reshape(-1, 2).T
    heads = g_bias.shape[1]
    bias_row = jnp.pad(g_bias.reshape(1, -1), ((0, 0), (0, WIDE - 2 * heads)))
    small = jnp.concatenate([g_gain1, g_gain2, bias_row, jnp.zeros((SMALL - 3, WIDE), F32)], axis=0)
    sum_a, sum_b, small = sum_call(gk, rg, uk, ru, down, rda, rdb, qk, vo, small)
    sum_a = sum_a.reshape(2, 4, HALF_ROWS, WIDE)
    sum_b = sum_b.reshape(2, 4, HALF_ROWS, WIDE)
    width = w_qkv.shape[2]
    g_gate_up = join_call(sum_a, sum_b)
    g_down = jnp.stack([sum_a[:, 2], sum_b[:, 2]]).astype(F32).reshape(w_down.shape)
    qk = sum_a[:, 3].reshape(2 * HALF_ROWS, WIDE)
    v_rows = sum_b[0, 3]
    v_cols = jnp.concatenate([v_rows[:, :width], v_rows[:, width:]], axis=0)
    g_qkv = jnp.stack([qk[:, :width], qk[:, width:], v_cols]).astype(F32)
    g_out = sum_b[1, 3].astype(F32)
    g_bias = small[2, : 2 * heads].reshape(2, heads)
    return (
        block_output, input_grad, small[0], jnp.transpose(g_qkv, (1, 0, 2)), g_bias, g_out, small[1], g_gate_up, g_down,
    )


def rope_tables(time_ids, head_dim):
    half_dim = head_dim // 2
    freqs = jnp.exp(jnp.arange(half_dim, dtype=jnp.float32) * (-2.0 * math.log(10000.0) / head_dim))
    angles = time_ids.astype(jnp.float32)[:, None] * freqs[None, :]
    return (jnp.cos(angles)[:, None, :], jnp.sin(angles)[:, None, :])


def rotate(vectors, cosine, sine_part):
    half_dim = vectors.shape[-1] // 2
    first_half = vectors[..., :half_dim]
    second_half = vectors[..., half_dim:]
    return jnp.concatenate(
        [
            first_half * cosine - second_half * sine_part,
            second_half * cosine + first_half * sine_part,
        ],
        axis=-1,
    )


def rotate_back(grads, cosine, sine_part):
    half_dim = grads.shape[-1] // 2
    first_half = grads[..., :half_dim]
    second_half = grads[..., half_dim:]
    return jnp.concatenate(
        [
            first_half * cosine + second_half * sine_part,
            second_half * cosine - first_half * sine_part,
        ],
        axis=-1,
    )


def norm_rows(rows_now, gain):
    inverse = lax.rsqrt(jnp.mean(rows_now * rows_now, axis=-1, keepdims=True) + EPSILON)
    return (rows_now * inverse * gain, inverse)


def plain_norm_back(rows_now, inverse, gain, grads):
    scaled = grads * gain
    gain_grad = jnp.sum(grads * rows_now * inverse, axis=0)
    rows_grad = inverse * scaled - rows_now * (inverse * inverse * inverse) * jnp.mean(
        scaled * rows_now, axis=-1, keepdims=True
    )
    return (rows_grad, gain_grad)


def scores_of(queries, keys_rot, same_var, allowed, head_bias, score_scale):
    raw_scores = (
        jnp.einsum("sqhd,skhd->shqk", queries, keys_rot, preferred_element_type=jnp.float32)
        * score_scale
    )
    biased = raw_scores + jnp.where(
        same_var[:, None], head_bias[0][None, :, None, None], head_bias[1][None, :, None, None]
    )
    return jnp.where(allowed[:, None], biased, MASKED)


def plain_local(
    block_input,
    segments,
    variates,
    time_ids,
    attn_gain,
    w_qkv,
    head_bias,
    w_out,
    ffn_gain,
    w_gate_up,
    w_down,
    cotangent,
):
    row_count = block_input.shape[0]
    heads_here = head_bias.shape[1]
    head_dim = w_qkv.shape[2] // heads_here
    seq_count = row_count // LEN
    score_scale = head_dim ** (-0.5)
    input_rows = block_input.astype(jnp.float32)
    attn_normed, attn_inverse = norm_rows(input_rows, attn_gain)
    attn_normed_low = attn_normed.astype(jnp.bfloat16)
    projected = jnp.einsum(
        "td,dck->tck", attn_normed_low, w_qkv, preferred_element_type=jnp.float32
    )
    cosine, sine_part = rope_tables(time_ids, head_dim)
    head_shape = (row_count, heads_here, head_dim)
    seq_shape = (seq_count, LEN, heads_here, head_dim)
    queries = (
        rotate(projected[:, 0].reshape(head_shape), cosine, sine_part)
        .astype(jnp.bfloat16)
        .reshape(seq_shape)
    )
    keys_rot = (
        rotate(projected[:, 1].reshape(head_shape), cosine, sine_part)
        .astype(jnp.bfloat16)
        .reshape(seq_shape)
    )
    values = projected[:, 2].astype(jnp.bfloat16).reshape(seq_shape)
    seg_ids = segments.reshape(seq_count, LEN)
    var_ids = variates.reshape(seq_count, LEN)
    allowed = seg_ids[:, :, None] == seg_ids[:, None, :]
    same_var = var_ids[:, :, None] == var_ids[:, None, :]
    scores = scores_of(queries, keys_rot, same_var, allowed, head_bias, score_scale)
    row_max = jnp.max(scores, axis=-1, keepdims=True)
    exp_total = jnp.sum(jnp.exp(scores - row_max), axis=-1, keepdims=True)
    log_total = row_max + jnp.log(exp_total)
    probs_low = jnp.exp(scores - log_total).astype(jnp.bfloat16)
    attended = jnp.einsum("shqk,skhd->sqhd", probs_low, values, preferred_element_type=jnp.float32)
    attended = attended.reshape(row_count, heads_here * head_dim).astype(jnp.bfloat16)
    attn_branch = lax.psum(
        jnp.dot(attended, w_out, preferred_element_type=jnp.float32).astype(jnp.bfloat16), "tensor"
    ).astype(jnp.float32)
    mid_rows = input_rows + attn_branch
    ffn_normed, ffn_inverse = norm_rows(mid_rows, ffn_gain)
    ffn_normed_low = ffn_normed.astype(jnp.bfloat16)
    gate_up = jnp.einsum(
        "td,dcf->tcf", ffn_normed_low, w_gate_up, preferred_element_type=jnp.float32
    )
    gate_vals = gate_up[:, 0]
    up_vals = gate_up[:, 1]
    sigmoid_gate = jax.nn.sigmoid(gate_vals)
    silu_gate = gate_vals * sigmoid_gate
    hidden_low = (silu_gate * up_vals).astype(jnp.bfloat16)
    ffn_branch = lax.psum(
        jnp.dot(hidden_low, w_down, preferred_element_type=jnp.float32).astype(jnp.bfloat16),
        "tensor",
    ).astype(jnp.float32)
    block_output = (mid_rows + ffn_branch).astype(jnp.bfloat16)
    grad_down = jnp.einsum("tf,td->fd", hidden_low, cotangent, preferred_element_type=jnp.float32)
    grad_hidden = jnp.einsum("td,fd->tf", cotangent, w_down, preferred_element_type=jnp.float32)
    grad_gate = grad_hidden * up_vals * sigmoid_gate * (1.0 + gate_vals * (1.0 - sigmoid_gate))
    grad_up = grad_hidden * silu_gate
    grad_gate_up = jnp.stack([grad_gate, grad_up], axis=1).astype(jnp.bfloat16)
    grad_w_gate_up = jnp.einsum(
        "td,tcf->dcf", ffn_normed_low, grad_gate_up, preferred_element_type=jnp.float32
    )
    grad_ffn_normed = lax.psum(
        jnp.einsum(
            "tcf,dcf->td", grad_gate_up, w_gate_up, preferred_element_type=jnp.float32
        ).astype(jnp.bfloat16),
        "tensor",
    ).astype(jnp.float32)
    norm_grad_mid, grad_ffn_gain = plain_norm_back(mid_rows, ffn_inverse, ffn_gain, grad_ffn_normed)
    grad_mid = cotangent.astype(jnp.float32) + norm_grad_mid
    grad_branch = grad_mid.astype(jnp.bfloat16)
    grad_w_out = jnp.einsum("tk,td->kd", attended, grad_branch, preferred_element_type=jnp.float32)
    grad_attended = jnp.einsum("td,kd->tk", grad_branch, w_out, preferred_element_type=jnp.float32)
    grad_attended = grad_attended.astype(jnp.bfloat16).reshape(seq_shape)
    scores_again = scores_of(queries, keys_rot, same_var, allowed, head_bias, score_scale)
    probs_again = jnp.exp(scores_again - log_total)
    probs_again_low = probs_again.astype(jnp.bfloat16)
    grad_probs = jnp.einsum(
        "sqhd,skhd->shqk", grad_attended, values, preferred_element_type=jnp.float32
    )
    grad_values = jnp.einsum(
        "shqk,sqhd->skhd", probs_again_low, grad_attended, preferred_element_type=jnp.float32
    )
    grad_scores = probs_again * (
        grad_probs - jnp.sum(probs_again * grad_probs, axis=-1, keepdims=True)
    )
    grad_scores_low = grad_scores.astype(jnp.bfloat16)
    same_low = same_var.astype(jnp.bfloat16)
    other_low = jnp.logical_not(same_var).astype(jnp.bfloat16)
    grad_bias = jnp.stack(
        [
            jnp.einsum(
                "shqk,sqk->h", grad_scores_low, same_low, preferred_element_type=jnp.float32
            ),
            jnp.einsum(
                "shqk,sqk->h", grad_scores_low, other_low, preferred_element_type=jnp.float32
            ),
        ],
        axis=0,
    )
    grad_queries = (
        jnp.einsum("shqk,skhd->sqhd", grad_scores_low, keys_rot, preferred_element_type=jnp.float32)
        * score_scale
    )
    grad_keys = (
        jnp.einsum("shqk,sqhd->skhd", grad_scores_low, queries, preferred_element_type=jnp.float32)
        * score_scale
    )
    grad_query_lin = rotate_back(grad_queries.reshape(head_shape), cosine, sine_part).reshape(
        row_count, heads_here * head_dim
    )
    grad_key_lin = rotate_back(grad_keys.reshape(head_shape), cosine, sine_part).reshape(
        row_count, heads_here * head_dim
    )
    grad_value_lin = grad_values.reshape(row_count, heads_here * head_dim)
    grad_projected = jnp.stack([grad_query_lin, grad_key_lin, grad_value_lin], axis=1).astype(
        jnp.bfloat16
    )
    grad_w_qkv = jnp.einsum(
        "td,tck->dck", attn_normed_low, grad_projected, preferred_element_type=jnp.float32
    )
    grad_attn_normed = lax.psum(
        jnp.einsum("tck,dck->td", grad_projected, w_qkv, preferred_element_type=jnp.float32).astype(
            jnp.bfloat16
        ),
        "tensor",
    ).astype(jnp.float32)
    norm_grad_input, grad_attn_gain = plain_norm_back(
        input_rows, attn_inverse, attn_gain, grad_attn_normed
    )
    input_grad = grad_mid + norm_grad_input
    grad_attn_gain, grad_w_qkv, grad_bias, grad_w_out, grad_ffn_gain, grad_w_gate_up, grad_down = (
        lax.psum(
            (
                grad_attn_gain,
                grad_w_qkv,
                grad_bias,
                grad_w_out,
                grad_ffn_gain,
                grad_w_gate_up,
                grad_down,
            ),
            "dp",
        )
    )
    return (
        block_output,
        input_grad,
        grad_attn_gain,
        grad_w_qkv,
        grad_bias,
        grad_w_out,
        grad_ffn_gain,
        grad_w_gate_up,
        grad_down,
    )


def solution(mesh):
    placed = (
        P("dp", None), P("dp"), P("dp"), P("dp"), P(), P(None, None, "tensor"), P(None, "tensor"),
        P("tensor", None), P(), P(None, None, "tensor"), P("tensor", None), P("dp", None),
    )
    fast = (mesh.shape["dp"], mesh.shape["tensor"]) == (16, 2)
    return jax.shard_map(
        fast_local if fast else plain_local,
        mesh=mesh,
        in_specs=placed,
        out_specs=(
            P("dp", None), P("dp", None), P(), P(None, None, "tensor"), P(None, "tensor"), P("tensor", None), P(),
            P(None, None, "tensor"), P("tensor", None),
        ),
        check_vma=False,
    )
```

```python
import functools
import math

import jax
import jax.numpy as jnp
from jax import lax
from jax.experimental import pallas as pl
from jax.experimental.pallas import tpu as pltpu
from jax.sharding import PartitionSpec as P

LEN = 1024
EPSILON = 1e-05
MASKED = -1000000000.0
BF = jnp.bfloat16
F32 = jnp.float32
MESH = pl.DeviceIdType.MESH
VMEM_LIMIT = 60 * 1024 * 1024
LANES = 128
HEAD = 64
VAR_COLS = 4
SEG_COL = 12
ONE_COL = 20
ROWS = 16
LAG = 3
HALF_ROWS = 512
GROUP_ROWS = 4 * HALF_ROWS
WIDE = 1024
SMALL = 8
FFN_ROWS = 256
FFN_COLS = 512


def dot_nn(a, b):
    return lax.dot_general(a, b, (((1,), (0,)), ((), ())), preferred_element_type=F32)


def dot_nt(a, b):
    return lax.dot_general(a, b, (((1,), (1,)), ((), ())), preferred_element_type=F32)


def dot_tn(a, b):
    return lax.dot_general(a, b, (((0,), (0,)), ((), ())), preferred_element_type=F32)


def whole_spec():
    return pl.BlockSpec(memory_space=pltpu.VMEM)


def split3(v):
    hi = v.astype(BF).astype(F32)
    mid = (v - hi).astype(BF).astype(F32)
    return hi, mid, v - hi - mid


def half_swap(u):
    lane = lax.broadcasted_iota(jnp.int32, u.shape, 1) % HEAD
    return jnp.where(lane < HEAD // 2, pltpu.roll(u, LANES - HEAD // 2, 1), pltpu.roll(u, HEAD // 2, 1))


def qkv_body(x_ref, gain_ref, w_ref, cos_ref, sin_ref, xn_ref, q_ref, k_ref, v_ref):
    x = x_ref[...].astype(F32)
    inv = lax.rsqrt(jnp.mean(x * x, axis=-1, keepdims=True) + EPSILON)
    xn = (x * inv * gain_ref[...]).astype(BF)
    xn_ref[...] = xn
    cosine = cos_ref[...]
    sine = sin_ref[...]
    for part, out, factor in ((0, q_ref, HEAD**-0.5), (1, k_ref, 1.0)):
        lin = dot_nn(xn, w_ref[part])
        for s in range(lin.shape[1] // LANES):
            u = lin[:, s * LANES : (s + 1) * LANES]
            rot = (u * cosine + half_swap(u) * sine).astype(BF)
            if factor != 1.0:
                rot = (rot.astype(F32) * factor).astype(BF)
            out[:, s * LANES : (s + 1) * LANES] = rot
    v_ref[...] = dot_nn(xn, w_ref[2]).astype(BF)


def qkv_call(x, gain, w, cosine, sine):
    rows, dim = x.shape
    width = w.shape[2]
    blk = min(256, rows)
    row = lambda cols: pl.BlockSpec((blk, cols), lambda i: (i, 0))
    return pl.pallas_call(
        qkv_body,
        grid=(rows // blk,),
        out_shape=[jax.ShapeDtypeStruct((rows, dim), BF)] + [jax.ShapeDtypeStruct((rows, width), BF)] * 3,
        in_specs=[
            row(dim),
            pl.BlockSpec((1, dim), lambda i: (0, 0)),
            pl.BlockSpec(w.shape, lambda i: (0, 0, 0)),
            row(LANES),
            row(LANES),
        ],
        out_specs=[row(dim), row(width), row(width), row(width)],
        compiler_params=pltpu.CompilerParams(vmem_limit_bytes=VMEM_LIMIT),
        name="qkv",
    )(x, gain, w, cosine, sine)


def attn_fwd_body(
    q_ref, k_ref, v_ref, base_ref, segq_ref, extk_ref, bias_ref, w_ref, o_ref, o32_ref, extq_ref, wg_ref, wu_ref
):
    rows = q_ref.shape[0]
    for t in range(w_ref.shape[1] // 8):
        turned = jnp.swapaxes(w_ref[:, t * 8 : (t + 1) * 8, :].astype(F32), 0, 1)
        for k in range(8):
            s = t * 4 + k // 2
            (wg_ref, wu_ref)[k % 2][:, s * LANES : (s + 1) * LANES] = turned[k].astype(BF)
    blk = 256
    lane = lax.broadcasted_iota(jnp.int32, (blk, LANES), 1)
    kx = jnp.concatenate([k_ref[...], extk_ref[...]], axis=1)
    ones = jnp.ones((rows, LANES), BF)
    vx = jnp.concatenate([v_ref[...], ones], axis=1)
    for i in range(rows // blk):
        sl = slice(i * blk, (i + 1) * blk)
        q = q_ref[sl, :].astype(F32)
        base = base_ref[sl, :]
        segq = segq_ref[sl, :]
        outs = []
        for h in range(2):
            ext = base * bias_ref[0, h : h + 1, :] + segq
            mine = (lane >= HEAD) if h else (lane < HEAD)
            qx = jnp.concatenate([jnp.where(mine, q, 0.0), ext], axis=1).astype(BF)
            s = dot_nt(qx, kx)
            top = jnp.max(s, axis=-1, keepdims=True)
            p = jnp.exp(s - top).astype(BF)
            ox = dot_nn(p, vx)
            total = ox[:, LANES:]
            outs.append(ox[:, :LANES] / total)
            lse = top + jnp.log(total)
            hi, mid, low = split3(lse)
            ext = jnp.where(
                lane == ONE_COL, -hi, jnp.where(lane == ONE_COL + 1, -mid, jnp.where(lane == ONE_COL + 2, -low, ext))
            )
            extq_ref[0, h, sl, :] = ext.astype(BF)
        o = jnp.where(lane < HEAD, outs[0], outs[1])
        o32_ref[sl, :] = o
        o_ref[sl, :] = o.astype(BF)


def attn_fwd_call(q, k, v, base, segq, extk, bias_rows, w_pairs):
    rows, width = q.shape
    pairs = width // LANES
    dim, tiles, _ = w_pairs.shape
    share = dim // pairs
    half_w = pl.BlockSpec((share, tiles * LANES // 2), lambda p: (p, 0))
    col = pl.BlockSpec((rows, LANES), lambda p: (0, p))
    full = pl.BlockSpec((rows, LANES), lambda p: (0, 0))
    return pl.pallas_call(
        attn_fwd_body,
        grid=(pairs,),
        out_shape=[
            jax.ShapeDtypeStruct((rows, width), BF),
            jax.ShapeDtypeStruct((rows, width), F32),
            jax.ShapeDtypeStruct((pairs, 2, rows, LANES), BF),
            jax.ShapeDtypeStruct((dim, tiles * LANES // 2), BF),
            jax.ShapeDtypeStruct((dim, tiles * LANES // 2), BF),
        ],
        in_specs=[
            col, col, col, full, full, full,
            pl.BlockSpec((1, 2, LANES), lambda p: (p, 0, 0)),
            pl.BlockSpec((share, tiles, LANES), lambda p: (p, 0, 0)),
        ],
        out_specs=[col, col, pl.BlockSpec((1, 2, rows, LANES), lambda p: (p, 0, 0, 0)), half_w, half_w],
        compiler_params=pltpu.CompilerParams(vmem_limit_bytes=VMEM_LIMIT),
        name="attn_fwd",
    )(q, k, v, base, segq, extk, bias_rows, w_pairs)


def attn_bwd_body(
    q_ref, k_ref, v_ref, do_ref, o32_ref, extq_ref, extk_ref, oh_ref, cos_ref, sin_ref, dq_ref, dk_ref, dv_ref, gb_ref, dqt_ref
):
    rows = q_ref.shape[0]
    blk = 256
    lane = lax.broadcasted_iota(jnp.int32, (blk, LANES), 1)
    kx = jnp.concatenate([k_ref[...], extk_ref[...]], axis=1)
    kxt = kx.T
    lane_all = lax.broadcasted_iota(jnp.int32, (rows, LANES), 1)
    vx = jnp.concatenate([v_ref[...], jnp.where(lane_all < 3, 1.0, 0.0).astype(BF)], axis=1)
    dv = jnp.zeros((rows, LANES), F32)
    dk = jnp.zeros((rows, LANES), F32)
    for h in range(2):
        same = jnp.zeros((8, blk), F32)
        other = jnp.zeros((8, blk), F32)
        for i in range(rows // blk):
            sl = slice(i * blk, (i + 1) * blk)
            mine = (lane >= HEAD) if h else (lane < HEAD)
            q = jnp.where(mine, q_ref[sl, :].astype(F32), 0.0).astype(BF)
            do32 = jnp.where(mine, do_ref[sl, :].astype(F32), 0.0)
            do = do32.astype(BF)
            delta = jnp.sum(do32 * o32_ref[sl, :], axis=-1, keepdims=True)
            hi, mid, low = split3(delta)
            dext = jnp.where(lane == 0, -hi, jnp.where(lane == 1, -mid, jnp.where(lane == 2, -low, 0.0))).astype(BF)
            st = dot_nt(kx, jnp.concatenate([q, extq_ref[0, h, sl, :]], axis=1))
            pt = jnp.exp(st)
            dpt = dot_nt(vx, jnp.concatenate([do, dext], axis=1))
            dst = (pt * dpt).astype(BF)
            dv = dv + dot_nn(pt.astype(BF), do)
            dk = dk + dot_nn(dst, q)
            dqt = dot_nn(kxt, dst)
            dqt_ref[h * HEAD : (h + 1) * HEAD, sl] = dqt[h * HEAD : (h + 1) * HEAD, :]
            g = dqt[LANES : LANES + 8, :]
            oh = oh_ref[0, :, sl]
            same = same + g * oh
            other = other + g * oh_ref[1, :, sl]
        gb_ref[0, h, 0] = same
        gb_ref[0, h, 1] = other
    cosine = cos_ref[...]
    sine = sin_ref[...]
    dq = dqt_ref[...].T * HEAD**-0.5
    dq_ref[...] = (dq * cosine - half_swap(dq) * sine).astype(BF)
    dk_ref[...] = (dk * cosine - half_swap(dk) * sine).astype(BF)
    dv_ref[...] = dv.astype(BF)


def attn_bwd_call(q, k, v, do, o32, extq, extk, onehot, cosine, sine):
    rows, width = q.shape
    pairs = width // LANES
    col = pl.BlockSpec((rows, LANES), lambda p: (0, p))
    full = pl.BlockSpec((rows, LANES), lambda p: (0, 0))
    blk = 256
    return pl.pallas_call(
        attn_bwd_body,
        grid=(pairs,),
        out_shape=[jax.ShapeDtypeStruct((rows, width), BF)] * 3 + [jax.ShapeDtypeStruct((pairs, 2, 2, 8, blk), F32)],
        in_specs=[
            col, col, col, col, col,
            pl.BlockSpec((1, 2, rows, LANES), lambda p: (p, 0, 0, 0)),
            full,
            pl.BlockSpec((2, 8, rows), lambda p: (0, 0, 0)),
            full, full,
        ],
        out_specs=[col, col, col, pl.BlockSpec((1, 2, 2, 8, blk), lambda p: (p, 0, 0, 0, 0))],
        scratch_shapes=[pltpu.VMEM((LANES, rows), F32)],
        compiler_params=pltpu.CompilerParams(vmem_limit_bytes=VMEM_LIMIT),
        name="attn_bwd",
    )(q, k, v, do, o32, extq, extk, onehot, cosine, sine)


def partner_barrier():
    dp = lax.axis_index("dp")
    other = 1 - lax.axis_index("tensor")
    barrier = pltpu.get_barrier_semaphore()
    pl.semaphore_signal(barrier, inc=1, device_id=(dp, other), device_id_type=MESH)
    pl.semaphore_wait(barrier, 1)
    return (dp, other)


def send_rows(src, dst, sl, ssem, rsem, peer):
    return pltpu.make_async_remote_copy(
        src_ref=src.at[sl], dst_ref=dst.at[sl], send_sem=ssem, recv_sem=rsem, device_id=peer, device_id_type=MESH
    )


CHUNKS = 4


def attn_out_body(x_ref, o_ref, w_ref, gain_ref, mid_ref, xn_ref, mine, theirs, ssem, rsem):
    peer = partner_barrier()
    rows = x_ref.shape[0]
    blk = rows // CHUNKS
    copies = []
    for c in range(CHUNKS):
        sl = slice(c * blk, (c + 1) * blk)
        mine[sl, :] = dot_nn(o_ref[sl, :], w_ref[...]).astype(BF)
        copy = send_rows(mine, theirs, pl.ds(c * blk, blk), ssem.at[c], rsem.at[c], peer)
        copy.start()
        copies.append(copy)
    for c in range(CHUNKS):
        sl = slice(c * blk, (c + 1) * blk)
        copies[c].wait_recv()
        mid = x_ref[sl, :].astype(F32) + (mine[sl, :].astype(F32) + theirs[sl, :].astype(F32))
        inv = lax.rsqrt(jnp.mean(mid * mid, axis=-1, keepdims=True) + EPSILON)
        mid_ref[sl, :] = mid
        xn_ref[sl, :] = (mid * inv * gain_ref[...]).astype(BF)
    for c in range(CHUNKS):
        copies[c].wait_send()


def attn_out_call(x, o, w, gain):
    rows, dim = x.shape
    return pl.pallas_call(
        attn_out_body,
        out_shape=[jax.ShapeDtypeStruct((rows, dim), F32), jax.ShapeDtypeStruct((rows, dim), BF)],
        in_specs=[whole_spec()] * 4,
        out_specs=[whole_spec()] * 2,
        scratch_shapes=[
            pltpu.VMEM((rows, dim), BF),
            pltpu.VMEM((rows, dim), BF),
            pltpu.SemaphoreType.DMA((CHUNKS,)),
            pltpu.SemaphoreType.DMA((CHUNKS,)),
        ],
        compiler_params=pltpu.CompilerParams(collective_id=1, has_side_effects=True, vmem_limit_bytes=VMEM_LIMIT),
        name="attn_out",
    )(x, o, w, gain)


def ffn_body(
    bits, xn_ref, ct_ref, wg_ref, wu_ref, wd_ref,
    out_ref, gx_ref, gd_ref, gk_ref, gs_ref, uk_ref, us_ref, acc_o, acc_g, hid, dg, du, xt,
):
    j = pl.program_id(0)
    rows = xn_ref.shape[0]
    blk = FFN_ROWS

    @pl.when(j == 0)
    def _():
        acc_o[...] = jnp.zeros_like(acc_o)
        acc_g[...] = jnp.zeros_like(acc_g)
        xt[...] = xn_ref[...].T

    wg = wg_ref[...]
    wu = wu_ref[...]
    wd = wd_ref[...]
    for i in range(rows // blk):
        sl = slice(i * blk, (i + 1) * blk)
        xn = xn_ref[sl, :]
        gate = dot_nn(xn, wg)
        up = dot_nn(xn, wu)
        gh = dot_nt(ct_ref[sl, :], wd)
        sig = jax.nn.sigmoid(gate)
        silu = gate * sig
        hidden = (silu * up).astype(BF)
        dgate = (gh * up * sig * (1.0 + gate * (1.0 - sig))).astype(BF)
        dup = (gh * silu).astype(BF)
        hid[sl, :] = hidden
        dg[sl, :] = dgate
        du[sl, :] = dup
        acc_o[sl, :] += dot_nn(hidden, wd)
        acc_g[sl, :] += dot_nt(dgate, wg) + dot_nt(dup, wu)
    gd_ref[0, 0] = dot_tn(hid[...], ct_ref[...]).astype(BF)
    for part, keep, send, bit in ((dg, gk_ref, gs_ref, bits[0]), (du, uk_ref, us_ref, bits[1])):
        for out, half in ((keep, bit), (send, 1 - bit)):
            rows_at = pl.ds(pl.multiple_of(half * HALF_ROWS, HALF_ROWS), HALF_ROWS)
            out[0] = dot_nn(xt[rows_at, :], part[...]).astype(BF)

    @pl.when(j == pl.num_programs(0) - 1)
    def _():
        out_ref[...] = acc_o[...].astype(BF)
        gx_ref[...] = acc_g[...].astype(BF)


def ffn_call(xn, ct, wg, wu, wd, bits):
    rows, dim = xn.shape
    hidden = wd.shape[0]
    blk = FFN_COLS
    per = WIDE // blk
    full = pl.BlockSpec((rows, dim), lambda j, b: (0, 0))
    colw = pl.BlockSpec((dim, blk), lambda j, b: (0, j))
    roww = pl.BlockSpec((blk, dim), lambda j, b: (j, 0))
    grad = pl.BlockSpec((1, HALF_ROWS, blk), lambda j, b: (j // per, 0, lax.rem(j, per)))

    def down_at(j, b):
        group = j // per
        half = lax.rem(j, per) // (per // 2)
        bit = jnp.where(group == 0, b[0], b[1])
        return (jnp.where(half == bit, 0, 1), group, lax.rem(j, per // 2), 0)

    return pl.pallas_call(
        ffn_body,
        grid_spec=pltpu.PrefetchScalarGridSpec(
            num_scalar_prefetch=1,
            grid=(hidden // blk,),
            in_specs=[full, full, colw, colw, roww],
            out_specs=[full, full, pl.BlockSpec((1, 1, blk, dim), down_at), grad, grad, grad, grad],
            scratch_shapes=[pltpu.VMEM((rows, dim), F32)] * 2 + [pltpu.VMEM((rows, blk), BF)] * 3
            + [pltpu.VMEM((dim, rows), BF)],
        ),
        out_shape=[
            jax.ShapeDtypeStruct((rows, dim), BF),
            jax.ShapeDtypeStruct((rows, dim), BF),
            jax.ShapeDtypeStruct((2, 2, HALF_ROWS, dim), BF),
        ]
        + [jax.ShapeDtypeStruct((2, HALF_ROWS, dim), BF)] * 4,
        compiler_params=pltpu.CompilerParams(vmem_limit_bytes=VMEM_LIMIT),
        name="ffn",
    )(bits, xn, ct, wg, wu, wd)


def pair_rows(w):
    dim, two, width = w.shape
    tiled = jnp.transpose(w.reshape(dim, two, width // LANES, LANES), (0, 2, 1, 3))
    return tiled.reshape(dim, two * width // LANES, LANES)


def widen_body(ga_ref, gb_ref, da_ref, db_ref, aa_ref, v_ref, o_ref, gu_ref, down_ref, qkv_ref, out_ref):
    tiles = WIDE // LANES
    for f in range(2):
        for q in range(tiles // 4):
            parts = []
            for k in range(8):
                s = q * 4 + k // 2
                parts.append((ga_ref, gb_ref)[k % 2][0, f, :, s * LANES : (s + 1) * LANES].astype(F32))
            at = (f * tiles + q * 4) * 2
            gu_ref[:, at : at + 8, :] = jnp.swapaxes(jnp.stack(parts), 0, 1)
    down_ref[0, 0] = da_ref[0, 0].astype(F32)
    down_ref[1, 0] = db_ref[0, 0].astype(F32)
    width = qkv_ref.shape[2]
    qkv_ref[0] = aa_ref[0, 0, :, :width].astype(F32)
    qkv_ref[1] = aa_ref[0, 0, :, width:].astype(F32)
    qkv_ref[2] = v_ref[0, 0].astype(F32)
    out_ref[...] = o_ref[0, 0].astype(F32)


def widen_call(a, b):
    blk = 256
    half = HALF_ROWS // blk
    tiles = 4 * WIDE // LANES
    width = WIDE // 2
    gate = pl.BlockSpec((1, 2, blk, WIDE), lambda i: (i // half, 0, lax.rem(i, half), 0))
    block = lambda n: pl.BlockSpec((1, 1, blk, WIDE), lambda i: (i // half, n, lax.rem(i, half), 0))
    gu, down, qkv, out = pl.pallas_call(
        widen_body,
        grid=(2 * half,),
        out_shape=[
            jax.ShapeDtypeStruct((2 * HALF_ROWS, tiles, LANES), F32),
            jax.ShapeDtypeStruct((2, 2, HALF_ROWS, WIDE), F32),
            jax.ShapeDtypeStruct((3, 2 * HALF_ROWS, width), F32),
            jax.ShapeDtypeStruct((HALF_ROWS, WIDE), F32),
        ],
        in_specs=[
            gate, gate, block(2), block(2), block(3),
            pl.BlockSpec((1, 1, blk, width), lambda i: (0, 3, lax.rem(i, half), i // half)),
            pl.BlockSpec((1, 1, blk // 2, WIDE), lambda i: (1, 3, i, 0)),
        ],
        out_specs=[
            pl.BlockSpec((blk, tiles, LANES), lambda i: (i, 0, 0)),
            pl.BlockSpec((2, 1, blk, WIDE), lambda i: (0, i // half, lax.rem(i, half), 0)),
            pl.BlockSpec((3, blk, width), lambda i: (0, i, 0)),
            pl.BlockSpec((blk // 2, WIDE), lambda i: (i, 0)),
        ],
        compiler_params=pltpu.CompilerParams(vmem_limit_bytes=VMEM_LIMIT),
        name="widen",
    )(a, b, a, b, a, b, b)
    gu = jnp.transpose(gu.reshape(2 * HALF_ROWS, tiles // 2, 2, LANES), (0, 2, 1, 3)).reshape(2 * HALF_ROWS, 2, 2 * WIDE)
    return gu, down.reshape(4 * HALF_ROWS, WIDE), qkv, out


def norm_back(rows_now, gain, grads):
    inv = lax.rsqrt(jnp.mean(rows_now * rows_now, axis=-1, keepdims=True) + EPSILON)
    scaled = grads * gain
    gain_grad = jnp.sum(grads * rows_now * inv, axis=0, keepdims=True)
    back = inv * scaled - rows_now * (inv * inv * inv) * jnp.mean(scaled * rows_now, axis=-1, keepdims=True)
    return back, gain_grad


def ffn_back_body(
    gx_ref, fo_ref, mid_ref, ct_ref, gain_ref, w_ref, out_ref, gm_ref, do_ref, gg_ref, gx_in, fo_in, ssem, rsem
):
    peer = partner_barrier()
    rows = mid_ref.shape[0]
    blk = rows // CHUNKS
    copies = []
    for n, (src, dst) in enumerate(((gx_ref, gx_in), (fo_ref, fo_in))):
        for c in range(CHUNKS):
            at = n * CHUNKS + c
            copy = send_rows(src, dst, pl.ds(c * blk, blk), ssem.at[at], rsem.at[at], peer)
            copy.start()
            copies.append(copy)
    gain_sum = jnp.zeros((1, mid_ref.shape[1]), F32)
    for c in range(CHUNKS):
        sl = slice(c * blk, (c + 1) * blk)
        copies[c].wait_recv()
        grads = gx_ref[sl, :].astype(F32) + gx_in[sl, :].astype(F32)
        back, gain_grad = norm_back(mid_ref[sl, :], gain_ref[...], grads)
        gain_sum = gain_sum + gain_grad
        gm = ct_ref[sl, :].astype(F32) + back
        gm_ref[sl, :] = gm
        do_ref[sl, :] = dot_nt(gm.astype(BF), w_ref[...]).astype(BF)
    gg_ref[...] = gain_sum
    for c in range(CHUNKS):
        sl = slice(c * blk, (c + 1) * blk)
        copies[CHUNKS + c].wait_recv()
        out_ref[sl, :] = (mid_ref[sl, :] + (fo_ref[sl, :].astype(F32) + fo_in[sl, :].astype(F32))).astype(BF)
    for copy in copies:
        copy.wait_send()


def ffn_back_call(gx, fo, mid, ct, gain, w):
    rows, dim = mid.shape
    width = w.shape[0]
    return pl.pallas_call(
        ffn_back_body,
        out_shape=[
            jax.ShapeDtypeStruct((rows, dim), BF),
            jax.ShapeDtypeStruct((rows, dim), F32),
            jax.ShapeDtypeStruct((rows, width), BF),
            jax.ShapeDtypeStruct((1, dim), F32),
        ],
        in_specs=[whole_spec()] * 6,
        out_specs=[whole_spec()] * 4,
        scratch_shapes=[
            pltpu.VMEM((rows, dim), BF),
            pltpu.VMEM((rows, dim), BF),
            pltpu.SemaphoreType.DMA((2 * CHUNKS,)),
            pltpu.SemaphoreType.DMA((2 * CHUNKS,)),
        ],
        compiler_params=pltpu.CompilerParams(collective_id=2, has_side_effects=True, vmem_limit_bytes=VMEM_LIMIT),
        name="ffn_back",
    )(gx, fo, mid, ct, gain, w)


def qkv_back_body(
    dq_ref, dk_ref, dv_ref, w_ref, xn_ref, x_ref, gain_ref, gm_ref, at_ref,
    ig_ref, qk_ref, vo_ref, gg_ref, mine, theirs, ssem, rsem,
):
    peer = partner_barrier()
    rows = x_ref.shape[0]
    blk = rows // CHUNKS
    width = dq_ref.shape[1]
    copies = []
    for c in range(CHUNKS):
        sl = slice(c * blk, (c + 1) * blk)
        total = dot_nt(dq_ref[sl, :], w_ref[0])
        total = total + dot_nt(dk_ref[sl, :], w_ref[1])
        total = total + dot_nt(dv_ref[sl, :], w_ref[2])
        mine[sl, :] = total.astype(BF)
        copy = send_rows(mine, theirs, pl.ds(c * blk, blk), ssem.at[c], rsem.at[c], peer)
        copy.start()
        copies.append(copy)
    qk_ref[:, :width] = dot_tn(xn_ref[...], dq_ref[...]).astype(BF)
    qk_ref[:, width:] = dot_tn(xn_ref[...], dk_ref[...]).astype(BF)
    grad_v = dot_tn(xn_ref[...], dv_ref[...]).astype(BF)
    vo_ref[:HALF_ROWS, :width] = grad_v[:HALF_ROWS]
    vo_ref[:HALF_ROWS, width:] = grad_v[HALF_ROWS:]
    vo_ref[HALF_ROWS:, :] = dot_tn(at_ref[...], gm_ref[...].astype(BF)).astype(BF)
    gain_sum = jnp.zeros((1, x_ref.shape[1]), F32)
    for c in range(CHUNKS):
        sl = slice(c * blk, (c + 1) * blk)
        copies[c].wait_recv()
        grads = mine[sl, :].astype(F32) + theirs[sl, :].astype(F32)
        back, gain_grad = norm_back(x_ref[sl, :].astype(F32), gain_ref[...], grads)
        gain_sum = gain_sum + gain_grad
        ig_ref[sl, :] = gm_ref[sl, :] + back
    gg_ref[...] = gain_sum
    for copy in copies:
        copy.wait_send()


def qkv_back_call(dq, dk, dv, w, xn, x, gain, gm, at):
    rows, dim = x.shape
    return pl.pallas_call(
        qkv_back_body,
        out_shape=[
            jax.ShapeDtypeStruct((rows, dim), F32),
            jax.ShapeDtypeStruct((dim, dim), BF),
            jax.ShapeDtypeStruct((dim, dim), BF),
            jax.ShapeDtypeStruct((1, dim), F32),
        ],
        in_specs=[whole_spec()] * 9,
        out_specs=[whole_spec()] * 4,
        scratch_shapes=[
            pltpu.VMEM((rows, dim), BF),
            pltpu.VMEM((rows, dim), BF),
            pltpu.SemaphoreType.DMA((CHUNKS,)),
            pltpu.SemaphoreType.DMA((CHUNKS,)),
        ],
        compiler_params=pltpu.CompilerParams(collective_id=3, has_side_effects=True, vmem_limit_bytes=VMEM_LIMIT),
        name="qkv_back",
    )(dq, dk, dv, w, xn, x, gain, gm, at)


def peers_of(dp):
    z = dp // 4
    y = (dp // 2) % 2
    x = dp % 2
    at = lambda zz, yy, xx: zz * 4 + yy * 2 + xx
    return z, y, x, at(z, y, 1 - x), at(z, 1 - y, x), at(z + 1 - 2 * (z % 2), y, x), at(3 - z, y, x)


def sum_body(
    gk, rg, uk, ru, dk, rda, rdb, qk, vo, small_in, out_a, out_b, small_out,
    L, S, Z, R, Y, F, sb, st, loc, s1s, s1r, sends, zr, rr, yr, ar, xr, lo, ss, sr,
):
    dp = lax.axis_index("dp")
    t = lax.axis_index("tensor")
    z, y, x, px, py, zn, mm = peers_of(dp)
    is_mid = (z == 1) | (z == 2)
    is_end = (z == 0) | (z == 3)
    mine = jnp.where(z == 2, WIDE // 2, 0)
    others = WIDE // 2 - mine
    n = GROUP_ROWS // ROWS
    first = (px, py)
    last = (py, px)
    outs = (out_a, out_b)
    owner = (x, y)

    def remote(src, dst, ssem, rsem, peer):
        return pltpu.make_async_remote_copy(
            src_ref=src, dst_ref=dst, send_sem=ssem, recv_sem=rsem, device_id=(peer, t), device_id_type=MESH
        )

    def loads(g, b):
        rows = pl.ds(b * HALF_ROWS, HALF_ROWS)
        if b < 2:
            srcs = ((gk, uk)[g].at[b], (rg, ru)[g].at[b])
        elif b == 2:
            srcs = (dk.at[0, g], (rda, rdb)[g].at[...])
        else:
            srcs = ((qk, vo)[g].at[pl.ds(pl.multiple_of(owner[g] * HALF_ROWS, HALF_ROWS), HALF_ROWS)],)
        return [
            pltpu.make_async_copy(src, (L, S)[k].at[g, rows], loc.at[g, b, k]) for k, src in enumerate(srcs)
        ]

    for b in range(4):
        for g in range(2):
            for copy in loads(g, b):
                copy.start()

    barrier = pltpu.get_barrier_semaphore()
    others_z = [lax.rem(z + k, 4) * 4 + y * 2 + x for k in range(1, 4)]
    for peer in [px, py] + others_z:
        pl.semaphore_signal(barrier, inc=1, device_id=(peer, t), device_id_type=MESH)
    pl.semaphore_wait(barrier, 5)

    def first_exchange(g):
        away = pl.ds(pl.multiple_of((1 - owner[g]) * HALF_ROWS, HALF_ROWS), HALF_ROWS)
        return remote(
            (qk, vo)[g].at[away], S.at[g, pl.ds(3 * HALF_ROWS, HALF_ROWS)], s1s.at[g], s1r.at[g], first[g]
        )

    small_x = remote(small_in, sb.at[0], ss.at[0], sr.at[0], px)
    small_y = remote(st.at[0], sb.at[1], ss.at[1], sr.at[1], py)
    small_z = [remote(st.at[1], sb.at[2 + z], ss.at[2 + k], sr.at[2 + z], others_z[k]) for k in range(3)]
    small_x.start()
    for g in range(2):
        first_exchange(g).start()

    def rows_of(i):
        return pl.ds(pl.multiple_of(i * ROWS, ROWS), ROWS)

    def cols_of(at):
        return pl.ds(pl.multiple_of(at, WIDE // 2), WIDE // 2)

    def z_copy(g, i):
        return remote(L.at[g, rows_of(i)], Z.at[g, rows_of(i)], sends.at[g, 0], zr.at[g, i], zn)

    def r_copy(g, i):
        return remote(L.at[g, rows_of(i), cols_of(others)], R.at[g, rows_of(i)], sends.at[g, 1], rr.at[g, i], mm)

    def y_copy(g, i):
        return remote(R.at[g, rows_of(i)], Y.at[g, rows_of(i)], sends.at[g, 2], yr.at[g, i], last[g])

    def a_copy(g, i, at):
        return remote(F.at[g, rows_of(i), cols_of(at)], F.at[g, rows_of(i), cols_of(at)], sends.at[g, 3], ar.at[g, i], mm)

    def o_copy(g, i):
        return remote(F.at[g, rows_of(i)], F.at[g, rows_of(i)], sends.at[g, 4], zr.at[g, i], zn)

    def x_copy(g, i):
        return remote(F.at[g, rows_of(i)], outs[g].at[owner[g], rows_of(i)], sends.at[g, 5], xr.at[g], first[g])

    def l_copy(g, i):
        return pltpu.make_async_copy(F.at[g, rows_of(i)], outs[g].at[owner[g], rows_of(i)], lo.at[g])

    def body(i, carry):
        @pl.when((i < n) & (lax.rem(i, n // 4) == 0))
        def _():
            for b in range(4):
                @pl.when(i == b * (n // 4))
                def _():
                    for g in range(2):
                        for copy in loads(g, b):
                            copy.wait()
                        if b == 3:
                            first_exchange(g).wait_recv()

        @pl.when(is_end & (i < n))
        def _():
            for g in range(2):
                r = rows_of(i)
                L[g, r, :] = (L[g, r, :].astype(F32) + S[g, r, :].astype(F32)).astype(BF)
                z_copy(g, i).start()

        @pl.when(is_mid)
        def _():
            j = i - 4 * LAG

            @pl.when((j >= 0) & (j < n))
            def _():
                for g in range(2):
                    a_copy(g, j, others).wait_recv()
                    o_copy(g, j).start()
                    x_copy(g, j).start()
                    l_copy(g, j).start()

            j3 = i - 3 * LAG

            @pl.when((j3 >= 0) & (j3 < n))
            def _():
                for g in range(2):
                    y_copy(g, j3).wait_recv()
                    r = rows_of(j3)
                    F[g, r, cols_of(mine)] = (R[g, r, :].astype(F32) + Y[g, r, :].astype(F32)).astype(BF)
                    a_copy(g, j3, mine).start()

            j2 = i - 2 * LAG

            @pl.when((j2 >= 0) & (j2 < n))
            def _():
                for g in range(2):
                    r_copy(g, j2).wait_recv()
                    r = rows_of(j2)
                    R[g, r, :] = (R[g, r, :].astype(F32) + L[g, r, cols_of(mine)].astype(F32)).astype(BF)
                    y_copy(g, j2).start()

            j1 = i - LAG

            @pl.when((j1 >= 0) & (j1 < n))
            def _():
                for g in range(2):
                    z_copy(g, j1).wait_recv()
                    r = rows_of(j1)
                    L[g, r, :] = (L[g, r, :].astype(F32) + S[g, r, :].astype(F32) + Z[g, r, :].astype(F32)).astype(BF)
                    r_copy(g, j1).start()

        @pl.when(is_end)
        def _():
            j = i - 5 * LAG

            @pl.when((j >= 0) & (j < n))
            def _():
                for g in range(2):
                    o_copy(g, j).wait_recv()
                    x_copy(g, j).start()
                    l_copy(g, j).start()

        @pl.when(i == n // 8)
        def _():
            small_x.wait_recv()
            st[0] = small_in[...] + sb[0]
            small_y.start()

        @pl.when(i == n // 4)
        def _():
            small_y.wait_recv()
            st[1] = st[0] + sb[1]
            for copy in small_z:
                copy.start()

        return carry

    lax.fori_loop(0, n + 5 * LAG, body, 0)

    for k in range(3):
        remote(st.at[1], sb.at[2 + lax.rem(z + k + 1, 4)], ss.at[2 + k], sr.at[2 + lax.rem(z + k + 1, 4)], others_z[k]).wait_recv()
    sb[2 + z] = st[1]
    small_out[...] = (sb[2] + sb[3]) + (sb[4] + sb[5])

    small_x.wait_send()
    small_y.wait_send()
    for copy in small_z:
        copy.wait_send()
    for g in range(2):
        first_exchange(g).wait_send()
        away = 1 - owner[g]

        @pl.when(is_end)
        def _():
            remote(L.at[g], Z.at[g], sends.at[g, 0], zr.at[g, 0], zn).wait_send()

        @pl.when(is_mid)
        def _():
            half = pl.ds(0, WIDE // 2)
            remote(R.at[g], Y.at[g], sends.at[g, 1], rr.at[g, 0], mm).wait_send()
            remote(R.at[g], Y.at[g], sends.at[g, 2], yr.at[g, 0], last[g]).wait_send()
            remote(R.at[g], Y.at[g], sends.at[g, 3], ar.at[g, 0], mm).wait_send()
            remote(F.at[g], F.at[g], sends.at[g, 4], zr.at[g, 0], zn).wait_send()

        whole = remote(F.at[g], outs[g].at[away], sends.at[g, 5], xr.at[g], first[g])
        whole.wait_send()
        whole.wait_recv()
        pltpu.make_async_copy(F.at[g], outs[g].at[owner[g]], lo.at[g]).wait()


def sum_call(gk, rg, uk, ru, dk, rda, rdb, qk, vo, small):
    any_spec = pl.BlockSpec(memory_space=pl.ANY)
    n = GROUP_ROWS // ROWS
    full = pltpu.VMEM((2, GROUP_ROWS, WIDE), BF)
    half = pltpu.VMEM((2, GROUP_ROWS, WIDE // 2), BF)
    dma = pltpu.SemaphoreType.DMA
    return pl.pallas_call(
        sum_body,
        out_shape=[jax.ShapeDtypeStruct((2, GROUP_ROWS, WIDE), BF)] * 2 + [jax.ShapeDtypeStruct((SMALL, WIDE), F32)],
        in_specs=[any_spec] * 9 + [whole_spec()],
        out_specs=[any_spec] * 2 + [whole_spec()],
        scratch_shapes=[
            full, full, full, half, half, full,
            pltpu.VMEM((6, SMALL, WIDE), F32),
            pltpu.VMEM((2, SMALL, WIDE), F32),
            dma((2, 4, 2)), dma((2,)), dma((2,)), dma((2, 6)),
            dma((2, n)), dma((2, n)), dma((2, n)), dma((2, n)),
            dma((2,)), dma((2,)), dma((5,)), dma((6,)),
        ],
        compiler_params=pltpu.CompilerParams(collective_id=4, has_side_effects=True, vmem_limit_bytes=VMEM_LIMIT),
        name="grad_sum",
    )(gk, rg, uk, ru, dk, rda, rdb, qk, vo, small)


def first_swap(sends, bit):
    pairs = [(d, d ^ bit) for d in range(16)]
    return [lax.ppermute(s, "dp", pairs) for s in sends]


def tables(time_ids):
    half = HEAD // 2
    freqs = jnp.exp(jnp.arange(half, dtype=F32) * (-2.0 * math.log(10000.0) / HEAD))
    angles = time_ids.astype(F32)[:, None] * jnp.tile(freqs, LANES // half)[None, :]
    sign = jnp.where(jnp.arange(LANES) % HEAD < half, -1.0, 1.0)
    return jnp.cos(angles), jnp.sin(angles) * sign[None, :]


def mask_tables(segments, variates, head_bias):
    lane = jnp.arange(LANES)[None, :]
    var_here = (lane % VAR_COLS == variates[:, None]) & (lane < 3 * VAR_COLS)
    seg_here = (lane - SEG_COL == segments[:, None]) & (lane >= SEG_COL) & (lane < ONE_COL)
    seg_cols = (lane >= SEG_COL) & (lane < ONE_COL)
    ones = (lane >= ONE_COL) & (lane < ONE_COL + 3)
    base = jnp.where(var_here, 1.0, 0.0)
    segq = jnp.where(seg_cols & ~seg_here, MASKED, 0.0)
    extk = jnp.where(var_here | seg_here | ones, 1.0, 0.0).astype(BF)
    gap = head_bias[0] - head_bias[1]
    hi = lax.reduce_precision(gap, 8, 7)
    mid = lax.reduce_precision(gap - hi, 8, 7)
    low = gap - hi - mid
    kind = lane // VAR_COLS
    rows = jnp.where(kind == 0, hi[:, None], jnp.where(kind == 1, mid[:, None], jnp.where(kind == 2, low[:, None], 0.0)))
    match = jnp.arange(8)[:, None] == variates[None, :]
    valid = jnp.arange(8)[:, None] < VAR_COLS
    onehot = jnp.stack([jnp.where(match, 1.0, 0.0), jnp.where(valid & ~match, 1.0, 0.0)])
    return base, segq, extk, rows.reshape(-1, 2, LANES), onehot


def fast_local(
    block_input, segments, variates, time_ids, attn_gain, w_qkv, head_bias, w_out, ffn_gain, w_gate_up, w_down, cotangent
):
    dp = lax.axis_index("dp")
    bits = jnp.stack([dp % 2, (dp // 2) % 2]).astype(jnp.int32)
    w3 = jnp.transpose(w_qkv, (1, 0, 2))
    cosine, sine = tables(time_ids)
    base, segq, extk, bias_rows, onehot = mask_tables(segments, variates, head_bias)
    gain1 = attn_gain[None, :]
    gain2 = ffn_gain[None, :]
    xn, q, k, v = qkv_call(block_input, gain1, w3, cosine, sine)
    attended, o32, extq, wg, wu = attn_fwd_call(q, k, v, base, segq, extk, bias_rows, pair_rows(w_gate_up))
    mid, xn2 = attn_out_call(block_input, attended, w_out, gain2)
    ffn_part, gx_part, down, gk, gs, uk, us = ffn_call(xn2, cotangent, wg, wu, w_down, bits)
    rg, rda = first_swap([gs, down[1, 0]], 1)
    ru, rdb = first_swap([us, down[1, 1]], 2)
    block_output, grad_mid, do, g_gain2 = ffn_back_call(gx_part, ffn_part, mid, cotangent, gain2, w_out)
    dq, dk, dv, gb = attn_bwd_call(q, k, v, do, o32, extq, extk, onehot, cosine, sine)
    input_grad, qk, vo, g_gain1 = qkv_back_call(dq, dk, dv, w3, xn, block_input, gain1, grad_mid, attended)
    g_bias = jnp.sum(gb, axis=(3, 4)).reshape(-1, 2).T
    heads = g_bias.shape[1]
    bias_row = jnp.pad(g_bias.reshape(1, -1), ((0, 0), (0, WIDE - 2 * heads)))
    small = jnp.concatenate([g_gain1, g_gain2, bias_row, jnp.zeros((SMALL - 3, WIDE), F32)], axis=0)
    sum_a, sum_b, small = sum_call(gk, rg, uk, ru, down, rda, rdb, qk, vo, small)
    sum_a = sum_a.reshape(2, 4, HALF_ROWS, WIDE)
    sum_b = sum_b.reshape(2, 4, HALF_ROWS, WIDE)
    g_gate_up, g_down, g_qkv, g_out = widen_call(sum_a, sum_b)
    g_bias = small[2, : 2 * heads].reshape(2, heads)
    return (
        block_output, input_grad, small[0], jnp.transpose(g_qkv, (1, 0, 2)), g_bias, g_out, small[1], g_gate_up, g_down,
    )


def rope_tables(time_ids, head_dim):
    half_dim = head_dim // 2
    freqs = jnp.exp(jnp.arange(half_dim, dtype=jnp.float32) * (-2.0 * math.log(10000.0) / head_dim))
    angles = time_ids.astype(jnp.float32)[:, None] * freqs[None, :]
    return (jnp.cos(angles)[:, None, :], jnp.sin(angles)[:, None, :])


def rotate(vectors, cosine, sine_part):
    half_dim = vectors.shape[-1] // 2
    first_half = vectors[..., :half_dim]
    second_half = vectors[..., half_dim:]
    return jnp.concatenate(
        [
            first_half * cosine - second_half * sine_part,
            second_half * cosine + first_half * sine_part,
        ],
        axis=-1,
    )


def rotate_back(grads, cosine, sine_part):
    half_dim = grads.shape[-1] // 2
    first_half = grads[..., :half_dim]
    second_half = grads[..., half_dim:]
    return jnp.concatenate(
        [
            first_half * cosine + second_half * sine_part,
            second_half * cosine - first_half * sine_part,
        ],
        axis=-1,
    )


def norm_rows(rows_now, gain):
    inverse = lax.rsqrt(jnp.mean(rows_now * rows_now, axis=-1, keepdims=True) + EPSILON)
    return (rows_now * inverse * gain, inverse)


def plain_norm_back(rows_now, inverse, gain, grads):
    scaled = grads * gain
    gain_grad = jnp.sum(grads * rows_now * inverse, axis=0)
    rows_grad = inverse * scaled - rows_now * (inverse * inverse * inverse) * jnp.mean(
        scaled * rows_now, axis=-1, keepdims=True
    )
    return (rows_grad, gain_grad)


def scores_of(queries, keys_rot, same_var, allowed, head_bias, score_scale):
    raw_scores = (
        jnp.einsum("sqhd,skhd->shqk", queries, keys_rot, preferred_element_type=jnp.float32)
        * score_scale
    )
    biased = raw_scores + jnp.where(
        same_var[:, None], head_bias[0][None, :, None, None], head_bias[1][None, :, None, None]
    )
    return jnp.where(allowed[:, None], biased, MASKED)


def plain_local(
    block_input,
    segments,
    variates,
    time_ids,
    attn_gain,
    w_qkv,
    head_bias,
    w_out,
    ffn_gain,
    w_gate_up,
    w_down,
    cotangent,
):
    row_count = block_input.shape[0]
    heads_here = head_bias.shape[1]
    head_dim = w_qkv.shape[2] // heads_here
    seq_count = row_count // LEN
    score_scale = head_dim ** (-0.5)
    input_rows = block_input.astype(jnp.float32)
    attn_normed, attn_inverse = norm_rows(input_rows, attn_gain)
    attn_normed_low = attn_normed.astype(jnp.bfloat16)
    projected = jnp.einsum(
        "td,dck->tck", attn_normed_low, w_qkv, preferred_element_type=jnp.float32
    )
    cosine, sine_part = rope_tables(time_ids, head_dim)
    head_shape = (row_count, heads_here, head_dim)
    seq_shape = (seq_count, LEN, heads_here, head_dim)
    queries = (
        rotate(projected[:, 0].reshape(head_shape), cosine, sine_part)
        .astype(jnp.bfloat16)
        .reshape(seq_shape)
    )
    keys_rot = (
        rotate(projected[:, 1].reshape(head_shape), cosine, sine_part)
        .astype(jnp.bfloat16)
        .reshape(seq_shape)
    )
    values = projected[:, 2].astype(jnp.bfloat16).reshape(seq_shape)
    seg_ids = segments.reshape(seq_count, LEN)
    var_ids = variates.reshape(seq_count, LEN)
    allowed = seg_ids[:, :, None] == seg_ids[:, None, :]
    same_var = var_ids[:, :, None] == var_ids[:, None, :]
    scores = scores_of(queries, keys_rot, same_var, allowed, head_bias, score_scale)
    row_max = jnp.max(scores, axis=-1, keepdims=True)
    exp_total = jnp.sum(jnp.exp(scores - row_max), axis=-1, keepdims=True)
    log_total = row_max + jnp.log(exp_total)
    probs_low = jnp.exp(scores - log_total).astype(jnp.bfloat16)
    attended = jnp.einsum("shqk,skhd->sqhd", probs_low, values, preferred_element_type=jnp.float32)
    attended = attended.reshape(row_count, heads_here * head_dim).astype(jnp.bfloat16)
    attn_branch = lax.psum(
        jnp.dot(attended, w_out, preferred_element_type=jnp.float32).astype(jnp.bfloat16), "tensor"
    ).astype(jnp.float32)
    mid_rows = input_rows + attn_branch
    ffn_normed, ffn_inverse = norm_rows(mid_rows, ffn_gain)
    ffn_normed_low = ffn_normed.astype(jnp.bfloat16)
    gate_up = jnp.einsum(
        "td,dcf->tcf", ffn_normed_low, w_gate_up, preferred_element_type=jnp.float32
    )
    gate_vals = gate_up[:, 0]
    up_vals = gate_up[:, 1]
    sigmoid_gate = jax.nn.sigmoid(gate_vals)
    silu_gate = gate_vals * sigmoid_gate
    hidden_low = (silu_gate * up_vals).astype(jnp.bfloat16)
    ffn_branch = lax.psum(
        jnp.dot(hidden_low, w_down, preferred_element_type=jnp.float32).astype(jnp.bfloat16),
        "tensor",
    ).astype(jnp.float32)
    block_output = (mid_rows + ffn_branch).astype(jnp.bfloat16)
    grad_down = jnp.einsum("tf,td->fd", hidden_low, cotangent, preferred_element_type=jnp.float32)
    grad_hidden = jnp.einsum("td,fd->tf", cotangent, w_down, preferred_element_type=jnp.float32)
    grad_gate = grad_hidden * up_vals * sigmoid_gate * (1.0 + gate_vals * (1.0 - sigmoid_gate))
    grad_up = grad_hidden * silu_gate
    grad_gate_up = jnp.stack([grad_gate, grad_up], axis=1).astype(jnp.bfloat16)
    grad_w_gate_up = jnp.einsum(
        "td,tcf->dcf", ffn_normed_low, grad_gate_up, preferred_element_type=jnp.float32
    )
    grad_ffn_normed = lax.psum(
        jnp.einsum(
            "tcf,dcf->td", grad_gate_up, w_gate_up, preferred_element_type=jnp.float32
        ).astype(jnp.bfloat16),
        "tensor",
    ).astype(jnp.float32)
    norm_grad_mid, grad_ffn_gain = plain_norm_back(mid_rows, ffn_inverse, ffn_gain, grad_ffn_normed)
    grad_mid = cotangent.astype(jnp.float32) + norm_grad_mid
    grad_branch = grad_mid.astype(jnp.bfloat16)
    grad_w_out = jnp.einsum("tk,td->kd", attended, grad_branch, preferred_element_type=jnp.float32)
    grad_attended = jnp.einsum("td,kd->tk", grad_branch, w_out, preferred_element_type=jnp.float32)
    grad_attended = grad_attended.astype(jnp.bfloat16).reshape(seq_shape)
    scores_again = scores_of(queries, keys_rot, same_var, allowed, head_bias, score_scale)
    probs_again = jnp.exp(scores_again - log_total)
    probs_again_low = probs_again.astype(jnp.bfloat16)
    grad_probs = jnp.einsum(
        "sqhd,skhd->shqk", grad_attended, values, preferred_element_type=jnp.float32
    )
    grad_values = jnp.einsum(
        "shqk,sqhd->skhd", probs_again_low, grad_attended, preferred_element_type=jnp.float32
    )
    grad_scores = probs_again * (
        grad_probs - jnp.sum(probs_again * grad_probs, axis=-1, keepdims=True)
    )
    grad_scores_low = grad_scores.astype(jnp.bfloat16)
    same_low = same_var.astype(jnp.bfloat16)
    other_low = jnp.logical_not(same_var).astype(jnp.bfloat16)
    grad_bias = jnp.stack(
        [
            jnp.einsum(
                "shqk,sqk->h", grad_scores_low, same_low, preferred_element_type=jnp.float32
            ),
            jnp.einsum(
                "shqk,sqk->h", grad_scores_low, other_low, preferred_element_type=jnp.float32
            ),
        ],
        axis=0,
    )
    grad_queries = (
        jnp.einsum("shqk,skhd->sqhd", grad_scores_low, keys_rot, preferred_element_type=jnp.float32)
        * score_scale
    )
    grad_keys = (
        jnp.einsum("shqk,sqhd->skhd", grad_scores_low, queries, preferred_element_type=jnp.float32)
        * score_scale
    )
    grad_query_lin = rotate_back(grad_queries.reshape(head_shape), cosine, sine_part).reshape(
        row_count, heads_here * head_dim
    )
    grad_key_lin = rotate_back(grad_keys.reshape(head_shape), cosine, sine_part).reshape(
        row_count, heads_here * head_dim
    )
    grad_value_lin = grad_values.reshape(row_count, heads_here * head_dim)
    grad_projected = jnp.stack([grad_query_lin, grad_key_lin, grad_value_lin], axis=1).astype(
        jnp.bfloat16
    )
    grad_w_qkv = jnp.einsum(
        "td,tck->dck", attn_normed_low, grad_projected, preferred_element_type=jnp.float32
    )
    grad_attn_normed = lax.psum(
        jnp.einsum("tck,dck->td", grad_projected, w_qkv, preferred_element_type=jnp.float32).astype(
            jnp.bfloat16
        ),
        "tensor",
    ).astype(jnp.float32)
    norm_grad_input, grad_attn_gain = plain_norm_back(
        input_rows, attn_inverse, attn_gain, grad_attn_normed
    )
    input_grad = grad_mid + norm_grad_input
    grad_attn_gain, grad_w_qkv, grad_bias, grad_w_out, grad_ffn_gain, grad_w_gate_up, grad_down = (
        lax.psum(
            (
                grad_attn_gain,
                grad_w_qkv,
                grad_bias,
                grad_w_out,
                grad_ffn_gain,
                grad_w_gate_up,
                grad_down,
            ),
            "dp",
        )
    )
    return (
        block_output,
        input_grad,
        grad_attn_gain,
        grad_w_qkv,
        grad_bias,
        grad_w_out,
        grad_ffn_gain,
        grad_w_gate_up,
        grad_down,
    )


def solution(mesh):
    placed = (
        P("dp", None), P("dp"), P("dp"), P("dp"), P(), P(None, None, "tensor"), P(None, "tensor"),
        P("tensor", None), P(), P(None, None, "tensor"), P("tensor", None), P("dp", None),
    )
    fast = (mesh.shape["dp"], mesh.shape["tensor"]) == (16, 2)
    return jax.shard_map(
        fast_local if fast else plain_local,
        mesh=mesh,
        in_specs=placed,
        out_specs=(
            P("dp", None), P("dp", None), P(), P(None, None, "tensor"), P(None, "tensor"), P("tensor", None), P(),
            P(None, None, "tensor"), P("tensor", None),
        ),
        check_vma=False,
    )
```

```python
import functools
import math

import jax
import jax.numpy as jnp
from jax import lax
from jax.experimental import pallas as pl
from jax.experimental.pallas import tpu as pltpu
from jax.sharding import PartitionSpec as P

LEN = 1024
EPSILON = 1e-05
MASKED = -1000000000.0
BF = jnp.bfloat16
F32 = jnp.float32
MESH = pl.DeviceIdType.MESH
VMEM_LIMIT = 60 * 1024 * 1024
LANES = 128
HEAD = 64
VAR_COLS = 4
SEG_COL = 12
ONE_COL = 20
ROWS = 32
LAGS = (2, 4, 6, 8, 10)
SPACE = 1
SWAP_ROWS = 64
SWAP_STEP = 2
HALF_ROWS = 512
GROUP_ROWS = 4 * HALF_ROWS
WIDE = 1024
SMALL = 8
FFN_ROWS = 512
FFN_COLS = 256


def dot_nn(a, b):
    return lax.dot_general(a, b, (((1,), (0,)), ((), ())), preferred_element_type=F32)


def dot_nt(a, b):
    return lax.dot_general(a, b, (((1,), (1,)), ((), ())), preferred_element_type=F32)


def dot_tn(a, b):
    return lax.dot_general(a, b, (((0,), (0,)), ((), ())), preferred_element_type=F32)


def whole_spec():
    return pl.BlockSpec(memory_space=pltpu.VMEM)


def split3(v):
    hi = v.astype(BF).astype(F32)
    mid = (v - hi).astype(BF).astype(F32)
    return hi, mid, v - hi - mid


def half_swap(u):
    lane = lax.broadcasted_iota(jnp.int32, u.shape, 1) % HEAD
    return jnp.where(lane < HEAD // 2, pltpu.roll(u, LANES - HEAD // 2, 1), pltpu.roll(u, HEAD // 2, 1))


def qkv_body(x_ref, gain_ref, w_ref, cos_ref, sin_ref, xn_ref, q_ref, k_ref, v_ref):
    x = x_ref[...].astype(F32)
    inv = lax.rsqrt(jnp.mean(x * x, axis=-1, keepdims=True) + EPSILON)
    xn = (x * inv * gain_ref[...]).astype(BF)
    xn_ref[...] = xn
    cosine = cos_ref[...]
    sine = sin_ref[...]
    for part, out, factor in ((0, q_ref, HEAD**-0.5), (1, k_ref, 1.0)):
        lin = dot_nn(xn, w_ref[part])
        for s in range(lin.shape[1] // LANES):
            u = lin[:, s * LANES : (s + 1) * LANES]
            rot = (u * cosine + half_swap(u) * sine).astype(BF)
            if factor != 1.0:
                rot = (rot.astype(F32) * factor).astype(BF)
            out[:, s * LANES : (s + 1) * LANES] = rot
    v_ref[...] = dot_nn(xn, w_ref[2]).astype(BF)


def qkv_call(x, gain, w, cosine, sine):
    rows, dim = x.shape
    width = w.shape[2]
    blk = min(256, rows)
    row = lambda cols: pl.BlockSpec((blk, cols), lambda i: (i, 0))
    return pl.pallas_call(
        qkv_body,
        grid=(rows // blk,),
        out_shape=[jax.ShapeDtypeStruct((rows, dim), BF)] + [jax.ShapeDtypeStruct((rows, width), BF)] * 3,
        in_specs=[
            row(dim),
            pl.BlockSpec((1, dim), lambda i: (0, 0)),
            pl.BlockSpec(w.shape, lambda i: (0, 0, 0)),
            row(LANES),
            row(LANES),
        ],
        out_specs=[row(dim), row(width), row(width), row(width)],
        compiler_params=pltpu.CompilerParams(vmem_limit_bytes=VMEM_LIMIT),
        name="qkv",
    )(x, gain, w, cosine, sine)


def attn_fwd_body(
    q_ref, k_ref, v_ref, base_ref, segq_ref, extk_ref, bias_ref, w_ref, o_ref, o32_ref, extq_ref, wg_ref, wu_ref
):
    rows = q_ref.shape[0]
    for t in range(w_ref.shape[1] // 8):
        turned = jnp.swapaxes(w_ref[:, t * 8 : (t + 1) * 8, :].astype(F32), 0, 1)
        for k in range(8):
            s = t * 4 + k // 2
            (wg_ref, wu_ref)[k % 2][:, s * LANES : (s + 1) * LANES] = turned[k].astype(BF)
    blk = 256
    lane = lax.broadcasted_iota(jnp.int32, (blk, LANES), 1)
    kx = jnp.concatenate([k_ref[...], extk_ref[...]], axis=1)
    ones = jnp.ones((rows, LANES), BF)
    vx = jnp.concatenate([v_ref[...], ones], axis=1)
    for i in range(rows // blk):
        sl = slice(i * blk, (i + 1) * blk)
        q = q_ref[sl, :].astype(F32)
        base = base_ref[sl, :]
        segq = segq_ref[sl, :]
        outs = []
        for h in range(2):
            ext = base * bias_ref[0, h : h + 1, :] + segq
            mine = (lane >= HEAD) if h else (lane < HEAD)
            qx = jnp.concatenate([jnp.where(mine, q, 0.0), ext], axis=1).astype(BF)
            s = dot_nt(qx, kx)
            top = jnp.max(s, axis=-1, keepdims=True)
            p = jnp.exp(s - top).astype(BF)
            ox = dot_nn(p, vx)
            total = ox[:, LANES:]
            outs.append(ox[:, :LANES] / total)
            lse = top + jnp.log(total)
            hi, mid, low = split3(lse)
            ext = jnp.where(
                lane == ONE_COL, -hi, jnp.where(lane == ONE_COL + 1, -mid, jnp.where(lane == ONE_COL + 2, -low, ext))
            )
            extq_ref[0, h, sl, :] = ext.astype(BF)
        o = jnp.where(lane < HEAD, outs[0], outs[1])
        o32_ref[sl, :] = o
        o_ref[sl, :] = o.astype(BF)


def attn_fwd_call(q, k, v, base, segq, extk, bias_rows, w_pairs):
    rows, width = q.shape
    pairs = width // LANES
    dim, tiles, _ = w_pairs.shape
    share = dim // pairs
    half_w = pl.BlockSpec((share, tiles * LANES // 2), lambda p: (p, 0))
    col = pl.BlockSpec((rows, LANES), lambda p: (0, p))
    full = pl.BlockSpec((rows, LANES), lambda p: (0, 0))
    return pl.pallas_call(
        attn_fwd_body,
        grid=(pairs,),
        out_shape=[
            jax.ShapeDtypeStruct((rows, width), BF),
            jax.ShapeDtypeStruct((rows, width), F32),
            jax.ShapeDtypeStruct((pairs, 2, rows, LANES), BF),
            jax.ShapeDtypeStruct((dim, tiles * LANES // 2), BF),
            jax.ShapeDtypeStruct((dim, tiles * LANES // 2), BF),
        ],
        in_specs=[
            col, col, col, full, full, full,
            pl.BlockSpec((1, 2, LANES), lambda p: (p, 0, 0)),
            pl.BlockSpec((share, tiles, LANES), lambda p: (p, 0, 0)),
        ],
        out_specs=[col, col, pl.BlockSpec((1, 2, rows, LANES), lambda p: (p, 0, 0, 0)), half_w, half_w],
        compiler_params=pltpu.CompilerParams(vmem_limit_bytes=VMEM_LIMIT),
        name="attn_fwd",
    )(q, k, v, base, segq, extk, bias_rows, w_pairs)


def attn_bwd_body(
    q_ref, k_ref, v_ref, do_ref, o32_ref, extq_ref, extk_ref, oh_ref, cos_ref, sin_ref, d_ref, gb_ref, dqt_ref
):
    rows = q_ref.shape[0]
    blk = 256
    lane = lax.broadcasted_iota(jnp.int32, (blk, LANES), 1)
    kx = jnp.concatenate([k_ref[...], extk_ref[...]], axis=1)
    kxt = kx.T
    lane_all = lax.broadcasted_iota(jnp.int32, (rows, LANES), 1)
    vx = jnp.concatenate([v_ref[...], jnp.where(lane_all < 3, 1.0, 0.0).astype(BF)], axis=1)
    dv = jnp.zeros((rows, LANES), F32)
    dk = jnp.zeros((rows, LANES), F32)
    for h in range(2):
        same = jnp.zeros((8, blk), F32)
        other = jnp.zeros((8, blk), F32)
        for i in range(rows // blk):
            sl = slice(i * blk, (i + 1) * blk)
            mine = (lane >= HEAD) if h else (lane < HEAD)
            q = jnp.where(mine, q_ref[sl, :].astype(F32), 0.0).astype(BF)
            do32 = jnp.where(mine, do_ref[sl, :].astype(F32), 0.0)
            do = do32.astype(BF)
            delta = jnp.sum(do32 * o32_ref[sl, :], axis=-1, keepdims=True)
            hi, mid, low = split3(delta)
            dext = jnp.where(lane == 0, -hi, jnp.where(lane == 1, -mid, jnp.where(lane == 2, -low, 0.0))).astype(BF)
            st = dot_nt(kx, jnp.concatenate([q, extq_ref[0, h, sl, :]], axis=1))
            pt = jnp.exp(st)
            dpt = dot_nt(vx, jnp.concatenate([do, dext], axis=1))
            dst = (pt * dpt).astype(BF)
            dv = dv + dot_nn(pt.astype(BF), do)
            dk = dk + dot_nn(dst, q)
            dqt = dot_nn(kxt, dst)
            dqt_ref[h * HEAD : (h + 1) * HEAD, sl] = dqt[h * HEAD : (h + 1) * HEAD, :]
            g = dqt[LANES : LANES + 8, :]
            oh = oh_ref[0, :, sl]
            same = same + g * oh
            other = other + g * oh_ref[1, :, sl]
        gb_ref[0, h, 0] = same
        gb_ref[0, h, 1] = other
    cosine = cos_ref[...]
    sine = sin_ref[...]
    dq = dqt_ref[...].T * HEAD**-0.5
    d_ref[0] = (dq * cosine - half_swap(dq) * sine).astype(BF)
    d_ref[1] = (dk * cosine - half_swap(dk) * sine).astype(BF)
    d_ref[2] = dv.astype(BF)


def attn_bwd_call(q, k, v, do, o32, extq, extk, onehot, cosine, sine):
    rows, width = q.shape
    pairs = width // LANES
    col = pl.BlockSpec((rows, LANES), lambda p: (0, p))
    full = pl.BlockSpec((rows, LANES), lambda p: (0, 0))
    blk = 256
    return pl.pallas_call(
        attn_bwd_body,
        grid=(pairs,),
        out_shape=[jax.ShapeDtypeStruct((3, rows, width), BF), jax.ShapeDtypeStruct((pairs, 2, 2, 8, blk), F32)],
        in_specs=[
            col, col, col, col, col,
            pl.BlockSpec((1, 2, rows, LANES), lambda p: (p, 0, 0, 0)),
            full,
            pl.BlockSpec((2, 8, rows), lambda p: (0, 0, 0)),
            full, full,
        ],
        out_specs=[pl.BlockSpec((3, rows, LANES), lambda p: (0, 0, p)), pl.BlockSpec((1, 2, 2, 8, blk), lambda p: (p, 0, 0, 0, 0))],
        scratch_shapes=[pltpu.VMEM((LANES, rows), F32)],
        compiler_params=pltpu.CompilerParams(vmem_limit_bytes=VMEM_LIMIT),
        name="attn_bwd",
    )(q, k, v, do, o32, extq, extk, onehot, cosine, sine)


def partner_barrier():
    dp = lax.axis_index("dp")
    other = 1 - lax.axis_index("tensor")
    barrier = pltpu.get_barrier_semaphore()
    pl.semaphore_signal(barrier, inc=1, device_id=(dp, other), device_id_type=MESH)
    pl.semaphore_wait(barrier, 1)
    return (dp, other)


def send_rows(src, dst, sl, ssem, rsem, peer):
    return pltpu.make_async_remote_copy(
        src_ref=src.at[sl], dst_ref=dst.at[sl], send_sem=ssem, recv_sem=rsem, device_id=peer, device_id_type=MESH
    )


CHUNKS = 4


def attn_out_body(x_ref, o_ref, w_ref, gain_ref, mid_ref, xn_ref, mine, theirs, ssem, rsem):
    peer = partner_barrier()
    rows = x_ref.shape[0]
    blk = rows // CHUNKS
    copies = []
    for c in range(CHUNKS):
        sl = slice(c * blk, (c + 1) * blk)
        mine[sl, :] = dot_nn(o_ref[sl, :], w_ref[...]).astype(BF)
        copy = send_rows(mine, theirs, pl.ds(c * blk, blk), ssem.at[c], rsem.at[c], peer)
        copy.start()
        copies.append(copy)
    for c in range(CHUNKS):
        sl = slice(c * blk, (c + 1) * blk)
        copies[c].wait_recv()
        mid = x_ref[sl, :].astype(F32) + (mine[sl, :].astype(F32) + theirs[sl, :].astype(F32))
        inv = lax.rsqrt(jnp.mean(mid * mid, axis=-1, keepdims=True) + EPSILON)
        mid_ref[sl, :] = mid
        xn_ref[sl, :] = (mid * inv * gain_ref[...]).astype(BF)
    for c in range(CHUNKS):
        copies[c].wait_send()


def attn_out_call(x, o, w, gain):
    rows, dim = x.shape
    return pl.pallas_call(
        attn_out_body,
        out_shape=[jax.ShapeDtypeStruct((rows, dim), F32), jax.ShapeDtypeStruct((rows, dim), BF)],
        in_specs=[whole_spec()] * 4,
        out_specs=[whole_spec()] * 2,
        scratch_shapes=[
            pltpu.VMEM((rows, dim), BF),
            pltpu.VMEM((rows, dim), BF),
            pltpu.SemaphoreType.DMA((CHUNKS,)),
            pltpu.SemaphoreType.DMA((CHUNKS,)),
        ],
        compiler_params=pltpu.CompilerParams(collective_id=1, has_side_effects=True, vmem_limit_bytes=VMEM_LIMIT),
        name="attn_out",
    )(x, o, w, gain)


LATE = 4
SLOTS = 4
PART = FFN_COLS // 4


def sent(copy):
    copy.wait_send() if copy.is_remote else copy.wait()


def grid_bits():
    dp = lax.axis_index("dp")
    return dp, dp % 2, (dp // 2) % 2, peers_of(dp)[3], peers_of(dp)[4]


def ffn_body(
    xn_ref, ct_ref, wg_ref, wu_ref, wd_ref,
    out_ref, gx_ref, gk_ref, uk_ref, rg, ru, dk, rd, late_x, late_y,
    acc_o, acc_g, hid, dg, du, xt, away_w, away_d, ws, wr, ds, dr,
):
    j = pl.program_id(0)
    t = lax.axis_index("tensor")
    dp, x, y, px, py = grid_bits()
    steps = pl.num_programs(0)
    rows = xn_ref.shape[0]
    blk = wd_ref.shape[0]
    per = WIDE // blk
    early = 2 * per - LATE
    slot = lax.rem(j, SLOTS)
    near = (px, py)
    bits = (x, y)
    arrays = ((rg, late_x), (ru, late_y))

    def remote(src, dst, ssem, rsem, peer):
        return pltpu.make_async_remote_copy(
            src_ref=src, dst_ref=dst, send_sem=ssem, recv_sem=rsem, device_id=(peer, t), device_id_type=MESH
        )

    def wide_early(k, at):
        cols = pl.ds(pl.multiple_of(lax.rem(at, per) * blk, blk), blk)
        s = lax.rem(at, SLOTS)
        return remote(away_w.at[k, s], arrays[k][0].at[:, cols], ws.at[k, s], wr.at[k], near[k])

    def wide_late(k, at):
        cols = pl.ds(pl.multiple_of((at - early) * blk, blk), blk)
        s = lax.rem(at, SLOTS)
        return pltpu.make_async_copy(away_w.at[k, s], arrays[k][1].at[pl.ds(0, HALF_ROWS), cols], ws.at[k, s])

    def wide_do(at, act):
        for k in range(2):

            @pl.when(at < early)
            def _():
                act(wide_early(k, at))

            @pl.when(at >= early)
            def _():
                act(wide_late(k, at))

    def down_rows(g, half):
        return pl.ds(pl.multiple_of(g * 2 * PART + half * PART, PART), PART)

    def down_keep(g, at):
        s = lax.rem(at, SLOTS)
        return pltpu.make_async_copy(
            away_d.at[s, down_rows(g, bits[g])], dk.at[g, pl.ds(pl.multiple_of(at * PART, PART), PART)], ds.at[g, s]
        )

    def down_send(g, at):
        s = lax.rem(at, SLOTS)
        rows_at = pl.ds(pl.multiple_of(at * PART, PART), PART)
        return remote(away_d.at[s, down_rows(g, 1 - bits[g])], rd.at[g, rows_at], ds.at[2 + g, s], dr.at[g], near[g])

    def down_late(g, at):
        s = lax.rem(at, SLOTS)
        rows_at = pl.ds(pl.multiple_of(HALF_ROWS + (at - early) * PART, PART), PART)
        return pltpu.make_async_copy(
            away_d.at[s, down_rows(g, 1 - bits[g])], arrays[g][1].at[rows_at], ds.at[2 + g, s]
        )

    def down_do(at, act):
        for g in range(2):
            act(down_keep(g, at))

            @pl.when(at < early)
            def _():
                act(down_send(g, at))

            @pl.when(at >= early)
            def _():
                act(down_late(g, at))

    @pl.when(j == 0)
    def _():
        barrier = pltpu.get_barrier_semaphore()
        for peer in near:
            pl.semaphore_signal(barrier, inc=1, device_id=(peer, t), device_id_type=MESH)
        pl.semaphore_wait(barrier, 2)
        acc_o[...] = jnp.zeros_like(acc_o)
        acc_g[...] = jnp.zeros_like(acc_g)
        xt[...] = xn_ref[...].T

    wg = wg_ref[...]
    wu = wu_ref[...]
    wd = wd_ref[...]
    for i in range(rows // FFN_ROWS):
        sl = slice(i * FFN_ROWS, (i + 1) * FFN_ROWS)
        xn = xn_ref[sl, :]
        gate = dot_nn(xn, wg)
        up = dot_nn(xn, wu)
        gh = dot_nt(ct_ref[sl, :], wd)
        sig = jax.nn.sigmoid(gate)
        silu = gate * sig
        hidden = (silu * up).astype(BF)
        dgate = (gh * up * sig * (1.0 + gate * (1.0 - sig))).astype(BF)
        dup = (gh * silu).astype(BF)
        hid[sl, :] = hidden
        dg[sl, :] = dgate
        du[sl, :] = dup
        acc_o[sl, :] += dot_nn(hidden, wd)
        acc_g[sl, :] += dot_nt(dgate, wg) + dot_nt(dup, wu)

    @pl.when(j >= SLOTS)
    def _():
        wide_do(j - SLOTS, sent)
        down_do(j - SLOTS, sent)

    away_d[slot] = dot_tn(hid[...], ct_ref[...]).astype(BF)
    down_do(j, lambda copy: copy.start())
    for k, (part, keep, bit) in enumerate(((dg, gk_ref, x), (du, uk_ref, y))):
        rows_at = lambda half: pl.ds(pl.multiple_of(half * HALF_ROWS, HALF_ROWS), HALF_ROWS)
        away_w[k, slot] = dot_nn(xt[rows_at(1 - bit), :], part[...]).astype(BF)
        keep[0] = dot_nn(xt[rows_at(bit), :], part[...]).astype(BF)
    wide_do(j, lambda copy: copy.start())

    @pl.when(j == steps - 1)
    def _():
        out_ref[...] = acc_o[...].astype(BF)
        gx_ref[...] = acc_g[...].astype(BF)
        for back in range(SLOTS, 0, -1):
            wide_do(steps - back, sent)
            down_do(steps - back, sent)
        for k in range(2):
            part = arrays[k][0].at[:, pl.ds(0, early * blk)]
            remote(part, part, ws.at[k, 0], wr.at[k], near[k]).wait_recv()
        for g in range(2):
            part = rd.at[g, pl.ds(0, early * PART)]
            remote(part, part, ds.at[g, 0], dr.at[g], near[g]).wait_recv()


def ffn_call(xn, ct, wg, wu, wd):
    rows, dim = xn.shape
    hidden = wd.shape[0]
    blk = FFN_COLS
    per = WIDE // blk
    full = pl.BlockSpec((rows, dim), lambda j: (0, 0))
    colw = pl.BlockSpec((dim, blk), lambda j: (0, j))
    roww = pl.BlockSpec((blk, dim), lambda j: (j, 0))
    grad = pl.BlockSpec((1, HALF_ROWS, blk), lambda j: (j // per, 0, lax.rem(j, per)))
    any_spec = pl.BlockSpec(memory_space=pl.ANY)
    wide = jax.ShapeDtypeStruct((2, HALF_ROWS, dim), BF)
    early = hidden // blk - LATE
    come = jax.ShapeDtypeStruct((HALF_ROWS, early * blk), BF)
    late = jax.ShapeDtypeStruct((HALF_ROWS + LATE * PART, LATE * blk), BF)
    dma = pltpu.SemaphoreType.DMA
    return pl.pallas_call(
        ffn_body,
        grid=(hidden // blk,),
        in_specs=[full, full, colw, colw, roww],
        out_specs=[full, full, grad, grad] + [any_spec] * 6,
        out_shape=[jax.ShapeDtypeStruct((rows, dim), BF)] * 2
        + [wide, wide, come, come, wide, jax.ShapeDtypeStruct((2, early * PART, dim), BF), late, late],
        scratch_shapes=[pltpu.VMEM((rows, dim), F32)] * 2
        + [pltpu.VMEM((rows, blk), BF)] * 3
        + [
            pltpu.VMEM((dim, rows), BF),
            pltpu.VMEM((2, SLOTS, HALF_ROWS, blk), BF),
            pltpu.VMEM((SLOTS, blk, dim), BF),
            dma((2, SLOTS)), dma((2,)), dma((4, SLOTS)), dma((2,)),
        ],
        compiler_params=pltpu.CompilerParams(collective_id=5, has_side_effects=True, vmem_limit_bytes=VMEM_LIMIT),
        name="ffn",
    )(xn, ct, wg, wu, wd)


def pair_rows(w):
    dim, two, width = w.shape
    tiled = jnp.transpose(w.reshape(dim, two, width // LANES, LANES), (0, 2, 1, 3))
    return tiled.reshape(dim, two * width // LANES, LANES)


def widen_body(ga_ref, gb_ref, da_ref, db_ref, aa_ref, v_ref, o_ref, gu_ref, down_ref, qkv_ref, out_ref):
    tiles = WIDE // LANES
    for f in range(2):
        for q in range(tiles // 4):
            parts = []
            for k in range(8):
                s = q * 4 + k // 2
                parts.append((ga_ref, gb_ref)[k % 2][0, f, :, s * LANES : (s + 1) * LANES].astype(F32))
            at = (f * tiles + q * 4) * 2
            gu_ref[:, at : at + 8, :] = jnp.swapaxes(jnp.stack(parts), 0, 1)
    down_ref[:, 0, 0] = da_ref[0, 0].astype(F32).reshape(down_ref.shape[0], PART, WIDE)
    down_ref[:, 1, 0] = db_ref[0, 0].astype(F32).reshape(down_ref.shape[0], PART, WIDE)
    width = qkv_ref.shape[2]
    qkv_ref[0] = aa_ref[0, 0, :, :width].astype(F32)
    qkv_ref[1] = aa_ref[0, 0, :, width:].astype(F32)
    qkv_ref[2] = v_ref[0, 0].astype(F32)
    out_ref[...] = o_ref[0, 0].astype(F32)


def widen_call(a, b):
    blk = 256
    half = HALF_ROWS // blk
    tiles = 4 * WIDE // LANES
    width = WIDE // 2
    gate = pl.BlockSpec((1, 2, blk, WIDE), lambda i: (i // half, 0, lax.rem(i, half), 0))
    block = lambda n: pl.BlockSpec((1, 1, blk, WIDE), lambda i: (i // half, n, lax.rem(i, half), 0))
    gu, down, qkv, out = pl.pallas_call(
        widen_body,
        grid=(2 * half,),
        out_shape=[
            jax.ShapeDtypeStruct((2 * HALF_ROWS, tiles, LANES), F32),
            jax.ShapeDtypeStruct((HALF_ROWS // PART, 2, 2, PART, WIDE), F32),
            jax.ShapeDtypeStruct((3, 2 * HALF_ROWS, width), F32),
            jax.ShapeDtypeStruct((HALF_ROWS, WIDE), F32),
        ],
        in_specs=[
            gate, gate, block(2), block(2), block(3),
            pl.BlockSpec((1, 1, blk, width), lambda i: (0, 3, lax.rem(i, half), i // half)),
            pl.BlockSpec((1, 1, blk // 2, WIDE), lambda i: (1, 3, i, 0)),
        ],
        out_specs=[
            pl.BlockSpec((blk, tiles, LANES), lambda i: (i, 0, 0)),
            pl.BlockSpec((blk // PART, 2, 1, PART, WIDE), lambda i: (lax.rem(i, half), 0, i // half, 0, 0)),
            pl.BlockSpec((3, blk, width), lambda i: (0, i, 0)),
            pl.BlockSpec((blk // 2, WIDE), lambda i: (i, 0)),
        ],
        compiler_params=pltpu.CompilerParams(vmem_limit_bytes=VMEM_LIMIT),
        name="widen",
    )(a, b, a, b, a, b, b)
    gu = jnp.transpose(gu.reshape(2 * HALF_ROWS, tiles // 2, 2, LANES), (0, 2, 1, 3)).reshape(2 * HALF_ROWS, 2, 2 * WIDE)
    return gu, down.reshape(4 * HALF_ROWS, WIDE), qkv, out


def norm_back(rows_now, gain, grads):
    inv = lax.rsqrt(jnp.mean(rows_now * rows_now, axis=-1, keepdims=True) + EPSILON)
    scaled = grads * gain
    gain_grad = jnp.sum(grads * rows_now * inv, axis=0, keepdims=True)
    back = inv * scaled - rows_now * (inv * inv * inv) * jnp.mean(scaled * rows_now, axis=-1, keepdims=True)
    return back, gain_grad


def ffn_back_body(
    gx_ref, fo_ref, mid_ref, ct_ref, gain_ref, w_ref, at_ref,
    out_ref, gm_ref, do_ref, gw_ref, gg_ref, gx_in, fo_in, gb, ssem, rsem,
):
    peer = partner_barrier()
    rows = mid_ref.shape[0]
    blk = rows // CHUNKS
    copies = []
    for n, (src, dst) in enumerate(((gx_ref, gx_in), (fo_ref, fo_in))):
        for c in range(CHUNKS):
            at = n * CHUNKS + c
            copy = send_rows(src, dst, pl.ds(c * blk, blk), ssem.at[at], rsem.at[at], peer)
            copy.start()
            copies.append(copy)
    gain_sum = jnp.zeros((1, mid_ref.shape[1]), F32)
    for c in range(CHUNKS):
        sl = slice(c * blk, (c + 1) * blk)
        copies[c].wait_recv()
        grads = gx_ref[sl, :].astype(F32) + gx_in[sl, :].astype(F32)
        back, gain_grad = norm_back(mid_ref[sl, :], gain_ref[...], grads)
        gain_sum = gain_sum + gain_grad
        gm = ct_ref[sl, :].astype(F32) + back
        gm_ref[sl, :] = gm
        gb[sl, :] = gm.astype(BF)
        do_ref[sl, :] = dot_nt(gb[sl, :], w_ref[...]).astype(BF)
    gg_ref[...] = gain_sum
    gw_ref[...] = dot_tn(at_ref[...], gb[...]).astype(BF)
    for c in range(CHUNKS):
        sl = slice(c * blk, (c + 1) * blk)
        copies[CHUNKS + c].wait_recv()
        out_ref[sl, :] = (mid_ref[sl, :] + (fo_ref[sl, :].astype(F32) + fo_in[sl, :].astype(F32))).astype(BF)
    for copy in copies:
        copy.wait_send()


def ffn_back_call(gx, fo, mid, ct, gain, w, at):
    rows, dim = mid.shape
    width = w.shape[0]
    return pl.pallas_call(
        ffn_back_body,
        out_shape=[
            jax.ShapeDtypeStruct((rows, dim), BF),
            jax.ShapeDtypeStruct((rows, dim), F32),
            jax.ShapeDtypeStruct((rows, width), BF),
            jax.ShapeDtypeStruct((width, dim), BF),
            jax.ShapeDtypeStruct((1, dim), F32),
        ],
        in_specs=[whole_spec()] * 7,
        out_specs=[whole_spec()] * 5,
        scratch_shapes=[
            pltpu.VMEM((rows, dim), BF),
            pltpu.VMEM((rows, dim), BF),
            pltpu.VMEM((rows, dim), BF),
            pltpu.SemaphoreType.DMA((2 * CHUNKS,)),
            pltpu.SemaphoreType.DMA((2 * CHUNKS,)),
        ],
        compiler_params=pltpu.CompilerParams(collective_id=2, has_side_effects=True, vmem_limit_bytes=VMEM_LIMIT),
        name="ffn_back",
    )(gx, fo, mid, ct, gain, w, at)


def peers_of(dp):
    z = dp // 4
    y = (dp // 2) % 2
    x = dp % 2
    at = lambda zz, yy, xx: zz * 4 + yy * 2 + xx
    return z, y, x, at(z, y, 1 - x), at(z, 1 - y, x), at(z + 1 - 2 * (z % 2), y, x), at(3 - z, y, x)


def sum_body(
    gk, rg, uk, ru, late_x, late_y, dk, rd, go, dqkv, w3, xn, xin, gmid, gain_ref, small_in, out_a, out_b, ig, small_out,
    L, S, Z, R, Y, sb, st, dl, wb, xb, mine_rows, their_rows, away_rows, xc, gc, ic,
    loc, s1s, s1r, sends, zr, rr, yr, ar, xr, lo, ss, sr, ld, cs, cr, xg, io,
):
    dp = lax.axis_index("dp")
    t = lax.axis_index("tensor")
    z, y, x, px, py, zn, mm = peers_of(dp)
    is_mid = (z == 1) | (z == 2)
    is_end = (z == 0) | (z == 3)
    mine = jnp.where(z == 2, WIDE // 2, 0)
    others = WIDE // 2 - mine
    n = GROUP_ROWS // ROWS
    per = n // 4
    first = (px, py)
    last = (py, px)
    outs = (out_a, out_b)
    owner = (x, y)
    F = S

    def remote(src, dst, ssem, rsem, peer, core=t):
        return pltpu.make_async_remote_copy(
            src_ref=src, dst_ref=dst, send_sem=ssem, recv_sem=rsem, device_id=(peer, core), device_id_type=MESH
        )

    def loads(g, b):
        rows = pl.ds(b * HALF_ROWS, HALF_ROWS)
        copies = [((gk, uk)[g].at[b] if b < 2 else dk.at[g], L.at[g, rows])]
        near = (rg, ru)[g]
        late = (late_x, late_y)[g]
        top = pl.ds(0, HALF_ROWS)
        if b == 0:
            copies.append((near.at[:, pl.ds(0, WIDE)], S.at[g, rows]))
        elif b == 1:
            cut = near.shape[1] - WIDE
            if cut:
                copies.append((near.at[:, pl.ds(WIDE, cut)], S.at[g, rows, pl.ds(0, cut)]))
            copies.append((late.at[top], S.at[g, rows, pl.ds(cut, WIDE - cut)]))
        else:
            cut = rd.shape[1]
            copies.append((rd.at[g], S.at[g, pl.ds(b * HALF_ROWS, cut)]))
            for part in range((HALF_ROWS - cut) // PART):
                copies.append(
                    (late.at[pl.ds(HALF_ROWS + part * PART, PART)], S.at[g, pl.ds(b * HALF_ROWS + cut + part * PART, PART)])
                )
        return [pltpu.make_async_copy(src, dst, loc.at[g, b, k]) for k, (src, dst) in enumerate(copies)]

    own_loads = [pltpu.make_async_copy(src, dst, ld.at[k]) for k, (src, dst) in enumerate(((dqkv, dl), (w3, wb), (xn, xb)))]
    for b in range(3):
        for g in range(2):
            for copy in loads(g, b):
                copy.start()
    for copy in own_loads:
        copy.start()

    tail = pl.ds(3 * HALF_ROWS, HALF_ROWS)

    def out_load(kept):
        return pltpu.make_async_copy(go, L.at[1, tail] if kept else away_rows.at[1], loc.at[1, 3, 0])

    def out_load_do(act):
        @pl.when(y == 1)
        def _():
            act(out_load(True))

        @pl.when(y == 0)
        def _():
            act(out_load(False))

    out_load_do(lambda copy: copy.start())

    barrier = pltpu.get_barrier_semaphore()
    others_z = [lax.rem(z + k, 4) * 4 + y * 2 + x for k in range(1, 4)]
    for peer in [px, py] + others_z:
        pl.semaphore_signal(barrier, inc=1, device_id=(peer, t), device_id_type=MESH)
    pl.semaphore_signal(barrier, inc=1, device_id=(dp, 1 - t), device_id_type=MESH)
    pl.semaphore_wait(barrier, 6)

    def first_exchange(g):
        return remote(away_rows.at[g], S.at[g, tail], s1s.at[g], s1r.at[g], first[g])

    def first_part(g, c):
        at = pl.multiple_of(c * SWAP_ROWS, SWAP_ROWS)
        dst = S.at[g, pl.ds(3 * HALF_ROWS + at, SWAP_ROWS)]
        return remote(away_rows.at[g, pl.ds(at, SWAP_ROWS)], dst, s1s.at[g], s1r.at[g], first[g])

    small_x = remote(st.at[2], sb.at[0], ss.at[0], sr.at[0], px)
    small_y = remote(st.at[0], sb.at[1], ss.at[1], sr.at[1], py)
    small_z = [remote(st.at[1], sb.at[2 + z], ss.at[2 + k], sr.at[2 + z], others_z[k]) for k in range(3)]

    def rows_of(i):
        return pl.ds(pl.multiple_of(i * ROWS, ROWS), ROWS)

    def cols_of(at):
        return pl.ds(pl.multiple_of(at, WIDE // 2), WIDE // 2)

    def z_copy(g, i):
        return remote(L.at[g, rows_of(i)], Z.at[g, rows_of(i)], sends.at[g, 0], zr.at[g, i], zn)

    def r_copy(g, i):
        return remote(L.at[g, rows_of(i), cols_of(others)], R.at[g, rows_of(i)], sends.at[g, 1], rr.at[g, i], mm)

    def y_copy(g, i):
        return remote(R.at[g, rows_of(i)], Y.at[g, rows_of(i)], sends.at[g, 2], yr.at[g, i], last[g])

    def a_copy(g, i, at):
        return remote(F.at[g, rows_of(i), cols_of(at)], F.at[g, rows_of(i), cols_of(at)], sends.at[g, 3], ar.at[g, i], mm)

    def o_copy(g, i):
        return remote(F.at[g, rows_of(i)], F.at[g, rows_of(i)], sends.at[g, 4], zr.at[g, i], zn)

    def x_copy(g, i):
        return remote(F.at[g, rows_of(i)], outs[g].at[owner[g], rows_of(i)], sends.at[g, 5], xr.at[g], first[g])

    def l_copy(g, i):
        return pltpu.make_async_copy(F.at[g, rows_of(i)], outs[g].at[owner[g], rows_of(i)], lo.at[g])

    def end_in(g, j):
        r = rows_of(j)
        L[g, r, :] = (L[g, r, :].astype(F32) + S[g, r, :].astype(F32)).astype(BF)
        z_copy(g, j).start()

    def end_out(g, j):
        o_copy(g, j).wait_recv()
        x_copy(g, j).start()
        l_copy(g, j).start()

    def mid_out(g, j):
        a_copy(g, j, others).wait_recv()
        o_copy(g, j).start()
        x_copy(g, j).start()
        l_copy(g, j).start()

    def mid_join(g, j):
        y_copy(g, j).wait_recv()
        r = rows_of(j)
        F[g, r, cols_of(mine)] = (R[g, r, :].astype(F32) + Y[g, r, :].astype(F32)).astype(BF)
        a_copy(g, j, mine).start()

    def mid_half(g, j):
        r_copy(g, j).wait_recv()
        r = rows_of(j)
        R[g, r, :] = (R[g, r, :].astype(F32) + L[g, r, cols_of(mine)].astype(F32)).astype(BF)
        y_copy(g, j).start()

    def mid_in(g, j):
        z_copy(g, j).wait_recv()
        r = rows_of(j)
        L[g, r, :] = (L[g, r, :].astype(F32) + S[g, r, :].astype(F32) + Z[g, r, :].astype(F32)).astype(BF)
        r_copy(g, j).start()

    def stage(act, g, j):
        @pl.when((j >= 0) & (j < n))
        def _():
            act(g, j)

    seq = xin.shape[0]
    blk = seq // CHUNKS
    width = dl.shape[2]

    def piece_rows(c):
        return pl.ds(c * blk, blk)

    def core_copy(c):
        return remote(mine_rows.at[piece_rows(c)], their_rows.at[piece_rows(c)], cs.at[c], cr.at[c], dp, 1 - t)

    def norm_loads(c):
        return [
            pltpu.make_async_copy(xin.at[piece_rows(c)], xc.at[c % 2], xg.at[c % 2, 0]),
            pltpu.make_async_copy(gmid.at[piece_rows(c)], gc.at[c % 2], xg.at[c % 2, 1]),
        ]

    def ig_copy(c):
        return pltpu.make_async_copy(ic.at[c % 2], ig.at[piece_rows(c)], io.at[c % 2])

    def piece_start():
        for copy in own_loads:
            copy.wait()

    def piece_part(c):
        r = piece_rows(c)
        total = dot_nt(dl[0, r, :], wb[0]) + dot_nt(dl[1, r, :], wb[1]) + dot_nt(dl[2, r, :], wb[2])
        mine_rows[r, :] = total.astype(BF)
        core_copy(c).start()

    def row_half(half):
        return pl.ds(pl.multiple_of(half * HALF_ROWS, HALF_ROWS), HALF_ROWS)

    def piece_qk(k):
        cols = pl.ds(k * width, width)
        L[0, tail, cols] = dot_tn(xb[:, row_half(x)], dl[k]).astype(BF)
        away_rows[0, :, cols] = dot_tn(xb[:, row_half(1 - x)], dl[k]).astype(BF)

    def piece_v():
        for k in range(2):
            cols = pl.ds(k * width, width)
            grad = dot_tn(xb[:, k * HALF_ROWS : (k + 1) * HALF_ROWS], dl[2]).astype(BF)

            @pl.when(y == 0)
            def _():
                L[1, tail, cols] = grad

            @pl.when(y == 1)
            def _():
                away_rows[1, :, cols] = grad

    def piece_send():
        out_load_do(lambda copy: copy.wait())
        for copy in norm_loads(0):
            copy.start()
        st[2] = small_in[...]

    def piece_norm(c):
        if c + 1 < CHUNKS:
            for copy in norm_loads(c + 1):
                copy.start()
        for copy in norm_loads(c):
            copy.wait()
        core_copy(c).wait_recv()
        if c >= 2:
            ig_copy(c - 2).wait()
        r = piece_rows(c)
        grads = mine_rows[r, :].astype(F32) + their_rows[r, :].astype(F32)
        back, gain_grad = norm_back(xc[c % 2].astype(F32), gain_ref[...], grads)
        st[2, 0:1, :] = st[2, 0:1, :] + gain_grad
        ic[c % 2] = gc[c % 2] + back
        ig_copy(c).start()

    def small_first():
        small_x.start()

    def small_second():
        small_x.wait_recv()
        st[0] = st[2] + sb[0]
        small_y.start()

    def small_third():
        small_y.wait_recv()
        st[1] = st[0] + sb[1]
        for copy in small_z:
            copy.start()

    pieces = (
        [piece_start]
        + [functools.partial(piece_part, c) for c in range(CHUNKS)]
        + [functools.partial(piece_qk, k) for k in range(2)]
        + [piece_v, piece_send]
        + [functools.partial(piece_norm, c) for c in range(CHUNKS)]
        + [small_first, small_second, small_third]
    )

    def body(i, carry):
        for b in range(4):

            @pl.when(i == b * per)
            def _():
                for g in range(2):
                    if b < 3:
                        for copy in loads(g, b):
                            copy.wait()
                    if b == 3:
                        first_exchange(g).wait_recv()

        @pl.when(is_end)
        def _():
            for g in range(2):
                stage(end_in, g, i)
                stage(end_out, g, i - LAGS[4])

        @pl.when(is_mid)
        def _():
            for g in range(2):
                stage(mid_out, g, i - LAGS[3])
                stage(mid_join, g, i - LAGS[2])
                stage(mid_half, g, i - LAGS[1])
                stage(mid_in, g, i - LAGS[0])

        begin = 2 + SPACE * (CHUNKS + 4)
        c = (i - begin) // SWAP_STEP

        @pl.when((i >= begin) & (c < HALF_ROWS // SWAP_ROWS) & (lax.rem(i - begin, SWAP_STEP) == 0))
        def _():
            for g in range(2):
                first_part(g, c).start()

        for k, piece in enumerate(pieces):

            @pl.when(i == 1 + SPACE * k)
            def _():
                piece()

        return carry

    lax.fori_loop(0, n + LAGS[4], body, 0)

    for k in range(3):
        zz = lax.rem(z + k + 1, 4)
        remote(st.at[1], sb.at[2 + zz], ss.at[2 + k], sr.at[2 + zz], others_z[k]).wait_recv()
    sb[2 + z] = st[1]
    small_out[...] = (sb[2] + sb[3]) + (sb[4] + sb[5])

    small_x.wait_send()
    small_y.wait_send()
    for copy in small_z:
        copy.wait_send()
    for c in range(CHUNKS):
        core_copy(c).wait_send()
    for c in (CHUNKS - 2, CHUNKS - 1):
        ig_copy(c).wait()
    for g in range(2):
        first_exchange(g).wait_send()
        away = 1 - owner[g]

        @pl.when(is_end)
        def _():
            remote(L.at[g], Z.at[g], sends.at[g, 0], zr.at[g, 0], zn).wait_send()

        @pl.when(is_mid)
        def _():
            remote(R.at[g], Y.at[g], sends.at[g, 1], rr.at[g, 0], mm).wait_send()
            remote(R.at[g], Y.at[g], sends.at[g, 2], yr.at[g, 0], last[g]).wait_send()
            remote(R.at[g], Y.at[g], sends.at[g, 3], ar.at[g, 0], mm).wait_send()
            remote(F.at[g], F.at[g], sends.at[g, 4], zr.at[g, 0], zn).wait_send()

        whole = remote(F.at[g], outs[g].at[away], sends.at[g, 5], xr.at[g], first[g])
        whole.wait_send()
        whole.wait_recv()
        pltpu.make_async_copy(F.at[g], outs[g].at[owner[g]], lo.at[g]).wait()


def sum_call(gk, rg, uk, ru, late_x, late_y, dk, rd, go, dqkv, w3, xn, xin, gmid, gain, small):
    any_spec = pl.BlockSpec(memory_space=pl.ANY)
    n = GROUP_ROWS // ROWS
    rows, dim = xin.shape
    blk = rows // CHUNKS
    full = pltpu.VMEM((2, GROUP_ROWS, WIDE), BF)
    half = pltpu.VMEM((2, GROUP_ROWS, WIDE // 2), BF)
    dma = pltpu.SemaphoreType.DMA
    return pl.pallas_call(
        sum_body,
        out_shape=[jax.ShapeDtypeStruct((2, GROUP_ROWS, WIDE), BF)] * 2
        + [jax.ShapeDtypeStruct((rows, dim), F32), jax.ShapeDtypeStruct((SMALL, WIDE), F32)],
        in_specs=[any_spec] * 14 + [whole_spec()] * 2,
        out_specs=[any_spec] * 3 + [whole_spec()],
        scratch_shapes=[
            full, full, full, half, half,
            pltpu.VMEM((6, SMALL, WIDE), F32),
            pltpu.VMEM((3, SMALL, WIDE), F32),
            pltpu.VMEM(dqkv.shape, BF),
            pltpu.VMEM(w3.shape, BF),
            pltpu.VMEM((rows, dim), BF),
            pltpu.VMEM((rows, dim), BF),
            pltpu.VMEM((rows, dim), BF),
            pltpu.VMEM((2, HALF_ROWS, WIDE), BF),
            pltpu.VMEM((2, blk, dim), BF),
            pltpu.VMEM((2, blk, dim), F32),
            pltpu.VMEM((2, blk, dim), F32),
            dma((2, 4, 8)), dma((2,)), dma((2,)), dma((2, 6)),
            dma((2, n)), dma((2, n)), dma((2, n)), dma((2, n)),
            dma((2,)), dma((2,)), dma((5,)), dma((6,)),
            dma((3,)), dma((CHUNKS,)), dma((CHUNKS,)), dma((2, 2)), dma((2,)),
        ],
        compiler_params=pltpu.CompilerParams(collective_id=4, has_side_effects=True, vmem_limit_bytes=VMEM_LIMIT),
        name="grad_sum",
    )(gk, rg, uk, ru, late_x, late_y, dk, rd, go, dqkv, w3, xn, xin, gmid, gain, small)


def tables(time_ids):
    half = HEAD // 2
    freqs = jnp.exp(jnp.arange(half, dtype=F32) * (-2.0 * math.log(10000.0) / HEAD))
    angles = time_ids.astype(F32)[:, None] * jnp.tile(freqs, LANES // half)[None, :]
    sign = jnp.where(jnp.arange(LANES) % HEAD < half, -1.0, 1.0)
    return jnp.cos(angles), jnp.sin(angles) * sign[None, :]


def mask_tables(segments, variates, head_bias):
    lane = jnp.arange(LANES)[None, :]
    var_here = (lane % VAR_COLS == variates[:, None]) & (lane < 3 * VAR_COLS)
    seg_here = (lane - SEG_COL == segments[:, None]) & (lane >= SEG_COL) & (lane < ONE_COL)
    seg_cols = (lane >= SEG_COL) & (lane < ONE_COL)
    ones = (lane >= ONE_COL) & (lane < ONE_COL + 3)
    base = jnp.where(var_here, 1.0, 0.0)
    segq = jnp.where(seg_cols & ~seg_here, MASKED, 0.0)
    extk = jnp.where(var_here | seg_here | ones, 1.0, 0.0).astype(BF)
    gap = head_bias[0] - head_bias[1]
    hi = lax.reduce_precision(gap, 8, 7)
    mid = lax.reduce_precision(gap - hi, 8, 7)
    low = gap - hi - mid
    kind = lane // VAR_COLS
    rows = jnp.where(kind == 0, hi[:, None], jnp.where(kind == 1, mid[:, None], jnp.where(kind == 2, low[:, None], 0.0)))
    match = jnp.arange(8)[:, None] == variates[None, :]
    valid = jnp.arange(8)[:, None] < VAR_COLS
    onehot = jnp.stack([jnp.where(match, 1.0, 0.0), jnp.where(valid & ~match, 1.0, 0.0)])
    return base, segq, extk, rows.reshape(-1, 2, LANES), onehot


def fast_local(
    block_input, segments, variates, time_ids, attn_gain, w_qkv, head_bias, w_out, ffn_gain, w_gate_up, w_down, cotangent
):
    w3 = jnp.transpose(w_qkv, (1, 0, 2))
    cosine, sine = tables(time_ids)
    base, segq, extk, bias_rows, onehot = mask_tables(segments, variates, head_bias)
    gain1 = attn_gain[None, :]
    gain2 = ffn_gain[None, :]
    xn, q, k, v = qkv_call(block_input, gain1, w3, cosine, sine)
    attended, o32, extq, wg, wu = attn_fwd_call(q, k, v, base, segq, extk, bias_rows, pair_rows(w_gate_up))
    mid, xn2 = attn_out_call(block_input, attended, w_out, gain2)
    ffn_part, gx_part, gk, uk, rg, ru, dk, rd, late_x, late_y = ffn_call(xn2, cotangent, wg, wu, w_down)
    late_x = lax.ppermute(late_x, "dp", [(d, d ^ 1) for d in range(16)])
    late_y = lax.ppermute(late_y, "dp", [(d, d ^ 2) for d in range(16)])
    block_output, grad_mid, do, g_out, g_gain2 = ffn_back_call(
        gx_part, ffn_part, mid, cotangent, gain2, w_out, attended
    )
    dqkv, gb = attn_bwd_call(q, k, v, do, o32, extq, extk, onehot, cosine, sine)
    g_bias = jnp.sum(gb, axis=(3, 4)).reshape(-1, 2).T
    heads = g_bias.shape[1]
    bias_row = jnp.pad(g_bias.reshape(1, -1), ((0, 0), (0, WIDE - 2 * heads)))
    zero = jnp.zeros((1, WIDE), F32)
    small = jnp.concatenate([zero, g_gain2, bias_row, jnp.zeros((SMALL - 3, WIDE), F32)], axis=0)
    sum_a, sum_b, input_grad, small = sum_call(
        gk, rg, uk, ru, late_x, late_y, dk, rd, g_out, dqkv, w3, xn, block_input, grad_mid, gain1, small
    )
    sum_a = sum_a.reshape(2, 4, HALF_ROWS, WIDE)
    sum_b = sum_b.reshape(2, 4, HALF_ROWS, WIDE)
    g_gate_up, g_down, g_qkv, g_out = widen_call(sum_a, sum_b)
    g_bias = small[2, : 2 * heads].reshape(2, heads)
    return (
        block_output, input_grad, small[0], jnp.transpose(g_qkv, (1, 0, 2)), g_bias, g_out, small[1], g_gate_up, g_down,
    )


def rope_tables(time_ids, head_dim):
    half_dim = head_dim // 2
    freqs = jnp.exp(jnp.arange(half_dim, dtype=jnp.float32) * (-2.0 * math.log(10000.0) / head_dim))
    angles = time_ids.astype(jnp.float32)[:, None] * freqs[None, :]
    return (jnp.cos(angles)[:, None, :], jnp.sin(angles)[:, None, :])


def rotate(vectors, cosine, sine_part):
    half_dim = vectors.shape[-1] // 2
    first_half = vectors[..., :half_dim]
    second_half = vectors[..., half_dim:]
    return jnp.concatenate(
        [
            first_half * cosine - second_half * sine_part,
            second_half * cosine + first_half * sine_part,
        ],
        axis=-1,
    )


def rotate_back(grads, cosine, sine_part):
    half_dim = grads.shape[-1] // 2
    first_half = grads[..., :half_dim]
    second_half = grads[..., half_dim:]
    return jnp.concatenate(
        [
            first_half * cosine + second_half * sine_part,
            second_half * cosine - first_half * sine_part,
        ],
        axis=-1,
    )


def norm_rows(rows_now, gain):
    inverse = lax.rsqrt(jnp.mean(rows_now * rows_now, axis=-1, keepdims=True) + EPSILON)
    return (rows_now * inverse * gain, inverse)


def plain_norm_back(rows_now, inverse, gain, grads):
    scaled = grads * gain
    gain_grad = jnp.sum(grads * rows_now * inverse, axis=0)
    rows_grad = inverse * scaled - rows_now * (inverse * inverse * inverse) * jnp.mean(
        scaled * rows_now, axis=-1, keepdims=True
    )
    return (rows_grad, gain_grad)


def scores_of(queries, keys_rot, same_var, allowed, head_bias, score_scale):
    raw_scores = (
        jnp.einsum("sqhd,skhd->shqk", queries, keys_rot, preferred_element_type=jnp.float32)
        * score_scale
    )
    biased = raw_scores + jnp.where(
        same_var[:, None], head_bias[0][None, :, None, None], head_bias[1][None, :, None, None]
    )
    return jnp.where(allowed[:, None], biased, MASKED)


def plain_local(
    block_input,
    segments,
    variates,
    time_ids,
    attn_gain,
    w_qkv,
    head_bias,
    w_out,
    ffn_gain,
    w_gate_up,
    w_down,
    cotangent,
):
    row_count = block_input.shape[0]
    heads_here = head_bias.shape[1]
    head_dim = w_qkv.shape[2] // heads_here
    seq_count = row_count // LEN
    score_scale = head_dim ** (-0.5)
    input_rows = block_input.astype(jnp.float32)
    attn_normed, attn_inverse = norm_rows(input_rows, attn_gain)
    attn_normed_low = attn_normed.astype(jnp.bfloat16)
    projected = jnp.einsum(
        "td,dck->tck", attn_normed_low, w_qkv, preferred_element_type=jnp.float32
    )
    cosine, sine_part = rope_tables(time_ids, head_dim)
    head_shape = (row_count, heads_here, head_dim)
    seq_shape = (seq_count, LEN, heads_here, head_dim)
    queries = (
        rotate(projected[:, 0].reshape(head_shape), cosine, sine_part)
        .astype(jnp.bfloat16)
        .reshape(seq_shape)
    )
    keys_rot = (
        rotate(projected[:, 1].reshape(head_shape), cosine, sine_part)
        .astype(jnp.bfloat16)
        .reshape(seq_shape)
    )
    values = projected[:, 2].astype(jnp.bfloat16).reshape(seq_shape)
    seg_ids = segments.reshape(seq_count, LEN)
    var_ids = variates.reshape(seq_count, LEN)
    allowed = seg_ids[:, :, None] == seg_ids[:, None, :]
    same_var = var_ids[:, :, None] == var_ids[:, None, :]
    scores = scores_of(queries, keys_rot, same_var, allowed, head_bias, score_scale)
    row_max = jnp.max(scores, axis=-1, keepdims=True)
    exp_total = jnp.sum(jnp.exp(scores - row_max), axis=-1, keepdims=True)
    log_total = row_max + jnp.log(exp_total)
    probs_low = jnp.exp(scores - log_total).astype(jnp.bfloat16)
    attended = jnp.einsum("shqk,skhd->sqhd", probs_low, values, preferred_element_type=jnp.float32)
    attended = attended.reshape(row_count, heads_here * head_dim).astype(jnp.bfloat16)
    attn_branch = lax.psum(
        jnp.dot(attended, w_out, preferred_element_type=jnp.float32).astype(jnp.bfloat16), "tensor"
    ).astype(jnp.float32)
    mid_rows = input_rows + attn_branch
    ffn_normed, ffn_inverse = norm_rows(mid_rows, ffn_gain)
    ffn_normed_low = ffn_normed.astype(jnp.bfloat16)
    gate_up = jnp.einsum(
        "td,dcf->tcf", ffn_normed_low, w_gate_up, preferred_element_type=jnp.float32
    )
    gate_vals = gate_up[:, 0]
    up_vals = gate_up[:, 1]
    sigmoid_gate = jax.nn.sigmoid(gate_vals)
    silu_gate = gate_vals * sigmoid_gate
    hidden_low = (silu_gate * up_vals).astype(jnp.bfloat16)
    ffn_branch = lax.psum(
        jnp.dot(hidden_low, w_down, preferred_element_type=jnp.float32).astype(jnp.bfloat16),
        "tensor",
    ).astype(jnp.float32)
    block_output = (mid_rows + ffn_branch).astype(jnp.bfloat16)
    grad_down = jnp.einsum("tf,td->fd", hidden_low, cotangent, preferred_element_type=jnp.float32)
    grad_hidden = jnp.einsum("td,fd->tf", cotangent, w_down, preferred_element_type=jnp.float32)
    grad_gate = grad_hidden * up_vals * sigmoid_gate * (1.0 + gate_vals * (1.0 - sigmoid_gate))
    grad_up = grad_hidden * silu_gate
    grad_gate_up = jnp.stack([grad_gate, grad_up], axis=1).astype(jnp.bfloat16)
    grad_w_gate_up = jnp.einsum(
        "td,tcf->dcf", ffn_normed_low, grad_gate_up, preferred_element_type=jnp.float32
    )
    grad_ffn_normed = lax.psum(
        jnp.einsum(
            "tcf,dcf->td", grad_gate_up, w_gate_up, preferred_element_type=jnp.float32
        ).astype(jnp.bfloat16),
        "tensor",
    ).astype(jnp.float32)
    norm_grad_mid, grad_ffn_gain = plain_norm_back(mid_rows, ffn_inverse, ffn_gain, grad_ffn_normed)
    grad_mid = cotangent.astype(jnp.float32) + norm_grad_mid
    grad_branch = grad_mid.astype(jnp.bfloat16)
    grad_w_out = jnp.einsum("tk,td->kd", attended, grad_branch, preferred_element_type=jnp.float32)
    grad_attended = jnp.einsum("td,kd->tk", grad_branch, w_out, preferred_element_type=jnp.float32)
    grad_attended = grad_attended.astype(jnp.bfloat16).reshape(seq_shape)
    scores_again = scores_of(queries, keys_rot, same_var, allowed, head_bias, score_scale)
    probs_again = jnp.exp(scores_again - log_total)
    probs_again_low = probs_again.astype(jnp.bfloat16)
    grad_probs = jnp.einsum(
        "sqhd,skhd->shqk", grad_attended, values, preferred_element_type=jnp.float32
    )
    grad_values = jnp.einsum(
        "shqk,sqhd->skhd", probs_again_low, grad_attended, preferred_element_type=jnp.float32
    )
    grad_scores = probs_again * (
        grad_probs - jnp.sum(probs_again * grad_probs, axis=-1, keepdims=True)
    )
    grad_scores_low = grad_scores.astype(jnp.bfloat16)
    same_low = same_var.astype(jnp.bfloat16)
    other_low = jnp.logical_not(same_var).astype(jnp.bfloat16)
    grad_bias = jnp.stack(
        [
            jnp.einsum(
                "shqk,sqk->h", grad_scores_low, same_low, preferred_element_type=jnp.float32
            ),
            jnp.einsum(
                "shqk,sqk->h", grad_scores_low, other_low, preferred_element_type=jnp.float32
            ),
        ],
        axis=0,
    )
    grad_queries = (
        jnp.einsum("shqk,skhd->sqhd", grad_scores_low, keys_rot, preferred_element_type=jnp.float32)
        * score_scale
    )
    grad_keys = (
        jnp.einsum("shqk,sqhd->skhd", grad_scores_low, queries, preferred_element_type=jnp.float32)
        * score_scale
    )
    grad_query_lin = rotate_back(grad_queries.reshape(head_shape), cosine, sine_part).reshape(
        row_count, heads_here * head_dim
    )
    grad_key_lin = rotate_back(grad_keys.reshape(head_shape), cosine, sine_part).reshape(
        row_count, heads_here * head_dim
    )
    grad_value_lin = grad_values.reshape(row_count, heads_here * head_dim)
    grad_projected = jnp.stack([grad_query_lin, grad_key_lin, grad_value_lin], axis=1).astype(
        jnp.bfloat16
    )
    grad_w_qkv = jnp.einsum(
        "td,tck->dck", attn_normed_low, grad_projected, preferred_element_type=jnp.float32
    )
    grad_attn_normed = lax.psum(
        jnp.einsum("tck,dck->td", grad_projected, w_qkv, preferred_element_type=jnp.float32).astype(
            jnp.bfloat16
        ),
        "tensor",
    ).astype(jnp.float32)
    norm_grad_input, grad_attn_gain = plain_norm_back(
        input_rows, attn_inverse, attn_gain, grad_attn_normed
    )
    input_grad = grad_mid + norm_grad_input
    grad_attn_gain, grad_w_qkv, grad_bias, grad_w_out, grad_ffn_gain, grad_w_gate_up, grad_down = (
        lax.psum(
            (
                grad_attn_gain,
                grad_w_qkv,
                grad_bias,
                grad_w_out,
                grad_ffn_gain,
                grad_w_gate_up,
                grad_down,
            ),
            "dp",
        )
    )
    return (
        block_output,
        input_grad,
        grad_attn_gain,
        grad_w_qkv,
        grad_bias,
        grad_w_out,
        grad_ffn_gain,
        grad_w_gate_up,
        grad_down,
    )


def solution(mesh):
    placed = (
        P("dp", None), P("dp"), P("dp"), P("dp"), P(), P(None, None, "tensor"), P(None, "tensor"),
        P("tensor", None), P(), P(None, None, "tensor"), P("tensor", None), P("dp", None),
    )
    fast = (mesh.shape["dp"], mesh.shape["tensor"]) == (16, 2)
    return jax.shard_map(
        fast_local if fast else plain_local,
        mesh=mesh,
        in_specs=placed,
        out_specs=(
            P("dp", None), P("dp", None), P(), P(None, None, "tensor"), P(None, "tensor"), P("tensor", None), P(),
            P(None, None, "tensor"), P("tensor", None),
        ),
        check_vma=False,
    )
```

```python
import functools
import math

import jax
import jax.numpy as jnp
from jax import lax
from jax.experimental import pallas as pl
from jax.experimental.pallas import tpu as pltpu
from jax.sharding import PartitionSpec as P

LEN = 1024
EPSILON = 1e-05
MASKED = -1000000000.0
BF = jnp.bfloat16
F32 = jnp.float32
MESH = pl.DeviceIdType.MESH
VMEM_LIMIT = 60 * 1024 * 1024
LANES = 128
HEAD = 64
VAR_COLS = 4
SEG_COL = 12
ONE_COL = 20
ROWS = 32
LAGS = (2, 4, 6, 8, 10)
SWAP_ROWS = 32
HALF_ROWS = 512
QUARTER_ROWS = HALF_ROWS // 2
GROUP_ROWS = 4 * HALF_ROWS
KEPT_ROWS = GROUP_ROWS - QUARTER_ROWS
WIDE = 1024
SMALL = 8
FFN_ROWS = 512
FFN_COLS = 256


def dot_nn(a, b):
    return lax.dot_general(a, b, (((1,), (0,)), ((), ())), preferred_element_type=F32)


def dot_nt(a, b):
    return lax.dot_general(a, b, (((1,), (1,)), ((), ())), preferred_element_type=F32)


def dot_tn(a, b):
    return lax.dot_general(a, b, (((0,), (0,)), ((), ())), preferred_element_type=F32)


def whole_spec():
    return pl.BlockSpec(memory_space=pltpu.VMEM)


def split3(v):
    hi = v.astype(BF).astype(F32)
    mid = (v - hi).astype(BF).astype(F32)
    return hi, mid, v - hi - mid


def half_swap(u):
    lane = lax.broadcasted_iota(jnp.int32, u.shape, 1) % HEAD
    return jnp.where(lane < HEAD // 2, pltpu.roll(u, LANES - HEAD // 2, 1), pltpu.roll(u, HEAD // 2, 1))


def qkv_body(x_ref, gain_ref, w_ref, cos_ref, sin_ref, xn_ref, q_ref, k_ref, v_ref):
    x = x_ref[...].astype(F32)
    inv = lax.rsqrt(jnp.mean(x * x, axis=-1, keepdims=True) + EPSILON)
    xn = (x * inv * gain_ref[...]).astype(BF)
    xn_ref[...] = xn
    cosine = cos_ref[...]
    sine = sin_ref[...]
    for part, out, factor in ((0, q_ref, HEAD**-0.5), (1, k_ref, 1.0)):
        lin = dot_nn(xn, w_ref[part])
        for s in range(lin.shape[1] // LANES):
            u = lin[:, s * LANES : (s + 1) * LANES]
            rot = (u * cosine + half_swap(u) * sine).astype(BF)
            if factor != 1.0:
                rot = (rot.astype(F32) * factor).astype(BF)
            out[:, s * LANES : (s + 1) * LANES] = rot
    v_ref[...] = dot_nn(xn, w_ref[2]).astype(BF)


def qkv_call(x, gain, w, cosine, sine):
    rows, dim = x.shape
    width = w.shape[2]
    blk = min(256, rows)
    row = lambda cols: pl.BlockSpec((blk, cols), lambda i: (i, 0))
    return pl.pallas_call(
        qkv_body,
        grid=(rows // blk,),
        out_shape=[jax.ShapeDtypeStruct((rows, dim), BF)] + [jax.ShapeDtypeStruct((rows, width), BF)] * 3,
        in_specs=[
            row(dim),
            pl.BlockSpec((1, dim), lambda i: (0, 0)),
            pl.BlockSpec(w.shape, lambda i: (0, 0, 0)),
            row(LANES),
            row(LANES),
        ],
        out_specs=[row(dim), row(width), row(width), row(width)],
        compiler_params=pltpu.CompilerParams(vmem_limit_bytes=VMEM_LIMIT),
        name="qkv",
    )(x, gain, w, cosine, sine)


def attn_fwd_body(
    q_ref, k_ref, v_ref, base_ref, segq_ref, extk_ref, bias_ref, w_ref, o_ref, o32_ref, extq_ref, wg_ref, wu_ref
):
    rows = q_ref.shape[0]
    for t in range(w_ref.shape[1] // 8):
        turned = jnp.swapaxes(w_ref[:, t * 8 : (t + 1) * 8, :].astype(F32), 0, 1)
        for k in range(8):
            s = t * 4 + k // 2
            (wg_ref, wu_ref)[k % 2][:, s * LANES : (s + 1) * LANES] = turned[k].astype(BF)
    blk = 256
    lane = lax.broadcasted_iota(jnp.int32, (blk, LANES), 1)
    kx = jnp.concatenate([k_ref[...], extk_ref[...]], axis=1)
    ones = jnp.ones((rows, LANES), BF)
    vx = jnp.concatenate([v_ref[...], ones], axis=1)
    for i in range(rows // blk):
        sl = slice(i * blk, (i + 1) * blk)
        q = q_ref[sl, :].astype(F32)
        base = base_ref[sl, :]
        segq = segq_ref[sl, :]
        outs = []
        for h in range(2):
            ext = base * bias_ref[0, h : h + 1, :] + segq
            mine = (lane >= HEAD) if h else (lane < HEAD)
            qx = jnp.concatenate([jnp.where(mine, q, 0.0), ext], axis=1).astype(BF)
            s = dot_nt(qx, kx)
            top = jnp.max(s, axis=-1, keepdims=True)
            p = jnp.exp(s - top).astype(BF)
            ox = dot_nn(p, vx)
            total = ox[:, LANES:]
            outs.append(ox[:, :LANES] / total)
            lse = top + jnp.log(total)
            hi, mid, low = split3(lse)
            ext = jnp.where(
                lane == ONE_COL, -hi, jnp.where(lane == ONE_COL + 1, -mid, jnp.where(lane == ONE_COL + 2, -low, ext))
            )
            extq_ref[0, h, sl, :] = ext.astype(BF)
        o = jnp.where(lane < HEAD, outs[0], outs[1])
        o32_ref[sl, :] = o
        o_ref[sl, :] = o.astype(BF)


def attn_fwd_call(q, k, v, base, segq, extk, bias_rows, w_pairs):
    rows, width = q.shape
    pairs = width // LANES
    dim, tiles, _ = w_pairs.shape
    share = dim // pairs
    half_w = pl.BlockSpec((share, tiles * LANES // 2), lambda p: (p, 0))
    col = pl.BlockSpec((rows, LANES), lambda p: (0, p))
    full = pl.BlockSpec((rows, LANES), lambda p: (0, 0))
    return pl.pallas_call(
        attn_fwd_body,
        grid=(pairs,),
        out_shape=[
            jax.ShapeDtypeStruct((rows, width), BF),
            jax.ShapeDtypeStruct((rows, width), F32),
            jax.ShapeDtypeStruct((pairs, 2, rows, LANES), BF),
            jax.ShapeDtypeStruct((dim, tiles * LANES // 2), BF),
            jax.ShapeDtypeStruct((dim, tiles * LANES // 2), BF),
        ],
        in_specs=[
            col, col, col, full, full, full,
            pl.BlockSpec((1, 2, LANES), lambda p: (p, 0, 0)),
            pl.BlockSpec((share, tiles, LANES), lambda p: (p, 0, 0)),
        ],
        out_specs=[col, col, pl.BlockSpec((1, 2, rows, LANES), lambda p: (p, 0, 0, 0)), half_w, half_w],
        compiler_params=pltpu.CompilerParams(vmem_limit_bytes=VMEM_LIMIT),
        name="attn_fwd",
    )(q, k, v, base, segq, extk, bias_rows, w_pairs)


def attn_bwd_body(
    q_ref, k_ref, v_ref, do_ref, o32_ref, extq_ref, extk_ref, oh_ref, cos_ref, sin_ref, d_ref, gb_ref, dqt_ref
):
    rows = q_ref.shape[0]
    blk = 256
    lane = lax.broadcasted_iota(jnp.int32, (blk, LANES), 1)
    kx = jnp.concatenate([k_ref[...], extk_ref[...]], axis=1)
    kxt = kx.T
    lane_all = lax.broadcasted_iota(jnp.int32, (rows, LANES), 1)
    vx = jnp.concatenate([v_ref[...], jnp.where(lane_all < 3, 1.0, 0.0).astype(BF)], axis=1)
    dv = jnp.zeros((rows, LANES), F32)
    dk = jnp.zeros((rows, LANES), F32)
    for h in range(2):
        same = jnp.zeros((8, blk), F32)
        other = jnp.zeros((8, blk), F32)
        for i in range(rows // blk):
            sl = slice(i * blk, (i + 1) * blk)
            mine = (lane >= HEAD) if h else (lane < HEAD)
            q = jnp.where(mine, q_ref[sl, :].astype(F32), 0.0).astype(BF)
            do32 = jnp.where(mine, do_ref[sl, :].astype(F32), 0.0)
            do = do32.astype(BF)
            delta = jnp.sum(do32 * o32_ref[sl, :], axis=-1, keepdims=True)
            hi, mid, low = split3(delta)
            dext = jnp.where(lane == 0, -hi, jnp.where(lane == 1, -mid, jnp.where(lane == 2, -low, 0.0))).astype(BF)
            st = dot_nt(kx, jnp.concatenate([q, extq_ref[0, h, sl, :]], axis=1))
            pt = jnp.exp(st)
            dpt = dot_nt(vx, jnp.concatenate([do, dext], axis=1))
            dst = (pt * dpt).astype(BF)
            dv = dv + dot_nn(pt.astype(BF), do)
            dk = dk + dot_nn(dst, q)
            dqt = dot_nn(kxt, dst)
            dqt_ref[h * HEAD : (h + 1) * HEAD, sl] = dqt[h * HEAD : (h + 1) * HEAD, :]
            g = dqt[LANES : LANES + 8, :]
            oh = oh_ref[0, :, sl]
            same = same + g * oh
            other = other + g * oh_ref[1, :, sl]
        gb_ref[0, h, 0] = same
        gb_ref[0, h, 1] = other
    cosine = cos_ref[...]
    sine = sin_ref[...]
    dq = dqt_ref[...].T * HEAD**-0.5
    d_ref[0] = (dq * cosine - half_swap(dq) * sine).astype(BF)
    d_ref[1] = (dk * cosine - half_swap(dk) * sine).astype(BF)
    d_ref[2] = dv.astype(BF)


def attn_bwd_call(q, k, v, do, o32, extq, extk, onehot, cosine, sine):
    rows, width = q.shape
    pairs = width // LANES
    col = pl.BlockSpec((rows, LANES), lambda p: (0, p))
    full = pl.BlockSpec((rows, LANES), lambda p: (0, 0))
    blk = 256
    return pl.pallas_call(
        attn_bwd_body,
        grid=(pairs,),
        out_shape=[jax.ShapeDtypeStruct((3, rows, width), BF), jax.ShapeDtypeStruct((pairs, 2, 2, 8, blk), F32)],
        in_specs=[
            col, col, col, col, col,
            pl.BlockSpec((1, 2, rows, LANES), lambda p: (p, 0, 0, 0)),
            full,
            pl.BlockSpec((2, 8, rows), lambda p: (0, 0, 0)),
            full, full,
        ],
        out_specs=[pl.BlockSpec((3, rows, LANES), lambda p: (0, 0, p)), pl.BlockSpec((1, 2, 2, 8, blk), lambda p: (p, 0, 0, 0, 0))],
        scratch_shapes=[pltpu.VMEM((LANES, rows), F32)],
        compiler_params=pltpu.CompilerParams(vmem_limit_bytes=VMEM_LIMIT),
        name="attn_bwd",
    )(q, k, v, do, o32, extq, extk, onehot, cosine, sine)


def partner_barrier():
    dp = lax.axis_index("dp")
    other = 1 - lax.axis_index("tensor")
    barrier = pltpu.get_barrier_semaphore()
    pl.semaphore_signal(barrier, inc=1, device_id=(dp, other), device_id_type=MESH)
    pl.semaphore_wait(barrier, 1)
    return (dp, other)


def send_rows(src, dst, sl, ssem, rsem, peer):
    return pltpu.make_async_remote_copy(
        src_ref=src.at[sl], dst_ref=dst.at[sl], send_sem=ssem, recv_sem=rsem, device_id=peer, device_id_type=MESH
    )


CHUNKS = 4


def attn_out_body(x_ref, o_ref, w_ref, gain_ref, mid_ref, xn_ref, mine, theirs, ssem, rsem):
    peer = partner_barrier()
    rows = x_ref.shape[0]
    blk = rows // CHUNKS
    copies = []
    for c in range(CHUNKS):
        sl = slice(c * blk, (c + 1) * blk)
        mine[sl, :] = dot_nn(o_ref[sl, :], w_ref[...]).astype(BF)
        copy = send_rows(mine, theirs, pl.ds(c * blk, blk), ssem.at[c], rsem.at[c], peer)
        copy.start()
        copies.append(copy)
    for c in range(CHUNKS):
        sl = slice(c * blk, (c + 1) * blk)
        copies[c].wait_recv()
        mid = x_ref[sl, :].astype(F32) + (mine[sl, :].astype(F32) + theirs[sl, :].astype(F32))
        inv = lax.rsqrt(jnp.mean(mid * mid, axis=-1, keepdims=True) + EPSILON)
        mid_ref[sl, :] = mid
        xn_ref[sl, :] = (mid * inv * gain_ref[...]).astype(BF)
    for c in range(CHUNKS):
        copies[c].wait_send()


def attn_out_call(x, o, w, gain):
    rows, dim = x.shape
    return pl.pallas_call(
        attn_out_body,
        out_shape=[jax.ShapeDtypeStruct((rows, dim), F32), jax.ShapeDtypeStruct((rows, dim), BF)],
        in_specs=[whole_spec()] * 4,
        out_specs=[whole_spec()] * 2,
        scratch_shapes=[
            pltpu.VMEM((rows, dim), BF),
            pltpu.VMEM((rows, dim), BF),
            pltpu.SemaphoreType.DMA((CHUNKS,)),
            pltpu.SemaphoreType.DMA((CHUNKS,)),
        ],
        compiler_params=pltpu.CompilerParams(collective_id=1, has_side_effects=True, vmem_limit_bytes=VMEM_LIMIT),
        name="attn_out",
    )(x, o, w, gain)


LATE = 4
SLOTS = 4
PART = FFN_COLS // 4


def sent(copy):
    copy.wait_send() if copy.is_remote else copy.wait()


def grid_bits():
    dp = lax.axis_index("dp")
    return dp, dp % 2, (dp // 2) % 2, peers_of(dp)[3], peers_of(dp)[4]


def ffn_body(
    xn_ref, ct_ref, wg_ref, wu_ref, wd_ref,
    out_ref, gx_ref, gk_ref, uk_ref, rg, ru, dk, rd, late_x, late_y,
    acc_o, acc_g, hid, dg, du, xt, away_w, away_d, ws, wr, ds, dr,
):
    j = pl.program_id(0)
    t = lax.axis_index("tensor")
    dp, x, y, px, py = grid_bits()
    steps = pl.num_programs(0)
    rows = xn_ref.shape[0]
    blk = wd_ref.shape[0]
    per = WIDE // blk
    early = 2 * per - LATE
    slot = lax.rem(j, SLOTS)
    near = (px, py)
    bits = (x, y)
    arrays = ((rg, late_x), (ru, late_y))

    def remote(src, dst, ssem, rsem, peer):
        return pltpu.make_async_remote_copy(
            src_ref=src, dst_ref=dst, send_sem=ssem, recv_sem=rsem, device_id=(peer, t), device_id_type=MESH
        )

    def wide_early(k, at):
        cols = pl.ds(pl.multiple_of(lax.rem(at, per) * blk, blk), blk)
        s = lax.rem(at, SLOTS)
        return remote(away_w.at[k, s], arrays[k][0].at[:, cols], ws.at[k, s], wr.at[k], near[k])

    def wide_late(k, at):
        cols = pl.ds(pl.multiple_of((at - early) * blk, blk), blk)
        s = lax.rem(at, SLOTS)
        return pltpu.make_async_copy(away_w.at[k, s], arrays[k][1].at[pl.ds(0, HALF_ROWS), cols], ws.at[k, s])

    def wide_do(at, act):
        for k in range(2):

            @pl.when(at < early)
            def _():
                act(wide_early(k, at))

            @pl.when(at >= early)
            def _():
                act(wide_late(k, at))

    def down_rows(g, half):
        return pl.ds(pl.multiple_of(g * 2 * PART + half * PART, PART), PART)

    def down_keep(g, at):
        s = lax.rem(at, SLOTS)
        return pltpu.make_async_copy(
            away_d.at[s, down_rows(g, bits[g])], dk.at[g, pl.ds(pl.multiple_of(at * PART, PART), PART)], ds.at[g, s]
        )

    def down_send(g, at):
        s = lax.rem(at, SLOTS)
        rows_at = pl.ds(pl.multiple_of(at * PART, PART), PART)
        return remote(away_d.at[s, down_rows(g, 1 - bits[g])], rd.at[g, rows_at], ds.at[2 + g, s], dr.at[g], near[g])

    def down_late(g, at):
        s = lax.rem(at, SLOTS)
        rows_at = pl.ds(pl.multiple_of(HALF_ROWS + (at - early) * PART, PART), PART)
        return pltpu.make_async_copy(
            away_d.at[s, down_rows(g, 1 - bits[g])], arrays[g][1].at[rows_at], ds.at[2 + g, s]
        )

    def down_do(at, act):
        for g in range(2):
            act(down_keep(g, at))

            @pl.when(at < early)
            def _():
                act(down_send(g, at))

            @pl.when(at >= early)
            def _():
                act(down_late(g, at))

    @pl.when(j == 0)
    def _():
        barrier = pltpu.get_barrier_semaphore()
        for peer in near:
            pl.semaphore_signal(barrier, inc=1, device_id=(peer, t), device_id_type=MESH)
        pl.semaphore_wait(barrier, 2)
        acc_o[...] = jnp.zeros_like(acc_o)
        acc_g[...] = jnp.zeros_like(acc_g)
        xt[...] = xn_ref[...].T

    wg = wg_ref[...]
    wu = wu_ref[...]
    wd = wd_ref[...]
    for i in range(rows // FFN_ROWS):
        sl = slice(i * FFN_ROWS, (i + 1) * FFN_ROWS)
        xn = xn_ref[sl, :]
        gate = dot_nn(xn, wg)
        up = dot_nn(xn, wu)
        gh = dot_nt(ct_ref[sl, :], wd)
        sig = jax.nn.sigmoid(gate)
        silu = gate * sig
        hidden = (silu * up).astype(BF)
        dgate = (gh * up * sig * (1.0 + gate * (1.0 - sig))).astype(BF)
        dup = (gh * silu).astype(BF)
        hid[sl, :] = hidden
        dg[sl, :] = dgate
        du[sl, :] = dup
        acc_o[sl, :] += dot_nn(hidden, wd)
        acc_g[sl, :] += dot_nt(dgate, wg) + dot_nt(dup, wu)

    @pl.when(j >= SLOTS)
    def _():
        wide_do(j - SLOTS, sent)
        down_do(j - SLOTS, sent)

    away_d[slot] = dot_tn(hid[...], ct_ref[...]).astype(BF)
    down_do(j, lambda copy: copy.start())
    for k, (part, keep, bit) in enumerate(((dg, gk_ref, x), (du, uk_ref, y))):
        rows_at = lambda half: pl.ds(pl.multiple_of(half * HALF_ROWS, HALF_ROWS), HALF_ROWS)
        away_w[k, slot] = dot_nn(xt[rows_at(1 - bit), :], part[...]).astype(BF)
        keep[0] = dot_nn(xt[rows_at(bit), :], part[...]).astype(BF)
    wide_do(j, lambda copy: copy.start())

    @pl.when(j == steps - 1)
    def _():
        out_ref[...] = acc_o[...].astype(BF)
        gx_ref[...] = acc_g[...].astype(BF)
        for back in range(SLOTS, 0, -1):
            wide_do(steps - back, sent)
            down_do(steps - back, sent)
        for k in range(2):
            part = arrays[k][0].at[:, pl.ds(0, early * blk)]
            remote(part, part, ws.at[k, 0], wr.at[k], near[k]).wait_recv()
        for g in range(2):
            part = rd.at[g, pl.ds(0, early * PART)]
            remote(part, part, ds.at[g, 0], dr.at[g], near[g]).wait_recv()


def ffn_call(xn, ct, wg, wu, wd):
    rows, dim = xn.shape
    hidden = wd.shape[0]
    blk = FFN_COLS
    per = WIDE // blk
    full = pl.BlockSpec((rows, dim), lambda j: (0, 0))
    colw = pl.BlockSpec((dim, blk), lambda j: (0, j))
    roww = pl.BlockSpec((blk, dim), lambda j: (j, 0))
    grad = pl.BlockSpec((1, HALF_ROWS, blk), lambda j: (j // per, 0, lax.rem(j, per)))
    any_spec = pl.BlockSpec(memory_space=pl.ANY)
    wide = jax.ShapeDtypeStruct((2, HALF_ROWS, dim), BF)
    early = hidden // blk - LATE
    come = jax.ShapeDtypeStruct((HALF_ROWS, early * blk), BF)
    late = jax.ShapeDtypeStruct((HALF_ROWS + LATE * PART, LATE * blk), BF)
    dma = pltpu.SemaphoreType.DMA
    return pl.pallas_call(
        ffn_body,
        grid=(hidden // blk,),
        in_specs=[full, full, colw, colw, roww],
        out_specs=[full, full, grad, grad] + [any_spec] * 6,
        out_shape=[jax.ShapeDtypeStruct((rows, dim), BF)] * 2
        + [wide, wide, come, come, wide, jax.ShapeDtypeStruct((2, early * PART, dim), BF), late, late],
        scratch_shapes=[pltpu.VMEM((rows, dim), F32)] * 2
        + [pltpu.VMEM((rows, blk), BF)] * 3
        + [
            pltpu.VMEM((dim, rows), BF),
            pltpu.VMEM((2, SLOTS, HALF_ROWS, blk), BF),
            pltpu.VMEM((SLOTS, blk, dim), BF),
            dma((2, SLOTS)), dma((2,)), dma((4, SLOTS)), dma((2,)),
        ],
        compiler_params=pltpu.CompilerParams(collective_id=5, has_side_effects=True, vmem_limit_bytes=VMEM_LIMIT),
        name="ffn",
    )(xn, ct, wg, wu, wd)


def pair_rows(w):
    dim, two, width = w.shape
    tiled = jnp.transpose(w.reshape(dim, two, width // LANES, LANES), (0, 2, 1, 3))
    return tiled.reshape(dim, two * width // LANES, LANES)


def widen_body(ga_ref, gb_ref, da_ref, db_ref, aa_ref, v_ref, o_ref, gu_ref, down_ref, qkv_ref, out_ref):
    tiles = WIDE // LANES
    for f in range(2):
        for q in range(tiles // 4):
            parts = []
            for k in range(8):
                s = q * 4 + k // 2
                parts.append((ga_ref, gb_ref)[k % 2][0, f, :, s * LANES : (s + 1) * LANES].astype(F32))
            at = (f * tiles + q * 4) * 2
            gu_ref[:, at : at + 8, :] = jnp.swapaxes(jnp.stack(parts), 0, 1)
    down_ref[:, 0, 0] = da_ref[0, 0].astype(F32).reshape(down_ref.shape[0], PART, WIDE)
    down_ref[:, 1, 0] = db_ref[0, 0].astype(F32).reshape(down_ref.shape[0], PART, WIDE)
    width = qkv_ref.shape[2]
    qkv_ref[0] = aa_ref[0, 0, :, :width].astype(F32)
    qkv_ref[1] = aa_ref[0, 0, :, width:].astype(F32)
    qkv_ref[2] = v_ref[0, 0].astype(F32)
    out_ref[...] = o_ref[0, 0].astype(F32)


def widen_call(a, b):
    blk = 256
    half = HALF_ROWS // blk
    tiles = 4 * WIDE // LANES
    width = WIDE // 2
    gate = pl.BlockSpec((1, 2, blk, WIDE), lambda i: (i // half, 0, lax.rem(i, half), 0))
    block = lambda n: pl.BlockSpec((1, 1, blk, WIDE), lambda i: (i // half, n, lax.rem(i, half), 0))
    gu, down, qkv, out = pl.pallas_call(
        widen_body,
        grid=(2 * half,),
        out_shape=[
            jax.ShapeDtypeStruct((2 * HALF_ROWS, tiles, LANES), F32),
            jax.ShapeDtypeStruct((HALF_ROWS // PART, 2, 2, PART, WIDE), F32),
            jax.ShapeDtypeStruct((3, 2 * HALF_ROWS, width), F32),
            jax.ShapeDtypeStruct((HALF_ROWS, WIDE), F32),
        ],
        in_specs=[
            gate, gate, block(2), block(2), block(3),
            pl.BlockSpec((1, 1, blk, width), lambda i: (0, 3, lax.rem(i, half), i // half)),
            pl.BlockSpec((1, 1, blk // 2, WIDE), lambda i: (1, 3, i, 0)),
        ],
        out_specs=[
            pl.BlockSpec((blk, tiles, LANES), lambda i: (i, 0, 0)),
            pl.BlockSpec((blk // PART, 2, 1, PART, WIDE), lambda i: (lax.rem(i, half), 0, i // half, 0, 0)),
            pl.BlockSpec((3, blk, width), lambda i: (0, i, 0)),
            pl.BlockSpec((blk // 2, WIDE), lambda i: (i, 0)),
        ],
        compiler_params=pltpu.CompilerParams(vmem_limit_bytes=VMEM_LIMIT),
        name="widen",
    )(a, b, a, b, a, b, b)
    gu = jnp.transpose(gu.reshape(2 * HALF_ROWS, tiles // 2, 2, LANES), (0, 2, 1, 3)).reshape(2 * HALF_ROWS, 2, 2 * WIDE)
    return gu, down.reshape(4 * HALF_ROWS, WIDE), qkv, out


def norm_back(rows_now, gain, grads):
    inv = lax.rsqrt(jnp.mean(rows_now * rows_now, axis=-1, keepdims=True) + EPSILON)
    scaled = grads * gain
    gain_grad = jnp.sum(grads * rows_now * inv, axis=0, keepdims=True)
    back = inv * scaled - rows_now * (inv * inv * inv) * jnp.mean(scaled * rows_now, axis=-1, keepdims=True)
    return back, gain_grad


def ffn_back_body(
    gx_ref, fo_ref, mid_ref, ct_ref, gain_ref, w_ref, at_ref,
    out_ref, gm_ref, do_ref, gw_ref, gg_ref, gx_in, fo_in, gb, ssem, rsem,
):
    peer = partner_barrier()
    rows = mid_ref.shape[0]
    blk = rows // CHUNKS
    copies = []
    for n, (src, dst) in enumerate(((gx_ref, gx_in), (fo_ref, fo_in))):
        for c in range(CHUNKS):
            at = n * CHUNKS + c
            copy = send_rows(src, dst, pl.ds(c * blk, blk), ssem.at[at], rsem.at[at], peer)
            copy.start()
            copies.append(copy)
    gain_sum = jnp.zeros((1, mid_ref.shape[1]), F32)
    for c in range(CHUNKS):
        sl = slice(c * blk, (c + 1) * blk)
        copies[c].wait_recv()
        grads = gx_ref[sl, :].astype(F32) + gx_in[sl, :].astype(F32)
        back, gain_grad = norm_back(mid_ref[sl, :], gain_ref[...], grads)
        gain_sum = gain_sum + gain_grad
        gm = ct_ref[sl, :].astype(F32) + back
        gm_ref[sl, :] = gm
        gb[sl, :] = gm.astype(BF)
        do_ref[sl, :] = dot_nt(gb[sl, :], w_ref[...]).astype(BF)
    gg_ref[...] = gain_sum
    gw_ref[...] = dot_tn(at_ref[...], gb[...]).astype(BF)
    for c in range(CHUNKS):
        sl = slice(c * blk, (c + 1) * blk)
        copies[CHUNKS + c].wait_recv()
        out_ref[sl, :] = (mid_ref[sl, :] + (fo_ref[sl, :].astype(F32) + fo_in[sl, :].astype(F32))).astype(BF)
    for copy in copies:
        copy.wait_send()


def ffn_back_call(gx, fo, mid, ct, gain, w, at):
    rows, dim = mid.shape
    width = w.shape[0]
    return pl.pallas_call(
        ffn_back_body,
        out_shape=[
            jax.ShapeDtypeStruct((rows, dim), BF),
            jax.ShapeDtypeStruct((rows, dim), F32),
            jax.ShapeDtypeStruct((rows, width), BF),
            jax.ShapeDtypeStruct((width, dim), BF),
            jax.ShapeDtypeStruct((1, dim), F32),
        ],
        in_specs=[whole_spec()] * 7,
        out_specs=[whole_spec()] * 5,
        scratch_shapes=[
            pltpu.VMEM((rows, dim), BF),
            pltpu.VMEM((rows, dim), BF),
            pltpu.VMEM((rows, dim), BF),
            pltpu.SemaphoreType.DMA((2 * CHUNKS,)),
            pltpu.SemaphoreType.DMA((2 * CHUNKS,)),
        ],
        compiler_params=pltpu.CompilerParams(collective_id=2, has_side_effects=True, vmem_limit_bytes=VMEM_LIMIT),
        name="ffn_back",
    )(gx, fo, mid, ct, gain, w, at)


def peers_of(dp):
    z = dp // 4
    y = (dp // 2) % 2
    x = dp % 2
    at = lambda zz, yy, xx: zz * 4 + yy * 2 + xx
    return z, y, x, at(z, y, 1 - x), at(z, 1 - y, x), at(z + 1 - 2 * (z % 2), y, x), at(3 - z, y, x)


def sum_body(
    gk, rg, uk, ru, late_x, late_y, dk, rd, go, dqkv, w3, xn, xin, gmid, gain_ref, small_in, out_a, out_b, ig, small_out,
    L, S, Z, R, Y, DL, DS, DA, G, sb, st, dl, wb, xb, mine_rows, their_rows, away_rows, xc, gc, ic,
    loc, s1s, s1r, sends, zr, rr, yr, ar, xr, lo, ss, sr, ld, cs, cr, xg, io, s2s, s2r, gs, gr,
):
    dp = lax.axis_index("dp")
    t = lax.axis_index("tensor")
    z, y, x, px, py, zn, mm = peers_of(dp)
    is_mid = (z == 1) | (z == 2)
    is_end = (z == 0) | (z == 3)
    mine = jnp.where(z == 2, WIDE // 2, 0)
    others = WIDE // 2 - mine
    n = KEPT_ROWS // ROWS
    cut_at = 2 * HALF_ROWS // ROWS
    tail_at = (2 * HALF_ROWS + QUARTER_ROWS) // ROWS
    starts = (0, HALF_ROWS // ROWS, cut_at, tail_at)
    first = (px, py)
    last = (py, px)
    outs = (out_a, out_b)
    owner = (x, y)
    bit = (y, x)
    F = S

    def remote(src, dst, ssem, rsem, peer, core=t):
        return pltpu.make_async_remote_copy(
            src_ref=src, dst_ref=dst, send_sem=ssem, recv_sem=rsem, device_id=(peer, core), device_id_type=MESH
        )

    def loads(g, b):
        rows = pl.ds(b * HALF_ROWS, HALF_ROWS)
        near = (rg, ru)[g]
        late = (late_x, late_y)[g]
        top = pl.ds(0, HALF_ROWS)
        if b < 2:
            copies = [((gk, uk)[g].at[b], L.at[g, rows])]
        else:
            copies = [(dk.at[g], DL.at[g])]
        if b == 0:
            copies.append((near.at[:, pl.ds(0, WIDE)], S.at[g, rows]))
        elif b == 1:
            cut = near.shape[1] - WIDE
            if cut:
                copies.append((near.at[:, pl.ds(WIDE, cut)], S.at[g, rows, pl.ds(0, cut)]))
            copies.append((late.at[top], S.at[g, rows, pl.ds(cut, WIDE - cut)]))
        else:
            cut = rd.shape[1]
            copies.append((rd.at[g], DS.at[g, pl.ds(0, cut)]))
            copies.append((late.at[pl.ds(HALF_ROWS, HALF_ROWS - cut)], DS.at[g, pl.ds(cut, HALF_ROWS - cut)]))
        return [pltpu.make_async_copy(src, dst, loc.at[g, b, k]) for k, (src, dst) in enumerate(copies)]

    own_loads = [pltpu.make_async_copy(src, dst, ld.at[k]) for k, (src, dst) in enumerate(((dqkv, dl), (w3, wb), (xn, xb)))]
    for b in range(3):
        for g in range(2):
            for copy in loads(g, b):
                copy.start()
    for copy in own_loads:
        copy.start()

    tail = pl.ds(2 * HALF_ROWS + QUARTER_ROWS, HALF_ROWS)

    def out_load(kept):
        return pltpu.make_async_copy(go, L.at[1, tail] if kept else away_rows.at[1], loc.at[1, 3, 0])

    def out_load_do(act):
        @pl.when(y == 1)
        def _():
            act(out_load(True))

        @pl.when(y == 0)
        def _():
            act(out_load(False))

    out_load_do(lambda copy: copy.start())

    barrier = pltpu.get_barrier_semaphore()
    others_z = [lax.rem(z + k, 4) * 4 + y * 2 + x for k in range(1, 4)]
    for peer in [px, py] + others_z:
        pl.semaphore_signal(barrier, inc=1, device_id=(peer, t), device_id_type=MESH)
    pl.semaphore_signal(barrier, inc=1, device_id=(dp, 1 - t), device_id_type=MESH)
    pl.semaphore_wait(barrier, 6)

    def first_exchange(g):
        return remote(away_rows.at[g], S.at[g, tail], s1s.at[g], s1r.at[g], first[g])

    def first_part(g, c):
        at = pl.multiple_of(c * SWAP_ROWS, SWAP_ROWS)
        dst = S.at[g, pl.ds(2 * HALF_ROWS + QUARTER_ROWS + at, SWAP_ROWS)]
        return remote(away_rows.at[g, pl.ds(at, SWAP_ROWS)], dst, s1s.at[g], s1r.at[g], first[g])

    quarter = pl.ds(2 * HALF_ROWS, QUARTER_ROWS)

    def second_exchange(g):
        return remote(DA.at[g], S.at[g, quarter], s2s.at[g], s2r.at[g], last[g])

    def second_part(g, c):
        at = pl.multiple_of(c * SWAP_ROWS, SWAP_ROWS)
        rows = pl.ds(at, SWAP_ROWS)
        dst = S.at[g, pl.ds(2 * HALF_ROWS + at, SWAP_ROWS)]
        return remote(DA.at[g, rows], dst, s2s.at[g], s2r.at[g], last[g])

    def down_quarter(half):
        return pl.ds(pl.multiple_of(half * QUARTER_ROWS, QUARTER_ROWS), QUARTER_ROWS)

    def piece_down(g):
        for copy in loads(g, 2):
            copy.wait()
        keep = down_quarter(bit[g])
        away = down_quarter(1 - bit[g])
        L[g, quarter, :] = (DL[g, keep, :].astype(F32) + DS[g, keep, :].astype(F32)).astype(BF)
        DA[g] = (DL[g, away, :].astype(F32) + DS[g, away, :].astype(F32)).astype(BF)

    def piece_swap(c):
        for g in range(2):
            first_part(g, c).start()

    def piece_second(c):
        for g in range(2):
            second_part(g, c).start()

    small_x = remote(st.at[2], sb.at[0], ss.at[0], sr.at[0], px)
    small_y = remote(st.at[0], sb.at[1], ss.at[1], sr.at[1], py)
    small_z = [remote(st.at[1], sb.at[2 + z], ss.at[2 + k], sr.at[2 + z], others_z[k]) for k in range(3)]

    def rows_of(i):
        return pl.ds(pl.multiple_of(i * ROWS, ROWS), ROWS)

    def cols_of(at):
        return pl.ds(pl.multiple_of(at, WIDE // 2), WIDE // 2)

    def z_copy(g, i):
        return remote(L.at[g, rows_of(i)], Z.at[g, rows_of(i)], sends.at[g, 0], zr.at[g, i], zn)

    def r_copy(g, i):
        return remote(L.at[g, rows_of(i), cols_of(others)], R.at[g, rows_of(i)], sends.at[g, 1], rr.at[g, i], mm)

    def y_copy(g, i):
        return remote(R.at[g, rows_of(i)], Y.at[g, rows_of(i)], sends.at[g, 2], yr.at[g, i], last[g])

    def a_copy(g, i, at):
        return remote(F.at[g, rows_of(i), cols_of(at)], F.at[g, rows_of(i), cols_of(at)], sends.at[g, 3], ar.at[g, i], mm)

    def o_copy(g, i):
        return remote(F.at[g, rows_of(i)], F.at[g, rows_of(i)], sends.at[g, 4], zr.at[g, i], zn)

    def out_rows(g, i):
        shift = jnp.where(i < cut_at, 0, jnp.where(i < tail_at, bit[g] * QUARTER_ROWS, QUARTER_ROWS))
        return pl.ds(pl.multiple_of(i * ROWS + shift, ROWS), ROWS)

    def x_copy(g, i):
        return remote(F.at[g, rows_of(i)], outs[g].at[owner[g], out_rows(g, i)], sends.at[g, 5], xr.at[g], first[g])

    def l_copy(g, i):
        return pltpu.make_async_copy(F.at[g, rows_of(i)], outs[g].at[owner[g], out_rows(g, i)], lo.at[g])

    def quarter_rows(i):
        return pl.ds(pl.multiple_of((i - cut_at) * ROWS, ROWS), ROWS)

    def g_copy(g, i):
        return remote(F.at[g, rows_of(i)], G.at[g, quarter_rows(i)], gs.at[g], gr.at[g, i - cut_at], last[g])

    def pass_on(g, i):
        rows = pl.ds(pl.multiple_of(i * ROWS + (1 - bit[g]) * QUARTER_ROWS, ROWS), ROWS)
        src = G.at[g, quarter_rows(i)]
        g_copy(g, i).wait_recv()
        remote(src, outs[g].at[owner[g], rows], sends.at[g, 5], xr.at[g], first[g]).start()
        pltpu.make_async_copy(src, outs[g].at[owner[g], rows], lo.at[g]).start()

    def is_cut(i):
        return (i >= cut_at) & (i < tail_at)

    def finish(g, i):
        x_copy(g, i).start()
        l_copy(g, i).start()

        @pl.when(is_cut(i))
        def _():
            g_copy(g, i).start()

    def end_in(g, j):
        r = rows_of(j)
        L[g, r, :] = (L[g, r, :].astype(F32) + S[g, r, :].astype(F32)).astype(BF)
        z_copy(g, j).start()

    def end_out(g, j):
        o_copy(g, j).wait_recv()
        finish(g, j)

    def mid_out(g, j):
        a_copy(g, j, others).wait_recv()
        o_copy(g, j).start()
        finish(g, j)

    def mid_join(g, j):
        @pl.when(jnp.logical_not(is_cut(j)))
        def _():
            y_copy(g, j).wait_recv()
            r = rows_of(j)
            F[g, r, cols_of(mine)] = (R[g, r, :].astype(F32) + Y[g, r, :].astype(F32)).astype(BF)
            a_copy(g, j, mine).start()

    def mid_half(g, j):
        r_copy(g, j).wait_recv()
        r = rows_of(j)
        total = (R[g, r, :].astype(F32) + L[g, r, cols_of(mine)].astype(F32)).astype(BF)

        @pl.when(is_cut(j))
        def _():
            F[g, r, cols_of(mine)] = total
            a_copy(g, j, mine).start()

        @pl.when(jnp.logical_not(is_cut(j)))
        def _():
            R[g, r, :] = total
            y_copy(g, j).start()

    def mid_in(g, j):
        z_copy(g, j).wait_recv()
        r = rows_of(j)
        L[g, r, :] = (L[g, r, :].astype(F32) + S[g, r, :].astype(F32) + Z[g, r, :].astype(F32)).astype(BF)
        r_copy(g, j).start()

    def stage(act, g, j):
        @pl.when((j >= 0) & (j < n))
        def _():
            act(g, j)

    seq = xin.shape[0]
    blk = seq // CHUNKS
    width = dl.shape[2]

    def piece_rows(c):
        return pl.ds(pl.multiple_of(c * blk, blk), blk)

    def core_copy(c):
        return remote(mine_rows.at[piece_rows(c)], their_rows.at[piece_rows(c)], cs.at[c], cr.at[c], dp, 1 - t)

    def norm_loads(c):
        return [
            pltpu.make_async_copy(xin.at[piece_rows(c)], xc.at[lax.rem(c, 2)], xg.at[lax.rem(c, 2), 0]),
            pltpu.make_async_copy(gmid.at[piece_rows(c)], gc.at[lax.rem(c, 2)], xg.at[lax.rem(c, 2), 1]),
        ]

    def ig_copy(c):
        return pltpu.make_async_copy(ic.at[lax.rem(c, 2)], ig.at[piece_rows(c)], io.at[lax.rem(c, 2)])

    def piece_start():
        for copy in own_loads:
            copy.wait()

    def piece_part(c):
        r = piece_rows(c)
        total = dot_nt(dl[0, r, :], wb[0]) + dot_nt(dl[1, r, :], wb[1]) + dot_nt(dl[2, r, :], wb[2])
        mine_rows[r, :] = total.astype(BF)
        core_copy(c).start()

    def row_half(half):
        return pl.ds(pl.multiple_of(half * HALF_ROWS, HALF_ROWS), HALF_ROWS)

    def piece_qk(k):
        cols = pl.ds(k * width, width)
        L[0, tail, cols] = dot_tn(xb[:, row_half(x)], dl[k]).astype(BF)
        away_rows[0, :, cols] = dot_tn(xb[:, row_half(1 - x)], dl[k]).astype(BF)

    def piece_v():
        for k in range(2):
            cols = pl.ds(k * width, width)
            grad = dot_tn(xb[:, k * HALF_ROWS : (k + 1) * HALF_ROWS], dl[2]).astype(BF)

            @pl.when(y == 0)
            def _():
                L[1, tail, cols] = grad

            @pl.when(y == 1)
            def _():
                away_rows[1, :, cols] = grad

    def piece_send():
        out_load_do(lambda copy: copy.wait())
        for copy in norm_loads(0):
            copy.start()
        st[2] = small_in[...]

    def piece_norm(c):
        @pl.when(c + 1 < CHUNKS)
        def _():
            for copy in norm_loads(c + 1):
                copy.start()

        for copy in norm_loads(c):
            copy.wait()
        core_copy(c).wait_recv()

        @pl.when(c >= 2)
        def _():
            ig_copy(c - 2).wait()

        r = piece_rows(c)
        grads = mine_rows[r, :].astype(F32) + their_rows[r, :].astype(F32)
        s = lax.rem(c, 2)
        back, gain_grad = norm_back(xc[s].astype(F32), gain_ref[...], grads)
        st[2, 0:1, :] = st[2, 0:1, :] + gain_grad
        ic[s] = gc[s] + back
        ig_copy(c).start()

    def small_first():
        small_x.start()

    def small_second():
        small_x.wait_recv()
        st[0] = st[2] + sb[0]
        small_y.start()

    def small_third():
        small_y.wait_recv()
        st[1] = st[0] + sb[1]
        for copy in small_z:
            copy.start()

    pieces = [
        (1, 1, lambda c: piece_down(0)),
        (2, 1, lambda c: piece_down(1)),
        (3, QUARTER_ROWS // SWAP_ROWS, piece_second),
        (3, 1, lambda c: piece_start()),
        (4, CHUNKS, piece_part),
        (4 + CHUNKS, 1, lambda c: piece_qk(0)),
        (5 + CHUNKS, 1, lambda c: piece_qk(1)),
        (6 + CHUNKS, 1, lambda c: piece_v()),
        (7 + CHUNKS, 1, lambda c: piece_send()),
        (8 + CHUNKS, HALF_ROWS // SWAP_ROWS, piece_swap),
        (9 + CHUNKS, CHUNKS, piece_norm),
        (10 + 2 * CHUNKS, 1, lambda c: small_first()),
        (14 + 2 * CHUNKS, 1, lambda c: small_second()),
        (18 + 2 * CHUNKS, 1, lambda c: small_third()),
    ]

    def body(i, carry):
        for b in range(4):

            @pl.when(i == starts[b])
            def _():
                for g in range(2):
                    if b < 2:
                        for copy in loads(g, b):
                            copy.wait()
                    elif b == 2:
                        second_exchange(g).wait_recv()
                    else:
                        first_exchange(g).wait_recv()

        @pl.when(is_end)
        def _():
            for g in range(2):
                stage(end_in, g, i)
                stage(end_out, g, i - LAGS[4])

        @pl.when(is_mid)
        def _():
            for g in range(2):
                stage(mid_out, g, i - LAGS[3])
                stage(mid_join, g, i - LAGS[2])
                stage(mid_half, g, i - LAGS[1])
                stage(mid_in, g, i - LAGS[0])

        for g in range(2):
            j = i - LAGS[4] - 2

            @pl.when(is_cut(j))
            def _():
                pass_on(g, j)

        for begin, steps, piece in pieces:

            @pl.when((i >= begin) & (i < begin + steps))
            def _():
                piece(i - begin)

        return carry

    lax.fori_loop(0, n + LAGS[4], body, 0)

    for k in range(3):
        zz = lax.rem(z + k + 1, 4)
        remote(st.at[1], sb.at[2 + zz], ss.at[2 + k], sr.at[2 + zz], others_z[k]).wait_recv()
    sb[2 + z] = st[1]
    small_out[...] = (sb[2] + sb[3]) + (sb[4] + sb[5])

    small_x.wait_send()
    small_y.wait_send()
    for copy in small_z:
        copy.wait_send()
    for c in range(CHUNKS):
        core_copy(c).wait_send()
    for c in (CHUNKS - 2, CHUNKS - 1):
        ig_copy(c).wait()
    for g in range(2):
        first_exchange(g).wait_send()
        away = 1 - owner[g]

        @pl.when(is_end)
        def _():
            remote(L.at[g], Z.at[g], sends.at[g, 0], zr.at[g, 0], zn).wait_send()

        @pl.when(is_mid)
        def _():
            remote(R.at[g], Y.at[g], sends.at[g, 1], rr.at[g, 0], mm).wait_send()
            some = pl.ds(0, KEPT_ROWS - QUARTER_ROWS)
            remote(R.at[g, some], Y.at[g, some], sends.at[g, 2], yr.at[g, 0], last[g]).wait_send()
            remote(R.at[g], Y.at[g], sends.at[g, 3], ar.at[g, 0], mm).wait_send()
            remote(F.at[g], F.at[g], sends.at[g, 4], zr.at[g, 0], zn).wait_send()

        second_exchange(g).wait_send()
        remote(G.at[g], G.at[g], gs.at[g], gr.at[g, 0], last[g]).wait_send()
        whole = remote(outs[g].at[away], outs[g].at[away], sends.at[g, 5], xr.at[g], first[g])
        whole.wait_send()
        whole.wait_recv()
        pltpu.make_async_copy(outs[g].at[owner[g]], outs[g].at[owner[g]], lo.at[g]).wait()


def sum_call(gk, rg, uk, ru, late_x, late_y, dk, rd, go, dqkv, w3, xn, xin, gmid, gain, small):
    any_spec = pl.BlockSpec(memory_space=pl.ANY)
    n = KEPT_ROWS // ROWS
    rows, dim = xin.shape
    blk = rows // CHUNKS
    full = pltpu.VMEM((2, KEPT_ROWS, WIDE), BF)
    half = pltpu.VMEM((2, KEPT_ROWS, WIDE // 2), BF)
    quarter = pltpu.VMEM((2, QUARTER_ROWS, WIDE), BF)
    down = pltpu.VMEM((2, HALF_ROWS, WIDE), BF)
    dma = pltpu.SemaphoreType.DMA
    return pl.pallas_call(
        sum_body,
        out_shape=[jax.ShapeDtypeStruct((2, GROUP_ROWS, WIDE), BF)] * 2
        + [jax.ShapeDtypeStruct((rows, dim), F32), jax.ShapeDtypeStruct((SMALL, WIDE), F32)],
        in_specs=[any_spec] * 14 + [whole_spec()] * 2,
        out_specs=[any_spec] * 3 + [whole_spec()],
        scratch_shapes=[
            full, full, full, half, half, down, down, quarter, quarter,
            pltpu.VMEM((6, SMALL, WIDE), F32),
            pltpu.VMEM((3, SMALL, WIDE), F32),
            pltpu.VMEM(dqkv.shape, BF),
            pltpu.VMEM(w3.shape, BF),
            pltpu.VMEM((rows, dim), BF),
            pltpu.VMEM((rows, dim), BF),
            pltpu.VMEM((rows, dim), BF),
            pltpu.VMEM((2, HALF_ROWS, WIDE), BF),
            pltpu.VMEM((2, blk, dim), BF),
            pltpu.VMEM((2, blk, dim), F32),
            pltpu.VMEM((2, blk, dim), F32),
            dma((2, 4, 8)), dma((2,)), dma((2,)), dma((2, 6)),
            dma((2, n)), dma((2, n)), dma((2, n)), dma((2, n)),
            dma((2,)), dma((2,)), dma((5,)), dma((6,)),
            dma((3,)), dma((CHUNKS,)), dma((CHUNKS,)), dma((2, 2)), dma((2,)),
            dma((2,)), dma((2,)), dma((2,)), dma((2, QUARTER_ROWS // ROWS)),
        ],
        compiler_params=pltpu.CompilerParams(collective_id=4, has_side_effects=True, vmem_limit_bytes=VMEM_LIMIT),
        name="grad_sum",
    )(gk, rg, uk, ru, late_x, late_y, dk, rd, go, dqkv, w3, xn, xin, gmid, gain, small)


def tables(time_ids):
    half = HEAD // 2
    freqs = jnp.exp(jnp.arange(half, dtype=F32) * (-2.0 * math.log(10000.0) / HEAD))
    angles = time_ids.astype(F32)[:, None] * jnp.tile(freqs, LANES // half)[None, :]
    sign = jnp.where(jnp.arange(LANES) % HEAD < half, -1.0, 1.0)
    return jnp.cos(angles), jnp.sin(angles) * sign[None, :]


def mask_tables(segments, variates, head_bias):
    lane = jnp.arange(LANES)[None, :]
    var_here = (lane % VAR_COLS == variates[:, None]) & (lane < 3 * VAR_COLS)
    seg_here = (lane - SEG_COL == segments[:, None]) & (lane >= SEG_COL) & (lane < ONE_COL)
    seg_cols = (lane >= SEG_COL) & (lane < ONE_COL)
    ones = (lane >= ONE_COL) & (lane < ONE_COL + 3)
    base = jnp.where(var_here, 1.0, 0.0)
    segq = jnp.where(seg_cols & ~seg_here, MASKED, 0.0)
    extk = jnp.where(var_here | seg_here | ones, 1.0, 0.0).astype(BF)
    gap = head_bias[0] - head_bias[1]
    hi = lax.reduce_precision(gap, 8, 7)
    mid = lax.reduce_precision(gap - hi, 8, 7)
    low = gap - hi - mid
    kind = lane // VAR_COLS
    rows = jnp.where(kind == 0, hi[:, None], jnp.where(kind == 1, mid[:, None], jnp.where(kind == 2, low[:, None], 0.0)))
    match = jnp.arange(8)[:, None] == variates[None, :]
    valid = jnp.arange(8)[:, None] < VAR_COLS
    onehot = jnp.stack([jnp.where(match, 1.0, 0.0), jnp.where(valid & ~match, 1.0, 0.0)])
    return base, segq, extk, rows.reshape(-1, 2, LANES), onehot


def fast_local(
    block_input, segments, variates, time_ids, attn_gain, w_qkv, head_bias, w_out, ffn_gain, w_gate_up, w_down, cotangent
):
    w3 = jnp.transpose(w_qkv, (1, 0, 2))
    cosine, sine = tables(time_ids)
    base, segq, extk, bias_rows, onehot = mask_tables(segments, variates, head_bias)
    gain1 = attn_gain[None, :]
    gain2 = ffn_gain[None, :]
    xn, q, k, v = qkv_call(block_input, gain1, w3, cosine, sine)
    attended, o32, extq, wg, wu = attn_fwd_call(q, k, v, base, segq, extk, bias_rows, pair_rows(w_gate_up))
    mid, xn2 = attn_out_call(block_input, attended, w_out, gain2)
    ffn_part, gx_part, gk, uk, rg, ru, dk, rd, late_x, late_y = ffn_call(xn2, cotangent, wg, wu, w_down)
    late_x = lax.ppermute(late_x, "dp", [(d, d ^ 1) for d in range(16)])
    late_y = lax.ppermute(late_y, "dp", [(d, d ^ 2) for d in range(16)])
    block_output, grad_mid, do, g_out, g_gain2 = ffn_back_call(
        gx_part, ffn_part, mid, cotangent, gain2, w_out, attended
    )
    dqkv, gb = attn_bwd_call(q, k, v, do, o32, extq, extk, onehot, cosine, sine)
    g_bias = jnp.sum(gb, axis=(3, 4)).reshape(-1, 2).T
    heads = g_bias.shape[1]
    bias_row = jnp.pad(g_bias.reshape(1, -1), ((0, 0), (0, WIDE - 2 * heads)))
    zero = jnp.zeros((1, WIDE), F32)
    small = jnp.concatenate([zero, g_gain2, bias_row, jnp.zeros((SMALL - 3, WIDE), F32)], axis=0)
    sum_a, sum_b, input_grad, small = sum_call(
        gk, rg, uk, ru, late_x, late_y, dk, rd, g_out, dqkv, w3, xn, block_input, grad_mid, gain1, small
    )
    sum_a = sum_a.reshape(2, 4, HALF_ROWS, WIDE)
    sum_b = sum_b.reshape(2, 4, HALF_ROWS, WIDE)
    g_gate_up, g_down, g_qkv, g_out = widen_call(sum_a, sum_b)
    g_bias = small[2, : 2 * heads].reshape(2, heads)
    return (
        block_output, input_grad, small[0], jnp.transpose(g_qkv, (1, 0, 2)), g_bias, g_out, small[1], g_gate_up, g_down,
    )


def rope_tables(time_ids, head_dim):
    half_dim = head_dim // 2
    freqs = jnp.exp(jnp.arange(half_dim, dtype=jnp.float32) * (-2.0 * math.log(10000.0) / head_dim))
    angles = time_ids.astype(jnp.float32)[:, None] * freqs[None, :]
    return (jnp.cos(angles)[:, None, :], jnp.sin(angles)[:, None, :])


def rotate(vectors, cosine, sine_part):
    half_dim = vectors.shape[-1] // 2
    first_half = vectors[..., :half_dim]
    second_half = vectors[..., half_dim:]
    return jnp.concatenate(
        [
            first_half * cosine - second_half * sine_part,
            second_half * cosine + first_half * sine_part,
        ],
        axis=-1,
    )


def rotate_back(grads, cosine, sine_part):
    half_dim = grads.shape[-1] // 2
    first_half = grads[..., :half_dim]
    second_half = grads[..., half_dim:]
    return jnp.concatenate(
        [
            first_half * cosine + second_half * sine_part,
            second_half * cosine - first_half * sine_part,
        ],
        axis=-1,
    )


def norm_rows(rows_now, gain):
    inverse = lax.rsqrt(jnp.mean(rows_now * rows_now, axis=-1, keepdims=True) + EPSILON)
    return (rows_now * inverse * gain, inverse)


def plain_norm_back(rows_now, inverse, gain, grads):
    scaled = grads * gain
    gain_grad = jnp.sum(grads * rows_now * inverse, axis=0)
    rows_grad = inverse * scaled - rows_now * (inverse * inverse * inverse) * jnp.mean(
        scaled * rows_now, axis=-1, keepdims=True
    )
    return (rows_grad, gain_grad)


def scores_of(queries, keys_rot, same_var, allowed, head_bias, score_scale):
    raw_scores = (
        jnp.einsum("sqhd,skhd->shqk", queries, keys_rot, preferred_element_type=jnp.float32)
        * score_scale
    )
    biased = raw_scores + jnp.where(
        same_var[:, None], head_bias[0][None, :, None, None], head_bias[1][None, :, None, None]
    )
    return jnp.where(allowed[:, None], biased, MASKED)


def plain_local(
    block_input,
    segments,
    variates,
    time_ids,
    attn_gain,
    w_qkv,
    head_bias,
    w_out,
    ffn_gain,
    w_gate_up,
    w_down,
    cotangent,
):
    row_count = block_input.shape[0]
    heads_here = head_bias.shape[1]
    head_dim = w_qkv.shape[2] // heads_here
    seq_count = row_count // LEN
    score_scale = head_dim ** (-0.5)
    input_rows = block_input.astype(jnp.float32)
    attn_normed, attn_inverse = norm_rows(input_rows, attn_gain)
    attn_normed_low = attn_normed.astype(jnp.bfloat16)
    projected = jnp.einsum(
        "td,dck->tck", attn_normed_low, w_qkv, preferred_element_type=jnp.float32
    )
    cosine, sine_part = rope_tables(time_ids, head_dim)
    head_shape = (row_count, heads_here, head_dim)
    seq_shape = (seq_count, LEN, heads_here, head_dim)
    queries = (
        rotate(projected[:, 0].reshape(head_shape), cosine, sine_part)
        .astype(jnp.bfloat16)
        .reshape(seq_shape)
    )
    keys_rot = (
        rotate(projected[:, 1].reshape(head_shape), cosine, sine_part)
        .astype(jnp.bfloat16)
        .reshape(seq_shape)
    )
    values = projected[:, 2].astype(jnp.bfloat16).reshape(seq_shape)
    seg_ids = segments.reshape(seq_count, LEN)
    var_ids = variates.reshape(seq_count, LEN)
    allowed = seg_ids[:, :, None] == seg_ids[:, None, :]
    same_var = var_ids[:, :, None] == var_ids[:, None, :]
    scores = scores_of(queries, keys_rot, same_var, allowed, head_bias, score_scale)
    row_max = jnp.max(scores, axis=-1, keepdims=True)
    exp_total = jnp.sum(jnp.exp(scores - row_max), axis=-1, keepdims=True)
    log_total = row_max + jnp.log(exp_total)
    probs_low = jnp.exp(scores - log_total).astype(jnp.bfloat16)
    attended = jnp.einsum("shqk,skhd->sqhd", probs_low, values, preferred_element_type=jnp.float32)
    attended = attended.reshape(row_count, heads_here * head_dim).astype(jnp.bfloat16)
    attn_branch = lax.psum(
        jnp.dot(attended, w_out, preferred_element_type=jnp.float32).astype(jnp.bfloat16), "tensor"
    ).astype(jnp.float32)
    mid_rows = input_rows + attn_branch
    ffn_normed, ffn_inverse = norm_rows(mid_rows, ffn_gain)
    ffn_normed_low = ffn_normed.astype(jnp.bfloat16)
    gate_up = jnp.einsum(
        "td,dcf->tcf", ffn_normed_low, w_gate_up, preferred_element_type=jnp.float32
    )
    gate_vals = gate_up[:, 0]
    up_vals = gate_up[:, 1]
    sigmoid_gate = jax.nn.sigmoid(gate_vals)
    silu_gate = gate_vals * sigmoid_gate
    hidden_low = (silu_gate * up_vals).astype(jnp.bfloat16)
    ffn_branch = lax.psum(
        jnp.dot(hidden_low, w_down, preferred_element_type=jnp.float32).astype(jnp.bfloat16),
        "tensor",
    ).astype(jnp.float32)
    block_output = (mid_rows + ffn_branch).astype(jnp.bfloat16)
    grad_down = jnp.einsum("tf,td->fd", hidden_low, cotangent, preferred_element_type=jnp.float32)
    grad_hidden = jnp.einsum("td,fd->tf", cotangent, w_down, preferred_element_type=jnp.float32)
    grad_gate = grad_hidden * up_vals * sigmoid_gate * (1.0 + gate_vals * (1.0 - sigmoid_gate))
    grad_up = grad_hidden * silu_gate
    grad_gate_up = jnp.stack([grad_gate, grad_up], axis=1).astype(jnp.bfloat16)
    grad_w_gate_up = jnp.einsum(
        "td,tcf->dcf", ffn_normed_low, grad_gate_up, preferred_element_type=jnp.float32
    )
    grad_ffn_normed = lax.psum(
        jnp.einsum(
            "tcf,dcf->td", grad_gate_up, w_gate_up, preferred_element_type=jnp.float32
        ).astype(jnp.bfloat16),
        "tensor",
    ).astype(jnp.float32)
    norm_grad_mid, grad_ffn_gain = plain_norm_back(mid_rows, ffn_inverse, ffn_gain, grad_ffn_normed)
    grad_mid = cotangent.astype(jnp.float32) + norm_grad_mid
    grad_branch = grad_mid.astype(jnp.bfloat16)
    grad_w_out = jnp.einsum("tk,td->kd", attended, grad_branch, preferred_element_type=jnp.float32)
    grad_attended = jnp.einsum("td,kd->tk", grad_branch, w_out, preferred_element_type=jnp.float32)
    grad_attended = grad_attended.astype(jnp.bfloat16).reshape(seq_shape)
    scores_again = scores_of(queries, keys_rot, same_var, allowed, head_bias, score_scale)
    probs_again = jnp.exp(scores_again - log_total)
    probs_again_low = probs_again.astype(jnp.bfloat16)
    grad_probs = jnp.einsum(
        "sqhd,skhd->shqk", grad_attended, values, preferred_element_type=jnp.float32
    )
    grad_values = jnp.einsum(
        "shqk,sqhd->skhd", probs_again_low, grad_attended, preferred_element_type=jnp.float32
    )
    grad_scores = probs_again * (
        grad_probs - jnp.sum(probs_again * grad_probs, axis=-1, keepdims=True)
    )
    grad_scores_low = grad_scores.astype(jnp.bfloat16)
    same_low = same_var.astype(jnp.bfloat16)
    other_low = jnp.logical_not(same_var).astype(jnp.bfloat16)
    grad_bias = jnp.stack(
        [
            jnp.einsum(
                "shqk,sqk->h", grad_scores_low, same_low, preferred_element_type=jnp.float32
            ),
            jnp.einsum(
                "shqk,sqk->h", grad_scores_low, other_low, preferred_element_type=jnp.float32
            ),
        ],
        axis=0,
    )
    grad_queries = (
        jnp.einsum("shqk,skhd->sqhd", grad_scores_low, keys_rot, preferred_element_type=jnp.float32)
        * score_scale
    )
    grad_keys = (
        jnp.einsum("shqk,sqhd->skhd", grad_scores_low, queries, preferred_element_type=jnp.float32)
        * score_scale
    )
    grad_query_lin = rotate_back(grad_queries.reshape(head_shape), cosine, sine_part).reshape(
        row_count, heads_here * head_dim
    )
    grad_key_lin = rotate_back(grad_keys.reshape(head_shape), cosine, sine_part).reshape(
        row_count, heads_here * head_dim
    )
    grad_value_lin = grad_values.reshape(row_count, heads_here * head_dim)
    grad_projected = jnp.stack([grad_query_lin, grad_key_lin, grad_value_lin], axis=1).astype(
        jnp.bfloat16
    )
    grad_w_qkv = jnp.einsum(
        "td,tck->dck", attn_normed_low, grad_projected, preferred_element_type=jnp.float32
    )
    grad_attn_normed = lax.psum(
        jnp.einsum("tck,dck->td", grad_projected, w_qkv, preferred_element_type=jnp.float32).astype(
            jnp.bfloat16
        ),
        "tensor",
    ).astype(jnp.float32)
    norm_grad_input, grad_attn_gain = plain_norm_back(
        input_rows, attn_inverse, attn_gain, grad_attn_normed
    )
    input_grad = grad_mid + norm_grad_input
    grad_attn_gain, grad_w_qkv, grad_bias, grad_w_out, grad_ffn_gain, grad_w_gate_up, grad_down = (
        lax.psum(
            (
                grad_attn_gain,
                grad_w_qkv,
                grad_bias,
                grad_w_out,
                grad_ffn_gain,
                grad_w_gate_up,
                grad_down,
            ),
            "dp",
        )
    )
    return (
        block_output,
        input_grad,
        grad_attn_gain,
        grad_w_qkv,
        grad_bias,
        grad_w_out,
        grad_ffn_gain,
        grad_w_gate_up,
        grad_down,
    )


def solution(mesh):
    placed = (
        P("dp", None), P("dp"), P("dp"), P("dp"), P(), P(None, None, "tensor"), P(None, "tensor"),
        P("tensor", None), P(), P(None, None, "tensor"), P("tensor", None), P("dp", None),
    )
    fast = (mesh.shape["dp"], mesh.shape["tensor"]) == (16, 2)
    return jax.shard_map(
        fast_local if fast else plain_local,
        mesh=mesh,
        in_specs=placed,
        out_specs=(
            P("dp", None), P("dp", None), P(), P(None, None, "tensor"), P(None, "tensor"), P("tensor", None), P(),
            P(None, None, "tensor"), P("tensor", None),
        ),
        check_vma=False,
    )
```

```python
import functools
import math

import jax
import jax.numpy as jnp
from jax import lax
from jax.experimental import pallas as pl
from jax.experimental.pallas import tpu as pltpu
from jax.sharding import PartitionSpec as P

LEN = 1024
EPSILON = 1e-05
MASKED = -1000000000.0
BF = jnp.bfloat16
F32 = jnp.float32
MESH = pl.DeviceIdType.MESH
VMEM_LIMIT = 60 * 1024 * 1024
LANES = 128
HEAD = 64
VAR_COLS = 4
SEG_COL = 12
ONE_COL = 20
ROWS = 32
LAGS = (2, 4, 6, 8, 10)
SWAP_ROWS = 32
HALF_ROWS = 512
QUARTER_ROWS = HALF_ROWS // 2
GROUP_ROWS = 4 * HALF_ROWS
KEPT_ROWS = GROUP_ROWS - QUARTER_ROWS
WIDE = 1024
SMALL = 8
QBLK = 256
FFN_ROWS = 512
FFN_COLS = 256


def dot_nn(a, b):
    return lax.dot_general(a, b, (((1,), (0,)), ((), ())), preferred_element_type=F32)


def dot_nt(a, b):
    return lax.dot_general(a, b, (((1,), (1,)), ((), ())), preferred_element_type=F32)


def dot_tn(a, b):
    return lax.dot_general(a, b, (((0,), (0,)), ((), ())), preferred_element_type=F32)


def whole_spec():
    return pl.BlockSpec(memory_space=pltpu.VMEM)


def split3(v):
    hi = v.astype(BF).astype(F32)
    mid = (v - hi).astype(BF).astype(F32)
    return hi, mid, v - hi - mid


def half_swap(u):
    lane = lax.broadcasted_iota(jnp.int32, u.shape, 1) % HEAD
    return jnp.where(lane < HEAD // 2, pltpu.roll(u, LANES - HEAD // 2, 1), pltpu.roll(u, HEAD // 2, 1))


def qkv_body(x_ref, gain_ref, w_ref, cos_ref, sin_ref, xn_ref, q_ref, k_ref, v_ref):
    x = x_ref[...].astype(F32)
    inv = lax.rsqrt(jnp.mean(x * x, axis=-1, keepdims=True) + EPSILON)
    xn = (x * inv * gain_ref[...]).astype(BF)
    xn_ref[...] = xn
    cosine = cos_ref[...]
    sine = sin_ref[...]
    for part, out, factor in ((0, q_ref, HEAD**-0.5), (1, k_ref, 1.0)):
        lin = dot_nn(xn, w_ref[part])
        for s in range(lin.shape[1] // LANES):
            u = lin[:, s * LANES : (s + 1) * LANES]
            rot = (u * cosine + half_swap(u) * sine).astype(BF)
            if factor != 1.0:
                rot = (rot.astype(F32) * factor).astype(BF)
            out[:, s * LANES : (s + 1) * LANES] = rot
    v_ref[...] = dot_nn(xn, w_ref[2]).astype(BF)


def qkv_call(x, gain, w, cosine, sine):
    rows, dim = x.shape
    width = w.shape[2]
    blk = min(256, rows)
    row = lambda cols: pl.BlockSpec((blk, cols), lambda i: (i, 0))
    return pl.pallas_call(
        qkv_body,
        grid=(rows // blk,),
        out_shape=[jax.ShapeDtypeStruct((rows, dim), BF)] + [jax.ShapeDtypeStruct((rows, width), BF)] * 3,
        in_specs=[
            row(dim),
            pl.BlockSpec((1, dim), lambda i: (0, 0)),
            pl.BlockSpec(w.shape, lambda i: (0, 0, 0)),
            row(LANES),
            row(LANES),
        ],
        out_specs=[row(dim), row(width), row(width), row(width)],
        compiler_params=pltpu.CompilerParams(vmem_limit_bytes=VMEM_LIMIT),
        name="qkv",
    )(x, gain, w, cosine, sine)


def attn_fwd_body(
    q_ref, k_ref, v_ref, base_ref, segq_ref, extk_ref, bias_ref, w_ref, o_ref, o32_ref, extq_ref, wg_ref, wu_ref
):
    rows = q_ref.shape[0]
    for t in range(w_ref.shape[1] // 8):
        turned = jnp.swapaxes(w_ref[:, t * 8 : (t + 1) * 8, :].astype(F32), 0, 1)
        for k in range(8):
            s = t * 4 + k // 2
            (wg_ref, wu_ref)[k % 2][:, s * LANES : (s + 1) * LANES] = turned[k].astype(BF)
    blk = 256
    lane = lax.broadcasted_iota(jnp.int32, (blk, LANES), 1)
    kind = lax.broadcasted_iota(jnp.int32, (1, LANES), 1) // VAR_COLS
    bias_rows = []
    for h in range(2):
        head = pl.program_id(0) * 2 + h
        hi, mid, low = split3(jnp.full((1, LANES), bias_ref[0, head] - bias_ref[1, head], F32))
        bias_rows.append(jnp.where(kind == 0, hi, jnp.where(kind == 1, mid, jnp.where(kind == 2, low, 0.0))))
    kx = jnp.concatenate([k_ref[...], extk_ref[...]], axis=1)
    ones = jnp.ones((rows, LANES), BF)
    vx = jnp.concatenate([v_ref[...], ones], axis=1)
    for i in range(rows // blk):
        sl = slice(i * blk, (i + 1) * blk)
        q = q_ref[sl, :].astype(F32)
        base = base_ref[sl, :]
        segq = segq_ref[sl, :]
        outs = []
        for h in range(2):
            ext = base * bias_rows[h] + segq
            mine = (lane >= HEAD) if h else (lane < HEAD)
            qx = jnp.concatenate([jnp.where(mine, q, 0.0), ext], axis=1).astype(BF)
            s = dot_nt(qx, kx)
            top = jnp.max(s, axis=-1, keepdims=True)
            p = jnp.exp(s - top).astype(BF)
            ox = dot_nn(p, vx)
            total = ox[:, LANES:]
            outs.append(ox[:, :LANES] / total)
            lse = top + jnp.log(total)
            hi, mid, low = split3(lse)
            ext = jnp.where(
                lane == ONE_COL, -hi, jnp.where(lane == ONE_COL + 1, -mid, jnp.where(lane == ONE_COL + 2, -low, ext))
            )
            extq_ref[0, h, sl, :] = ext.astype(BF)
        o = jnp.where(lane < HEAD, outs[0], outs[1])
        o32_ref[sl, :] = o
        o_ref[sl, :] = o.astype(BF)


def attn_fwd_call(q, k, v, base, segq, extk, head_bias, w_pairs):
    rows, width = q.shape
    pairs = width // LANES
    dim, tiles, _ = w_pairs.shape
    share = dim // pairs
    half_w = pl.BlockSpec((share, tiles * LANES // 2), lambda p: (p, 0))
    col = pl.BlockSpec((rows, LANES), lambda p: (0, p))
    full = pl.BlockSpec((rows, LANES), lambda p: (0, 0))
    return pl.pallas_call(
        attn_fwd_body,
        grid=(pairs,),
        out_shape=[
            jax.ShapeDtypeStruct((rows, width), BF),
            jax.ShapeDtypeStruct((rows, width), F32),
            jax.ShapeDtypeStruct((pairs, 2, rows, LANES), BF),
            jax.ShapeDtypeStruct((dim, tiles * LANES // 2), BF),
            jax.ShapeDtypeStruct((dim, tiles * LANES // 2), BF),
        ],
        in_specs=[
            col, col, col, full, full, full,
            pl.BlockSpec(memory_space=pltpu.SMEM),
            pl.BlockSpec((share, tiles, LANES), lambda p: (p, 0, 0)),
        ],
        out_specs=[col, col, pl.BlockSpec((1, 2, rows, LANES), lambda p: (p, 0, 0, 0)), half_w, half_w],
        compiler_params=pltpu.CompilerParams(vmem_limit_bytes=VMEM_LIMIT),
        name="attn_fwd",
    )(q, k, v, base, segq, extk, head_bias, w_pairs)


def attn_bwd_body(
    q_ref, k_ref, v_ref, do_ref, o32_ref, extq_ref, extk_ref, var_ref, cos_ref, sin_ref, d_ref, gb_ref, dqt_ref
):
    rows = q_ref.shape[0]
    blk = 256
    lane = lax.broadcasted_iota(jnp.int32, (blk, LANES), 1)
    kinds = lax.broadcasted_iota(jnp.int32, (8, blk), 0)
    kx = jnp.concatenate([k_ref[...], extk_ref[...]], axis=1)
    kxt = kx.T
    lane_all = lax.broadcasted_iota(jnp.int32, (rows, LANES), 1)
    vx = jnp.concatenate([v_ref[...], jnp.where(lane_all < 3, 1.0, 0.0).astype(BF)], axis=1)
    dv = jnp.zeros((rows, LANES), F32)
    dk = jnp.zeros((rows, LANES), F32)
    for h in range(2):
        same = jnp.zeros((8, blk), F32)
        other = jnp.zeros((8, blk), F32)
        for i in range(rows // blk):
            sl = slice(i * blk, (i + 1) * blk)
            mine = (lane >= HEAD) if h else (lane < HEAD)
            q = jnp.where(mine, q_ref[sl, :].astype(F32), 0.0).astype(BF)
            do32 = jnp.where(mine, do_ref[sl, :].astype(F32), 0.0)
            do = do32.astype(BF)
            delta = jnp.sum(do32 * o32_ref[sl, :], axis=-1, keepdims=True)
            hi, mid, low = split3(delta)
            dext = jnp.where(lane == 0, -hi, jnp.where(lane == 1, -mid, jnp.where(lane == 2, -low, 0.0))).astype(BF)
            st = dot_nt(kx, jnp.concatenate([q, extq_ref[0, h, sl, :]], axis=1))
            pt = jnp.exp(st)
            dpt = dot_nt(vx, jnp.concatenate([do, dext], axis=1))
            dst = (pt * dpt).astype(BF)
            dv = dv + dot_nn(pt.astype(BF), do)
            dk = dk + dot_nn(dst, q)
            dqt = dot_nn(kxt, dst)
            dqt_ref[h * HEAD : (h + 1) * HEAD, sl] = dqt[h * HEAD : (h + 1) * HEAD, :]
            g = dqt[LANES : LANES + 8, :]
            match = kinds == var_ref[:, sl]
            same = same + jnp.where(match, g, 0.0)
            other = other + jnp.where(match | (kinds >= VAR_COLS), 0.0, g)
        gb_ref[0, h, 0] = same
        gb_ref[0, h, 1] = other
    cosine = cos_ref[...]
    sine = sin_ref[...]
    dq = dqt_ref[...].T * HEAD**-0.5
    d_ref[0] = (dq * cosine - half_swap(dq) * sine).astype(BF)
    d_ref[1] = (dk * cosine - half_swap(dk) * sine).astype(BF)
    d_ref[2] = dv.astype(BF)


def attn_bwd_call(q, k, v, do, o32, extq, extk, variates, cosine, sine):
    rows, width = q.shape
    pairs = width // LANES
    col = pl.BlockSpec((rows, LANES), lambda p: (0, p))
    full = pl.BlockSpec((rows, LANES), lambda p: (0, 0))
    blk = 256
    return pl.pallas_call(
        attn_bwd_body,
        grid=(pairs,),
        out_shape=[jax.ShapeDtypeStruct((3, rows, width), BF), jax.ShapeDtypeStruct((pairs, 2, 2, 8, blk), F32)],
        in_specs=[
            col, col, col, col, col,
            pl.BlockSpec((1, 2, rows, LANES), lambda p: (p, 0, 0, 0)),
            full,
            pl.BlockSpec((1, rows), lambda p: (0, 0)),
            full, full,
        ],
        out_specs=[pl.BlockSpec((3, rows, LANES), lambda p: (0, 0, p)), pl.BlockSpec((1, 2, 2, 8, blk), lambda p: (p, 0, 0, 0, 0))],
        scratch_shapes=[pltpu.VMEM((LANES, rows), F32)],
        compiler_params=pltpu.CompilerParams(vmem_limit_bytes=VMEM_LIMIT),
        name="attn_bwd",
    )(q, k, v, do, o32, extq, extk, variates, cosine, sine)


def partner_barrier():
    dp = lax.axis_index("dp")
    other = 1 - lax.axis_index("tensor")
    barrier = pltpu.get_barrier_semaphore()
    pl.semaphore_signal(barrier, inc=1, device_id=(dp, other), device_id_type=MESH)
    pl.semaphore_wait(barrier, 1)
    return (dp, other)


def send_rows(src, dst, sl, ssem, rsem, peer):
    return pltpu.make_async_remote_copy(
        src_ref=src.at[sl], dst_ref=dst.at[sl], send_sem=ssem, recv_sem=rsem, device_id=peer, device_id_type=MESH
    )


CHUNKS = 4


def attn_out_body(x_ref, o_ref, w_ref, gain_ref, mid_ref, xn_ref, mine, theirs, ssem, rsem):
    peer = partner_barrier()
    rows = x_ref.shape[0]
    blk = rows // CHUNKS
    copies = []
    for c in range(CHUNKS):
        sl = slice(c * blk, (c + 1) * blk)
        mine[sl, :] = dot_nn(o_ref[sl, :], w_ref[...]).astype(BF)
        copy = send_rows(mine, theirs, pl.ds(c * blk, blk), ssem.at[c], rsem.at[c], peer)
        copy.start()
        copies.append(copy)
    for c in range(CHUNKS):
        sl = slice(c * blk, (c + 1) * blk)
        copies[c].wait_recv()
        mid = x_ref[sl, :].astype(F32) + (mine[sl, :].astype(F32) + theirs[sl, :].astype(F32))
        inv = lax.rsqrt(jnp.mean(mid * mid, axis=-1, keepdims=True) + EPSILON)
        mid_ref[sl, :] = mid
        xn_ref[sl, :] = (mid * inv * gain_ref[...]).astype(BF)
    for c in range(CHUNKS):
        copies[c].wait_send()


def attn_out_call(x, o, w, gain):
    rows, dim = x.shape
    return pl.pallas_call(
        attn_out_body,
        out_shape=[jax.ShapeDtypeStruct((rows, dim), F32), jax.ShapeDtypeStruct((rows, dim), BF)],
        in_specs=[whole_spec()] * 4,
        out_specs=[whole_spec()] * 2,
        scratch_shapes=[
            pltpu.VMEM((rows, dim), BF),
            pltpu.VMEM((rows, dim), BF),
            pltpu.SemaphoreType.DMA((CHUNKS,)),
            pltpu.SemaphoreType.DMA((CHUNKS,)),
        ],
        compiler_params=pltpu.CompilerParams(collective_id=1, has_side_effects=True, vmem_limit_bytes=VMEM_LIMIT),
        name="attn_out",
    )(x, o, w, gain)


LATE = 4
SLOTS = 4
PART = FFN_COLS // 4


def sent(copy):
    copy.wait_send() if copy.is_remote else copy.wait()


def grid_bits():
    dp = lax.axis_index("dp")
    return dp, dp % 2, (dp // 2) % 2, peers_of(dp)[3], peers_of(dp)[4]


def ffn_body(
    xn_ref, ct_ref, wg_ref, wu_ref, wd_ref,
    out_ref, gx_ref, gk_ref, uk_ref, rg, ru, dk, rd, late_x, late_y,
    acc_o, acc_g, hid, dg, du, xt, away_w, away_d, ws, wr, ds, dr,
):
    j = pl.program_id(0)
    t = lax.axis_index("tensor")
    dp, x, y, px, py = grid_bits()
    steps = pl.num_programs(0)
    rows = xn_ref.shape[0]
    blk = wd_ref.shape[0]
    per = WIDE // blk
    early = 2 * per - LATE
    slot = lax.rem(j, SLOTS)
    near = (px, py)
    bits = (x, y)
    arrays = ((rg, late_x), (ru, late_y))

    def remote(src, dst, ssem, rsem, peer):
        return pltpu.make_async_remote_copy(
            src_ref=src, dst_ref=dst, send_sem=ssem, recv_sem=rsem, device_id=(peer, t), device_id_type=MESH
        )

    def wide_early(k, at):
        cols = pl.ds(pl.multiple_of(lax.rem(at, per) * blk, blk), blk)
        s = lax.rem(at, SLOTS)
        return remote(away_w.at[k, s], arrays[k][0].at[:, cols], ws.at[k, s], wr.at[k], near[k])

    def wide_late(k, at):
        cols = pl.ds(pl.multiple_of((at - early) * blk, blk), blk)
        s = lax.rem(at, SLOTS)
        return pltpu.make_async_copy(away_w.at[k, s], arrays[k][1].at[pl.ds(0, HALF_ROWS), cols], ws.at[k, s])

    def wide_do(at, act):
        for k in range(2):

            @pl.when(at < early)
            def _():
                act(wide_early(k, at))

            @pl.when(at >= early)
            def _():
                act(wide_late(k, at))

    def down_rows(g, half):
        return pl.ds(pl.multiple_of(g * 2 * PART + half * PART, PART), PART)

    def down_keep(g, at):
        s = lax.rem(at, SLOTS)
        return pltpu.make_async_copy(
            away_d.at[s, down_rows(g, bits[g])], dk.at[g, pl.ds(pl.multiple_of(at * PART, PART), PART)], ds.at[g, s]
        )

    def down_send(g, at):
        s = lax.rem(at, SLOTS)
        rows_at = pl.ds(pl.multiple_of(at * PART, PART), PART)
        return remote(away_d.at[s, down_rows(g, 1 - bits[g])], rd.at[g, rows_at], ds.at[2 + g, s], dr.at[g], near[g])

    def down_late(g, at):
        s = lax.rem(at, SLOTS)
        rows_at = pl.ds(pl.multiple_of(HALF_ROWS + (at - early) * PART, PART), PART)
        return pltpu.make_async_copy(
            away_d.at[s, down_rows(g, 1 - bits[g])], arrays[g][1].at[rows_at], ds.at[2 + g, s]
        )

    def down_do(at, act):
        for g in range(2):
            act(down_keep(g, at))

            @pl.when(at < early)
            def _():
                act(down_send(g, at))

            @pl.when(at >= early)
            def _():
                act(down_late(g, at))

    @pl.when(j == 0)
    def _():
        barrier = pltpu.get_barrier_semaphore()
        for peer in near:
            pl.semaphore_signal(barrier, inc=1, device_id=(peer, t), device_id_type=MESH)
        pl.semaphore_wait(barrier, 2)
        acc_o[...] = jnp.zeros_like(acc_o)
        acc_g[...] = jnp.zeros_like(acc_g)
        xt[...] = xn_ref[...].T

    wg = wg_ref[...]
    wu = wu_ref[...]
    wd = wd_ref[...]
    for i in range(rows // FFN_ROWS):
        sl = slice(i * FFN_ROWS, (i + 1) * FFN_ROWS)
        xn = xn_ref[sl, :]
        gate = dot_nn(xn, wg)
        up = dot_nn(xn, wu)
        gh = dot_nt(ct_ref[sl, :], wd)
        sig = jax.nn.sigmoid(gate)
        silu = gate * sig
        hidden = (silu * up).astype(BF)
        dgate = (gh * up * sig * (1.0 + gate * (1.0 - sig))).astype(BF)
        dup = (gh * silu).astype(BF)
        hid[sl, :] = hidden
        dg[sl, :] = dgate
        du[sl, :] = dup
        acc_o[sl, :] += dot_nn(hidden, wd)
        acc_g[sl, :] += dot_nt(dgate, wg) + dot_nt(dup, wu)

    @pl.when(j >= SLOTS)
    def _():
        wide_do(j - SLOTS, sent)
        down_do(j - SLOTS, sent)

    away_d[slot] = dot_tn(hid[...], ct_ref[...]).astype(BF)
    down_do(j, lambda copy: copy.start())
    for k, (part, keep, bit) in enumerate(((dg, gk_ref, x), (du, uk_ref, y))):
        rows_at = lambda half: pl.ds(pl.multiple_of(half * HALF_ROWS, HALF_ROWS), HALF_ROWS)
        away_w[k, slot] = dot_nn(xt[rows_at(1 - bit), :], part[...]).astype(BF)
        keep[0] = dot_nn(xt[rows_at(bit), :], part[...]).astype(BF)
    wide_do(j, lambda copy: copy.start())

    @pl.when(j == steps - 1)
    def _():
        out_ref[...] = acc_o[...].astype(BF)
        gx_ref[...] = acc_g[...].astype(BF)
        for back in range(SLOTS, 0, -1):
            wide_do(steps - back, sent)
            down_do(steps - back, sent)
        for k in range(2):
            part = arrays[k][0].at[:, pl.ds(0, early * blk)]
            remote(part, part, ws.at[k, 0], wr.at[k], near[k]).wait_recv()
        for g in range(2):
            part = rd.at[g, pl.ds(0, early * PART)]
            remote(part, part, ds.at[g, 0], dr.at[g], near[g]).wait_recv()


def ffn_call(xn, ct, wg, wu, wd):
    rows, dim = xn.shape
    hidden = wd.shape[0]
    blk = FFN_COLS
    per = WIDE // blk
    full = pl.BlockSpec((rows, dim), lambda j: (0, 0))
    colw = pl.BlockSpec((dim, blk), lambda j: (0, j))
    roww = pl.BlockSpec((blk, dim), lambda j: (j, 0))
    grad = pl.BlockSpec((1, HALF_ROWS, blk), lambda j: (j // per, 0, lax.rem(j, per)))
    any_spec = pl.BlockSpec(memory_space=pl.ANY)
    wide = jax.ShapeDtypeStruct((2, HALF_ROWS, dim), BF)
    early = hidden // blk - LATE
    come = jax.ShapeDtypeStruct((HALF_ROWS, early * blk), BF)
    late = jax.ShapeDtypeStruct((HALF_ROWS + LATE * PART, LATE * blk), BF)
    dma = pltpu.SemaphoreType.DMA
    return pl.pallas_call(
        ffn_body,
        grid=(hidden // blk,),
        in_specs=[full, full, colw, colw, roww],
        out_specs=[full, full, grad, grad] + [any_spec] * 6,
        out_shape=[jax.ShapeDtypeStruct((rows, dim), BF)] * 2
        + [wide, wide, come, come, wide, jax.ShapeDtypeStruct((2, early * PART, dim), BF), late, late],
        scratch_shapes=[pltpu.VMEM((rows, dim), F32)] * 2
        + [pltpu.VMEM((rows, blk), BF)] * 3
        + [
            pltpu.VMEM((dim, rows), BF),
            pltpu.VMEM((2, SLOTS, HALF_ROWS, blk), BF),
            pltpu.VMEM((SLOTS, blk, dim), BF),
            dma((2, SLOTS)), dma((2,)), dma((4, SLOTS)), dma((2,)),
        ],
        compiler_params=pltpu.CompilerParams(collective_id=5, has_side_effects=True, vmem_limit_bytes=VMEM_LIMIT),
        name="ffn",
    )(xn, ct, wg, wu, wd)


def pair_rows(w):
    dim, two, width = w.shape
    tiled = jnp.transpose(w.reshape(dim, two, width // LANES, LANES), (0, 2, 1, 3))
    return tiled.reshape(dim, two * width // LANES, LANES)


def widen_body(
    ga_ref, gb_ref, da_ref, db_ref, aa_ref, v_ref, o_ref, small_ref,
    gu_ref, down_ref, qkv_ref, out_ref, g1_ref, g2_ref, gbias_ref,
):
    tiles = WIDE // LANES
    for f in range(2):
        for q in range(tiles // 4):
            parts = []
            for k in range(8):
                s = q * 4 + k // 2
                parts.append((ga_ref, gb_ref)[k % 2][0, f, :, s * LANES : (s + 1) * LANES].astype(F32))
            at = (f * tiles + q * 4) * 2
            gu_ref[:, at : at + 8, :] = jnp.swapaxes(jnp.stack(parts), 0, 1)
    down_ref[:, 0, 0] = da_ref[0, 0].astype(F32).reshape(down_ref.shape[0], PART, WIDE)
    down_ref[:, 1, 0] = db_ref[0, 0].astype(F32).reshape(down_ref.shape[0], PART, WIDE)
    width = qkv_ref.shape[2]
    qkv_ref[0] = aa_ref[0, 0, :, :width].astype(F32)
    qkv_ref[1] = aa_ref[0, 0, :, width:].astype(F32)
    qkv_ref[2] = v_ref[0, 0].astype(F32)
    out_ref[...] = o_ref[0, 0].astype(F32)

    @pl.when(pl.program_id(0) == 0)
    def _():
        g1_ref[...] = small_ref[0:1, :]
        g2_ref[...] = small_ref[1:2, :]
        row = lax.broadcasted_iota(jnp.int32, gbias_ref.shape, 0)
        col = lax.broadcasted_iota(jnp.int32, gbias_ref.shape, 1)
        total = jnp.zeros(gbias_ref.shape, F32)
        for h in range(gbias_ref.shape[1]):
            for s in range(2):
                at = (h % 2 * 2 + s) * QBLK
                one = jnp.sum(small_ref[2 + h // 2 : 3 + h // 2, at : at + QBLK], axis=1, keepdims=True)
                total = jnp.where((row == s) & (col == h), one, total)
        gbias_ref[...] = total


def widen_call(a, b, small, heads):
    blk = 256
    half = HALF_ROWS // blk
    tiles = 4 * WIDE // LANES
    width = WIDE // 2
    gate = pl.BlockSpec((1, 2, blk, WIDE), lambda i: (i // half, 0, lax.rem(i, half), 0))
    block = lambda n: pl.BlockSpec((1, 1, blk, WIDE), lambda i: (i // half, n, lax.rem(i, half), 0))
    fixed = lambda shape: pl.BlockSpec(shape, lambda i: (0, 0))
    gu, down, qkv, out, g1, g2, gbias = pl.pallas_call(
        widen_body,
        grid=(2 * half,),
        out_shape=[
            jax.ShapeDtypeStruct((2 * HALF_ROWS, tiles, LANES), F32),
            jax.ShapeDtypeStruct((HALF_ROWS // PART, 2, 2, PART, WIDE), F32),
            jax.ShapeDtypeStruct((3, 2 * HALF_ROWS, width), F32),
            jax.ShapeDtypeStruct((HALF_ROWS, WIDE), F32),
            jax.ShapeDtypeStruct((1, WIDE), F32),
            jax.ShapeDtypeStruct((1, WIDE), F32),
            jax.ShapeDtypeStruct((2, heads), F32),
        ],
        in_specs=[
            gate, gate, block(2), block(2), block(3),
            pl.BlockSpec((1, 1, blk, width), lambda i: (0, 3, lax.rem(i, half), i // half)),
            pl.BlockSpec((1, 1, blk // 2, WIDE), lambda i: (1, 3, i, 0)),
            fixed((SMALL, WIDE)),
        ],
        out_specs=[
            pl.BlockSpec((blk, tiles, LANES), lambda i: (i, 0, 0)),
            pl.BlockSpec((blk // PART, 2, 1, PART, WIDE), lambda i: (lax.rem(i, half), 0, i // half, 0, 0)),
            pl.BlockSpec((3, blk, width), lambda i: (0, i, 0)),
            pl.BlockSpec((blk // 2, WIDE), lambda i: (i, 0)),
            fixed((1, WIDE)),
            fixed((1, WIDE)),
            fixed((2, heads)),
        ],
        compiler_params=pltpu.CompilerParams(vmem_limit_bytes=VMEM_LIMIT),
        name="widen",
    )(a, b, a, b, a, b, b, small)
    gu = jnp.transpose(gu.reshape(2 * HALF_ROWS, tiles // 2, 2, LANES), (0, 2, 1, 3)).reshape(2 * HALF_ROWS, 2, 2 * WIDE)
    return gu, down.reshape(4 * HALF_ROWS, WIDE), qkv, out, g1, g2, gbias


def norm_back(rows_now, gain, grads):
    inv = lax.rsqrt(jnp.mean(rows_now * rows_now, axis=-1, keepdims=True) + EPSILON)
    scaled = grads * gain
    gain_grad = jnp.sum(grads * rows_now * inv, axis=0, keepdims=True)
    back = inv * scaled - rows_now * (inv * inv * inv) * jnp.mean(scaled * rows_now, axis=-1, keepdims=True)
    return back, gain_grad


def ffn_back_body(
    gain_ref, w_ref, at_ref, gx, fo, mid, ct,
    do_ref, gw_ref, gg_ref, out, gm,
    gx_in, fo_in, gx_v, fo_v, mid_v, ct_v, gm_v, out_v, gb, ssem, rsem, lsem, osem,
):
    rows = mid.shape[0]
    blk = rows // CHUNKS

    def rows_of(c):
        return pl.ds(c * blk, blk)

    loads = [
        [
            pltpu.make_async_copy(src.at[rows_of(c)], dst.at[rows_of(c)], lsem.at[k, c])
            for k, (src, dst) in enumerate(((gx, gx_v), (mid, mid_v), (ct, ct_v), (fo, fo_v)))
        ]
        for c in range(CHUNKS)
    ]
    for c in range(CHUNKS):
        for copy in loads[c]:
            copy.start()
    peer = partner_barrier()
    copies = []
    for n, (src, dst) in enumerate(((gx, gx_in), (fo, fo_in))):
        for c in range(CHUNKS):
            at = n * CHUNKS + c
            copy = send_rows(src, dst, rows_of(c), ssem.at[at], rsem.at[at], peer)
            copy.start()
            copies.append(copy)
    stores = []
    gain_sum = jnp.zeros((1, mid.shape[1]), F32)
    for c in range(CHUNKS):
        sl = slice(c * blk, (c + 1) * blk)
        for copy in loads[c][:3]:
            copy.wait()
        copies[c].wait_recv()
        grads = gx_v[sl, :].astype(F32) + gx_in[sl, :].astype(F32)
        back, gain_grad = norm_back(mid_v[sl, :], gain_ref[...], grads)
        gain_sum = gain_sum + gain_grad
        grad_mid = ct_v[sl, :].astype(F32) + back
        gm_v[sl, :] = grad_mid
        stores.append(pltpu.make_async_copy(gm_v.at[rows_of(c)], gm.at[rows_of(c)], osem.at[0, c]))
        stores[-1].start()
        gb[sl, :] = grad_mid.astype(BF)
        do_ref[sl, :] = dot_nt(gb[sl, :], w_ref[...]).astype(BF)
    gg_ref[...] = gain_sum
    for c in range(CHUNKS):
        sl = slice(c * blk, (c + 1) * blk)
        loads[c][3].wait()
        copies[CHUNKS + c].wait_recv()
        out_v[sl, :] = (mid_v[sl, :] + (fo_v[sl, :].astype(F32) + fo_in[sl, :].astype(F32))).astype(BF)
        stores.append(pltpu.make_async_copy(out_v.at[rows_of(c)], out.at[rows_of(c)], osem.at[1, c]))
        stores[-1].start()
    gw_ref[...] = dot_tn(at_ref[...], gb[...]).astype(BF)
    for copy in copies:
        copy.wait_send()
    for copy in stores:
        copy.wait()


def ffn_back_call(gx, fo, mid, ct, gain, w, at):
    rows, dim = mid.shape
    width = w.shape[0]
    any_spec = pl.BlockSpec(memory_space=pl.ANY)
    low = pltpu.VMEM((rows, dim), BF)
    wide = pltpu.VMEM((rows, dim), F32)
    dma = pltpu.SemaphoreType.DMA
    do, gw, gg, out, gm = pl.pallas_call(
        ffn_back_body,
        out_shape=[
            jax.ShapeDtypeStruct((rows, width), BF),
            jax.ShapeDtypeStruct((width, dim), BF),
            jax.ShapeDtypeStruct((1, dim), F32),
            jax.ShapeDtypeStruct((rows, dim), BF),
            jax.ShapeDtypeStruct((rows, dim), F32),
        ],
        in_specs=[whole_spec()] * 3 + [any_spec] * 4,
        out_specs=[whole_spec()] * 3 + [any_spec] * 2,
        scratch_shapes=[
            low, low, low, low, wide, low, wide, low, low,
            dma((2 * CHUNKS,)), dma((2 * CHUNKS,)), dma((4, CHUNKS)), dma((2, CHUNKS)),
        ],
        compiler_params=pltpu.CompilerParams(collective_id=2, has_side_effects=True, vmem_limit_bytes=VMEM_LIMIT),
        name="ffn_back",
    )(gain, w, at, gx, fo, mid, ct)
    return out, gm, do, gw, gg


def peers_of(dp):
    z = dp // 4
    y = (dp // 2) % 2
    x = dp % 2
    at = lambda zz, yy, xx: zz * 4 + yy * 2 + xx
    return z, y, x, at(z, y, 1 - x), at(z, 1 - y, x), at(z + 1 - 2 * (z % 2), y, x), at(3 - z, y, x)


def sum_body(
    gk, rg, uk, ru, late_x, late_y, dk, rd, go, dqkv, w3, xn, xin, gmid, gain_ref, gain2_ref, bias_ref, out_a, out_b, ig, small_out,
    L, S, Z, R, Y, DL, DS, DA, G, sb, st, dl, wb, xb, mine_rows, their_rows, away_rows, xc, gc, ic,
    loc, s1s, s1r, sends, zr, rr, yr, ar, xr, lo, ss, sr, ld, cs, cr, xg, io, s2s, s2r, gs, gr,
):
    dp = lax.axis_index("dp")
    t = lax.axis_index("tensor")
    z, y, x, px, py, zn, mm = peers_of(dp)
    is_mid = (z == 1) | (z == 2)
    is_end = (z == 0) | (z == 3)
    mine = jnp.where(z == 2, WIDE // 2, 0)
    others = WIDE // 2 - mine
    n = KEPT_ROWS // ROWS
    cut_at = 2 * HALF_ROWS // ROWS
    tail_at = (2 * HALF_ROWS + QUARTER_ROWS) // ROWS
    starts = (0, HALF_ROWS // ROWS, cut_at, tail_at)
    first = (px, py)
    last = (py, px)
    outs = (out_a, out_b)
    owner = (x, y)
    bit = (y, x)
    F = S

    def remote(src, dst, ssem, rsem, peer, core=t):
        return pltpu.make_async_remote_copy(
            src_ref=src, dst_ref=dst, send_sem=ssem, recv_sem=rsem, device_id=(peer, core), device_id_type=MESH
        )

    def loads(g, b):
        rows = pl.ds(b * HALF_ROWS, HALF_ROWS)
        near = (rg, ru)[g]
        late = (late_x, late_y)[g]
        top = pl.ds(0, HALF_ROWS)
        if b < 2:
            copies = [((gk, uk)[g].at[b], L.at[g, rows])]
        else:
            copies = [(dk.at[g], DL.at[g])]
        if b == 0:
            copies.append((near.at[:, pl.ds(0, WIDE)], S.at[g, rows]))
        elif b == 1:
            cut = near.shape[1] - WIDE
            if cut:
                copies.append((near.at[:, pl.ds(WIDE, cut)], S.at[g, rows, pl.ds(0, cut)]))
            copies.append((late.at[top], S.at[g, rows, pl.ds(cut, WIDE - cut)]))
        else:
            cut = rd.shape[1]
            copies.append((rd.at[g], DS.at[g, pl.ds(0, cut)]))
            copies.append((late.at[pl.ds(HALF_ROWS, HALF_ROWS - cut)], DS.at[g, pl.ds(cut, HALF_ROWS - cut)]))
        return [pltpu.make_async_copy(src, dst, loc.at[g, b, k]) for k, (src, dst) in enumerate(copies)]

    own_loads = [pltpu.make_async_copy(src, dst, ld.at[k]) for k, (src, dst) in enumerate(((dqkv, dl), (w3, wb), (xn, xb)))]
    for b in range(3):
        for g in range(2):
            for copy in loads(g, b):
                copy.start()
    for copy in own_loads:
        copy.start()

    tail = pl.ds(2 * HALF_ROWS + QUARTER_ROWS, HALF_ROWS)

    def out_load(kept):
        return pltpu.make_async_copy(go, L.at[1, tail] if kept else away_rows.at[1], loc.at[1, 3, 0])

    def out_load_do(act):
        @pl.when(y == 1)
        def _():
            act(out_load(True))

        @pl.when(y == 0)
        def _():
            act(out_load(False))

    out_load_do(lambda copy: copy.start())

    barrier = pltpu.get_barrier_semaphore()
    others_z = [lax.rem(z + k, 4) * 4 + y * 2 + x for k in range(1, 4)]
    for peer in [px, py] + others_z:
        pl.semaphore_signal(barrier, inc=1, device_id=(peer, t), device_id_type=MESH)
    pl.semaphore_signal(barrier, inc=1, device_id=(dp, 1 - t), device_id_type=MESH)
    pl.semaphore_wait(barrier, 6)

    def first_exchange(g):
        return remote(away_rows.at[g], S.at[g, tail], s1s.at[g], s1r.at[g], first[g])

    def first_part(g, c):
        at = pl.multiple_of(c * SWAP_ROWS, SWAP_ROWS)
        dst = S.at[g, pl.ds(2 * HALF_ROWS + QUARTER_ROWS + at, SWAP_ROWS)]
        return remote(away_rows.at[g, pl.ds(at, SWAP_ROWS)], dst, s1s.at[g], s1r.at[g], first[g])

    quarter = pl.ds(2 * HALF_ROWS, QUARTER_ROWS)

    def second_exchange(g):
        return remote(DA.at[g], S.at[g, quarter], s2s.at[g], s2r.at[g], last[g])

    def second_part(g, c):
        at = pl.multiple_of(c * SWAP_ROWS, SWAP_ROWS)
        rows = pl.ds(at, SWAP_ROWS)
        dst = S.at[g, pl.ds(2 * HALF_ROWS + at, SWAP_ROWS)]
        return remote(DA.at[g, rows], dst, s2s.at[g], s2r.at[g], last[g])

    def down_quarter(half):
        return pl.ds(pl.multiple_of(half * QUARTER_ROWS, QUARTER_ROWS), QUARTER_ROWS)

    def piece_down(g):
        for copy in loads(g, 2):
            copy.wait()
        keep = down_quarter(bit[g])
        away = down_quarter(1 - bit[g])
        L[g, quarter, :] = (DL[g, keep, :].astype(F32) + DS[g, keep, :].astype(F32)).astype(BF)
        DA[g] = (DL[g, away, :].astype(F32) + DS[g, away, :].astype(F32)).astype(BF)

    def piece_swap(c):
        for g in range(2):
            first_part(g, c).start()

    def piece_second(c):
        for g in range(2):
            second_part(g, c).start()

    small_x = remote(st.at[2], sb.at[0], ss.at[0], sr.at[0], px)
    small_y = remote(st.at[0], sb.at[1], ss.at[1], sr.at[1], py)
    small_z = [remote(st.at[1], sb.at[2 + z], ss.at[2 + k], sr.at[2 + z], others_z[k]) for k in range(3)]

    def rows_of(i):
        return pl.ds(pl.multiple_of(i * ROWS, ROWS), ROWS)

    def cols_of(at):
        return pl.ds(pl.multiple_of(at, WIDE // 2), WIDE // 2)

    def z_copy(g, i):
        return remote(L.at[g, rows_of(i)], Z.at[g, rows_of(i)], sends.at[g, 0], zr.at[g, i], zn)

    def r_copy(g, i):
        return remote(L.at[g, rows_of(i), cols_of(others)], R.at[g, rows_of(i)], sends.at[g, 1], rr.at[g, i], mm)

    def y_copy(g, i):
        return remote(R.at[g, rows_of(i)], Y.at[g, rows_of(i)], sends.at[g, 2], yr.at[g, i], last[g])

    def a_copy(g, i, at):
        return remote(F.at[g, rows_of(i), cols_of(at)], F.at[g, rows_of(i), cols_of(at)], sends.at[g, 3], ar.at[g, i], mm)

    def o_copy(g, i):
        return remote(F.at[g, rows_of(i)], F.at[g, rows_of(i)], sends.at[g, 4], zr.at[g, i], zn)

    def out_rows(g, i):
        shift = jnp.where(i < cut_at, 0, jnp.where(i < tail_at, bit[g] * QUARTER_ROWS, QUARTER_ROWS))
        return pl.ds(pl.multiple_of(i * ROWS + shift, ROWS), ROWS)

    def x_copy(g, i):
        return remote(F.at[g, rows_of(i)], outs[g].at[owner[g], out_rows(g, i)], sends.at[g, 5], xr.at[g], first[g])

    def l_copy(g, i):
        return pltpu.make_async_copy(F.at[g, rows_of(i)], outs[g].at[owner[g], out_rows(g, i)], lo.at[g])

    def quarter_rows(i):
        return pl.ds(pl.multiple_of((i - cut_at) * ROWS, ROWS), ROWS)

    def g_copy(g, i):
        return remote(F.at[g, rows_of(i)], G.at[g, quarter_rows(i)], gs.at[g], gr.at[g, i - cut_at], last[g])

    def pass_on(g, i):
        rows = pl.ds(pl.multiple_of(i * ROWS + (1 - bit[g]) * QUARTER_ROWS, ROWS), ROWS)
        src = G.at[g, quarter_rows(i)]
        g_copy(g, i).wait_recv()
        remote(src, outs[g].at[owner[g], rows], sends.at[g, 5], xr.at[g], first[g]).start()
        pltpu.make_async_copy(src, outs[g].at[owner[g], rows], lo.at[g]).start()

    def is_cut(i):
        return (i >= cut_at) & (i < tail_at)

    def finish(g, i):
        x_copy(g, i).start()
        l_copy(g, i).start()

        @pl.when(is_cut(i))
        def _():
            g_copy(g, i).start()

    def end_in(g, j):
        r = rows_of(j)
        L[g, r, :] = (L[g, r, :].astype(F32) + S[g, r, :].astype(F32)).astype(BF)
        z_copy(g, j).start()

    def end_out(g, j):
        o_copy(g, j).wait_recv()
        finish(g, j)

    def mid_out(g, j):
        a_copy(g, j, others).wait_recv()
        o_copy(g, j).start()
        finish(g, j)

    def mid_join(g, j):
        @pl.when(jnp.logical_not(is_cut(j)))
        def _():
            y_copy(g, j).wait_recv()
            r = rows_of(j)
            F[g, r, cols_of(mine)] = (R[g, r, :].astype(F32) + Y[g, r, :].astype(F32)).astype(BF)
            a_copy(g, j, mine).start()

    def mid_half(g, j):
        r_copy(g, j).wait_recv()
        r = rows_of(j)
        total = (R[g, r, :].astype(F32) + L[g, r, cols_of(mine)].astype(F32)).astype(BF)

        @pl.when(is_cut(j))
        def _():
            F[g, r, cols_of(mine)] = total
            a_copy(g, j, mine).start()

        @pl.when(jnp.logical_not(is_cut(j)))
        def _():
            R[g, r, :] = total
            y_copy(g, j).start()

    def mid_in(g, j):
        z_copy(g, j).wait_recv()
        r = rows_of(j)
        L[g, r, :] = (L[g, r, :].astype(F32) + S[g, r, :].astype(F32) + Z[g, r, :].astype(F32)).astype(BF)
        r_copy(g, j).start()

    def stage(act, g, j):
        @pl.when((j >= 0) & (j < n))
        def _():
            act(g, j)

    seq = xin.shape[0]
    blk = seq // CHUNKS
    width = dl.shape[2]

    def piece_rows(c):
        return pl.ds(pl.multiple_of(c * blk, blk), blk)

    def core_copy(c):
        return remote(mine_rows.at[piece_rows(c)], their_rows.at[piece_rows(c)], cs.at[c], cr.at[c], dp, 1 - t)

    def norm_loads(c):
        return [
            pltpu.make_async_copy(xin.at[piece_rows(c)], xc.at[lax.rem(c, 2)], xg.at[lax.rem(c, 2), 0]),
            pltpu.make_async_copy(gmid.at[piece_rows(c)], gc.at[lax.rem(c, 2)], xg.at[lax.rem(c, 2), 1]),
        ]

    def ig_copy(c):
        return pltpu.make_async_copy(ic.at[lax.rem(c, 2)], ig.at[piece_rows(c)], io.at[lax.rem(c, 2)])

    def piece_start():
        for copy in own_loads:
            copy.wait()

    def piece_part(c):
        r = piece_rows(c)
        total = dot_nt(dl[0, r, :], wb[0]) + dot_nt(dl[1, r, :], wb[1]) + dot_nt(dl[2, r, :], wb[2])
        mine_rows[r, :] = total.astype(BF)
        core_copy(c).start()

    def row_half(half):
        return pl.ds(pl.multiple_of(half * HALF_ROWS, HALF_ROWS), HALF_ROWS)

    def piece_qk(k):
        cols = pl.ds(k * width, width)
        L[0, tail, cols] = dot_tn(xb[:, row_half(x)], dl[k]).astype(BF)
        away_rows[0, :, cols] = dot_tn(xb[:, row_half(1 - x)], dl[k]).astype(BF)

    def piece_v():
        for k in range(2):
            cols = pl.ds(k * width, width)
            grad = dot_tn(xb[:, k * HALF_ROWS : (k + 1) * HALF_ROWS], dl[2]).astype(BF)

            @pl.when(y == 0)
            def _():
                L[1, tail, cols] = grad

            @pl.when(y == 1)
            def _():
                away_rows[1, :, cols] = grad

    def piece_send():
        out_load_do(lambda copy: copy.wait())
        for copy in norm_loads(0):
            copy.start()
        st[2] = jnp.zeros((SMALL, WIDE), F32)
        st[2, 1:2, :] = gain2_ref[...]
        for p in range(bias_ref.shape[0]):
            sums = [jnp.sum(bias_ref[p, h, s], axis=0, keepdims=True) for h in range(2) for s in range(2)]
            st[2, 2 + p : 3 + p, :] = jnp.concatenate(sums, axis=1)

    def piece_norm(c):
        @pl.when(c + 1 < CHUNKS)
        def _():
            for copy in norm_loads(c + 1):
                copy.start()

        for copy in norm_loads(c):
            copy.wait()
        core_copy(c).wait_recv()

        @pl.when(c >= 2)
        def _():
            ig_copy(c - 2).wait()

        r = piece_rows(c)
        grads = mine_rows[r, :].astype(F32) + their_rows[r, :].astype(F32)
        s = lax.rem(c, 2)
        back, gain_grad = norm_back(xc[s].astype(F32), gain_ref[...], grads)
        st[2, 0:1, :] = st[2, 0:1, :] + gain_grad
        ic[s] = gc[s] + back
        ig_copy(c).start()

    def small_first():
        small_x.start()

    def small_second():
        small_x.wait_recv()
        st[0] = st[2] + sb[0]
        small_y.start()

    def small_third():
        small_y.wait_recv()
        st[1] = st[0] + sb[1]
        for copy in small_z:
            copy.start()

    pieces = [
        (1, 1, lambda c: piece_down(0)),
        (2, 1, lambda c: piece_down(1)),
        (3, QUARTER_ROWS // SWAP_ROWS, piece_second),
        (3, 1, lambda c: piece_start()),
        (4, CHUNKS, piece_part),
        (4 + CHUNKS, 1, lambda c: piece_qk(0)),
        (5 + CHUNKS, 1, lambda c: piece_qk(1)),
        (6 + CHUNKS, 1, lambda c: piece_v()),
        (7 + CHUNKS, 1, lambda c: piece_send()),
        (8 + CHUNKS, HALF_ROWS // SWAP_ROWS, piece_swap),
        (9 + CHUNKS, CHUNKS, piece_norm),
        (10 + 2 * CHUNKS, 1, lambda c: small_first()),
        (14 + 2 * CHUNKS, 1, lambda c: small_second()),
        (18 + 2 * CHUNKS, 1, lambda c: small_third()),
    ]

    def body(i, carry):
        for b in range(4):

            @pl.when(i == starts[b])
            def _():
                for g in range(2):
                    if b < 2:
                        for copy in loads(g, b):
                            copy.wait()
                    elif b == 2:
                        second_exchange(g).wait_recv()
                    else:
                        first_exchange(g).wait_recv()

        @pl.when(is_end)
        def _():
            for g in range(2):
                stage(end_in, g, i)
                stage(end_out, g, i - LAGS[4])

        @pl.when(is_mid)
        def _():
            for g in range(2):
                stage(mid_out, g, i - LAGS[3])
                stage(mid_join, g, i - LAGS[2])
                stage(mid_half, g, i - LAGS[1])
                stage(mid_in, g, i - LAGS[0])

        for g in range(2):
            j = i - LAGS[4] - 2

            @pl.when(is_cut(j))
            def _():
                pass_on(g, j)

        for begin, steps, piece in pieces:

            @pl.when((i >= begin) & (i < begin + steps))
            def _():
                piece(i - begin)

        return carry

    lax.fori_loop(0, n + LAGS[4], body, 0)

    for k in range(3):
        zz = lax.rem(z + k + 1, 4)
        remote(st.at[1], sb.at[2 + zz], ss.at[2 + k], sr.at[2 + zz], others_z[k]).wait_recv()
    sb[2 + z] = st[1]
    small_out[...] = (sb[2] + sb[3]) + (sb[4] + sb[5])

    small_x.wait_send()
    small_y.wait_send()
    for copy in small_z:
        copy.wait_send()
    for c in range(CHUNKS):
        core_copy(c).wait_send()
    for c in (CHUNKS - 2, CHUNKS - 1):
        ig_copy(c).wait()
    for g in range(2):
        first_exchange(g).wait_send()
        away = 1 - owner[g]

        @pl.when(is_end)
        def _():
            remote(L.at[g], Z.at[g], sends.at[g, 0], zr.at[g, 0], zn).wait_send()

        @pl.when(is_mid)
        def _():
            remote(R.at[g], Y.at[g], sends.at[g, 1], rr.at[g, 0], mm).wait_send()
            some = pl.ds(0, KEPT_ROWS - QUARTER_ROWS)
            remote(R.at[g, some], Y.at[g, some], sends.at[g, 2], yr.at[g, 0], last[g]).wait_send()
            remote(R.at[g], Y.at[g], sends.at[g, 3], ar.at[g, 0], mm).wait_send()
            remote(F.at[g], F.at[g], sends.at[g, 4], zr.at[g, 0], zn).wait_send()

        second_exchange(g).wait_send()
        remote(G.at[g], G.at[g], gs.at[g], gr.at[g, 0], last[g]).wait_send()
        whole = remote(outs[g].at[away], outs[g].at[away], sends.at[g, 5], xr.at[g], first[g])
        whole.wait_send()
        whole.wait_recv()
        pltpu.make_async_copy(outs[g].at[owner[g]], outs[g].at[owner[g]], lo.at[g]).wait()


def sum_call(gk, rg, uk, ru, late_x, late_y, dk, rd, go, dqkv, w3, xn, xin, gmid, gain, gain2, bias):
    any_spec = pl.BlockSpec(memory_space=pl.ANY)
    n = KEPT_ROWS // ROWS
    rows, dim = xin.shape
    blk = rows // CHUNKS
    full = pltpu.VMEM((2, KEPT_ROWS, WIDE), BF)
    half = pltpu.VMEM((2, KEPT_ROWS, WIDE // 2), BF)
    quarter = pltpu.VMEM((2, QUARTER_ROWS, WIDE), BF)
    down = pltpu.VMEM((2, HALF_ROWS, WIDE), BF)
    dma = pltpu.SemaphoreType.DMA
    return pl.pallas_call(
        sum_body,
        out_shape=[jax.ShapeDtypeStruct((2, GROUP_ROWS, WIDE), BF)] * 2
        + [jax.ShapeDtypeStruct((rows, dim), F32), jax.ShapeDtypeStruct((SMALL, WIDE), F32)],
        in_specs=[any_spec] * 14 + [whole_spec()] * 3,
        out_specs=[any_spec] * 3 + [whole_spec()],
        scratch_shapes=[
            full, full, full, half, half, down, down, quarter, quarter,
            pltpu.VMEM((6, SMALL, WIDE), F32),
            pltpu.VMEM((3, SMALL, WIDE), F32),
            pltpu.VMEM(dqkv.shape, BF),
            pltpu.VMEM(w3.shape, BF),
            pltpu.VMEM((rows, dim), BF),
            pltpu.VMEM((rows, dim), BF),
            pltpu.VMEM((rows, dim), BF),
            pltpu.VMEM((2, HALF_ROWS, WIDE), BF),
            pltpu.VMEM((2, blk, dim), BF),
            pltpu.VMEM((2, blk, dim), F32),
            pltpu.VMEM((2, blk, dim), F32),
            dma((2, 4, 8)), dma((2,)), dma((2,)), dma((2, 6)),
            dma((2, n)), dma((2, n)), dma((2, n)), dma((2, n)),
            dma((2,)), dma((2,)), dma((5,)), dma((6,)),
            dma((3,)), dma((CHUNKS,)), dma((CHUNKS,)), dma((2, 2)), dma((2,)),
            dma((2,)), dma((2,)), dma((2,)), dma((2, QUARTER_ROWS // ROWS)),
        ],
        compiler_params=pltpu.CompilerParams(collective_id=4, has_side_effects=True, vmem_limit_bytes=VMEM_LIMIT),
        name="grad_sum",
    )(gk, rg, uk, ru, late_x, late_y, dk, rd, go, dqkv, w3, xn, xin, gmid, gain, gain2, bias)


def tables(time_ids):
    half = HEAD // 2
    freqs = jnp.exp(jnp.arange(half, dtype=F32) * (-2.0 * math.log(10000.0) / HEAD))
    angles = time_ids.astype(F32)[:, None] * jnp.tile(freqs, LANES // half)[None, :]
    sign = jnp.where(jnp.arange(LANES) % HEAD < half, -1.0, 1.0)
    return jnp.cos(angles), jnp.sin(angles) * sign[None, :]


def mask_tables(segments, variates):
    lane = jnp.arange(LANES)[None, :]
    var_here = (lane % VAR_COLS == variates[:, None]) & (lane < 3 * VAR_COLS)
    seg_here = (lane - SEG_COL == segments[:, None]) & (lane >= SEG_COL) & (lane < ONE_COL)
    seg_cols = (lane >= SEG_COL) & (lane < ONE_COL)
    ones = (lane >= ONE_COL) & (lane < ONE_COL + 3)
    base = jnp.where(var_here, 1.0, 0.0)
    segq = jnp.where(seg_cols & ~seg_here, MASKED, 0.0)
    extk = jnp.where(var_here | seg_here | ones, 1.0, 0.0).astype(BF)
    return base, segq, extk


def fast_local(
    block_input, segments, variates, time_ids, attn_gain, w_qkv, head_bias, w_out, ffn_gain, w_gate_up, w_down, cotangent
):
    w3 = jnp.transpose(w_qkv, (1, 0, 2))
    cosine, sine = tables(time_ids)
    base, segq, extk = mask_tables(segments, variates)
    gain1 = attn_gain[None, :]
    gain2 = ffn_gain[None, :]
    xn, q, k, v = qkv_call(block_input, gain1, w3, cosine, sine)
    attended, o32, extq, wg, wu = attn_fwd_call(q, k, v, base, segq, extk, head_bias, pair_rows(w_gate_up))
    mid, xn2 = attn_out_call(block_input, attended, w_out, gain2)
    ffn_part, gx_part, gk, uk, rg, ru, dk, rd, late_x, late_y = ffn_call(xn2, cotangent, wg, wu, w_down)
    late_x = lax.ppermute(late_x, "dp", [(d, d ^ 1) for d in range(16)])
    late_y = lax.ppermute(late_y, "dp", [(d, d ^ 2) for d in range(16)])
    block_output, grad_mid, do, g_out, g_gain2 = ffn_back_call(
        gx_part, ffn_part, mid, cotangent, gain2, w_out, attended
    )
    dqkv, g_bias = attn_bwd_call(q, k, v, do, o32, extq, extk, variates[None, :], cosine, sine)
    sum_a, sum_b, input_grad, small = sum_call(
        gk, rg, uk, ru, late_x, late_y, dk, rd, g_out, dqkv, w3, xn, block_input, grad_mid, gain1, g_gain2, g_bias
    )
    sum_a = sum_a.reshape(2, 4, HALF_ROWS, WIDE)
    sum_b = sum_b.reshape(2, 4, HALF_ROWS, WIDE)
    heads = head_bias.shape[1]
    g_gate_up, g_down, g_qkv, g_out, g_gain1, g_gain2, g_bias = widen_call(sum_a, sum_b, small, heads)
    return (
        block_output, input_grad, g_gain1[0], jnp.transpose(g_qkv, (1, 0, 2)), g_bias, g_out, g_gain2[0], g_gate_up, g_down,
    )


def rope_tables(time_ids, head_dim):
    half_dim = head_dim // 2
    freqs = jnp.exp(jnp.arange(half_dim, dtype=jnp.float32) * (-2.0 * math.log(10000.0) / head_dim))
    angles = time_ids.astype(jnp.float32)[:, None] * freqs[None, :]
    return (jnp.cos(angles)[:, None, :], jnp.sin(angles)[:, None, :])


def rotate(vectors, cosine, sine_part):
    half_dim = vectors.shape[-1] // 2
    first_half = vectors[..., :half_dim]
    second_half = vectors[..., half_dim:]
    return jnp.concatenate(
        [
            first_half * cosine - second_half * sine_part,
            second_half * cosine + first_half * sine_part,
        ],
        axis=-1,
    )


def rotate_back(grads, cosine, sine_part):
    half_dim = grads.shape[-1] // 2
    first_half = grads[..., :half_dim]
    second_half = grads[..., half_dim:]
    return jnp.concatenate(
        [
            first_half * cosine + second_half * sine_part,
            second_half * cosine - first_half * sine_part,
        ],
        axis=-1,
    )


def norm_rows(rows_now, gain):
    inverse = lax.rsqrt(jnp.mean(rows_now * rows_now, axis=-1, keepdims=True) + EPSILON)
    return (rows_now * inverse * gain, inverse)


def plain_norm_back(rows_now, inverse, gain, grads):
    scaled = grads * gain
    gain_grad = jnp.sum(grads * rows_now * inverse, axis=0)
    rows_grad = inverse * scaled - rows_now * (inverse * inverse * inverse) * jnp.mean(
        scaled * rows_now, axis=-1, keepdims=True
    )
    return (rows_grad, gain_grad)


def scores_of(queries, keys_rot, same_var, allowed, head_bias, score_scale):
    raw_scores = (
        jnp.einsum("sqhd,skhd->shqk", queries, keys_rot, preferred_element_type=jnp.float32)
        * score_scale
    )
    biased = raw_scores + jnp.where(
        same_var[:, None], head_bias[0][None, :, None, None], head_bias[1][None, :, None, None]
    )
    return jnp.where(allowed[:, None], biased, MASKED)


def plain_local(
    block_input,
    segments,
    variates,
    time_ids,
    attn_gain,
    w_qkv,
    head_bias,
    w_out,
    ffn_gain,
    w_gate_up,
    w_down,
    cotangent,
):
    row_count = block_input.shape[0]
    heads_here = head_bias.shape[1]
    head_dim = w_qkv.shape[2] // heads_here
    seq_count = row_count // LEN
    score_scale = head_dim ** (-0.5)
    input_rows = block_input.astype(jnp.float32)
    attn_normed, attn_inverse = norm_rows(input_rows, attn_gain)
    attn_normed_low = attn_normed.astype(jnp.bfloat16)
    projected = jnp.einsum(
        "td,dck->tck", attn_normed_low, w_qkv, preferred_element_type=jnp.float32
    )
    cosine, sine_part = rope_tables(time_ids, head_dim)
    head_shape = (row_count, heads_here, head_dim)
    seq_shape = (seq_count, LEN, heads_here, head_dim)
    queries = (
        rotate(projected[:, 0].reshape(head_shape), cosine, sine_part)
        .astype(jnp.bfloat16)
        .reshape(seq_shape)
    )
    keys_rot = (
        rotate(projected[:, 1].reshape(head_shape), cosine, sine_part)
        .astype(jnp.bfloat16)
        .reshape(seq_shape)
    )
    values = projected[:, 2].astype(jnp.bfloat16).reshape(seq_shape)
    seg_ids = segments.reshape(seq_count, LEN)
    var_ids = variates.reshape(seq_count, LEN)
    allowed = seg_ids[:, :, None] == seg_ids[:, None, :]
    same_var = var_ids[:, :, None] == var_ids[:, None, :]
    scores = scores_of(queries, keys_rot, same_var, allowed, head_bias, score_scale)
    row_max = jnp.max(scores, axis=-1, keepdims=True)
    exp_total = jnp.sum(jnp.exp(scores - row_max), axis=-1, keepdims=True)
    log_total = row_max + jnp.log(exp_total)
    probs_low = jnp.exp(scores - log_total).astype(jnp.bfloat16)
    attended = jnp.einsum("shqk,skhd->sqhd", probs_low, values, preferred_element_type=jnp.float32)
    attended = attended.reshape(row_count, heads_here * head_dim).astype(jnp.bfloat16)
    attn_branch = lax.psum(
        jnp.dot(attended, w_out, preferred_element_type=jnp.float32).astype(jnp.bfloat16), "tensor"
    ).astype(jnp.float32)
    mid_rows = input_rows + attn_branch
    ffn_normed, ffn_inverse = norm_rows(mid_rows, ffn_gain)
    ffn_normed_low = ffn_normed.astype(jnp.bfloat16)
    gate_up = jnp.einsum(
        "td,dcf->tcf", ffn_normed_low, w_gate_up, preferred_element_type=jnp.float32
    )
    gate_vals = gate_up[:, 0]
    up_vals = gate_up[:, 1]
    sigmoid_gate = jax.nn.sigmoid(gate_vals)
    silu_gate = gate_vals * sigmoid_gate
    hidden_low = (silu_gate * up_vals).astype(jnp.bfloat16)
    ffn_branch = lax.psum(
        jnp.dot(hidden_low, w_down, preferred_element_type=jnp.float32).astype(jnp.bfloat16),
        "tensor",
    ).astype(jnp.float32)
    block_output = (mid_rows + ffn_branch).astype(jnp.bfloat16)
    grad_down = jnp.einsum("tf,td->fd", hidden_low, cotangent, preferred_element_type=jnp.float32)
    grad_hidden = jnp.einsum("td,fd->tf", cotangent, w_down, preferred_element_type=jnp.float32)
    grad_gate = grad_hidden * up_vals * sigmoid_gate * (1.0 + gate_vals * (1.0 - sigmoid_gate))
    grad_up = grad_hidden * silu_gate
    grad_gate_up = jnp.stack([grad_gate, grad_up], axis=1).astype(jnp.bfloat16)
    grad_w_gate_up = jnp.einsum(
        "td,tcf->dcf", ffn_normed_low, grad_gate_up, preferred_element_type=jnp.float32
    )
    grad_ffn_normed = lax.psum(
        jnp.einsum(
            "tcf,dcf->td", grad_gate_up, w_gate_up, preferred_element_type=jnp.float32
        ).astype(jnp.bfloat16),
        "tensor",
    ).astype(jnp.float32)
    norm_grad_mid, grad_ffn_gain = plain_norm_back(mid_rows, ffn_inverse, ffn_gain, grad_ffn_normed)
    grad_mid = cotangent.astype(jnp.float32) + norm_grad_mid
    grad_branch = grad_mid.astype(jnp.bfloat16)
    grad_w_out = jnp.einsum("tk,td->kd", attended, grad_branch, preferred_element_type=jnp.float32)
    grad_attended = jnp.einsum("td,kd->tk", grad_branch, w_out, preferred_element_type=jnp.float32)
    grad_attended = grad_attended.astype(jnp.bfloat16).reshape(seq_shape)
    scores_again = scores_of(queries, keys_rot, same_var, allowed, head_bias, score_scale)
    probs_again = jnp.exp(scores_again - log_total)
    probs_again_low = probs_again.astype(jnp.bfloat16)
    grad_probs = jnp.einsum(
        "sqhd,skhd->shqk", grad_attended, values, preferred_element_type=jnp.float32
    )
    grad_values = jnp.einsum(
        "shqk,sqhd->skhd", probs_again_low, grad_attended, preferred_element_type=jnp.float32
    )
    grad_scores = probs_again * (
        grad_probs - jnp.sum(probs_again * grad_probs, axis=-1, keepdims=True)
    )
    grad_scores_low = grad_scores.astype(jnp.bfloat16)
    same_low = same_var.astype(jnp.bfloat16)
    other_low = jnp.logical_not(same_var).astype(jnp.bfloat16)
    grad_bias = jnp.stack(
        [
            jnp.einsum(
                "shqk,sqk->h", grad_scores_low, same_low, preferred_element_type=jnp.float32
            ),
            jnp.einsum(
                "shqk,sqk->h", grad_scores_low, other_low, preferred_element_type=jnp.float32
            ),
        ],
        axis=0,
    )
    grad_queries = (
        jnp.einsum("shqk,skhd->sqhd", grad_scores_low, keys_rot, preferred_element_type=jnp.float32)
        * score_scale
    )
    grad_keys = (
        jnp.einsum("shqk,sqhd->skhd", grad_scores_low, queries, preferred_element_type=jnp.float32)
        * score_scale
    )
    grad_query_lin = rotate_back(grad_queries.reshape(head_shape), cosine, sine_part).reshape(
        row_count, heads_here * head_dim
    )
    grad_key_lin = rotate_back(grad_keys.reshape(head_shape), cosine, sine_part).reshape(
        row_count, heads_here * head_dim
    )
    grad_value_lin = grad_values.reshape(row_count, heads_here * head_dim)
    grad_projected = jnp.stack([grad_query_lin, grad_key_lin, grad_value_lin], axis=1).astype(
        jnp.bfloat16
    )
    grad_w_qkv = jnp.einsum(
        "td,tck->dck", attn_normed_low, grad_projected, preferred_element_type=jnp.float32
    )
    grad_attn_normed = lax.psum(
        jnp.einsum("tck,dck->td", grad_projected, w_qkv, preferred_element_type=jnp.float32).astype(
            jnp.bfloat16
        ),
        "tensor",
    ).astype(jnp.float32)
    norm_grad_input, grad_attn_gain = plain_norm_back(
        input_rows, attn_inverse, attn_gain, grad_attn_normed
    )
    input_grad = grad_mid + norm_grad_input
    grad_attn_gain, grad_w_qkv, grad_bias, grad_w_out, grad_ffn_gain, grad_w_gate_up, grad_down = (
        lax.psum(
            (
                grad_attn_gain,
                grad_w_qkv,
                grad_bias,
                grad_w_out,
                grad_ffn_gain,
                grad_w_gate_up,
                grad_down,
            ),
            "dp",
        )
    )
    return (
        block_output,
        input_grad,
        grad_attn_gain,
        grad_w_qkv,
        grad_bias,
        grad_w_out,
        grad_ffn_gain,
        grad_w_gate_up,
        grad_down,
    )


def solution(mesh):
    placed = (
        P("dp", None), P("dp"), P("dp"), P("dp"), P(), P(None, None, "tensor"), P(None, "tensor"),
        P("tensor", None), P(), P(None, None, "tensor"), P("tensor", None), P("dp", None),
    )
    fast = (mesh.shape["dp"], mesh.shape["tensor"]) == (16, 2)
    return jax.shard_map(
        fast_local if fast else plain_local,
        mesh=mesh,
        in_specs=placed,
        out_specs=(
            P("dp", None), P("dp", None), P(), P(None, None, "tensor"), P(None, "tensor"), P("tensor", None), P(),
            P(None, None, "tensor"), P("tensor", None),
        ),
        check_vma=False,
    )
```

```python
import functools
import math

import jax
import jax.numpy as jnp
from jax import lax
from jax.experimental import pallas as pl
from jax.experimental.pallas import tpu as pltpu
from jax.sharding import PartitionSpec as P

LEN = 1024
EPSILON = 1e-05
MASKED = -1000000000.0
BF = jnp.bfloat16
F32 = jnp.float32
MESH = pl.DeviceIdType.MESH
VMEM_LIMIT = 60 * 1024 * 1024
LANES = 128
HEAD = 64
VAR_COLS = 4
SEG_COL = 12
ONE_COL = 20
ROWS = 32
LAGS = (2, 4, 6, 8, 10)
SWAP_ROWS = 32
HALF_ROWS = 512
QUARTER_ROWS = HALF_ROWS // 2
GROUP_ROWS = 4 * HALF_ROWS
KEPT_ROWS = GROUP_ROWS - QUARTER_ROWS
WIDE = 1024
SMALL = 8
QBLK = 256
FFN_ROWS = 256
FFN_COLS = 512


def dot_nn(a, b):
    return lax.dot_general(a, b, (((1,), (0,)), ((), ())), preferred_element_type=F32)


def dot_nt(a, b):
    return lax.dot_general(a, b, (((1,), (1,)), ((), ())), preferred_element_type=F32)


def dot_tn(a, b):
    return lax.dot_general(a, b, (((0,), (0,)), ((), ())), preferred_element_type=F32)


def whole_spec():
    return pl.BlockSpec(memory_space=pltpu.VMEM)


def split3(v):
    hi = v.astype(BF).astype(F32)
    mid = (v - hi).astype(BF).astype(F32)
    return hi, mid, v - hi - mid


def half_swap(u):
    lane = lax.broadcasted_iota(jnp.int32, u.shape, 1) % HEAD
    return jnp.where(lane < HEAD // 2, pltpu.roll(u, LANES - HEAD // 2, 1), pltpu.roll(u, HEAD // 2, 1))


def qkv_body(x_ref, gain_ref, w_ref, cos_ref, sin_ref, xn_ref, q_ref, k_ref, v_ref, cos_out, sin_out):
    x = x_ref[...].astype(F32)
    inv = lax.rsqrt(jnp.mean(x * x, axis=-1, keepdims=True) + EPSILON)
    xn = (x * inv * gain_ref[...]).astype(BF)
    xn_ref[...] = xn
    half = cos_ref[...].T
    cosine = jnp.concatenate([half] * 4, axis=1)
    half = sin_ref[...].T
    sine = jnp.concatenate([-half, half] * 2, axis=1)
    cos_out[...] = cosine
    sin_out[...] = sine
    for part, out, factor in ((0, q_ref, HEAD**-0.5), (1, k_ref, 1.0)):
        lin = dot_nn(xn, w_ref[part])
        for s in range(lin.shape[1] // LANES):
            u = lin[:, s * LANES : (s + 1) * LANES]
            rot = (u * cosine + half_swap(u) * sine).astype(BF)
            if factor != 1.0:
                rot = (rot.astype(F32) * factor).astype(BF)
            out[:, s * LANES : (s + 1) * LANES] = rot
    v_ref[...] = dot_nn(xn, w_ref[2]).astype(BF)


def qkv_call(x, gain, w, cosine, sine):
    rows, dim = x.shape
    width = w.shape[2]
    blk = min(256, rows)
    row = lambda cols: pl.BlockSpec((blk, cols), lambda i: (i, 0))
    return pl.pallas_call(
        qkv_body,
        grid=(rows // blk,),
        out_shape=[jax.ShapeDtypeStruct((rows, dim), BF)]
        + [jax.ShapeDtypeStruct((rows, width), BF)] * 3
        + [jax.ShapeDtypeStruct((rows, LANES), F32)] * 2,
        in_specs=[
            row(dim),
            pl.BlockSpec((1, dim), lambda i: (0, 0)),
            pl.BlockSpec(w.shape, lambda i: (0, 0, 0)),
            pl.BlockSpec((HEAD // 2, blk), lambda i: (0, i)),
            pl.BlockSpec((HEAD // 2, blk), lambda i: (0, i)),
        ],
        out_specs=[row(dim), row(width), row(width), row(width), row(LANES), row(LANES)],
        compiler_params=pltpu.CompilerParams(vmem_limit_bytes=VMEM_LIMIT),
        name="qkv",
    )(x, gain, w, cosine, sine)


def attn_fwd_body(
    q_ref, k_ref, v_ref, base_ref, segq_ref, extk_ref, bias_ref, o_ref, o32_ref, extq_ref
):
    rows = q_ref.shape[0]
    blk = 256
    lane = lax.broadcasted_iota(jnp.int32, (blk, LANES), 1)
    kind = lax.broadcasted_iota(jnp.int32, (1, LANES), 1) // VAR_COLS
    bias_rows = []
    for h in range(2):
        head = pl.program_id(0) * 2 + h
        hi, mid, low = split3(jnp.full((1, LANES), bias_ref[0, head] - bias_ref[1, head], F32))
        bias_rows.append(jnp.where(kind == 0, hi, jnp.where(kind == 1, mid, jnp.where(kind == 2, low, 0.0))))
    kx = jnp.concatenate([k_ref[...], extk_ref[...]], axis=1)
    ones = jnp.ones((rows, LANES), BF)
    vx = jnp.concatenate([v_ref[...], ones], axis=1)
    for i in range(rows // blk):
        sl = slice(i * blk, (i + 1) * blk)
        q = q_ref[sl, :].astype(F32)
        base = base_ref[sl, :]
        segq = segq_ref[sl, :]
        outs = []
        for h in range(2):
            ext = base * bias_rows[h] + segq
            mine = (lane >= HEAD) if h else (lane < HEAD)
            qx = jnp.concatenate([jnp.where(mine, q, 0.0), ext], axis=1).astype(BF)
            s = dot_nt(qx, kx)
            top = jnp.max(s, axis=-1, keepdims=True)
            p = jnp.exp(s - top).astype(BF)
            ox = dot_nn(p, vx)
            total = ox[:, LANES:]
            outs.append(ox[:, :LANES] / total)
            lse = top + jnp.log(total)
            hi, mid, low = split3(lse)
            ext = jnp.where(
                lane == ONE_COL, -hi, jnp.where(lane == ONE_COL + 1, -mid, jnp.where(lane == ONE_COL + 2, -low, ext))
            )
            extq_ref[0, h, sl, :] = ext.astype(BF)
        o = jnp.where(lane < HEAD, outs[0], outs[1])
        o32_ref[sl, :] = o
        o_ref[sl, :] = o.astype(BF)


def attn_fwd_call(q, k, v, base, segq, extk, head_bias):
    rows, width = q.shape
    pairs = width // LANES
    col = pl.BlockSpec((rows, LANES), lambda p: (0, p))
    full = pl.BlockSpec((rows, LANES), lambda p: (0, 0))
    return pl.pallas_call(
        attn_fwd_body,
        grid=(pairs,),
        out_shape=[
            jax.ShapeDtypeStruct((rows, width), BF),
            jax.ShapeDtypeStruct((rows, width), F32),
            jax.ShapeDtypeStruct((pairs, 2, rows, LANES), BF),
        ],
        in_specs=[
            col, col, col, full, full, full,
            pl.BlockSpec(memory_space=pltpu.SMEM),
        ],
        out_specs=[col, col, pl.BlockSpec((1, 2, rows, LANES), lambda p: (p, 0, 0, 0))],
        compiler_params=pltpu.CompilerParams(vmem_limit_bytes=VMEM_LIMIT),
        name="attn_fwd",
    )(q, k, v, base, segq, extk, head_bias)


def attn_bwd_body(
    q_ref, k_ref, v_ref, do_ref, o32_ref, extq_ref, extk_ref, var_ref, cos_ref, sin_ref, d_ref, gb_ref, dqt_ref
):
    rows = q_ref.shape[0]
    blk = 256
    lane = lax.broadcasted_iota(jnp.int32, (blk, LANES), 1)
    kinds = lax.broadcasted_iota(jnp.int32, (8, blk), 0)
    kx = jnp.concatenate([k_ref[...], extk_ref[...]], axis=1)
    kxt = kx.T
    lane_all = lax.broadcasted_iota(jnp.int32, (rows, LANES), 1)
    vx = jnp.concatenate([v_ref[...], jnp.where(lane_all < 3, 1.0, 0.0).astype(BF)], axis=1)
    dv = jnp.zeros((rows, LANES), F32)
    dk = jnp.zeros((rows, LANES), F32)
    for h in range(2):
        same = jnp.zeros((8, blk), F32)
        other = jnp.zeros((8, blk), F32)
        for i in range(rows // blk):
            sl = slice(i * blk, (i + 1) * blk)
            mine = (lane >= HEAD) if h else (lane < HEAD)
            q = jnp.where(mine, q_ref[sl, :].astype(F32), 0.0).astype(BF)
            do32 = jnp.where(mine, do_ref[sl, :].astype(F32), 0.0)
            do = do32.astype(BF)
            delta = jnp.sum(do32 * o32_ref[sl, :], axis=-1, keepdims=True)
            hi, mid, low = split3(delta)
            dext = jnp.where(lane == 0, -hi, jnp.where(lane == 1, -mid, jnp.where(lane == 2, -low, 0.0))).astype(BF)
            st = dot_nt(kx, jnp.concatenate([q, extq_ref[0, h, sl, :]], axis=1))
            pt = jnp.exp(st)
            dpt = dot_nt(vx, jnp.concatenate([do, dext], axis=1))
            dst = (pt * dpt).astype(BF)
            dv = dv + dot_nn(pt.astype(BF), do)
            dk = dk + dot_nn(dst, q)
            dqt = dot_nn(kxt, dst)
            dqt_ref[h * HEAD : (h + 1) * HEAD, sl] = dqt[h * HEAD : (h + 1) * HEAD, :]
            g = dqt[LANES : LANES + 8, :]
            match = kinds == var_ref[:, sl]
            same = same + jnp.where(match, g, 0.0)
            other = other + jnp.where(match | (kinds >= VAR_COLS), 0.0, g)
        gb_ref[0, h, 0] = same
        gb_ref[0, h, 1] = other
    cosine = cos_ref[...]
    sine = sin_ref[...]
    dq = dqt_ref[...].T * HEAD**-0.5
    d_ref[0] = (dq * cosine - half_swap(dq) * sine).astype(BF)
    d_ref[1] = (dk * cosine - half_swap(dk) * sine).astype(BF)
    d_ref[2] = dv.astype(BF)


def attn_bwd_call(q, k, v, do, o32, extq, extk, variates, cosine, sine):
    rows, width = q.shape
    pairs = width // LANES
    col = pl.BlockSpec((rows, LANES), lambda p: (0, p))
    full = pl.BlockSpec((rows, LANES), lambda p: (0, 0))
    blk = 256
    return pl.pallas_call(
        attn_bwd_body,
        grid=(pairs,),
        out_shape=[jax.ShapeDtypeStruct((3, rows, width), BF), jax.ShapeDtypeStruct((pairs, 2, 2, 8, blk), F32)],
        in_specs=[
            col, col, col, col, col,
            pl.BlockSpec((1, 2, rows, LANES), lambda p: (p, 0, 0, 0)),
            full,
            pl.BlockSpec((1, rows), lambda p: (0, 0)),
            full, full,
        ],
        out_specs=[pl.BlockSpec((3, rows, LANES), lambda p: (0, 0, p)), pl.BlockSpec((1, 2, 2, 8, blk), lambda p: (p, 0, 0, 0, 0))],
        scratch_shapes=[pltpu.VMEM((LANES, rows), F32)],
        compiler_params=pltpu.CompilerParams(vmem_limit_bytes=VMEM_LIMIT),
        name="attn_bwd",
    )(q, k, v, do, o32, extq, extk, variates, cosine, sine)


def partner_barrier():
    dp = lax.axis_index("dp")
    other = 1 - lax.axis_index("tensor")
    barrier = pltpu.get_barrier_semaphore()
    pl.semaphore_signal(barrier, inc=1, device_id=(dp, other), device_id_type=MESH)
    pl.semaphore_wait(barrier, 1)
    return (dp, other)


def send_rows(src, dst, sl, ssem, rsem, peer):
    return pltpu.make_async_remote_copy(
        src_ref=src.at[sl], dst_ref=dst.at[sl], send_sem=ssem, recv_sem=rsem, device_id=peer, device_id_type=MESH
    )


CHUNKS = 4


def attn_out_body(o_ref, w_ref, gain_ref, x, mid, xn, x_v, mid_v, xn_v, mine, theirs, ssem, rsem, lsem, osem):
    rows = x.shape[0]
    blk = rows // CHUNKS

    def rows_of(c):
        return pl.ds(pl.multiple_of(c * blk, blk), blk)

    def load(c):
        return pltpu.make_async_copy(x.at[rows_of(c)], x_v.at[rows_of(c)], lsem.at[c])

    def stores(c):
        return [
            pltpu.make_async_copy(mid_v.at[rows_of(c)], mid.at[rows_of(c)], osem.at[0, c]),
            pltpu.make_async_copy(xn_v.at[rows_of(c)], xn.at[rows_of(c)], osem.at[1, c]),
        ]

    for c in range(CHUNKS):
        load(c).start()
    peer = partner_barrier()

    def core_copy(c):
        return send_rows(mine, theirs, rows_of(c), ssem.at[c], rsem.at[c], peer)

    @pl.loop(0, CHUNKS)
    def _(c):
        mine[rows_of(c), :] = dot_nn(o_ref[rows_of(c), :], w_ref[...]).astype(BF)
        core_copy(c).start()

    @pl.loop(0, CHUNKS)
    def _(c):
        r = rows_of(c)
        load(c).wait()
        core_copy(c).wait_recv()
        total = x_v[r, :].astype(F32) + (mine[r, :].astype(F32) + theirs[r, :].astype(F32))
        inv = lax.rsqrt(jnp.mean(total * total, axis=-1, keepdims=True) + EPSILON)
        mid_v[r, :] = total
        xn_v[r, :] = (total * inv * gain_ref[...]).astype(BF)
        for copy in stores(c):
            copy.start()

    for c in range(CHUNKS):
        core_copy(c).wait_send()
        for copy in stores(c):
            copy.wait()


def attn_out_call(x, o, w, gain):
    rows, dim = x.shape
    any_spec = pl.BlockSpec(memory_space=pl.ANY)
    low = pltpu.VMEM((rows, dim), BF)
    dma = pltpu.SemaphoreType.DMA
    return pl.pallas_call(
        attn_out_body,
        out_shape=[jax.ShapeDtypeStruct((rows, dim), F32), jax.ShapeDtypeStruct((rows, dim), BF)],
        in_specs=[whole_spec()] * 3 + [any_spec],
        out_specs=[any_spec] * 2,
        scratch_shapes=[
            low, pltpu.VMEM((rows, dim), F32), low, low, low,
            dma((CHUNKS,)), dma((CHUNKS,)), dma((CHUNKS,)), dma((2, CHUNKS)),
        ],
        compiler_params=pltpu.CompilerParams(collective_id=1, has_side_effects=True, vmem_limit_bytes=VMEM_LIMIT),
        name="attn_out",
    )(o, w, gain, x)


LATE = 2
SLOTS = 2
PART = FFN_COLS // 4


def sent(copy):
    copy.wait_send() if copy.is_remote else copy.wait()


def grid_bits():
    dp = lax.axis_index("dp")
    return dp, dp % 2, (dp // 2) % 2, peers_of(dp)[3], peers_of(dp)[4]


def ffn_body(
    xn_ref, ct_ref, w0_ref, wn_ref, wd_ref,
    out_ref, gx_ref, gk_ref, uk_ref, rg, ru, dk, rd, late_x, late_y,
    acc_o, acc_g, hid, dg, du, xt, wgu, away_w, away_d, ws, wr, ds, dr,
):
    j = pl.program_id(0)
    t = lax.axis_index("tensor")
    dp, x, y, px, py = grid_bits()
    steps = pl.num_programs(0)
    rows = xn_ref.shape[0]
    blk = wd_ref.shape[0]
    per = WIDE // blk
    early = 2 * per - LATE
    slot = lax.rem(j, SLOTS)
    near = (px, py)
    bits = (x, y)
    arrays = ((rg, late_x), (ru, late_y))

    def remote(src, dst, ssem, rsem, peer):
        return pltpu.make_async_remote_copy(
            src_ref=src, dst_ref=dst, send_sem=ssem, recv_sem=rsem, device_id=(peer, t), device_id_type=MESH
        )

    def wide_early(k, at):
        cols = pl.ds(pl.multiple_of(lax.rem(at, per) * blk, blk), blk)
        s = lax.rem(at, SLOTS)
        return remote(away_w.at[k, s], arrays[k][0].at[:, cols], ws.at[k, s], wr.at[k], near[k])

    def wide_late(k, at):
        cols = pl.ds(pl.multiple_of((at - early) * blk, blk), blk)
        s = lax.rem(at, SLOTS)
        return pltpu.make_async_copy(away_w.at[k, s], arrays[k][1].at[pl.ds(0, HALF_ROWS), cols], ws.at[k, s])

    def wide_do(at, act):
        for k in range(2):

            @pl.when(at < early)
            def _():
                act(wide_early(k, at))

            @pl.when(at >= early)
            def _():
                act(wide_late(k, at))

    def down_rows(g, half):
        return pl.ds(pl.multiple_of(g * 2 * PART + half * PART, PART), PART)

    def down_keep(g, at):
        s = lax.rem(at, SLOTS)
        return pltpu.make_async_copy(
            away_d.at[s, down_rows(g, bits[g])], dk.at[g, pl.ds(pl.multiple_of(at * PART, PART), PART)], ds.at[g, s]
        )

    def down_send(g, at):
        s = lax.rem(at, SLOTS)
        rows_at = pl.ds(pl.multiple_of(at * PART, PART), PART)
        return remote(away_d.at[s, down_rows(g, 1 - bits[g])], rd.at[g, rows_at], ds.at[2 + g, s], dr.at[g], near[g])

    def down_late(g, at):
        s = lax.rem(at, SLOTS)
        rows_at = pl.ds(pl.multiple_of(HALF_ROWS + (at - early) * PART, PART), PART)
        return pltpu.make_async_copy(
            away_d.at[s, down_rows(g, 1 - bits[g])], arrays[g][1].at[rows_at], ds.at[2 + g, s]
        )

    def down_do(at, act):
        for g in range(2):
            act(down_keep(g, at))

            @pl.when(at < early)
            def _():
                act(down_send(g, at))

            @pl.when(at >= early)
            def _():
                act(down_late(g, at))

    def part_rows(src, to, r):
        turned = jnp.swapaxes(src[r].astype(F32), 0, 1)
        for k in range(8):
            s = k // 2
            wgu[to, k % 2, r, s * LANES : (s + 1) * LANES] = turned[k].astype(BF)

    @pl.when(j == 0)
    def _():
        barrier = pltpu.get_barrier_semaphore()
        for peer in near:
            pl.semaphore_signal(barrier, inc=1, device_id=(peer, t), device_id_type=MESH)
        pl.semaphore_wait(barrier, 2)
        acc_o[...] = jnp.zeros_like(acc_o)
        acc_g[...] = jnp.zeros_like(acc_g)
        xt[...] = xn_ref[...].T

        @pl.loop(0, rows // LANES)
        def _(c):
            part_rows(w0_ref, 0, pl.ds(pl.multiple_of(c * LANES, LANES), LANES))

    now = lax.rem(j, 2)
    wg = wgu[now, 0]
    wu = wgu[now, 1]
    wd = wd_ref[...]
    part_rows(wn_ref, 1 - now, slice(None))
    for i in range(rows // FFN_ROWS):
        sl = slice(i * FFN_ROWS, (i + 1) * FFN_ROWS)
        xn = xn_ref[sl, :]
        gate = dot_nn(xn, wg)
        up = dot_nn(xn, wu)
        gh = dot_nt(ct_ref[sl, :], wd)
        sig = jax.nn.sigmoid(gate)
        silu = gate * sig
        hidden = (silu * up).astype(BF)
        dgate = (gh * up * sig * (1.0 + gate * (1.0 - sig))).astype(BF)
        dup = (gh * silu).astype(BF)
        hid[sl, :] = hidden
        dg[sl, :] = dgate
        du[sl, :] = dup
        acc_o[sl, :] += dot_nn(hidden, wd)
        acc_g[sl, :] += dot_nt(dgate, wg) + dot_nt(dup, wu)

    @pl.when(j >= SLOTS)
    def _():
        wide_do(j - SLOTS, sent)
        down_do(j - SLOTS, sent)

    away_d[slot] = dot_tn(hid[...], ct_ref[...]).astype(BF)
    down_do(j, lambda copy: copy.start())
    for k, (part, keep, bit) in enumerate(((dg, gk_ref, x), (du, uk_ref, y))):
        rows_at = lambda half: pl.ds(pl.multiple_of(half * HALF_ROWS, HALF_ROWS), HALF_ROWS)
        away_w[k, slot] = dot_nn(xt[rows_at(1 - bit), :], part[...]).astype(BF)
        keep[0] = dot_nn(xt[rows_at(bit), :], part[...]).astype(BF)
    wide_do(j, lambda copy: copy.start())

    @pl.when(j == steps - 1)
    def _():
        out_ref[...] = acc_o[...].astype(BF)
        gx_ref[...] = acc_g[...].astype(BF)
        for back in range(SLOTS, 0, -1):
            wide_do(steps - back, sent)
            down_do(steps - back, sent)
        for k in range(2):
            part = arrays[k][0].at[:, pl.ds(0, early * blk)]
            remote(part, part, ws.at[k, 0], wr.at[k], near[k]).wait_recv()
        for g in range(2):
            part = rd.at[g, pl.ds(0, early * PART)]
            remote(part, part, ds.at[g, 0], dr.at[g], near[g]).wait_recv()


def ffn_call(xn, ct, w_pairs, wd):
    rows, dim = xn.shape
    hidden = wd.shape[0]
    blk = FFN_COLS
    per = WIDE // blk
    full = pl.BlockSpec((rows, dim), lambda j: (0, 0))
    steps = hidden // blk
    tiles = 2 * blk // LANES
    first_w = pl.BlockSpec((dim, tiles, LANES), lambda j: (0, 0, 0))
    next_w = pl.BlockSpec((dim, tiles, LANES), lambda j: (0, jnp.minimum(j + 1, steps - 1), 0))
    roww = pl.BlockSpec((blk, dim), lambda j: (j, 0))
    grad = pl.BlockSpec((1, HALF_ROWS, blk), lambda j: (j // per, 0, lax.rem(j, per)))
    any_spec = pl.BlockSpec(memory_space=pl.ANY)
    wide = jax.ShapeDtypeStruct((2, HALF_ROWS, dim), BF)
    early = hidden // blk - LATE
    come = jax.ShapeDtypeStruct((HALF_ROWS, early * blk), BF)
    late = jax.ShapeDtypeStruct((HALF_ROWS + LATE * PART, LATE * blk), BF)
    dma = pltpu.SemaphoreType.DMA
    return pl.pallas_call(
        ffn_body,
        grid=(hidden // blk,),
        in_specs=[full, full, first_w, next_w, roww],
        out_specs=[full, full, grad, grad] + [any_spec] * 6,
        out_shape=[jax.ShapeDtypeStruct((rows, dim), BF)] * 2
        + [wide, wide, come, come, wide, jax.ShapeDtypeStruct((2, early * PART, dim), BF), late, late],
        scratch_shapes=[pltpu.VMEM((rows, dim), F32)] * 2
        + [pltpu.VMEM((rows, blk), BF)] * 3
        + [
            pltpu.VMEM((dim, rows), BF),
            pltpu.VMEM((2, 2, dim, blk), BF),
            pltpu.VMEM((2, SLOTS, HALF_ROWS, blk), BF),
            pltpu.VMEM((SLOTS, blk, dim), BF),
            dma((2, SLOTS)), dma((2,)), dma((4, SLOTS)), dma((2,)),
        ],
        compiler_params=pltpu.CompilerParams(collective_id=5, has_side_effects=True, vmem_limit_bytes=VMEM_LIMIT),
        name="ffn",
    )(xn, ct, w_pairs, w_pairs, wd)


def pair_rows(w):
    dim, two, width = w.shape
    tiled = jnp.transpose(w.reshape(dim, two, width // LANES, LANES), (0, 2, 1, 3))
    return tiled.reshape(dim, two * width // LANES, LANES)


def widen_body(
    ga_ref, gb_ref, da_ref, db_ref, aa_ref, v_ref, o_ref, small_ref,
    gu_ref, down_ref, qkv_ref, out_ref, g1_ref, g2_ref, gbias_ref,
):
    tiles = WIDE // LANES
    for f in range(2):
        for q in range(tiles // 4):
            parts = []
            for k in range(8):
                s = q * 4 + k // 2
                parts.append((ga_ref, gb_ref)[k % 2][0, f, :, s * LANES : (s + 1) * LANES].astype(F32))
            at = (f * tiles + q * 4) * 2
            gu_ref[:, at : at + 8, :] = jnp.swapaxes(jnp.stack(parts), 0, 1)
    down_ref[:, 0, 0] = da_ref[0, 0].astype(F32).reshape(down_ref.shape[0], PART, WIDE)
    down_ref[:, 1, 0] = db_ref[0, 0].astype(F32).reshape(down_ref.shape[0], PART, WIDE)
    width = qkv_ref.shape[2]
    qkv_ref[0] = aa_ref[0, 0, :, :width].astype(F32)
    qkv_ref[1] = aa_ref[0, 0, :, width:].astype(F32)
    qkv_ref[2] = v_ref[0, 0].astype(F32)
    out_ref[...] = o_ref[0, 0].astype(F32)

    @pl.when(pl.program_id(0) == 0)
    def _():
        g1_ref[...] = small_ref[0:1, :]
        g2_ref[...] = small_ref[1:2, :]
        row = lax.broadcasted_iota(jnp.int32, gbias_ref.shape, 0)
        col = lax.broadcasted_iota(jnp.int32, gbias_ref.shape, 1)
        total = jnp.zeros(gbias_ref.shape, F32)
        for h in range(gbias_ref.shape[1]):
            for s in range(2):
                at = (h % 2 * 2 + s) * QBLK
                one = jnp.sum(small_ref[2 + h // 2 : 3 + h // 2, at : at + QBLK], axis=1, keepdims=True)
                total = jnp.where((row == s) & (col == h), one, total)
        gbias_ref[...] = total


def widen_call(a, b, small, heads):
    blk = 256
    half = HALF_ROWS // blk
    tiles = 4 * WIDE // LANES
    width = WIDE // 2
    gate = pl.BlockSpec((1, 2, blk, WIDE), lambda i: (i // half, 0, lax.rem(i, half), 0))
    block = lambda n: pl.BlockSpec((1, 1, blk, WIDE), lambda i: (i // half, n, lax.rem(i, half), 0))
    fixed = lambda shape: pl.BlockSpec(shape, lambda i: (0, 0))
    gu, down, qkv, out, g1, g2, gbias = pl.pallas_call(
        widen_body,
        grid=(2 * half,),
        out_shape=[
            jax.ShapeDtypeStruct((2 * HALF_ROWS, tiles, LANES), F32),
            jax.ShapeDtypeStruct((HALF_ROWS // PART, 2, 2, PART, WIDE), F32),
            jax.ShapeDtypeStruct((3, 2 * HALF_ROWS, width), F32),
            jax.ShapeDtypeStruct((HALF_ROWS, WIDE), F32),
            jax.ShapeDtypeStruct((1, WIDE), F32),
            jax.ShapeDtypeStruct((1, WIDE), F32),
            jax.ShapeDtypeStruct((2, heads), F32),
        ],
        in_specs=[
            gate, gate, block(2), block(2), block(3),
            pl.BlockSpec((1, 1, blk, width), lambda i: (0, 3, lax.rem(i, half), i // half)),
            pl.BlockSpec((1, 1, blk // 2, WIDE), lambda i: (1, 3, i, 0)),
            fixed((SMALL, WIDE)),
        ],
        out_specs=[
            pl.BlockSpec((blk, tiles, LANES), lambda i: (i, 0, 0)),
            pl.BlockSpec((blk // PART, 2, 1, PART, WIDE), lambda i: (lax.rem(i, half), 0, i // half, 0, 0)),
            pl.BlockSpec((3, blk, width), lambda i: (0, i, 0)),
            pl.BlockSpec((blk // 2, WIDE), lambda i: (i, 0)),
            fixed((1, WIDE)),
            fixed((1, WIDE)),
            fixed((2, heads)),
        ],
        compiler_params=pltpu.CompilerParams(vmem_limit_bytes=VMEM_LIMIT),
        name="widen",
    )(a, b, a, b, a, b, b, small)
    gu = jnp.transpose(gu.reshape(2 * HALF_ROWS, tiles // 2, 2, LANES), (0, 2, 1, 3)).reshape(2 * HALF_ROWS, 2, 2 * WIDE)
    return gu, down.reshape(4 * HALF_ROWS, WIDE), qkv, out, g1, g2, gbias


def norm_back(rows_now, gain, grads):
    inv = lax.rsqrt(jnp.mean(rows_now * rows_now, axis=-1, keepdims=True) + EPSILON)
    scaled = grads * gain
    gain_grad = jnp.sum(grads * rows_now * inv, axis=0, keepdims=True)
    back = inv * scaled - rows_now * (inv * inv * inv) * jnp.mean(scaled * rows_now, axis=-1, keepdims=True)
    return back, gain_grad


def ffn_back_body(
    gain_ref, w_ref, at_ref, gx, fo, mid, ct,
    do_ref, gw_ref, gg_ref, out, gm,
    gx_in, fo_in, gx_v, fo_v, mid_v, ct_v, gm_v, out_v, gb, ssem, rsem, lsem, osem,
):
    rows = mid.shape[0]
    blk = rows // CHUNKS

    def rows_of(c):
        return pl.ds(pl.multiple_of(c * blk, blk), blk)

    def load(k, c):
        src, dst = ((gx, gx_v), (mid, mid_v), (ct, ct_v), (fo, fo_v))[k]
        return pltpu.make_async_copy(src.at[rows_of(c)], dst.at[rows_of(c)], lsem.at[k, c])

    def store(k, c):
        src, dst = ((gm_v, gm), (out_v, out))[k]
        return pltpu.make_async_copy(src.at[rows_of(c)], dst.at[rows_of(c)], osem.at[k, c])

    for c in range(CHUNKS):
        for k in range(4):
            load(k, c).start()
    peer = partner_barrier()

    def core_copy(n, c):
        src, dst = ((gx, gx_in), (fo, fo_in))[n]
        return send_rows(src, dst, rows_of(c), ssem.at[n * CHUNKS + c], rsem.at[n * CHUNKS + c], peer)

    for n in range(2):
        for c in range(CHUNKS):
            core_copy(n, c).start()
    gg_ref[...] = jnp.zeros_like(gg_ref)

    @pl.loop(0, CHUNKS)
    def _(c):
        r = rows_of(c)
        for k in range(3):
            load(k, c).wait()
        core_copy(0, c).wait_recv()
        grads = gx_v[r, :].astype(F32) + gx_in[r, :].astype(F32)
        back, gain_grad = norm_back(mid_v[r, :], gain_ref[...], grads)
        gg_ref[...] += gain_grad
        grad_mid = ct_v[r, :].astype(F32) + back
        gm_v[r, :] = grad_mid
        store(0, c).start()
        low = grad_mid.astype(BF)
        gb[r, :] = low
        do_ref[r, :] = dot_nt(low, w_ref[...]).astype(BF)

    @pl.loop(0, CHUNKS)
    def _(c):
        r = rows_of(c)
        load(3, c).wait()
        core_copy(1, c).wait_recv()
        out_v[r, :] = (mid_v[r, :] + (fo_v[r, :].astype(F32) + fo_in[r, :].astype(F32))).astype(BF)
        store(1, c).start()

    gw_ref[...] = dot_tn(at_ref[...], gb[...]).astype(BF)
    for c in range(CHUNKS):
        for k in range(2):
            core_copy(k, c).wait_send()
            store(k, c).wait()


def ffn_back_call(gx, fo, mid, ct, gain, w, at):
    rows, dim = mid.shape
    width = w.shape[0]
    any_spec = pl.BlockSpec(memory_space=pl.ANY)
    low = pltpu.VMEM((rows, dim), BF)
    wide = pltpu.VMEM((rows, dim), F32)
    dma = pltpu.SemaphoreType.DMA
    do, gw, gg, out, gm = pl.pallas_call(
        ffn_back_body,
        out_shape=[
            jax.ShapeDtypeStruct((rows, width), BF),
            jax.ShapeDtypeStruct((width, dim), BF),
            jax.ShapeDtypeStruct((1, dim), F32),
            jax.ShapeDtypeStruct((rows, dim), BF),
            jax.ShapeDtypeStruct((rows, dim), F32),
        ],
        in_specs=[whole_spec()] * 3 + [any_spec] * 4,
        out_specs=[whole_spec()] * 3 + [any_spec] * 2,
        scratch_shapes=[
            low, low, low, low, wide, low, wide, low, low,
            dma((2 * CHUNKS,)), dma((2 * CHUNKS,)), dma((4, CHUNKS)), dma((2, CHUNKS)),
        ],
        compiler_params=pltpu.CompilerParams(collective_id=2, has_side_effects=True, vmem_limit_bytes=VMEM_LIMIT),
        name="ffn_back",
    )(gain, w, at, gx, fo, mid, ct)
    return out, gm, do, gw, gg


def peers_of(dp):
    z = dp // 4
    y = (dp // 2) % 2
    x = dp % 2
    at = lambda zz, yy, xx: zz * 4 + yy * 2 + xx
    return z, y, x, at(z, y, 1 - x), at(z, 1 - y, x), at(z + 1 - 2 * (z % 2), y, x), at(3 - z, y, x)


def sum_body(
    gk, rg, uk, ru, late_x, late_y, dk, rd, go, dqkv, w3, xn, xin, gmid, gain_ref, gain2_ref, bias_ref, out_a, out_b, ig, small_out,
    L, S, Z, R, Y, DL, DS, DA, G, sb, st, dl, wb, xb, mine_rows, their_rows, away_rows, xc, gc, ic,
    loc, s1s, s1r, sends, zr, rr, yr, ar, xr, lo, ss, sr, ld, cs, cr, xg, io, s2s, s2r, gs, gr,
):
    dp = lax.axis_index("dp")
    t = lax.axis_index("tensor")
    z, y, x, px, py, zn, mm = peers_of(dp)
    is_mid = (z == 1) | (z == 2)
    is_end = (z == 0) | (z == 3)
    mine = jnp.where(z == 2, WIDE // 2, 0)
    others = WIDE // 2 - mine
    n = KEPT_ROWS // ROWS
    cut_at = 2 * HALF_ROWS // ROWS
    tail_at = (2 * HALF_ROWS + QUARTER_ROWS) // ROWS
    starts = (0, HALF_ROWS // ROWS, cut_at, tail_at)
    first = (px, py)
    last = (py, px)
    outs = (out_a, out_b)
    owner = (x, y)
    bit = (y, x)
    F = S

    def remote(src, dst, ssem, rsem, peer, core=t):
        return pltpu.make_async_remote_copy(
            src_ref=src, dst_ref=dst, send_sem=ssem, recv_sem=rsem, device_id=(peer, core), device_id_type=MESH
        )

    def loads(g, b):
        rows = pl.ds(b * HALF_ROWS, HALF_ROWS)
        near = (rg, ru)[g]
        late = (late_x, late_y)[g]
        top = pl.ds(0, HALF_ROWS)
        if b < 2:
            copies = [((gk, uk)[g].at[b], L.at[g, rows])]
        else:
            copies = [(dk.at[g], DL.at[g])]
        if b == 0:
            copies.append((near.at[:, pl.ds(0, WIDE)], S.at[g, rows]))
        elif b == 1:
            cut = near.shape[1] - WIDE
            if cut:
                copies.append((near.at[:, pl.ds(WIDE, cut)], S.at[g, rows, pl.ds(0, cut)]))
            copies.append((late.at[top], S.at[g, rows, pl.ds(cut, WIDE - cut)]))
        else:
            cut = rd.shape[1]
            copies.append((rd.at[g], DS.at[g, pl.ds(0, cut)]))
            copies.append((late.at[pl.ds(HALF_ROWS, HALF_ROWS - cut)], DS.at[g, pl.ds(cut, HALF_ROWS - cut)]))
        return [pltpu.make_async_copy(src, dst, loc.at[g, b, k]) for k, (src, dst) in enumerate(copies)]

    own_loads = [pltpu.make_async_copy(src, dst, ld.at[k]) for k, (src, dst) in enumerate(((dqkv, dl), (w3, wb), (xn, xb)))]
    for b in range(3):
        for g in range(2):
            for copy in loads(g, b):
                copy.start()
    for copy in own_loads:
        copy.start()

    tail = pl.ds(2 * HALF_ROWS + QUARTER_ROWS, HALF_ROWS)

    def out_load(kept):
        return pltpu.make_async_copy(go, L.at[1, tail] if kept else away_rows.at[1], loc.at[1, 3, 0])

    def out_load_do(act):
        @pl.when(y == 1)
        def _():
            act(out_load(True))

        @pl.when(y == 0)
        def _():
            act(out_load(False))

    out_load_do(lambda copy: copy.start())

    barrier = pltpu.get_barrier_semaphore()
    others_z = [lax.rem(z + k, 4) * 4 + y * 2 + x for k in range(1, 4)]
    for peer in [px, py] + others_z:
        pl.semaphore_signal(barrier, inc=1, device_id=(peer, t), device_id_type=MESH)
    pl.semaphore_signal(barrier, inc=1, device_id=(dp, 1 - t), device_id_type=MESH)
    pl.semaphore_wait(barrier, 6)

    def first_exchange(g):
        return remote(away_rows.at[g], S.at[g, tail], s1s.at[g], s1r.at[g], first[g])

    def first_part(g, c):
        at = pl.multiple_of(c * SWAP_ROWS, SWAP_ROWS)
        dst = S.at[g, pl.ds(2 * HALF_ROWS + QUARTER_ROWS + at, SWAP_ROWS)]
        return remote(away_rows.at[g, pl.ds(at, SWAP_ROWS)], dst, s1s.at[g], s1r.at[g], first[g])

    quarter = pl.ds(2 * HALF_ROWS, QUARTER_ROWS)

    def second_exchange(g):
        return remote(DA.at[g], S.at[g, quarter], s2s.at[g], s2r.at[g], last[g])

    def second_part(g, c):
        at = pl.multiple_of(c * SWAP_ROWS, SWAP_ROWS)
        rows = pl.ds(at, SWAP_ROWS)
        dst = S.at[g, pl.ds(2 * HALF_ROWS + at, SWAP_ROWS)]
        return remote(DA.at[g, rows], dst, s2s.at[g], s2r.at[g], last[g])

    def down_quarter(half):
        return pl.ds(pl.multiple_of(half * QUARTER_ROWS, QUARTER_ROWS), QUARTER_ROWS)

    def piece_down(g):
        for copy in loads(g, 2):
            copy.wait()
        keep = down_quarter(bit[g])
        away = down_quarter(1 - bit[g])
        L[g, quarter, :] = (DL[g, keep, :].astype(F32) + DS[g, keep, :].astype(F32)).astype(BF)
        DA[g] = (DL[g, away, :].astype(F32) + DS[g, away, :].astype(F32)).astype(BF)

    def piece_swap(c):
        for g in range(2):
            first_part(g, c).start()

    def piece_second(c):
        for g in range(2):
            second_part(g, c).start()

    small_x = remote(st.at[2], sb.at[0], ss.at[0], sr.at[0], px)
    small_y = remote(st.at[0], sb.at[1], ss.at[1], sr.at[1], py)
    small_z = [remote(st.at[1], sb.at[2 + z], ss.at[2 + k], sr.at[2 + z], others_z[k]) for k in range(3)]

    def rows_of(i):
        return pl.ds(pl.multiple_of(i * ROWS, ROWS), ROWS)

    def cols_of(at):
        return pl.ds(pl.multiple_of(at, WIDE // 2), WIDE // 2)

    def z_copy(g, i):
        return remote(L.at[g, rows_of(i)], Z.at[g, rows_of(i)], sends.at[g, 0], zr.at[g, i], zn)

    def r_copy(g, i):
        return remote(L.at[g, rows_of(i), cols_of(others)], R.at[g, rows_of(i)], sends.at[g, 1], rr.at[g, i], mm)

    def y_copy(g, i):
        return remote(R.at[g, rows_of(i)], Y.at[g, rows_of(i)], sends.at[g, 2], yr.at[g, i], last[g])

    def a_copy(g, i, at):
        return remote(F.at[g, rows_of(i), cols_of(at)], F.at[g, rows_of(i), cols_of(at)], sends.at[g, 3], ar.at[g, i], mm)

    def o_copy(g, i):
        return remote(F.at[g, rows_of(i)], F.at[g, rows_of(i)], sends.at[g, 4], zr.at[g, i], zn)

    def out_rows(g, i):
        shift = jnp.where(i < cut_at, 0, jnp.where(i < tail_at, bit[g] * QUARTER_ROWS, QUARTER_ROWS))
        return pl.ds(pl.multiple_of(i * ROWS + shift, ROWS), ROWS)

    def x_copy(g, i):
        return remote(F.at[g, rows_of(i)], outs[g].at[owner[g], out_rows(g, i)], sends.at[g, 5], xr.at[g], first[g])

    def l_copy(g, i):
        return pltpu.make_async_copy(F.at[g, rows_of(i)], outs[g].at[owner[g], out_rows(g, i)], lo.at[g])

    def quarter_rows(i):
        return pl.ds(pl.multiple_of((i - cut_at) * ROWS, ROWS), ROWS)

    def g_copy(g, i):
        return remote(F.at[g, rows_of(i)], G.at[g, quarter_rows(i)], gs.at[g], gr.at[g, i - cut_at], last[g])

    def pass_on(g, i):
        rows = pl.ds(pl.multiple_of(i * ROWS + (1 - bit[g]) * QUARTER_ROWS, ROWS), ROWS)
        src = G.at[g, quarter_rows(i)]
        g_copy(g, i).wait_recv()
        remote(src, outs[g].at[owner[g], rows], sends.at[g, 5], xr.at[g], first[g]).start()
        pltpu.make_async_copy(src, outs[g].at[owner[g], rows], lo.at[g]).start()

    def is_cut(i):
        return (i >= cut_at) & (i < tail_at)

    def finish(g, i):
        x_copy(g, i).start()
        l_copy(g, i).start()

        @pl.when(is_cut(i))
        def _():
            g_copy(g, i).start()

    def end_in(g, j):
        r = rows_of(j)
        L[g, r, :] = (L[g, r, :].astype(F32) + S[g, r, :].astype(F32)).astype(BF)
        z_copy(g, j).start()

    def end_out(g, j):
        o_copy(g, j).wait_recv()
        finish(g, j)

    def mid_out(g, j):
        a_copy(g, j, others).wait_recv()
        o_copy(g, j).start()
        finish(g, j)

    def mid_join(g, j):
        @pl.when(jnp.logical_not(is_cut(j)))
        def _():
            y_copy(g, j).wait_recv()
            r = rows_of(j)
            F[g, r, cols_of(mine)] = (R[g, r, :].astype(F32) + Y[g, r, :].astype(F32)).astype(BF)
            a_copy(g, j, mine).start()

    def mid_half(g, j):
        r_copy(g, j).wait_recv()
        r = rows_of(j)
        total = (R[g, r, :].astype(F32) + L[g, r, cols_of(mine)].astype(F32)).astype(BF)

        @pl.when(is_cut(j))
        def _():
            F[g, r, cols_of(mine)] = total
            a_copy(g, j, mine).start()

        @pl.when(jnp.logical_not(is_cut(j)))
        def _():
            R[g, r, :] = total
            y_copy(g, j).start()

    def mid_in(g, j):
        z_copy(g, j).wait_recv()
        r = rows_of(j)
        L[g, r, :] = (L[g, r, :].astype(F32) + S[g, r, :].astype(F32) + Z[g, r, :].astype(F32)).astype(BF)
        r_copy(g, j).start()

    def stage(act, g, j):
        @pl.when((j >= 0) & (j < n))
        def _():
            act(g, j)

    seq = xin.shape[0]
    blk = seq // CHUNKS
    width = dl.shape[2]

    def piece_rows(c):
        return pl.ds(pl.multiple_of(c * blk, blk), blk)

    def core_copy(c):
        return remote(mine_rows.at[piece_rows(c)], their_rows.at[piece_rows(c)], cs.at[c], cr.at[c], dp, 1 - t)

    def norm_loads(c):
        return [
            pltpu.make_async_copy(xin.at[piece_rows(c)], xc.at[lax.rem(c, 2)], xg.at[lax.rem(c, 2), 0]),
            pltpu.make_async_copy(gmid.at[piece_rows(c)], gc.at[lax.rem(c, 2)], xg.at[lax.rem(c, 2), 1]),
        ]

    def ig_copy(c):
        return pltpu.make_async_copy(ic.at[lax.rem(c, 2)], ig.at[piece_rows(c)], io.at[lax.rem(c, 2)])

    def piece_start():
        for copy in own_loads:
            copy.wait()

    def piece_part(c):
        r = piece_rows(c)
        total = dot_nt(dl[0, r, :], wb[0]) + dot_nt(dl[1, r, :], wb[1]) + dot_nt(dl[2, r, :], wb[2])
        mine_rows[r, :] = total.astype(BF)
        core_copy(c).start()

    def row_half(half):
        return pl.ds(pl.multiple_of(half * HALF_ROWS, HALF_ROWS), HALF_ROWS)

    def piece_qk(k):
        cols = pl.ds(pl.multiple_of(k * width, width), width)
        L[0, tail, cols] = dot_tn(xb[:, row_half(x)], dl[k]).astype(BF)
        away_rows[0, :, cols] = dot_tn(xb[:, row_half(1 - x)], dl[k]).astype(BF)

    def piece_v():
        for k in range(2):
            cols = pl.ds(k * width, width)
            grad = dot_tn(xb[:, k * HALF_ROWS : (k + 1) * HALF_ROWS], dl[2]).astype(BF)

            @pl.when(y == 0)
            def _():
                L[1, tail, cols] = grad

            @pl.when(y == 1)
            def _():
                away_rows[1, :, cols] = grad

    def piece_send():
        out_load_do(lambda copy: copy.wait())
        for copy in norm_loads(0):
            copy.start()
        st[2] = jnp.zeros((SMALL, WIDE), F32)
        st[2, 1:2, :] = gain2_ref[...]
        for p in range(bias_ref.shape[0]):
            sums = [jnp.sum(bias_ref[p, h, s], axis=0, keepdims=True) for h in range(2) for s in range(2)]
            st[2, 2 + p : 3 + p, :] = jnp.concatenate(sums, axis=1)

    def piece_norm(c):
        @pl.when(c + 1 < CHUNKS)
        def _():
            for copy in norm_loads(c + 1):
                copy.start()

        for copy in norm_loads(c):
            copy.wait()
        core_copy(c).wait_recv()

        @pl.when(c >= 2)
        def _():
            ig_copy(c - 2).wait()

        r = piece_rows(c)
        grads = mine_rows[r, :].astype(F32) + their_rows[r, :].astype(F32)
        s = lax.rem(c, 2)
        back, gain_grad = norm_back(xc[s].astype(F32), gain_ref[...], grads)
        st[2, 0:1, :] = st[2, 0:1, :] + gain_grad
        ic[s] = gc[s] + back
        ig_copy(c).start()

    def small_first():
        small_x.start()

    def small_second():
        small_x.wait_recv()
        st[0] = st[2] + sb[0]
        small_y.start()

    def small_third():
        small_y.wait_recv()
        st[1] = st[0] + sb[1]
        for copy in small_z:
            copy.start()

    pieces = [
        (1, 1, lambda c: piece_down(0)),
        (2, 1, lambda c: piece_down(1)),
        (3, QUARTER_ROWS // SWAP_ROWS, piece_second),
        (3, 1, lambda c: piece_start()),
        (4, CHUNKS, piece_part),
        (4 + CHUNKS, 2, piece_qk),
        (6 + CHUNKS, 1, lambda c: piece_v()),
        (7 + CHUNKS, 1, lambda c: piece_send()),
        (8 + CHUNKS, HALF_ROWS // SWAP_ROWS, piece_swap),
        (9 + CHUNKS, CHUNKS, piece_norm),
        (10 + 2 * CHUNKS, 1, lambda c: small_first()),
        (14 + 2 * CHUNKS, 1, lambda c: small_second()),
        (18 + 2 * CHUNKS, 1, lambda c: small_third()),
    ]

    def body(i, carry):
        for b in range(4):

            @pl.when(i == starts[b])
            def _():
                for g in range(2):
                    if b < 2:
                        for copy in loads(g, b):
                            copy.wait()
                    elif b == 2:
                        second_exchange(g).wait_recv()
                    else:
                        first_exchange(g).wait_recv()

        @pl.when(is_end)
        def _():
            for g in range(2):
                stage(end_in, g, i)
                stage(end_out, g, i - LAGS[4])

        @pl.when(is_mid)
        def _():
            for g in range(2):
                stage(mid_out, g, i - LAGS[3])
                stage(mid_join, g, i - LAGS[2])
                stage(mid_half, g, i - LAGS[1])
                stage(mid_in, g, i - LAGS[0])

        for g in range(2):
            j = i - LAGS[4] - 2

            @pl.when(is_cut(j))
            def _():
                pass_on(g, j)

        for begin, steps, piece in pieces:

            @pl.when((i >= begin) & (i < begin + steps))
            def _():
                piece(i - begin)

        return carry

    lax.fori_loop(0, n + LAGS[4], body, 0)

    for k in range(3):
        zz = lax.rem(z + k + 1, 4)
        remote(st.at[1], sb.at[2 + zz], ss.at[2 + k], sr.at[2 + zz], others_z[k]).wait_recv()
    sb[2 + z] = st[1]
    small_out[...] = (sb[2] + sb[3]) + (sb[4] + sb[5])

    small_x.wait_send()
    small_y.wait_send()
    for copy in small_z:
        copy.wait_send()
    for c in range(CHUNKS):
        core_copy(c).wait_send()
    for c in (CHUNKS - 2, CHUNKS - 1):
        ig_copy(c).wait()
    for g in range(2):
        first_exchange(g).wait_send()
        away = 1 - owner[g]

        @pl.when(is_end)
        def _():
            remote(L.at[g], Z.at[g], sends.at[g, 0], zr.at[g, 0], zn).wait_send()

        @pl.when(is_mid)
        def _():
            remote(R.at[g], Y.at[g], sends.at[g, 1], rr.at[g, 0], mm).wait_send()
            some = pl.ds(0, KEPT_ROWS - QUARTER_ROWS)
            remote(R.at[g, some], Y.at[g, some], sends.at[g, 2], yr.at[g, 0], last[g]).wait_send()
            remote(R.at[g], Y.at[g], sends.at[g, 3], ar.at[g, 0], mm).wait_send()
            remote(F.at[g], F.at[g], sends.at[g, 4], zr.at[g, 0], zn).wait_send()

        second_exchange(g).wait_send()
        remote(G.at[g], G.at[g], gs.at[g], gr.at[g, 0], last[g]).wait_send()
        whole = remote(outs[g].at[away], outs[g].at[away], sends.at[g, 5], xr.at[g], first[g])
        whole.wait_send()
        whole.wait_recv()
        pltpu.make_async_copy(outs[g].at[owner[g]], outs[g].at[owner[g]], lo.at[g]).wait()


def sum_call(gk, rg, uk, ru, late_x, late_y, dk, rd, go, dqkv, w3, xn, xin, gmid, gain, gain2, bias):
    any_spec = pl.BlockSpec(memory_space=pl.ANY)
    n = KEPT_ROWS // ROWS
    rows, dim = xin.shape
    blk = rows // CHUNKS
    full = pltpu.VMEM((2, KEPT_ROWS, WIDE), BF)
    half = pltpu.VMEM((2, KEPT_ROWS, WIDE // 2), BF)
    quarter = pltpu.VMEM((2, QUARTER_ROWS, WIDE), BF)
    down = pltpu.VMEM((2, HALF_ROWS, WIDE), BF)
    dma = pltpu.SemaphoreType.DMA
    return pl.pallas_call(
        sum_body,
        out_shape=[jax.ShapeDtypeStruct((2, GROUP_ROWS, WIDE), BF)] * 2
        + [jax.ShapeDtypeStruct((rows, dim), F32), jax.ShapeDtypeStruct((SMALL, WIDE), F32)],
        in_specs=[any_spec] * 14 + [whole_spec()] * 3,
        out_specs=[any_spec] * 3 + [whole_spec()],
        scratch_shapes=[
            full, full, full, half, half, down, down, quarter, quarter,
            pltpu.VMEM((6, SMALL, WIDE), F32),
            pltpu.VMEM((3, SMALL, WIDE), F32),
            pltpu.VMEM(dqkv.shape, BF),
            pltpu.VMEM(w3.shape, BF),
            pltpu.VMEM((rows, dim), BF),
            pltpu.VMEM((rows, dim), BF),
            pltpu.VMEM((rows, dim), BF),
            pltpu.VMEM((2, HALF_ROWS, WIDE), BF),
            pltpu.VMEM((2, blk, dim), BF),
            pltpu.VMEM((2, blk, dim), F32),
            pltpu.VMEM((2, blk, dim), F32),
            dma((2, 4, 8)), dma((2,)), dma((2,)), dma((2, 6)),
            dma((2, n)), dma((2, n)), dma((2, n)), dma((2, n)),
            dma((2,)), dma((2,)), dma((5,)), dma((6,)),
            dma((3,)), dma((CHUNKS,)), dma((CHUNKS,)), dma((2, 2)), dma((2,)),
            dma((2,)), dma((2,)), dma((2,)), dma((2, QUARTER_ROWS // ROWS)),
        ],
        compiler_params=pltpu.CompilerParams(collective_id=4, has_side_effects=True, vmem_limit_bytes=VMEM_LIMIT),
        name="grad_sum",
    )(gk, rg, uk, ru, late_x, late_y, dk, rd, go, dqkv, w3, xn, xin, gmid, gain, gain2, bias)


def tables(time_ids):
    half = HEAD // 2
    freqs = jnp.exp(jnp.arange(half, dtype=F32) * (-2.0 * math.log(10000.0) / HEAD))
    angles = freqs[:, None] * time_ids.astype(F32)[None, :]
    return jnp.cos(angles), jnp.sin(angles)


def mask_tables(segments, variates):
    lane = jnp.arange(LANES)[None, :]
    var_here = (lane % VAR_COLS == variates[:, None]) & (lane < 3 * VAR_COLS)
    seg_here = (lane - SEG_COL == segments[:, None]) & (lane >= SEG_COL) & (lane < ONE_COL)
    seg_cols = (lane >= SEG_COL) & (lane < ONE_COL)
    ones = (lane >= ONE_COL) & (lane < ONE_COL + 3)
    base = jnp.where(var_here, 1.0, 0.0)
    segq = jnp.where(seg_cols & ~seg_here, MASKED, 0.0)
    extk = jnp.where(var_here | seg_here | ones, 1.0, 0.0).astype(BF)
    return base, segq, extk


def fast_local(
    block_input, segments, variates, time_ids, attn_gain, w_qkv, head_bias, w_out, ffn_gain, w_gate_up, w_down, cotangent
):
    w3 = jnp.transpose(w_qkv, (1, 0, 2))
    cosine, sine = tables(time_ids)
    base, segq, extk = mask_tables(segments, variates)
    gain1 = attn_gain[None, :]
    gain2 = ffn_gain[None, :]
    xn, q, k, v, cosine, sine = qkv_call(block_input, gain1, w3, cosine, sine)
    attended, o32, extq = attn_fwd_call(q, k, v, base, segq, extk, head_bias)
    mid, xn2 = attn_out_call(block_input, attended, w_out, gain2)
    ffn_part, gx_part, gk, uk, rg, ru, dk, rd, late_x, late_y = ffn_call(xn2, cotangent, pair_rows(w_gate_up), w_down)
    late_x = lax.ppermute(late_x, "dp", [(d, d ^ 1) for d in range(16)])
    late_y = lax.ppermute(late_y, "dp", [(d, d ^ 2) for d in range(16)])
    block_output, grad_mid, do, g_out, g_gain2 = ffn_back_call(
        gx_part, ffn_part, mid, cotangent, gain2, w_out, attended
    )
    dqkv, g_bias = attn_bwd_call(q, k, v, do, o32, extq, extk, variates[None, :], cosine, sine)
    sum_a, sum_b, input_grad, small = sum_call(
        gk, rg, uk, ru, late_x, late_y, dk, rd, g_out, dqkv, w3, xn, block_input, grad_mid, gain1, g_gain2, g_bias
    )
    sum_a = sum_a.reshape(2, 4, HALF_ROWS, WIDE)
    sum_b = sum_b.reshape(2, 4, HALF_ROWS, WIDE)
    heads = head_bias.shape[1]
    g_gate_up, g_down, g_qkv, g_out, g_gain1, g_gain2, g_bias = widen_call(sum_a, sum_b, small, heads)
    return (
        block_output, input_grad, g_gain1[0], jnp.transpose(g_qkv, (1, 0, 2)), g_bias, g_out, g_gain2[0], g_gate_up, g_down,
    )


def rope_tables(time_ids, head_dim):
    half_dim = head_dim // 2
    freqs = jnp.exp(jnp.arange(half_dim, dtype=jnp.float32) * (-2.0 * math.log(10000.0) / head_dim))
    angles = time_ids.astype(jnp.float32)[:, None] * freqs[None, :]
    return (jnp.cos(angles)[:, None, :], jnp.sin(angles)[:, None, :])


def rotate(vectors, cosine, sine_part):
    half_dim = vectors.shape[-1] // 2
    first_half = vectors[..., :half_dim]
    second_half = vectors[..., half_dim:]
    return jnp.concatenate(
        [
            first_half * cosine - second_half * sine_part,
            second_half * cosine + first_half * sine_part,
        ],
        axis=-1,
    )


def rotate_back(grads, cosine, sine_part):
    half_dim = grads.shape[-1] // 2
    first_half = grads[..., :half_dim]
    second_half = grads[..., half_dim:]
    return jnp.concatenate(
        [
            first_half * cosine + second_half * sine_part,
            second_half * cosine - first_half * sine_part,
        ],
        axis=-1,
    )


def norm_rows(rows_now, gain):
    inverse = lax.rsqrt(jnp.mean(rows_now * rows_now, axis=-1, keepdims=True) + EPSILON)
    return (rows_now * inverse * gain, inverse)


def plain_norm_back(rows_now, inverse, gain, grads):
    scaled = grads * gain
    gain_grad = jnp.sum(grads * rows_now * inverse, axis=0)
    rows_grad = inverse * scaled - rows_now * (inverse * inverse * inverse) * jnp.mean(
        scaled * rows_now, axis=-1, keepdims=True
    )
    return (rows_grad, gain_grad)


def scores_of(queries, keys_rot, same_var, allowed, head_bias, score_scale):
    raw_scores = (
        jnp.einsum("sqhd,skhd->shqk", queries, keys_rot, preferred_element_type=jnp.float32)
        * score_scale
    )
    biased = raw_scores + jnp.where(
        same_var[:, None], head_bias[0][None, :, None, None], head_bias[1][None, :, None, None]
    )
    return jnp.where(allowed[:, None], biased, MASKED)


def plain_local(
    block_input,
    segments,
    variates,
    time_ids,
    attn_gain,
    w_qkv,
    head_bias,
    w_out,
    ffn_gain,
    w_gate_up,
    w_down,
    cotangent,
):
    row_count = block_input.shape[0]
    heads_here = head_bias.shape[1]
    head_dim = w_qkv.shape[2] // heads_here
    seq_count = row_count // LEN
    score_scale = head_dim ** (-0.5)
    input_rows = block_input.astype(jnp.float32)
    attn_normed, attn_inverse = norm_rows(input_rows, attn_gain)
    attn_normed_low = attn_normed.astype(jnp.bfloat16)
    projected = jnp.einsum(
        "td,dck->tck", attn_normed_low, w_qkv, preferred_element_type=jnp.float32
    )
    cosine, sine_part = rope_tables(time_ids, head_dim)
    head_shape = (row_count, heads_here, head_dim)
    seq_shape = (seq_count, LEN, heads_here, head_dim)
    queries = (
        rotate(projected[:, 0].reshape(head_shape), cosine, sine_part)
        .astype(jnp.bfloat16)
        .reshape(seq_shape)
    )
    keys_rot = (
        rotate(projected[:, 1].reshape(head_shape), cosine, sine_part)
        .astype(jnp.bfloat16)
        .reshape(seq_shape)
    )
    values = projected[:, 2].astype(jnp.bfloat16).reshape(seq_shape)
    seg_ids = segments.reshape(seq_count, LEN)
    var_ids = variates.reshape(seq_count, LEN)
    allowed = seg_ids[:, :, None] == seg_ids[:, None, :]
    same_var = var_ids[:, :, None] == var_ids[:, None, :]
    scores = scores_of(queries, keys_rot, same_var, allowed, head_bias, score_scale)
    row_max = jnp.max(scores, axis=-1, keepdims=True)
    exp_total = jnp.sum(jnp.exp(scores - row_max), axis=-1, keepdims=True)
    log_total = row_max + jnp.log(exp_total)
    probs_low = jnp.exp(scores - log_total).astype(jnp.bfloat16)
    attended = jnp.einsum("shqk,skhd->sqhd", probs_low, values, preferred_element_type=jnp.float32)
    attended = attended.reshape(row_count, heads_here * head_dim).astype(jnp.bfloat16)
    attn_branch = lax.psum(
        jnp.dot(attended, w_out, preferred_element_type=jnp.float32).astype(jnp.bfloat16), "tensor"
    ).astype(jnp.float32)
    mid_rows = input_rows + attn_branch
    ffn_normed, ffn_inverse = norm_rows(mid_rows, ffn_gain)
    ffn_normed_low = ffn_normed.astype(jnp.bfloat16)
    gate_up = jnp.einsum(
        "td,dcf->tcf", ffn_normed_low, w_gate_up, preferred_element_type=jnp.float32
    )
    gate_vals = gate_up[:, 0]
    up_vals = gate_up[:, 1]
    sigmoid_gate = jax.nn.sigmoid(gate_vals)
    silu_gate = gate_vals * sigmoid_gate
    hidden_low = (silu_gate * up_vals).astype(jnp.bfloat16)
    ffn_branch = lax.psum(
        jnp.dot(hidden_low, w_down, preferred_element_type=jnp.float32).astype(jnp.bfloat16),
        "tensor",
    ).astype(jnp.float32)
    block_output = (mid_rows + ffn_branch).astype(jnp.bfloat16)
    grad_down = jnp.einsum("tf,td->fd", hidden_low, cotangent, preferred_element_type=jnp.float32)
    grad_hidden = jnp.einsum("td,fd->tf", cotangent, w_down, preferred_element_type=jnp.float32)
    grad_gate = grad_hidden * up_vals * sigmoid_gate * (1.0 + gate_vals * (1.0 - sigmoid_gate))
    grad_up = grad_hidden * silu_gate
    grad_gate_up = jnp.stack([grad_gate, grad_up], axis=1).astype(jnp.bfloat16)
    grad_w_gate_up = jnp.einsum(
        "td,tcf->dcf", ffn_normed_low, grad_gate_up, preferred_element_type=jnp.float32
    )
    grad_ffn_normed = lax.psum(
        jnp.einsum(
            "tcf,dcf->td", grad_gate_up, w_gate_up, preferred_element_type=jnp.float32
        ).astype(jnp.bfloat16),
        "tensor",
    ).astype(jnp.float32)
    norm_grad_mid, grad_ffn_gain = plain_norm_back(mid_rows, ffn_inverse, ffn_gain, grad_ffn_normed)
    grad_mid = cotangent.astype(jnp.float32) + norm_grad_mid
    grad_branch = grad_mid.astype(jnp.bfloat16)
    grad_w_out = jnp.einsum("tk,td->kd", attended, grad_branch, preferred_element_type=jnp.float32)
    grad_attended = jnp.einsum("td,kd->tk", grad_branch, w_out, preferred_element_type=jnp.float32)
    grad_attended = grad_attended.astype(jnp.bfloat16).reshape(seq_shape)
    scores_again = scores_of(queries, keys_rot, same_var, allowed, head_bias, score_scale)
    probs_again = jnp.exp(scores_again - log_total)
    probs_again_low = probs_again.astype(jnp.bfloat16)
    grad_probs = jnp.einsum(
        "sqhd,skhd->shqk", grad_attended, values, preferred_element_type=jnp.float32
    )
    grad_values = jnp.einsum(
        "shqk,sqhd->skhd", probs_again_low, grad_attended, preferred_element_type=jnp.float32
    )
    grad_scores = probs_again * (
        grad_probs - jnp.sum(probs_again * grad_probs, axis=-1, keepdims=True)
    )
    grad_scores_low = grad_scores.astype(jnp.bfloat16)
    same_low = same_var.astype(jnp.bfloat16)
    other_low = jnp.logical_not(same_var).astype(jnp.bfloat16)
    grad_bias = jnp.stack(
        [
            jnp.einsum(
                "shqk,sqk->h", grad_scores_low, same_low, preferred_element_type=jnp.float32
            ),
            jnp.einsum(
                "shqk,sqk->h", grad_scores_low, other_low, preferred_element_type=jnp.float32
            ),
        ],
        axis=0,
    )
    grad_queries = (
        jnp.einsum("shqk,skhd->sqhd", grad_scores_low, keys_rot, preferred_element_type=jnp.float32)
        * score_scale
    )
    grad_keys = (
        jnp.einsum("shqk,sqhd->skhd", grad_scores_low, queries, preferred_element_type=jnp.float32)
        * score_scale
    )
    grad_query_lin = rotate_back(grad_queries.reshape(head_shape), cosine, sine_part).reshape(
        row_count, heads_here * head_dim
    )
    grad_key_lin = rotate_back(grad_keys.reshape(head_shape), cosine, sine_part).reshape(
        row_count, heads_here * head_dim
    )
    grad_value_lin = grad_values.reshape(row_count, heads_here * head_dim)
    grad_projected = jnp.stack([grad_query_lin, grad_key_lin, grad_value_lin], axis=1).astype(
        jnp.bfloat16
    )
    grad_w_qkv = jnp.einsum(
        "td,tck->dck", attn_normed_low, grad_projected, preferred_element_type=jnp.float32
    )
    grad_attn_normed = lax.psum(
        jnp.einsum("tck,dck->td", grad_projected, w_qkv, preferred_element_type=jnp.float32).astype(
            jnp.bfloat16
        ),
        "tensor",
    ).astype(jnp.float32)
    norm_grad_input, grad_attn_gain = plain_norm_back(
        input_rows, attn_inverse, attn_gain, grad_attn_normed
    )
    input_grad = grad_mid + norm_grad_input
    grad_attn_gain, grad_w_qkv, grad_bias, grad_w_out, grad_ffn_gain, grad_w_gate_up, grad_down = (
        lax.psum(
            (
                grad_attn_gain,
                grad_w_qkv,
                grad_bias,
                grad_w_out,
                grad_ffn_gain,
                grad_w_gate_up,
                grad_down,
            ),
            "dp",
        )
    )
    return (
        block_output,
        input_grad,
        grad_attn_gain,
        grad_w_qkv,
        grad_bias,
        grad_w_out,
        grad_ffn_gain,
        grad_w_gate_up,
        grad_down,
    )


def solution(mesh):
    placed = (
        P("dp", None), P("dp"), P("dp"), P("dp"), P(), P(None, None, "tensor"), P(None, "tensor"),
        P("tensor", None), P(), P(None, None, "tensor"), P("tensor", None), P("dp", None),
    )
    fast = (mesh.shape["dp"], mesh.shape["tensor"]) == (16, 2)
    return jax.shard_map(
        fast_local if fast else plain_local,
        mesh=mesh,
        in_specs=placed,
        out_specs=(
            P("dp", None), P("dp", None), P(), P(None, None, "tensor"), P(None, "tensor"), P("tensor", None), P(),
            P(None, None, "tensor"), P("tensor", None),
        ),
        check_vma=False,
    )
```

```python
import functools
import math

import jax
import jax.numpy as jnp
from jax import lax
from jax.experimental import pallas as pl
from jax.experimental.pallas import tpu as pltpu
from jax.sharding import PartitionSpec as P

LEN = 1024
EPSILON = 1e-05
MASKED = -1000000000.0
BF = jnp.bfloat16
F32 = jnp.float32
MESH = pl.DeviceIdType.MESH
VMEM_LIMIT = 60 * 1024 * 1024
LANES = 128
HEAD = 64
VAR_COLS = 4
SEG_COL = 12
ONE_COL = 20
ROWS = 32
LAGS = (2, 4, 6, 8, 10)
SWAP_ROWS = 32
HALF_ROWS = 512
QUARTER_ROWS = HALF_ROWS // 2
GROUP_ROWS = 4 * HALF_ROWS
KEPT_ROWS = GROUP_ROWS - QUARTER_ROWS
WIDE = 1024
SMALL = 8
QBLK = 256
FFN_ROWS = 512
FFN_COLS = 512


def dot_nn(a, b):
    return lax.dot_general(a, b, (((1,), (0,)), ((), ())), preferred_element_type=F32)


def dot_nt(a, b):
    return lax.dot_general(a, b, (((1,), (1,)), ((), ())), preferred_element_type=F32)


def dot_tn(a, b):
    return lax.dot_general(a, b, (((0,), (0,)), ((), ())), preferred_element_type=F32)


def whole_spec():
    return pl.BlockSpec(memory_space=pltpu.VMEM)


def split3(v):
    hi = v.astype(BF).astype(F32)
    mid = (v - hi).astype(BF).astype(F32)
    return hi, mid, v - hi - mid


def half_swap(u):
    lane = lax.broadcasted_iota(jnp.int32, u.shape, 1) % HEAD
    return jnp.where(lane < HEAD // 2, pltpu.roll(u, LANES - HEAD // 2, 1), pltpu.roll(u, HEAD // 2, 1))


def qkv_body(x_ref, gain_ref, w_ref, cos_ref, sin_ref, xn_ref, q_ref, k_ref, v_ref, cos_out, sin_out):
    x = x_ref[...].astype(F32)
    inv = lax.rsqrt(jnp.mean(x * x, axis=-1, keepdims=True) + EPSILON)
    xn = (x * inv * gain_ref[...]).astype(BF)
    xn_ref[...] = xn
    half = cos_ref[...].T
    cosine = jnp.concatenate([half] * 4, axis=1)
    half = sin_ref[...].T
    sine = jnp.concatenate([-half, half] * 2, axis=1)
    cos_out[...] = cosine
    sin_out[...] = sine
    for part, out, factor in ((0, q_ref, HEAD**-0.5), (1, k_ref, 1.0)):
        lin = dot_nn(xn, w_ref[part])
        for s in range(lin.shape[1] // LANES):
            u = lin[:, s * LANES : (s + 1) * LANES]
            rot = (u * cosine + half_swap(u) * sine).astype(BF)
            if factor != 1.0:
                rot = (rot.astype(F32) * factor).astype(BF)
            out[:, s * LANES : (s + 1) * LANES] = rot
    v_ref[...] = dot_nn(xn, w_ref[2]).astype(BF)


def qkv_call(x, gain, w, cosine, sine):
    rows, dim = x.shape
    width = w.shape[2]
    blk = min(256, rows)
    row = lambda cols: pl.BlockSpec((blk, cols), lambda i: (i, 0))
    return pl.pallas_call(
        qkv_body,
        grid=(rows // blk,),
        out_shape=[jax.ShapeDtypeStruct((rows, dim), BF)]
        + [jax.ShapeDtypeStruct((rows, width), BF)] * 3
        + [jax.ShapeDtypeStruct((rows, LANES), F32)] * 2,
        in_specs=[
            row(dim),
            pl.BlockSpec((1, dim), lambda i: (0, 0)),
            pl.BlockSpec(w.shape, lambda i: (0, 0, 0)),
            pl.BlockSpec((HEAD // 2, blk), lambda i: (0, i)),
            pl.BlockSpec((HEAD // 2, blk), lambda i: (0, i)),
        ],
        out_specs=[row(dim), row(width), row(width), row(width), row(LANES), row(LANES)],
        compiler_params=pltpu.CompilerParams(vmem_limit_bytes=VMEM_LIMIT),
        name="qkv",
    )(x, gain, w, cosine, sine)


def attn_fwd_body(
    q_ref, k_ref, v_ref, base_ref, segq_ref, extk_ref, bias_ref, o_ref, o32_ref, extq_ref
):
    rows = q_ref.shape[0]
    blk = 256
    lane = lax.broadcasted_iota(jnp.int32, (blk, LANES), 1)
    kind = lax.broadcasted_iota(jnp.int32, (1, LANES), 1) // VAR_COLS
    bias_rows = []
    for h in range(2):
        head = pl.program_id(0) * 2 + h
        hi, mid, low = split3(jnp.full((1, LANES), bias_ref[0, head] - bias_ref[1, head], F32))
        bias_rows.append(jnp.where(kind == 0, hi, jnp.where(kind == 1, mid, jnp.where(kind == 2, low, 0.0))))
    kx = jnp.concatenate([k_ref[...], extk_ref[...]], axis=1)
    ones = jnp.ones((rows, LANES), BF)
    vx = jnp.concatenate([v_ref[...], ones], axis=1)
    for i in range(rows // blk):
        sl = slice(i * blk, (i + 1) * blk)
        q = q_ref[sl, :].astype(F32)
        base = base_ref[sl, :]
        segq = segq_ref[sl, :]
        outs = []
        for h in range(2):
            ext = base * bias_rows[h] + segq
            mine = (lane >= HEAD) if h else (lane < HEAD)
            qx = jnp.concatenate([jnp.where(mine, q, 0.0), ext], axis=1).astype(BF)
            s = dot_nt(qx, kx)
            top = jnp.max(s, axis=-1, keepdims=True)
            p = jnp.exp(s - top).astype(BF)
            ox = dot_nn(p, vx)
            total = ox[:, LANES:]
            outs.append(ox[:, :LANES] / total)
            lse = top + jnp.log(total)
            hi, mid, low = split3(lse)
            ext = jnp.where(
                lane == ONE_COL, -hi, jnp.where(lane == ONE_COL + 1, -mid, jnp.where(lane == ONE_COL + 2, -low, ext))
            )
            extq_ref[0, h, sl, :] = ext.astype(BF)
        o = jnp.where(lane < HEAD, outs[0], outs[1])
        o32_ref[sl, :] = o
        o_ref[sl, :] = o.astype(BF)


def attn_fwd_call(q, k, v, base, segq, extk, head_bias):
    rows, width = q.shape
    pairs = width // LANES
    col = pl.BlockSpec((rows, LANES), lambda p: (0, p))
    full = pl.BlockSpec((rows, LANES), lambda p: (0, 0))
    return pl.pallas_call(
        attn_fwd_body,
        grid=(pairs,),
        out_shape=[
            jax.ShapeDtypeStruct((rows, width), BF),
            jax.ShapeDtypeStruct((rows, width), F32),
            jax.ShapeDtypeStruct((pairs, 2, rows, LANES), BF),
        ],
        in_specs=[
            col, col, col, full, full, full,
            pl.BlockSpec(memory_space=pltpu.SMEM),
        ],
        out_specs=[col, col, pl.BlockSpec((1, 2, rows, LANES), lambda p: (p, 0, 0, 0))],
        compiler_params=pltpu.CompilerParams(vmem_limit_bytes=VMEM_LIMIT),
        name="attn_fwd",
    )(q, k, v, base, segq, extk, head_bias)


def attn_bwd_body(
    q_ref, k_ref, v_ref, do_ref, o32_ref, extq_ref, extk_ref, var_ref, cos_ref, sin_ref, d_ref, gb_ref, dqt_ref
):
    rows = q_ref.shape[0]
    blk = 256
    lane = lax.broadcasted_iota(jnp.int32, (blk, LANES), 1)
    kinds = lax.broadcasted_iota(jnp.int32, (8, blk), 0)
    kx = jnp.concatenate([k_ref[...], extk_ref[...]], axis=1)
    kxt = kx.T
    lane_all = lax.broadcasted_iota(jnp.int32, (rows, LANES), 1)
    vx = jnp.concatenate([v_ref[...], jnp.where(lane_all < 3, 1.0, 0.0).astype(BF)], axis=1)
    dv = jnp.zeros((rows, LANES), F32)
    dk = jnp.zeros((rows, LANES), F32)
    for h in range(2):
        same = jnp.zeros((8, blk), F32)
        other = jnp.zeros((8, blk), F32)
        for i in range(rows // blk):
            sl = slice(i * blk, (i + 1) * blk)
            mine = (lane >= HEAD) if h else (lane < HEAD)
            q = jnp.where(mine, q_ref[sl, :].astype(F32), 0.0).astype(BF)
            do32 = jnp.where(mine, do_ref[sl, :].astype(F32), 0.0)
            do = do32.astype(BF)
            delta = jnp.sum(do32 * o32_ref[sl, :], axis=-1, keepdims=True)
            hi, mid, low = split3(delta)
            dext = jnp.where(lane == 0, -hi, jnp.where(lane == 1, -mid, jnp.where(lane == 2, -low, 0.0))).astype(BF)
            st = dot_nt(kx, jnp.concatenate([q, extq_ref[0, h, sl, :]], axis=1))
            pt = jnp.exp(st)
            dpt = dot_nt(vx, jnp.concatenate([do, dext], axis=1))
            dst = (pt * dpt).astype(BF)
            dv = dv + dot_nn(pt.astype(BF), do)
            dk = dk + dot_nn(dst, q)
            dqt = dot_nn(kxt, dst)
            dqt_ref[h * HEAD : (h + 1) * HEAD, sl] = dqt[h * HEAD : (h + 1) * HEAD, :]
            g = dqt[LANES : LANES + 8, :]
            match = kinds == var_ref[:, sl]
            same = same + jnp.where(match, g, 0.0)
            other = other + jnp.where(match | (kinds >= VAR_COLS), 0.0, g)
        gb_ref[0, h, 0] = same
        gb_ref[0, h, 1] = other
    cosine = cos_ref[...]
    sine = sin_ref[...]
    dq = dqt_ref[...].T * HEAD**-0.5
    d_ref[0] = (dq * cosine - half_swap(dq) * sine).astype(BF)
    d_ref[1] = (dk * cosine - half_swap(dk) * sine).astype(BF)
    d_ref[2] = dv.astype(BF)


def attn_bwd_call(q, k, v, do, o32, extq, extk, variates, cosine, sine):
    rows, width = q.shape
    pairs = width // LANES
    col = pl.BlockSpec((rows, LANES), lambda p: (0, p))
    full = pl.BlockSpec((rows, LANES), lambda p: (0, 0))
    blk = 256
    return pl.pallas_call(
        attn_bwd_body,
        grid=(pairs,),
        out_shape=[jax.ShapeDtypeStruct((3, rows, width), BF), jax.ShapeDtypeStruct((pairs, 2, 2, 8, blk), F32)],
        in_specs=[
            col, col, col, col, col,
            pl.BlockSpec((1, 2, rows, LANES), lambda p: (p, 0, 0, 0)),
            full,
            pl.BlockSpec((1, rows), lambda p: (0, 0)),
            full, full,
        ],
        out_specs=[pl.BlockSpec((3, rows, LANES), lambda p: (0, 0, p)), pl.BlockSpec((1, 2, 2, 8, blk), lambda p: (p, 0, 0, 0, 0))],
        scratch_shapes=[pltpu.VMEM((LANES, rows), F32)],
        compiler_params=pltpu.CompilerParams(vmem_limit_bytes=VMEM_LIMIT),
        name="attn_bwd",
    )(q, k, v, do, o32, extq, extk, variates, cosine, sine)


def partner_barrier():
    dp = lax.axis_index("dp")
    other = 1 - lax.axis_index("tensor")
    barrier = pltpu.get_barrier_semaphore()
    pl.semaphore_signal(barrier, inc=1, device_id=(dp, other), device_id_type=MESH)
    pl.semaphore_wait(barrier, 1)
    return (dp, other)


def send_rows(src, dst, sl, ssem, rsem, peer):
    return pltpu.make_async_remote_copy(
        src_ref=src.at[sl], dst_ref=dst.at[sl], send_sem=ssem, recv_sem=rsem, device_id=peer, device_id_type=MESH
    )


CHUNKS = 4


def attn_out_body(o_ref, w_ref, gain_ref, x, mid, xn, x_v, mid_v, xn_v, mine, theirs, ssem, rsem, lsem, osem):
    rows = x.shape[0]
    blk = rows // CHUNKS

    def rows_of(c):
        return pl.ds(pl.multiple_of(c * blk, blk), blk)

    def load(c):
        return pltpu.make_async_copy(x.at[rows_of(c)], x_v.at[rows_of(c)], lsem.at[c])

    def stores(c):
        return [
            pltpu.make_async_copy(mid_v.at[rows_of(c)], mid.at[rows_of(c)], osem.at[0, c]),
            pltpu.make_async_copy(xn_v.at[rows_of(c)], xn.at[rows_of(c)], osem.at[1, c]),
        ]

    for c in range(CHUNKS):
        load(c).start()
    peer = partner_barrier()

    def core_copy(c):
        return send_rows(mine, theirs, rows_of(c), ssem.at[c], rsem.at[c], peer)

    @pl.loop(0, CHUNKS)
    def _(c):
        mine[rows_of(c), :] = dot_nn(o_ref[rows_of(c), :], w_ref[...]).astype(BF)
        core_copy(c).start()

    @pl.loop(0, CHUNKS)
    def _(c):
        r = rows_of(c)
        load(c).wait()
        core_copy(c).wait_recv()
        total = x_v[r, :].astype(F32) + (mine[r, :].astype(F32) + theirs[r, :].astype(F32))
        inv = lax.rsqrt(jnp.mean(total * total, axis=-1, keepdims=True) + EPSILON)
        mid_v[r, :] = total
        xn_v[r, :] = (total * inv * gain_ref[...]).astype(BF)
        for copy in stores(c):
            copy.start()

    for c in range(CHUNKS):
        core_copy(c).wait_send()
        for copy in stores(c):
            copy.wait()


def attn_out_call(x, o, w, gain):
    rows, dim = x.shape
    any_spec = pl.BlockSpec(memory_space=pl.ANY)
    low = pltpu.VMEM((rows, dim), BF)
    dma = pltpu.SemaphoreType.DMA
    return pl.pallas_call(
        attn_out_body,
        out_shape=[jax.ShapeDtypeStruct((rows, dim), F32), jax.ShapeDtypeStruct((rows, dim), BF)],
        in_specs=[whole_spec()] * 3 + [any_spec],
        out_specs=[any_spec] * 2,
        scratch_shapes=[
            low, pltpu.VMEM((rows, dim), F32), low, low, low,
            dma((CHUNKS,)), dma((CHUNKS,)), dma((CHUNKS,)), dma((2, CHUNKS)),
        ],
        compiler_params=pltpu.CompilerParams(collective_id=1, has_side_effects=True, vmem_limit_bytes=VMEM_LIMIT),
        name="attn_out",
    )(o, w, gain, x)


LATE = 2
SLOTS = 2
PART = FFN_COLS // 4


def sent(copy):
    copy.wait_send() if copy.is_remote else copy.wait()


def grid_bits():
    dp = lax.axis_index("dp")
    return dp, dp % 2, (dp // 2) % 2, peers_of(dp)[3], peers_of(dp)[4]


def ffn_body(
    xn_ref, ct_ref, w0_ref, wn_ref, wd_ref,
    out_ref, gx_ref, gk_ref, uk_ref, rg, ru, dk, rd, late_x, late_y,
    acc_o, acc_g, hid, dg, du, xt, wgu, away_w, away_d, ws, wr, ds, dr,
):
    j = pl.program_id(0)
    t = lax.axis_index("tensor")
    dp, x, y, px, py = grid_bits()
    steps = pl.num_programs(0)
    rows = xn_ref.shape[0]
    blk = wd_ref.shape[0]
    per = WIDE // blk
    early = 2 * per - LATE
    slot = lax.rem(j, SLOTS)
    near = (px, py)
    bits = (x, y)
    arrays = ((rg, late_x), (ru, late_y))

    def remote(src, dst, ssem, rsem, peer):
        return pltpu.make_async_remote_copy(
            src_ref=src, dst_ref=dst, send_sem=ssem, recv_sem=rsem, device_id=(peer, t), device_id_type=MESH
        )

    def wide_early(k, at):
        cols = pl.ds(pl.multiple_of(lax.rem(at, per) * blk, blk), blk)
        s = lax.rem(at, SLOTS)
        return remote(away_w.at[k, s], arrays[k][0].at[:, cols], ws.at[k, s], wr.at[k], near[k])

    def wide_late(k, at):
        cols = pl.ds(pl.multiple_of((at - early) * blk, blk), blk)
        s = lax.rem(at, SLOTS)
        return pltpu.make_async_copy(away_w.at[k, s], arrays[k][1].at[pl.ds(0, HALF_ROWS), cols], ws.at[k, s])

    def wide_do(at, act):
        for k in range(2):

            @pl.when(at < early)
            def _():
                act(wide_early(k, at))

            @pl.when(at >= early)
            def _():
                act(wide_late(k, at))

    def down_rows(g, half):
        return pl.ds(pl.multiple_of(g * 2 * PART + half * PART, PART), PART)

    def down_keep(g, at):
        s = lax.rem(at, SLOTS)
        return pltpu.make_async_copy(
            away_d.at[s, down_rows(g, bits[g])], dk.at[g, pl.ds(pl.multiple_of(at * PART, PART), PART)], ds.at[g, s]
        )

    def down_send(g, at):
        s = lax.rem(at, SLOTS)
        rows_at = pl.ds(pl.multiple_of(at * PART, PART), PART)
        return remote(away_d.at[s, down_rows(g, 1 - bits[g])], rd.at[g, rows_at], ds.at[2 + g, s], dr.at[g], near[g])

    def down_late(g, at):
        s = lax.rem(at, SLOTS)
        rows_at = pl.ds(pl.multiple_of(HALF_ROWS + (at - early) * PART, PART), PART)
        return pltpu.make_async_copy(
            away_d.at[s, down_rows(g, 1 - bits[g])], arrays[g][1].at[rows_at], ds.at[2 + g, s]
        )

    def down_do(at, act):
        for g in range(2):
            act(down_keep(g, at))

            @pl.when(at < early)
            def _():
                act(down_send(g, at))

            @pl.when(at >= early)
            def _():
                act(down_late(g, at))

    def part_rows(src, to, r):
        turned = jnp.swapaxes(src[r].astype(F32), 0, 1)
        for k in range(8):
            s = k // 2
            wgu[to, k % 2, r, s * LANES : (s + 1) * LANES] = turned[k].astype(BF)

    @pl.when(j == 0)
    def _():
        barrier = pltpu.get_barrier_semaphore()
        for peer in near:
            pl.semaphore_signal(barrier, inc=1, device_id=(peer, t), device_id_type=MESH)
        pl.semaphore_wait(barrier, 2)
        acc_o[...] = jnp.zeros_like(acc_o)
        acc_g[...] = jnp.zeros_like(acc_g)
        xt[...] = xn_ref[...].T

        @pl.loop(0, rows // LANES)
        def _(c):
            part_rows(w0_ref, 0, pl.ds(pl.multiple_of(c * LANES, LANES), LANES))

    now = lax.rem(j, 2)
    wg = wgu[now, 0]
    wu = wgu[now, 1]
    wd = wd_ref[...]
    part_rows(wn_ref, 1 - now, slice(None))
    for i in range(rows // FFN_ROWS):
        sl = slice(i * FFN_ROWS, (i + 1) * FFN_ROWS)
        xn = xn_ref[sl, :]
        gate = dot_nn(xn, wg)
        up = dot_nn(xn, wu)
        gh = dot_nt(ct_ref[sl, :], wd)
        sig = jax.nn.sigmoid(gate)
        silu = gate * sig
        hidden = (silu * up).astype(BF)
        dgate = (gh * up * sig * (1.0 + gate * (1.0 - sig))).astype(BF)
        dup = (gh * silu).astype(BF)
        hid[sl, :] = hidden
        dg[sl, :] = dgate
        du[sl, :] = dup
        acc_o[sl, :] += dot_nn(hidden, wd)
        acc_g[sl, :] += dot_nt(dgate, wg) + dot_nt(dup, wu)

    @pl.when(j >= SLOTS)
    def _():
        wide_do(j - SLOTS, sent)
        down_do(j - SLOTS, sent)

    away_d[slot] = dot_tn(hid[...], ct_ref[...]).astype(BF)
    down_do(j, lambda copy: copy.start())
    for k, (part, keep, bit) in enumerate(((dg, gk_ref, x), (du, uk_ref, y))):
        rows_at = lambda half: pl.ds(pl.multiple_of(half * HALF_ROWS, HALF_ROWS), HALF_ROWS)
        away_w[k, slot] = dot_nn(xt[rows_at(1 - bit), :], part[...]).astype(BF)
        keep[0] = dot_nn(xt[rows_at(bit), :], part[...]).astype(BF)
    wide_do(j, lambda copy: copy.start())

    @pl.when(j == steps - 1)
    def _():
        out_ref[...] = acc_o[...].astype(BF)
        gx_ref[...] = acc_g[...].astype(BF)
        for back in range(SLOTS, 0, -1):
            wide_do(steps - back, sent)
            down_do(steps - back, sent)
        for k in range(2):
            part = arrays[k][0].at[:, pl.ds(0, early * blk)]
            remote(part, part, ws.at[k, 0], wr.at[k], near[k]).wait_recv()
        for g in range(2):
            part = rd.at[g, pl.ds(0, early * PART)]
            remote(part, part, ds.at[g, 0], dr.at[g], near[g]).wait_recv()


def ffn_call(xn, ct, w_pairs, wd):
    rows, dim = xn.shape
    hidden = wd.shape[0]
    blk = FFN_COLS
    per = WIDE // blk
    full = pl.BlockSpec((rows, dim), lambda j: (0, 0))
    steps = hidden // blk
    tiles = 2 * blk // LANES
    first_w = pl.BlockSpec((dim, tiles, LANES), lambda j: (0, 0, 0))
    next_w = pl.BlockSpec((dim, tiles, LANES), lambda j: (0, jnp.minimum(j + 1, steps - 1), 0))
    roww = pl.BlockSpec((blk, dim), lambda j: (j, 0))
    grad = pl.BlockSpec((1, HALF_ROWS, blk), lambda j: (j // per, 0, lax.rem(j, per)))
    any_spec = pl.BlockSpec(memory_space=pl.ANY)
    wide = jax.ShapeDtypeStruct((2, HALF_ROWS, dim), BF)
    early = hidden // blk - LATE
    come = jax.ShapeDtypeStruct((HALF_ROWS, early * blk), BF)
    late = jax.ShapeDtypeStruct((HALF_ROWS + LATE * PART, LATE * blk), BF)
    dma = pltpu.SemaphoreType.DMA
    return pl.pallas_call(
        ffn_body,
        grid=(hidden // blk,),
        in_specs=[full, full, first_w, next_w, roww],
        out_specs=[full, full, grad, grad] + [any_spec] * 6,
        out_shape=[jax.ShapeDtypeStruct((rows, dim), BF)] * 2
        + [wide, wide, come, come, wide, jax.ShapeDtypeStruct((2, early * PART, dim), BF), late, late],
        scratch_shapes=[pltpu.VMEM((rows, dim), F32)] * 2
        + [pltpu.VMEM((rows, blk), BF)] * 3
        + [
            pltpu.VMEM((dim, rows), BF),
            pltpu.VMEM((2, 2, dim, blk), BF),
            pltpu.VMEM((2, SLOTS, HALF_ROWS, blk), BF),
            pltpu.VMEM((SLOTS, blk, dim), BF),
            dma((2, SLOTS)), dma((2,)), dma((4, SLOTS)), dma((2,)),
        ],
        compiler_params=pltpu.CompilerParams(collective_id=5, has_side_effects=True, vmem_limit_bytes=VMEM_LIMIT),
        name="ffn",
    )(xn, ct, w_pairs, w_pairs, wd)


def pair_rows(w):
    dim, two, width = w.shape
    tiled = jnp.transpose(w.reshape(dim, two, width // LANES, LANES), (0, 2, 1, 3))
    return tiled.reshape(dim, two * width // LANES, LANES)


def widen_body(
    ga_ref, gb_ref, da_ref, db_ref, aa_ref, v_ref, o_ref, small_ref, rows_ref, ig_ref,
    gu_ref, down_ref, qkv_ref, out_ref, g1_ref, g2_ref, gbias_ref, rows_out, ig_out,
):
    tiles = WIDE // LANES
    for f in range(2):
        for q in range(tiles // 4):
            parts = []
            for k in range(8):
                s = q * 4 + k // 2
                parts.append((ga_ref, gb_ref)[k % 2][0, f, :, s * LANES : (s + 1) * LANES].astype(F32))
            at = (f * tiles + q * 4) * 2
            gu_ref[:, at : at + 8, :] = jnp.swapaxes(jnp.stack(parts), 0, 1)
    down_ref[:, 0, 0] = da_ref[0, 0].astype(F32).reshape(down_ref.shape[0], PART, WIDE)
    down_ref[:, 1, 0] = db_ref[0, 0].astype(F32).reshape(down_ref.shape[0], PART, WIDE)
    width = qkv_ref.shape[2]
    qkv_ref[0] = aa_ref[0, 0, :, :width].astype(F32)
    qkv_ref[1] = aa_ref[0, 0, :, width:].astype(F32)
    qkv_ref[2] = v_ref[0, 0].astype(F32)
    out_ref[...] = o_ref[0, 0].astype(F32)
    rows_out[...] = rows_ref[...]
    ig_out[...] = ig_ref[...]

    @pl.when(pl.program_id(0) == 0)
    def _():
        g1_ref[...] = small_ref[0:1, :]
        g2_ref[...] = small_ref[1:2, :]
        row = lax.broadcasted_iota(jnp.int32, gbias_ref.shape, 0)
        col = lax.broadcasted_iota(jnp.int32, gbias_ref.shape, 1)
        total = jnp.zeros(gbias_ref.shape, F32)
        for h in range(gbias_ref.shape[1]):
            for s in range(2):
                at = (h % 2 * 2 + s) * QBLK
                one = jnp.sum(small_ref[2 + h // 2 : 3 + h // 2, at : at + QBLK], axis=1, keepdims=True)
                total = jnp.where((row == s) & (col == h), one, total)
        gbias_ref[...] = total


def widen_call(a, b, small, heads, block_output, input_grad):
    blk = 256
    half = HALF_ROWS // blk
    tiles = 4 * WIDE // LANES
    width = WIDE // 2
    gate = pl.BlockSpec((1, 2, blk, WIDE), lambda i: (i // half, 0, lax.rem(i, half), 0))
    block = lambda n: pl.BlockSpec((1, 1, blk, WIDE), lambda i: (i // half, n, lax.rem(i, half), 0))
    fixed = lambda shape: pl.BlockSpec(shape, lambda i: (0, 0))
    rows = block_output.shape[0]
    steps = 2 * half
    share = pl.BlockSpec((rows // steps, WIDE), lambda i: (i, 0))
    gu, down, qkv, out, g1, g2, gbias, block_output, input_grad = pl.pallas_call(
        widen_body,
        grid=(2 * half,),
        out_shape=[
            jax.ShapeDtypeStruct((2 * HALF_ROWS, tiles, LANES), F32),
            jax.ShapeDtypeStruct((HALF_ROWS // PART, 2, 2, PART, WIDE), F32),
            jax.ShapeDtypeStruct((3, 2 * HALF_ROWS, width), F32),
            jax.ShapeDtypeStruct((HALF_ROWS, WIDE), F32),
            jax.ShapeDtypeStruct((1, WIDE), F32),
            jax.ShapeDtypeStruct((1, WIDE), F32),
            jax.ShapeDtypeStruct((2, heads), F32),
            jax.ShapeDtypeStruct(block_output.shape, BF),
            jax.ShapeDtypeStruct(input_grad.shape, F32),
        ],
        in_specs=[
            gate, gate, block(2), block(2), block(3),
            pl.BlockSpec((1, 1, blk, width), lambda i: (0, 3, lax.rem(i, half), i // half)),
            pl.BlockSpec((1, 1, blk // 2, WIDE), lambda i: (1, 3, i, 0)),
            fixed((SMALL, WIDE)),
            share,
            share,
        ],
        out_specs=[
            pl.BlockSpec((blk, tiles, LANES), lambda i: (i, 0, 0)),
            pl.BlockSpec((blk // PART, 2, 1, PART, WIDE), lambda i: (lax.rem(i, half), 0, i // half, 0, 0)),
            pl.BlockSpec((3, blk, width), lambda i: (0, i, 0)),
            pl.BlockSpec((blk // 2, WIDE), lambda i: (i, 0)),
            fixed((1, WIDE)),
            fixed((1, WIDE)),
            fixed((2, heads)),
            share,
            share,
        ],
        compiler_params=pltpu.CompilerParams(vmem_limit_bytes=VMEM_LIMIT),
        name="widen",
    )(a, b, a, b, a, b, b, small, block_output, input_grad)
    gu = jnp.transpose(gu.reshape(2 * HALF_ROWS, tiles // 2, 2, LANES), (0, 2, 1, 3)).reshape(2 * HALF_ROWS, 2, 2 * WIDE)
    return gu, down.reshape(4 * HALF_ROWS, WIDE), qkv, out, g1, g2, gbias, block_output, input_grad


def norm_back(rows_now, gain, grads):
    inv = lax.rsqrt(jnp.mean(rows_now * rows_now, axis=-1, keepdims=True) + EPSILON)
    scaled = grads * gain
    gain_grad = jnp.sum(grads * rows_now * inv, axis=0, keepdims=True)
    back = inv * scaled - rows_now * (inv * inv * inv) * jnp.mean(scaled * rows_now, axis=-1, keepdims=True)
    return back, gain_grad


def ffn_back_body(
    gain_ref, w_ref, at_ref, gx, fo, mid, ct,
    do_ref, gw_ref, gg_ref, out, gm,
    gx_in, fo_in, gx_v, fo_v, mid_v, ct_v, gm_v, out_v, gb, ssem, rsem, lsem, osem,
):
    rows = mid.shape[0]
    blk = rows // CHUNKS

    def rows_of(c):
        return pl.ds(pl.multiple_of(c * blk, blk), blk)

    def load(k, c):
        src, dst = ((gx, gx_v), (mid, mid_v), (ct, ct_v), (fo, fo_v))[k]
        return pltpu.make_async_copy(src.at[rows_of(c)], dst.at[rows_of(c)], lsem.at[k, c])

    def store(k, c):
        src, dst = ((gm_v, gm), (out_v, out))[k]
        return pltpu.make_async_copy(src.at[rows_of(c)], dst.at[rows_of(c)], osem.at[k, c])

    for c in range(CHUNKS):
        for k in range(4):
            load(k, c).start()
    peer = partner_barrier()

    def core_copy(n, c):
        src, dst = ((gx, gx_in), (fo, fo_in))[n]
        return send_rows(src, dst, rows_of(c), ssem.at[n * CHUNKS + c], rsem.at[n * CHUNKS + c], peer)

    for n in range(2):
        for c in range(CHUNKS):
            core_copy(n, c).start()
    gg_ref[...] = jnp.zeros_like(gg_ref)

    @pl.loop(0, CHUNKS)
    def _(c):
        r = rows_of(c)
        for k in range(3):
            load(k, c).wait()
        core_copy(0, c).wait_recv()
        grads = gx_v[r, :].astype(F32) + gx_in[r, :].astype(F32)
        back, gain_grad = norm_back(mid_v[r, :], gain_ref[...], grads)
        gg_ref[...] += gain_grad
        grad_mid = ct_v[r, :].astype(F32) + back
        gm_v[r, :] = grad_mid
        store(0, c).start()
        low = grad_mid.astype(BF)
        gb[r, :] = low
        do_ref[r, :] = dot_nt(low, w_ref[...]).astype(BF)

    @pl.loop(0, CHUNKS)
    def _(c):
        r = rows_of(c)
        load(3, c).wait()
        core_copy(1, c).wait_recv()
        out_v[r, :] = (mid_v[r, :] + (fo_v[r, :].astype(F32) + fo_in[r, :].astype(F32))).astype(BF)
        store(1, c).start()

    gw_ref[...] = dot_tn(at_ref[...], gb[...]).astype(BF)
    for c in range(CHUNKS):
        for k in range(2):
            core_copy(k, c).wait_send()
            store(k, c).wait()


def ffn_back_call(gx, fo, mid, ct, gain, w, at):
    rows, dim = mid.shape
    width = w.shape[0]
    any_spec = pl.BlockSpec(memory_space=pl.ANY)
    low = pltpu.VMEM((rows, dim), BF)
    wide = pltpu.VMEM((rows, dim), F32)
    dma = pltpu.SemaphoreType.DMA
    do, gw, gg, out, gm = pl.pallas_call(
        ffn_back_body,
        out_shape=[
            jax.ShapeDtypeStruct((rows, width), BF),
            jax.ShapeDtypeStruct((width, dim), BF),
            jax.ShapeDtypeStruct((1, dim), F32),
            jax.ShapeDtypeStruct((rows, dim), BF),
            jax.ShapeDtypeStruct((rows, dim), F32),
        ],
        in_specs=[whole_spec()] * 3 + [any_spec] * 4,
        out_specs=[whole_spec()] * 3 + [any_spec] * 2,
        scratch_shapes=[
            low, low, low, low, wide, low, wide, low, low,
            dma((2 * CHUNKS,)), dma((2 * CHUNKS,)), dma((4, CHUNKS)), dma((2, CHUNKS)),
        ],
        compiler_params=pltpu.CompilerParams(collective_id=2, has_side_effects=True, vmem_limit_bytes=VMEM_LIMIT),
        name="ffn_back",
    )(gain, w, at, gx, fo, mid, ct)
    return out, gm, do, gw, gg


def peers_of(dp):
    z = dp // 4
    y = (dp // 2) % 2
    x = dp % 2
    at = lambda zz, yy, xx: zz * 4 + yy * 2 + xx
    return z, y, x, at(z, y, 1 - x), at(z, 1 - y, x), at(z + 1 - 2 * (z % 2), y, x), at(3 - z, y, x)


def sum_body(
    gk, rg, uk, ru, late_x, late_y, dk, rd, go, dqkv, w3, xn, xin, gmid, gain_ref, gain2_ref, bias_ref, out_a, out_b, ig, small_out,
    L, S, Z, R, Y, DL, DS, DA, G, sb, st, dl, wb, xb, mine_rows, their_rows, away_rows, xc, gc, ic,
    loc, s1s, s1r, sends, zr, rr, yr, ar, xr, lo, ss, sr, ld, cs, cr, xg, io, s2s, s2r, gs, gr,
):
    dp = lax.axis_index("dp")
    t = lax.axis_index("tensor")
    z, y, x, px, py, zn, mm = peers_of(dp)
    is_mid = (z == 1) | (z == 2)
    is_end = (z == 0) | (z == 3)
    mine = jnp.where(z == 2, WIDE // 2, 0)
    others = WIDE // 2 - mine
    n = KEPT_ROWS // ROWS
    cut_at = 2 * HALF_ROWS // ROWS
    tail_at = (2 * HALF_ROWS + QUARTER_ROWS) // ROWS
    starts = (0, HALF_ROWS // ROWS, cut_at, tail_at)
    first = (px, py)
    last = (py, px)
    outs = (out_a, out_b)
    owner = (x, y)
    bit = (y, x)
    F = S

    def remote(src, dst, ssem, rsem, peer, core=t):
        return pltpu.make_async_remote_copy(
            src_ref=src, dst_ref=dst, send_sem=ssem, recv_sem=rsem, device_id=(peer, core), device_id_type=MESH
        )

    def loads(g, b):
        rows = pl.ds(b * HALF_ROWS, HALF_ROWS)
        near = (rg, ru)[g]
        late = (late_x, late_y)[g]
        top = pl.ds(0, HALF_ROWS)
        if b < 2:
            copies = [((gk, uk)[g].at[b], L.at[g, rows])]
        else:
            copies = [(dk.at[g], DL.at[g])]
        if b == 0:
            copies.append((near.at[:, pl.ds(0, WIDE)], S.at[g, rows]))
        elif b == 1:
            cut = near.shape[1] - WIDE
            if cut:
                copies.append((near.at[:, pl.ds(WIDE, cut)], S.at[g, rows, pl.ds(0, cut)]))
            copies.append((late.at[top], S.at[g, rows, pl.ds(cut, WIDE - cut)]))
        else:
            cut = rd.shape[1]
            copies.append((rd.at[g], DS.at[g, pl.ds(0, cut)]))
            copies.append((late.at[pl.ds(HALF_ROWS, HALF_ROWS - cut)], DS.at[g, pl.ds(cut, HALF_ROWS - cut)]))
        return [pltpu.make_async_copy(src, dst, loc.at[g, b, k]) for k, (src, dst) in enumerate(copies)]

    own_loads = [pltpu.make_async_copy(src, dst, ld.at[k]) for k, (src, dst) in enumerate(((dqkv, dl), (w3, wb), (xn, xb)))]
    for g in range(2):
        for copy in loads(g, 0):
            copy.start()

    tail = pl.ds(2 * HALF_ROWS + QUARTER_ROWS, HALF_ROWS)

    def out_load(kept):
        return pltpu.make_async_copy(go, L.at[1, tail] if kept else away_rows.at[1], loc.at[1, 3, 0])

    def out_load_do(act):
        @pl.when(y == 1)
        def _():
            act(out_load(True))

        @pl.when(y == 0)
        def _():
            act(out_load(False))

    barrier = pltpu.get_barrier_semaphore()
    others_z = [lax.rem(z + k, 4) * 4 + y * 2 + x for k in range(1, 4)]
    for peer in [px, py] + others_z:
        pl.semaphore_signal(barrier, inc=1, device_id=(peer, t), device_id_type=MESH)
    pl.semaphore_signal(barrier, inc=1, device_id=(dp, 1 - t), device_id_type=MESH)
    pl.semaphore_wait(barrier, 6)
    for b in (2, 1):
        for g in range(2):
            for copy in loads(g, b):
                copy.start()
    for copy in own_loads:
        copy.start()
    out_load_do(lambda copy: copy.start())

    def first_exchange(g):
        return remote(away_rows.at[g], S.at[g, tail], s1s.at[g], s1r.at[g], first[g])

    def first_part(g, c):
        at = pl.multiple_of(c * SWAP_ROWS, SWAP_ROWS)
        dst = S.at[g, pl.ds(2 * HALF_ROWS + QUARTER_ROWS + at, SWAP_ROWS)]
        return remote(away_rows.at[g, pl.ds(at, SWAP_ROWS)], dst, s1s.at[g], s1r.at[g], first[g])

    quarter = pl.ds(2 * HALF_ROWS, QUARTER_ROWS)

    def second_exchange(g):
        return remote(DA.at[g], S.at[g, quarter], s2s.at[g], s2r.at[g], last[g])

    def second_part(g, c):
        at = pl.multiple_of(c * SWAP_ROWS, SWAP_ROWS)
        rows = pl.ds(at, SWAP_ROWS)
        dst = S.at[g, pl.ds(2 * HALF_ROWS + at, SWAP_ROWS)]
        return remote(DA.at[g, rows], dst, s2s.at[g], s2r.at[g], last[g])

    def down_quarter(half):
        return pl.ds(pl.multiple_of(half * QUARTER_ROWS, QUARTER_ROWS), QUARTER_ROWS)

    def piece_down(g):
        for copy in loads(g, 2):
            copy.wait()
        keep = down_quarter(bit[g])
        away = down_quarter(1 - bit[g])
        L[g, quarter, :] = (DL[g, keep, :].astype(F32) + DS[g, keep, :].astype(F32)).astype(BF)
        DA[g] = (DL[g, away, :].astype(F32) + DS[g, away, :].astype(F32)).astype(BF)

    def piece_swap(c):
        for g in range(2):
            first_part(g, c).start()

    def piece_second(c):
        for g in range(2):
            second_part(g, c).start()

    small_x = remote(st.at[2], sb.at[0], ss.at[0], sr.at[0], px)
    small_y = remote(st.at[0], sb.at[1], ss.at[1], sr.at[1], py)
    small_z = [remote(st.at[1], sb.at[2 + z], ss.at[2 + k], sr.at[2 + z], others_z[k]) for k in range(3)]

    def rows_of(i):
        return pl.ds(pl.multiple_of(i * ROWS, ROWS), ROWS)

    def cols_of(at):
        return pl.ds(pl.multiple_of(at, WIDE // 2), WIDE // 2)

    def z_copy(g, i):
        return remote(L.at[g, rows_of(i)], Z.at[g, rows_of(i)], sends.at[g, 0], zr.at[g, i], zn)

    def r_copy(g, i):
        return remote(L.at[g, rows_of(i), cols_of(others)], R.at[g, rows_of(i)], sends.at[g, 1], rr.at[g, i], mm)

    def y_copy(g, i):
        return remote(R.at[g, rows_of(i)], Y.at[g, rows_of(i)], sends.at[g, 2], yr.at[g, i], last[g])

    def a_copy(g, i, at):
        return remote(F.at[g, rows_of(i), cols_of(at)], F.at[g, rows_of(i), cols_of(at)], sends.at[g, 3], ar.at[g, i], mm)

    def o_copy(g, i):
        return remote(F.at[g, rows_of(i)], F.at[g, rows_of(i)], sends.at[g, 4], zr.at[g, i], zn)

    def out_rows(g, i):
        shift = jnp.where(i < cut_at, 0, jnp.where(i < tail_at, bit[g] * QUARTER_ROWS, QUARTER_ROWS))
        return pl.ds(pl.multiple_of(i * ROWS + shift, ROWS), ROWS)

    def x_copy(g, i):
        return remote(F.at[g, rows_of(i)], outs[g].at[owner[g], out_rows(g, i)], sends.at[g, 5], xr.at[g], first[g])

    def l_copy(g, i):
        return pltpu.make_async_copy(F.at[g, rows_of(i)], outs[g].at[owner[g], out_rows(g, i)], lo.at[g])

    def quarter_rows(i):
        return pl.ds(pl.multiple_of((i - cut_at) * ROWS, ROWS), ROWS)

    def g_copy(g, i):
        return remote(F.at[g, rows_of(i)], G.at[g, quarter_rows(i)], gs.at[g], gr.at[g, i - cut_at], last[g])

    def pass_on(g, i):
        rows = pl.ds(pl.multiple_of(i * ROWS + (1 - bit[g]) * QUARTER_ROWS, ROWS), ROWS)
        src = G.at[g, quarter_rows(i)]
        g_copy(g, i).wait_recv()
        remote(src, outs[g].at[owner[g], rows], sends.at[g, 5], xr.at[g], first[g]).start()
        pltpu.make_async_copy(src, outs[g].at[owner[g], rows], lo.at[g]).start()

    def is_cut(i):
        return (i >= cut_at) & (i < tail_at)

    def finish(g, i):
        x_copy(g, i).start()
        l_copy(g, i).start()

        @pl.when(is_cut(i))
        def _():
            g_copy(g, i).start()

    def end_in(g, j):
        r = rows_of(j)
        L[g, r, :] = (L[g, r, :].astype(F32) + S[g, r, :].astype(F32)).astype(BF)
        z_copy(g, j).start()

    def end_out(g, j):
        o_copy(g, j).wait_recv()
        finish(g, j)

    def mid_out(g, j):
        a_copy(g, j, others).wait_recv()
        o_copy(g, j).start()
        finish(g, j)

    def mid_join(g, j):
        @pl.when(jnp.logical_not(is_cut(j)))
        def _():
            y_copy(g, j).wait_recv()
            r = rows_of(j)
            F[g, r, cols_of(mine)] = (R[g, r, :].astype(F32) + Y[g, r, :].astype(F32)).astype(BF)
            a_copy(g, j, mine).start()

    def mid_half(g, j):
        r_copy(g, j).wait_recv()
        r = rows_of(j)
        total = (R[g, r, :].astype(F32) + L[g, r, cols_of(mine)].astype(F32)).astype(BF)

        @pl.when(is_cut(j))
        def _():
            F[g, r, cols_of(mine)] = total
            a_copy(g, j, mine).start()

        @pl.when(jnp.logical_not(is_cut(j)))
        def _():
            R[g, r, :] = total
            y_copy(g, j).start()

    def mid_in(g, j):
        z_copy(g, j).wait_recv()
        r = rows_of(j)
        L[g, r, :] = (L[g, r, :].astype(F32) + S[g, r, :].astype(F32) + Z[g, r, :].astype(F32)).astype(BF)
        r_copy(g, j).start()

    def stage(act, g, j):
        @pl.when((j >= 0) & (j < n))
        def _():
            act(g, j)

    seq = xin.shape[0]
    blk = seq // CHUNKS
    width = dl.shape[2]

    def piece_rows(c):
        return pl.ds(pl.multiple_of(c * blk, blk), blk)

    def core_copy(c):
        return remote(mine_rows.at[piece_rows(c)], their_rows.at[piece_rows(c)], cs.at[c], cr.at[c], dp, 1 - t)

    def norm_loads(c):
        return [
            pltpu.make_async_copy(xin.at[piece_rows(c)], xc.at[lax.rem(c, 2)], xg.at[lax.rem(c, 2), 0]),
            pltpu.make_async_copy(gmid.at[piece_rows(c)], gc.at[lax.rem(c, 2)], xg.at[lax.rem(c, 2), 1]),
        ]

    def ig_copy(c):
        return pltpu.make_async_copy(ic.at[lax.rem(c, 2)], ig.at[piece_rows(c)], io.at[lax.rem(c, 2)])

    def piece_start():
        for copy in own_loads:
            copy.wait()

    def piece_part(c):
        r = piece_rows(c)
        total = dot_nt(dl[0, r, :], wb[0]) + dot_nt(dl[1, r, :], wb[1]) + dot_nt(dl[2, r, :], wb[2])
        mine_rows[r, :] = total.astype(BF)
        core_copy(c).start()

    def row_half(half):
        return pl.ds(pl.multiple_of(half * HALF_ROWS, HALF_ROWS), HALF_ROWS)

    def piece_qk(k):
        cols = pl.ds(pl.multiple_of(k * width, width), width)
        L[0, tail, cols] = dot_tn(xb[:, row_half(x)], dl[k]).astype(BF)
        away_rows[0, :, cols] = dot_tn(xb[:, row_half(1 - x)], dl[k]).astype(BF)

    def piece_v():
        for k in range(2):
            cols = pl.ds(k * width, width)
            grad = dot_tn(xb[:, k * HALF_ROWS : (k + 1) * HALF_ROWS], dl[2]).astype(BF)

            @pl.when(y == 0)
            def _():
                L[1, tail, cols] = grad

            @pl.when(y == 1)
            def _():
                away_rows[1, :, cols] = grad

    def piece_send():
        out_load_do(lambda copy: copy.wait())
        for copy in norm_loads(0):
            copy.start()
        st[2] = jnp.zeros((SMALL, WIDE), F32)
        st[2, 1:2, :] = gain2_ref[...]
        for p in range(bias_ref.shape[0]):
            sums = [jnp.sum(bias_ref[p, h, s], axis=0, keepdims=True) for h in range(2) for s in range(2)]
            st[2, 2 + p : 3 + p, :] = jnp.concatenate(sums, axis=1)

    def piece_norm(c):
        @pl.when(c + 1 < CHUNKS)
        def _():
            for copy in norm_loads(c + 1):
                copy.start()

        for copy in norm_loads(c):
            copy.wait()
        core_copy(c).wait_recv()

        @pl.when(c >= 2)
        def _():
            ig_copy(c - 2).wait()

        r = piece_rows(c)
        grads = mine_rows[r, :].astype(F32) + their_rows[r, :].astype(F32)
        s = lax.rem(c, 2)
        back, gain_grad = norm_back(xc[s].astype(F32), gain_ref[...], grads)
        st[2, 0:1, :] = st[2, 0:1, :] + gain_grad
        ic[s] = gc[s] + back
        ig_copy(c).start()

    def small_first():
        small_x.start()

    def small_second():
        small_x.wait_recv()
        st[0] = st[2] + sb[0]
        small_y.start()

    def small_third():
        small_y.wait_recv()
        st[1] = st[0] + sb[1]
        for copy in small_z:
            copy.start()

    pieces = [
        (1, 1, lambda c: piece_down(0)),
        (2, 1, lambda c: piece_down(1)),
        (3, QUARTER_ROWS // SWAP_ROWS, piece_second),
        (3, 1, lambda c: piece_start()),
        (4, CHUNKS, piece_part),
        (4 + CHUNKS, 2, piece_qk),
        (6 + CHUNKS, 1, lambda c: piece_v()),
        (7 + CHUNKS, 1, lambda c: piece_send()),
        (8 + CHUNKS, HALF_ROWS // SWAP_ROWS, piece_swap),
        (9 + CHUNKS, CHUNKS, piece_norm),
        (10 + 2 * CHUNKS, 1, lambda c: small_first()),
        (14 + 2 * CHUNKS, 1, lambda c: small_second()),
        (18 + 2 * CHUNKS, 1, lambda c: small_third()),
    ]

    def body(i, carry):
        for b in range(4):

            @pl.when(i == starts[b])
            def _():
                for g in range(2):
                    if b < 2:
                        for copy in loads(g, b):
                            copy.wait()
                    elif b == 2:
                        second_exchange(g).wait_recv()
                    else:
                        first_exchange(g).wait_recv()

        @pl.when(is_end)
        def _():
            for g in range(2):
                stage(end_in, g, i)
                stage(end_out, g, i - LAGS[4])

        @pl.when(is_mid)
        def _():
            for g in range(2):
                stage(mid_out, g, i - LAGS[3])
                stage(mid_join, g, i - LAGS[2])
                stage(mid_half, g, i - LAGS[1])
                stage(mid_in, g, i - LAGS[0])

        for g in range(2):
            j = i - LAGS[4] - 2

            @pl.when(is_cut(j))
            def _():
                pass_on(g, j)

        for begin, steps, piece in pieces:

            @pl.when((i >= begin) & (i < begin + steps))
            def _():
                piece(i - begin)

        return carry

    lax.fori_loop(0, n + LAGS[4], body, 0)

    for k in range(3):
        zz = lax.rem(z + k + 1, 4)
        remote(st.at[1], sb.at[2 + zz], ss.at[2 + k], sr.at[2 + zz], others_z[k]).wait_recv()
    sb[2 + z] = st[1]
    small_out[...] = (sb[2] + sb[3]) + (sb[4] + sb[5])

    small_x.wait_send()
    small_y.wait_send()
    for copy in small_z:
        copy.wait_send()
    for c in range(CHUNKS):
        core_copy(c).wait_send()
    for c in (CHUNKS - 2, CHUNKS - 1):
        ig_copy(c).wait()
    for g in range(2):
        first_exchange(g).wait_send()
        away = 1 - owner[g]

        @pl.when(is_end)
        def _():
            remote(L.at[g], Z.at[g], sends.at[g, 0], zr.at[g, 0], zn).wait_send()

        @pl.when(is_mid)
        def _():
            remote(R.at[g], Y.at[g], sends.at[g, 1], rr.at[g, 0], mm).wait_send()
            some = pl.ds(0, KEPT_ROWS - QUARTER_ROWS)
            remote(R.at[g, some], Y.at[g, some], sends.at[g, 2], yr.at[g, 0], last[g]).wait_send()
            remote(R.at[g], Y.at[g], sends.at[g, 3], ar.at[g, 0], mm).wait_send()
            remote(F.at[g], F.at[g], sends.at[g, 4], zr.at[g, 0], zn).wait_send()

        second_exchange(g).wait_send()
        remote(G.at[g], G.at[g], gs.at[g], gr.at[g, 0], last[g]).wait_send()
        whole = remote(outs[g].at[away], outs[g].at[away], sends.at[g, 5], xr.at[g], first[g])
        whole.wait_send()
        whole.wait_recv()
        pltpu.make_async_copy(outs[g].at[owner[g]], outs[g].at[owner[g]], lo.at[g]).wait()


def sum_call(gk, rg, uk, ru, late_x, late_y, dk, rd, go, dqkv, w3, xn, xin, gmid, gain, gain2, bias):
    any_spec = pl.BlockSpec(memory_space=pl.ANY)
    n = KEPT_ROWS // ROWS
    rows, dim = xin.shape
    blk = rows // CHUNKS
    full = pltpu.VMEM((2, KEPT_ROWS, WIDE), BF)
    half = pltpu.VMEM((2, KEPT_ROWS, WIDE // 2), BF)
    quarter = pltpu.VMEM((2, QUARTER_ROWS, WIDE), BF)
    down = pltpu.VMEM((2, HALF_ROWS, WIDE), BF)
    dma = pltpu.SemaphoreType.DMA
    return pl.pallas_call(
        sum_body,
        out_shape=[jax.ShapeDtypeStruct((2, GROUP_ROWS, WIDE), BF)] * 2
        + [jax.ShapeDtypeStruct((rows, dim), F32), jax.ShapeDtypeStruct((SMALL, WIDE), F32)],
        in_specs=[any_spec] * 14 + [whole_spec()] * 3,
        out_specs=[any_spec] * 3 + [whole_spec()],
        scratch_shapes=[
            full, full, full, half, half, down, down, quarter, quarter,
            pltpu.VMEM((6, SMALL, WIDE), F32),
            pltpu.VMEM((3, SMALL, WIDE), F32),
            pltpu.VMEM(dqkv.shape, BF),
            pltpu.VMEM(w3.shape, BF),
            pltpu.VMEM((rows, dim), BF),
            pltpu.VMEM((rows, dim), BF),
            pltpu.VMEM((rows, dim), BF),
            pltpu.VMEM((2, HALF_ROWS, WIDE), BF),
            pltpu.VMEM((2, blk, dim), BF),
            pltpu.VMEM((2, blk, dim), F32),
            pltpu.VMEM((2, blk, dim), F32),
            dma((2, 4, 8)), dma((2,)), dma((2,)), dma((2, 6)),
            dma((2, n)), dma((2, n)), dma((2, n)), dma((2, n)),
            dma((2,)), dma((2,)), dma((5,)), dma((6,)),
            dma((3,)), dma((CHUNKS,)), dma((CHUNKS,)), dma((2, 2)), dma((2,)),
            dma((2,)), dma((2,)), dma((2,)), dma((2, QUARTER_ROWS // ROWS)),
        ],
        compiler_params=pltpu.CompilerParams(collective_id=4, has_side_effects=True, vmem_limit_bytes=VMEM_LIMIT),
        name="grad_sum",
    )(gk, rg, uk, ru, late_x, late_y, dk, rd, go, dqkv, w3, xn, xin, gmid, gain, gain2, bias)


def tables(time_ids):
    half = HEAD // 2
    freqs = jnp.exp(jnp.arange(half, dtype=F32) * (-2.0 * math.log(10000.0) / HEAD))
    angles = freqs[:, None] * time_ids.astype(F32)[None, :]
    return jnp.cos(angles), jnp.sin(angles)


def mask_tables(segments, variates):
    lane = jnp.arange(LANES)[None, :]
    var_here = (lane % VAR_COLS == variates[:, None]) & (lane < 3 * VAR_COLS)
    seg_here = (lane - SEG_COL == segments[:, None]) & (lane >= SEG_COL) & (lane < ONE_COL)
    seg_cols = (lane >= SEG_COL) & (lane < ONE_COL)
    ones = (lane >= ONE_COL) & (lane < ONE_COL + 3)
    base = jnp.where(var_here, 1.0, 0.0)
    segq = jnp.where(seg_cols & ~seg_here, MASKED, 0.0)
    extk = jnp.where(var_here | seg_here | ones, 1.0, 0.0).astype(BF)
    return base, segq, extk


def fast_local(
    block_input, segments, variates, time_ids, attn_gain, w_qkv, head_bias, w_out, ffn_gain, w_gate_up, w_down, cotangent
):
    w3 = jnp.transpose(w_qkv, (1, 0, 2))
    cosine, sine = tables(time_ids)
    base, segq, extk = mask_tables(segments, variates)
    gain1 = attn_gain[None, :]
    gain2 = ffn_gain[None, :]
    xn, q, k, v, cosine, sine = qkv_call(block_input, gain1, w3, cosine, sine)
    attended, o32, extq = attn_fwd_call(q, k, v, base, segq, extk, head_bias)
    mid, xn2 = attn_out_call(block_input, attended, w_out, gain2)
    ffn_part, gx_part, gk, uk, rg, ru, dk, rd, late_x, late_y = ffn_call(xn2, cotangent, pair_rows(w_gate_up), w_down)
    late_x = lax.ppermute(late_x, "dp", [(d, d ^ 1) for d in range(16)])
    late_y = lax.ppermute(late_y, "dp", [(d, d ^ 2) for d in range(16)])
    block_output, grad_mid, do, g_out, g_gain2 = ffn_back_call(
        gx_part, ffn_part, mid, cotangent, gain2, w_out, attended
    )
    dqkv, g_bias = attn_bwd_call(q, k, v, do, o32, extq, extk, variates[None, :], cosine, sine)
    sum_a, sum_b, input_grad, small = sum_call(
        gk, rg, uk, ru, late_x, late_y, dk, rd, g_out, dqkv, w3, xn, block_input, grad_mid, gain1, g_gain2, g_bias
    )
    sum_a = sum_a.reshape(2, 4, HALF_ROWS, WIDE)
    sum_b = sum_b.reshape(2, 4, HALF_ROWS, WIDE)
    heads = head_bias.shape[1]
    g_gate_up, g_down, g_qkv, g_out, g_gain1, g_gain2, g_bias, block_output, input_grad = widen_call(
        sum_a, sum_b, small, heads, block_output, input_grad
    )
    return (
        block_output, input_grad, g_gain1[0], jnp.transpose(g_qkv, (1, 0, 2)), g_bias, g_out, g_gain2[0], g_gate_up, g_down,
    )


def rope_tables(time_ids, head_dim):
    half_dim = head_dim // 2
    freqs = jnp.exp(jnp.arange(half_dim, dtype=jnp.float32) * (-2.0 * math.log(10000.0) / head_dim))
    angles = time_ids.astype(jnp.float32)[:, None] * freqs[None, :]
    return (jnp.cos(angles)[:, None, :], jnp.sin(angles)[:, None, :])


def rotate(vectors, cosine, sine_part):
    half_dim = vectors.shape[-1] // 2
    first_half = vectors[..., :half_dim]
    second_half = vectors[..., half_dim:]
    return jnp.concatenate(
        [
            first_half * cosine - second_half * sine_part,
            second_half * cosine + first_half * sine_part,
        ],
        axis=-1,
    )


def rotate_back(grads, cosine, sine_part):
    half_dim = grads.shape[-1] // 2
    first_half = grads[..., :half_dim]
    second_half = grads[..., half_dim:]
    return jnp.concatenate(
        [
            first_half * cosine + second_half * sine_part,
            second_half * cosine - first_half * sine_part,
        ],
        axis=-1,
    )


def norm_rows(rows_now, gain):
    inverse = lax.rsqrt(jnp.mean(rows_now * rows_now, axis=-1, keepdims=True) + EPSILON)
    return (rows_now * inverse * gain, inverse)


def plain_norm_back(rows_now, inverse, gain, grads):
    scaled = grads * gain
    gain_grad = jnp.sum(grads * rows_now * inverse, axis=0)
    rows_grad = inverse * scaled - rows_now * (inverse * inverse * inverse) * jnp.mean(
        scaled * rows_now, axis=-1, keepdims=True
    )
    return (rows_grad, gain_grad)


def scores_of(queries, keys_rot, same_var, allowed, head_bias, score_scale):
    raw_scores = (
        jnp.einsum("sqhd,skhd->shqk", queries, keys_rot, preferred_element_type=jnp.float32)
        * score_scale
    )
    biased = raw_scores + jnp.where(
        same_var[:, None], head_bias[0][None, :, None, None], head_bias[1][None, :, None, None]
    )
    return jnp.where(allowed[:, None], biased, MASKED)


def plain_local(
    block_input,
    segments,
    variates,
    time_ids,
    attn_gain,
    w_qkv,
    head_bias,
    w_out,
    ffn_gain,
    w_gate_up,
    w_down,
    cotangent,
):
    row_count = block_input.shape[0]
    heads_here = head_bias.shape[1]
    head_dim = w_qkv.shape[2] // heads_here
    seq_count = row_count // LEN
    score_scale = head_dim ** (-0.5)
    input_rows = block_input.astype(jnp.float32)
    attn_normed, attn_inverse = norm_rows(input_rows, attn_gain)
    attn_normed_low = attn_normed.astype(jnp.bfloat16)
    projected = jnp.einsum(
        "td,dck->tck", attn_normed_low, w_qkv, preferred_element_type=jnp.float32
    )
    cosine, sine_part = rope_tables(time_ids, head_dim)
    head_shape = (row_count, heads_here, head_dim)
    seq_shape = (seq_count, LEN, heads_here, head_dim)
    queries = (
        rotate(projected[:, 0].reshape(head_shape), cosine, sine_part)
        .astype(jnp.bfloat16)
        .reshape(seq_shape)
    )
    keys_rot = (
        rotate(projected[:, 1].reshape(head_shape), cosine, sine_part)
        .astype(jnp.bfloat16)
        .reshape(seq_shape)
    )
    values = projected[:, 2].astype(jnp.bfloat16).reshape(seq_shape)
    seg_ids = segments.reshape(seq_count, LEN)
    var_ids = variates.reshape(seq_count, LEN)
    allowed = seg_ids[:, :, None] == seg_ids[:, None, :]
    same_var = var_ids[:, :, None] == var_ids[:, None, :]
    scores = scores_of(queries, keys_rot, same_var, allowed, head_bias, score_scale)
    row_max = jnp.max(scores, axis=-1, keepdims=True)
    exp_total = jnp.sum(jnp.exp(scores - row_max), axis=-1, keepdims=True)
    log_total = row_max + jnp.log(exp_total)
    probs_low = jnp.exp(scores - log_total).astype(jnp.bfloat16)
    attended = jnp.einsum("shqk,skhd->sqhd", probs_low, values, preferred_element_type=jnp.float32)
    attended = attended.reshape(row_count, heads_here * head_dim).astype(jnp.bfloat16)
    attn_branch = lax.psum(
        jnp.dot(attended, w_out, preferred_element_type=jnp.float32).astype(jnp.bfloat16), "tensor"
    ).astype(jnp.float32)
    mid_rows = input_rows + attn_branch
    ffn_normed, ffn_inverse = norm_rows(mid_rows, ffn_gain)
    ffn_normed_low = ffn_normed.astype(jnp.bfloat16)
    gate_up = jnp.einsum(
        "td,dcf->tcf", ffn_normed_low, w_gate_up, preferred_element_type=jnp.float32
    )
    gate_vals = gate_up[:, 0]
    up_vals = gate_up[:, 1]
    sigmoid_gate = jax.nn.sigmoid(gate_vals)
    silu_gate = gate_vals * sigmoid_gate
    hidden_low = (silu_gate * up_vals).astype(jnp.bfloat16)
    ffn_branch = lax.psum(
        jnp.dot(hidden_low, w_down, preferred_element_type=jnp.float32).astype(jnp.bfloat16),
        "tensor",
    ).astype(jnp.float32)
    block_output = (mid_rows + ffn_branch).astype(jnp.bfloat16)
    grad_down = jnp.einsum("tf,td->fd", hidden_low, cotangent, preferred_element_type=jnp.float32)
    grad_hidden = jnp.einsum("td,fd->tf", cotangent, w_down, preferred_element_type=jnp.float32)
    grad_gate = grad_hidden * up_vals * sigmoid_gate * (1.0 + gate_vals * (1.0 - sigmoid_gate))
    grad_up = grad_hidden * silu_gate
    grad_gate_up = jnp.stack([grad_gate, grad_up], axis=1).astype(jnp.bfloat16)
    grad_w_gate_up = jnp.einsum(
        "td,tcf->dcf", ffn_normed_low, grad_gate_up, preferred_element_type=jnp.float32
    )
    grad_ffn_normed = lax.psum(
        jnp.einsum(
            "tcf,dcf->td", grad_gate_up, w_gate_up, preferred_element_type=jnp.float32
        ).astype(jnp.bfloat16),
        "tensor",
    ).astype(jnp.float32)
    norm_grad_mid, grad_ffn_gain = plain_norm_back(mid_rows, ffn_inverse, ffn_gain, grad_ffn_normed)
    grad_mid = cotangent.astype(jnp.float32) + norm_grad_mid
    grad_branch = grad_mid.astype(jnp.bfloat16)
    grad_w_out = jnp.einsum("tk,td->kd", attended, grad_branch, preferred_element_type=jnp.float32)
    grad_attended = jnp.einsum("td,kd->tk", grad_branch, w_out, preferred_element_type=jnp.float32)
    grad_attended = grad_attended.astype(jnp.bfloat16).reshape(seq_shape)
    scores_again = scores_of(queries, keys_rot, same_var, allowed, head_bias, score_scale)
    probs_again = jnp.exp(scores_again - log_total)
    probs_again_low = probs_again.astype(jnp.bfloat16)
    grad_probs = jnp.einsum(
        "sqhd,skhd->shqk", grad_attended, values, preferred_element_type=jnp.float32
    )
    grad_values = jnp.einsum(
        "shqk,sqhd->skhd", probs_again_low, grad_attended, preferred_element_type=jnp.float32
    )
    grad_scores = probs_again * (
        grad_probs - jnp.sum(probs_again * grad_probs, axis=-1, keepdims=True)
    )
    grad_scores_low = grad_scores.astype(jnp.bfloat16)
    same_low = same_var.astype(jnp.bfloat16)
    other_low = jnp.logical_not(same_var).astype(jnp.bfloat16)
    grad_bias = jnp.stack(
        [
            jnp.einsum(
                "shqk,sqk->h", grad_scores_low, same_low, preferred_element_type=jnp.float32
            ),
            jnp.einsum(
                "shqk,sqk->h", grad_scores_low, other_low, preferred_element_type=jnp.float32
            ),
        ],
        axis=0,
    )
    grad_queries = (
        jnp.einsum("shqk,skhd->sqhd", grad_scores_low, keys_rot, preferred_element_type=jnp.float32)
        * score_scale
    )
    grad_keys = (
        jnp.einsum("shqk,sqhd->skhd", grad_scores_low, queries, preferred_element_type=jnp.float32)
        * score_scale
    )
    grad_query_lin = rotate_back(grad_queries.reshape(head_shape), cosine, sine_part).reshape(
        row_count, heads_here * head_dim
    )
    grad_key_lin = rotate_back(grad_keys.reshape(head_shape), cosine, sine_part).reshape(
        row_count, heads_here * head_dim
    )
    grad_value_lin = grad_values.reshape(row_count, heads_here * head_dim)
    grad_projected = jnp.stack([grad_query_lin, grad_key_lin, grad_value_lin], axis=1).astype(
        jnp.bfloat16
    )
    grad_w_qkv = jnp.einsum(
        "td,tck->dck", attn_normed_low, grad_projected, preferred_element_type=jnp.float32
    )
    grad_attn_normed = lax.psum(
        jnp.einsum("tck,dck->td", grad_projected, w_qkv, preferred_element_type=jnp.float32).astype(
            jnp.bfloat16
        ),
        "tensor",
    ).astype(jnp.float32)
    norm_grad_input, grad_attn_gain = plain_norm_back(
        input_rows, attn_inverse, attn_gain, grad_attn_normed
    )
    input_grad = grad_mid + norm_grad_input
    grad_attn_gain, grad_w_qkv, grad_bias, grad_w_out, grad_ffn_gain, grad_w_gate_up, grad_down = (
        lax.psum(
            (
                grad_attn_gain,
                grad_w_qkv,
                grad_bias,
                grad_w_out,
                grad_ffn_gain,
                grad_w_gate_up,
                grad_down,
            ),
            "dp",
        )
    )
    return (
        block_output,
        input_grad,
        grad_attn_gain,
        grad_w_qkv,
        grad_bias,
        grad_w_out,
        grad_ffn_gain,
        grad_w_gate_up,
        grad_down,
    )


def solution(mesh):
    placed = (
        P("dp", None), P("dp"), P("dp"), P("dp"), P(), P(None, None, "tensor"), P(None, "tensor"),
        P("tensor", None), P(), P(None, None, "tensor"), P("tensor", None), P("dp", None),
    )
    fast = (mesh.shape["dp"], mesh.shape["tensor"]) == (16, 2)
    return jax.shard_map(
        fast_local if fast else plain_local,
        mesh=mesh,
        in_specs=placed,
        out_specs=(
            P("dp", None), P("dp", None), P(), P(None, None, "tensor"), P(None, "tensor"), P("tensor", None), P(),
            P(None, None, "tensor"), P("tensor", None),
        ),
        check_vma=False,
    )
```

```python
import functools
import math

import jax
import jax.numpy as jnp
from jax import lax
from jax.experimental import pallas as pl
from jax.experimental.pallas import tpu as pltpu
from jax.sharding import PartitionSpec as P

LEN = 1024
EPSILON = 1e-05
MASKED = -1000000000.0
BF = jnp.bfloat16
F32 = jnp.float32
MESH = pl.DeviceIdType.MESH
VMEM_LIMIT = 60 * 1024 * 1024
VMEM_MOST = 67043328 - 512 * 1024
LANES = 128
HEAD = 64
VAR_COLS = 4
SEG_COL = 12
ONE_COL = 20
ROWS = 32
LAGS = (2, 4, 6, 8, 10)
SWAP_ROWS = 32
HALF_ROWS = 512
QUARTER_ROWS = HALF_ROWS // 2
GROUP_ROWS = 4 * HALF_ROWS
KEPT_ROWS = GROUP_ROWS - QUARTER_ROWS
WIDE = 1024
SMALL = 8
QBLK = 256
FFN_ROWS = 512
FFN_COLS = 512


def dot_nn(a, b):
    return lax.dot_general(a, b, (((1,), (0,)), ((), ())), preferred_element_type=F32)


def dot_nt(a, b):
    return lax.dot_general(a, b, (((1,), (1,)), ((), ())), preferred_element_type=F32)


def dot_tn(a, b):
    return lax.dot_general(a, b, (((0,), (0,)), ((), ())), preferred_element_type=F32)


def whole_spec():
    return pl.BlockSpec(memory_space=pltpu.VMEM)


def split3(v):
    hi = v.astype(BF).astype(F32)
    mid = (v - hi).astype(BF).astype(F32)
    return hi, mid, v - hi - mid


def half_swap(u):
    lane = lax.broadcasted_iota(jnp.int32, u.shape, 1) % HEAD
    return jnp.where(lane < HEAD // 2, pltpu.roll(u, LANES - HEAD // 2, 1), pltpu.roll(u, HEAD // 2, 1))


def qkv_body(x_ref, gain_ref, w_ref, cos_ref, sin_ref, xn_ref, q_ref, k_ref, v_ref, cos_out, sin_out):
    x = x_ref[...].astype(F32)
    inv = lax.rsqrt(jnp.mean(x * x, axis=-1, keepdims=True) + EPSILON)
    xn = (x * inv * gain_ref[...]).astype(BF)
    xn_ref[...] = xn
    half = cos_ref[...].T
    cosine = jnp.concatenate([half] * 4, axis=1)
    half = sin_ref[...].T
    sine = jnp.concatenate([-half, half] * 2, axis=1)
    cos_out[...] = cosine
    sin_out[...] = sine
    for part, out, factor in ((0, q_ref, HEAD**-0.5), (1, k_ref, 1.0)):
        lin = dot_nn(xn, w_ref[part])
        for s in range(lin.shape[1] // LANES):
            u = lin[:, s * LANES : (s + 1) * LANES]
            rot = (u * cosine + half_swap(u) * sine).astype(BF)
            if factor != 1.0:
                rot = (rot.astype(F32) * factor).astype(BF)
            out[:, s * LANES : (s + 1) * LANES] = rot
    v_ref[...] = dot_nn(xn, w_ref[2]).astype(BF)


def qkv_call(x, gain, w, cosine, sine):
    rows, dim = x.shape
    width = w.shape[2]
    blk = min(256, rows)
    row = lambda cols: pl.BlockSpec((blk, cols), lambda i: (i, 0))
    return pl.pallas_call(
        qkv_body,
        grid=(rows // blk,),
        out_shape=[jax.ShapeDtypeStruct((rows, dim), BF)]
        + [jax.ShapeDtypeStruct((rows, width), BF)] * 3
        + [jax.ShapeDtypeStruct((rows, LANES), F32)] * 2,
        in_specs=[
            row(dim),
            pl.BlockSpec((1, dim), lambda i: (0, 0)),
            pl.BlockSpec(w.shape, lambda i: (0, 0, 0)),
            pl.BlockSpec((HEAD // 2, blk), lambda i: (0, i)),
            pl.BlockSpec((HEAD // 2, blk), lambda i: (0, i)),
        ],
        out_specs=[row(dim), row(width), row(width), row(width), row(LANES), row(LANES)],
        compiler_params=pltpu.CompilerParams(vmem_limit_bytes=VMEM_LIMIT),
        name="qkv",
    )(x, gain, w, cosine, sine)


def attn_fwd_body(
    q_ref, k_ref, v_ref, base_ref, segq_ref, extk_ref, bias_ref, o_ref, o32_ref, extq_ref
):
    rows = q_ref.shape[0]
    blk = 256
    lane = lax.broadcasted_iota(jnp.int32, (blk, LANES), 1)
    kind = lax.broadcasted_iota(jnp.int32, (1, LANES), 1) // VAR_COLS
    bias_rows = []
    for h in range(2):
        head = pl.program_id(0) * 2 + h
        hi, mid, low = split3(jnp.full((1, LANES), bias_ref[0, head] - bias_ref[1, head], F32))
        bias_rows.append(jnp.where(kind == 0, hi, jnp.where(kind == 1, mid, jnp.where(kind == 2, low, 0.0))))
    kx = jnp.concatenate([k_ref[...], extk_ref[...]], axis=1)
    ones = jnp.ones((rows, LANES), BF)
    vx = jnp.concatenate([v_ref[...], ones], axis=1)
    for i in range(rows // blk):
        sl = slice(i * blk, (i + 1) * blk)
        q = q_ref[sl, :].astype(F32)
        base = base_ref[sl, :]
        segq = segq_ref[sl, :]
        outs = []
        for h in range(2):
            ext = base * bias_rows[h] + segq
            mine = (lane >= HEAD) if h else (lane < HEAD)
            qx = jnp.concatenate([jnp.where(mine, q, 0.0), ext], axis=1).astype(BF)
            s = dot_nt(qx, kx)
            top = jnp.max(s, axis=-1, keepdims=True)
            p = jnp.exp(s - top).astype(BF)
            ox = dot_nn(p, vx)
            total = ox[:, LANES:]
            outs.append(ox[:, :LANES] / total)
            lse = top + jnp.log(total)
            hi, mid, low = split3(lse)
            ext = jnp.where(
                lane == ONE_COL, -hi, jnp.where(lane == ONE_COL + 1, -mid, jnp.where(lane == ONE_COL + 2, -low, ext))
            )
            extq_ref[0, h, sl, :] = ext.astype(BF)
        o = jnp.where(lane < HEAD, outs[0], outs[1])
        o32_ref[sl, :] = o
        o_ref[sl, :] = o.astype(BF)


def attn_fwd_call(q, k, v, base, segq, extk, head_bias):
    rows, width = q.shape
    pairs = width // LANES
    col = pl.BlockSpec((rows, LANES), lambda p: (0, p))
    full = pl.BlockSpec((rows, LANES), lambda p: (0, 0))
    return pl.pallas_call(
        attn_fwd_body,
        grid=(pairs,),
        out_shape=[
            jax.ShapeDtypeStruct((rows, width), BF),
            jax.ShapeDtypeStruct((rows, width), F32),
            jax.ShapeDtypeStruct((pairs, 2, rows, LANES), BF),
        ],
        in_specs=[
            col, col, col, full, full, full,
            pl.BlockSpec(memory_space=pltpu.SMEM),
        ],
        out_specs=[col, col, pl.BlockSpec((1, 2, rows, LANES), lambda p: (p, 0, 0, 0))],
        compiler_params=pltpu.CompilerParams(vmem_limit_bytes=VMEM_LIMIT),
        name="attn_fwd",
    )(q, k, v, base, segq, extk, head_bias)


def attn_bwd_body(
    q_ref, k_ref, v_ref, do_ref, o32_ref, extq_ref, extk_ref, var_ref, cos_ref, sin_ref, d_ref, gb_ref, dqt_ref
):
    rows = q_ref.shape[0]
    blk = 256
    lane = lax.broadcasted_iota(jnp.int32, (blk, LANES), 1)
    kinds = lax.broadcasted_iota(jnp.int32, (8, blk), 0)
    kx = jnp.concatenate([k_ref[...], extk_ref[...]], axis=1)
    kxt = kx.T
    lane_all = lax.broadcasted_iota(jnp.int32, (rows, LANES), 1)
    vx = jnp.concatenate([v_ref[...], jnp.where(lane_all < 3, 1.0, 0.0).astype(BF)], axis=1)
    dv = jnp.zeros((rows, LANES), F32)
    dk = jnp.zeros((rows, LANES), F32)
    for h in range(2):
        same = jnp.zeros((8, blk), F32)
        other = jnp.zeros((8, blk), F32)
        for i in range(rows // blk):
            sl = slice(i * blk, (i + 1) * blk)
            mine = (lane >= HEAD) if h else (lane < HEAD)
            q = jnp.where(mine, q_ref[sl, :].astype(F32), 0.0).astype(BF)
            do32 = jnp.where(mine, do_ref[sl, :].astype(F32), 0.0)
            do = do32.astype(BF)
            delta = jnp.sum(do32 * o32_ref[sl, :], axis=-1, keepdims=True)
            hi, mid, low = split3(delta)
            dext = jnp.where(lane == 0, -hi, jnp.where(lane == 1, -mid, jnp.where(lane == 2, -low, 0.0))).astype(BF)
            st = dot_nt(kx, jnp.concatenate([q, extq_ref[0, h, sl, :]], axis=1))
            pt = jnp.exp(st)
            dpt = dot_nt(vx, jnp.concatenate([do, dext], axis=1))
            dst = (pt * dpt).astype(BF)
            dv = dv + dot_nn(pt.astype(BF), do)
            dk = dk + dot_nn(dst, q)
            dqt = dot_nn(kxt, dst)
            dqt_ref[h * HEAD : (h + 1) * HEAD, sl] = dqt[h * HEAD : (h + 1) * HEAD, :]
            g = dqt[LANES : LANES + 8, :]
            match = kinds == var_ref[:, sl]
            same = same + jnp.where(match, g, 0.0)
            other = other + jnp.where(match | (kinds >= VAR_COLS), 0.0, g)
        gb_ref[0, h, 0] = same
        gb_ref[0, h, 1] = other
    cosine = cos_ref[...]
    sine = sin_ref[...]
    dq = dqt_ref[...].T * HEAD**-0.5
    d_ref[0] = (dq * cosine - half_swap(dq) * sine).astype(BF)
    d_ref[1] = (dk * cosine - half_swap(dk) * sine).astype(BF)
    d_ref[2] = dv.astype(BF)


def attn_bwd_call(q, k, v, do, o32, extq, extk, variates, cosine, sine):
    rows, width = q.shape
    pairs = width // LANES
    col = pl.BlockSpec((rows, LANES), lambda p: (0, p))
    full = pl.BlockSpec((rows, LANES), lambda p: (0, 0))
    blk = 256
    return pl.pallas_call(
        attn_bwd_body,
        grid=(pairs,),
        out_shape=[jax.ShapeDtypeStruct((3, rows, width), BF), jax.ShapeDtypeStruct((pairs, 2, 2, 8, blk), F32)],
        in_specs=[
            col, col, col, col, col,
            pl.BlockSpec((1, 2, rows, LANES), lambda p: (p, 0, 0, 0)),
            full,
            pl.BlockSpec((1, rows), lambda p: (0, 0)),
            full, full,
        ],
        out_specs=[pl.BlockSpec((3, rows, LANES), lambda p: (0, 0, p)), pl.BlockSpec((1, 2, 2, 8, blk), lambda p: (p, 0, 0, 0, 0))],
        scratch_shapes=[pltpu.VMEM((LANES, rows), F32)],
        compiler_params=pltpu.CompilerParams(vmem_limit_bytes=VMEM_MOST),
        name="attn_bwd",
    )(q, k, v, do, o32, extq, extk, variates, cosine, sine)


def partner_barrier():
    dp = lax.axis_index("dp")
    other = 1 - lax.axis_index("tensor")
    barrier = pltpu.get_barrier_semaphore()
    pl.semaphore_signal(barrier, inc=1, device_id=(dp, other), device_id_type=MESH)
    pl.semaphore_wait(barrier, 1)
    return (dp, other)


def send_rows(src, dst, sl, ssem, rsem, peer):
    return pltpu.make_async_remote_copy(
        src_ref=src.at[sl], dst_ref=dst.at[sl], send_sem=ssem, recv_sem=rsem, device_id=peer, device_id_type=MESH
    )


CHUNKS = 4


def attn_out_body(o_ref, w_ref, gain_ref, x, mid, xn, x_v, mid_v, xn_v, mine, theirs, ssem, rsem, lsem, osem):
    rows = x.shape[0]
    blk = rows // CHUNKS

    def rows_of(c):
        return pl.ds(pl.multiple_of(c * blk, blk), blk)

    def load(c):
        return pltpu.make_async_copy(x.at[rows_of(c)], x_v.at[rows_of(c)], lsem.at[c])

    def stores(c):
        return [
            pltpu.make_async_copy(mid_v.at[rows_of(c)], mid.at[rows_of(c)], osem.at[0, c]),
            pltpu.make_async_copy(xn_v.at[rows_of(c)], xn.at[rows_of(c)], osem.at[1, c]),
        ]

    for c in range(CHUNKS):
        load(c).start()
    peer = partner_barrier()

    def core_copy(c):
        return send_rows(mine, theirs, rows_of(c), ssem.at[c], rsem.at[c], peer)

    @pl.loop(0, CHUNKS)
    def _(c):
        mine[rows_of(c), :] = dot_nn(o_ref[rows_of(c), :], w_ref[...]).astype(BF)
        core_copy(c).start()

    @pl.loop(0, CHUNKS)
    def _(c):
        r = rows_of(c)
        load(c).wait()
        core_copy(c).wait_recv()
        total = x_v[r, :].astype(F32) + (mine[r, :].astype(F32) + theirs[r, :].astype(F32))
        inv = lax.rsqrt(jnp.mean(total * total, axis=-1, keepdims=True) + EPSILON)
        mid_v[r, :] = total
        xn_v[r, :] = (total * inv * gain_ref[...]).astype(BF)
        for copy in stores(c):
            copy.start()

    for c in range(CHUNKS):
        core_copy(c).wait_send()
        for copy in stores(c):
            copy.wait()


def attn_out_call(x, o, w, gain):
    rows, dim = x.shape
    any_spec = pl.BlockSpec(memory_space=pl.ANY)
    low = pltpu.VMEM((rows, dim), BF)
    dma = pltpu.SemaphoreType.DMA
    return pl.pallas_call(
        attn_out_body,
        out_shape=[jax.ShapeDtypeStruct((rows, dim), F32), jax.ShapeDtypeStruct((rows, dim), BF)],
        in_specs=[whole_spec()] * 3 + [any_spec],
        out_specs=[any_spec] * 2,
        scratch_shapes=[
            low, pltpu.VMEM((rows, dim), F32), low, low, low,
            dma((CHUNKS,)), dma((CHUNKS,)), dma((CHUNKS,)), dma((2, CHUNKS)),
        ],
        compiler_params=pltpu.CompilerParams(collective_id=1, has_side_effects=True, vmem_limit_bytes=VMEM_LIMIT),
        name="attn_out",
    )(o, w, gain, x)


LATE = 2
SLOTS = 2
PART = FFN_COLS // 4


def sent(copy):
    copy.wait_send() if copy.is_remote else copy.wait()


def grid_bits():
    dp = lax.axis_index("dp")
    return dp, dp % 2, (dp // 2) % 2, peers_of(dp)[3], peers_of(dp)[4]


def ffn_body(
    xn_ref, ct_ref, w0_ref, wn_ref, wd_ref,
    out_ref, gx_ref, gk_ref, uk_ref, rg, ru, dk, rd, late_x, late_y,
    acc_o, acc_g, hid, dg, du, xt, wgu, away_w, away_d, ws, wr, ds, dr,
):
    j = pl.program_id(0)
    t = lax.axis_index("tensor")
    dp, x, y, px, py = grid_bits()
    steps = pl.num_programs(0)
    rows = xn_ref.shape[0]
    blk = wd_ref.shape[0]
    per = WIDE // blk
    early = 2 * per - LATE
    slot = lax.rem(j, SLOTS)
    near = (px, py)
    bits = (x, y)
    arrays = ((rg, late_x), (ru, late_y))

    def remote(src, dst, ssem, rsem, peer):
        return pltpu.make_async_remote_copy(
            src_ref=src, dst_ref=dst, send_sem=ssem, recv_sem=rsem, device_id=(peer, t), device_id_type=MESH
        )

    def wide_early(k, at):
        cols = pl.ds(pl.multiple_of(lax.rem(at, per) * blk, blk), blk)
        s = lax.rem(at, SLOTS)
        return remote(away_w.at[k, s], arrays[k][0].at[:, cols], ws.at[k, s], wr.at[k], near[k])

    def wide_late(k, at):
        cols = pl.ds(pl.multiple_of((at - early) * blk, blk), blk)
        s = lax.rem(at, SLOTS)
        return pltpu.make_async_copy(away_w.at[k, s], arrays[k][1].at[pl.ds(0, HALF_ROWS), cols], ws.at[k, s])

    def wide_do(at, act):
        for k in range(2):

            @pl.when(at < early)
            def _():
                act(wide_early(k, at))

            @pl.when(at >= early)
            def _():
                act(wide_late(k, at))

    def down_rows(g, half):
        return pl.ds(pl.multiple_of(g * 2 * PART + half * PART, PART), PART)

    def down_keep(g, at):
        s = lax.rem(at, SLOTS)
        return pltpu.make_async_copy(
            away_d.at[s, down_rows(g, bits[g])], dk.at[g, pl.ds(pl.multiple_of(at * PART, PART), PART)], ds.at[g, s]
        )

    def down_send(g, at):
        s = lax.rem(at, SLOTS)
        rows_at = pl.ds(pl.multiple_of(at * PART, PART), PART)
        return remote(away_d.at[s, down_rows(g, 1 - bits[g])], rd.at[g, rows_at], ds.at[2 + g, s], dr.at[g], near[g])

    def down_late(g, at):
        s = lax.rem(at, SLOTS)
        rows_at = pl.ds(pl.multiple_of(HALF_ROWS + (at - early) * PART, PART), PART)
        return pltpu.make_async_copy(
            away_d.at[s, down_rows(g, 1 - bits[g])], arrays[g][1].at[rows_at], ds.at[2 + g, s]
        )

    def down_do(at, act):
        for g in range(2):
            act(down_keep(g, at))

            @pl.when(at < early)
            def _():
                act(down_send(g, at))

            @pl.when(at >= early)
            def _():
                act(down_late(g, at))

    def part_rows(src, to, r):
        turned = jnp.swapaxes(src[r].astype(F32), 0, 1)
        for k in range(8):
            s = k // 2
            wgu[to, k % 2, r, s * LANES : (s + 1) * LANES] = turned[k].astype(BF)

    @pl.when(j == 0)
    def _():
        barrier = pltpu.get_barrier_semaphore()
        for peer in near:
            pl.semaphore_signal(barrier, inc=1, device_id=(peer, t), device_id_type=MESH)
        pl.semaphore_wait(barrier, 2)
        acc_o[...] = jnp.zeros_like(acc_o)
        acc_g[...] = jnp.zeros_like(acc_g)
        xt[...] = xn_ref[...].T

        @pl.loop(0, rows // LANES)
        def _(c):
            part_rows(w0_ref, 0, pl.ds(pl.multiple_of(c * LANES, LANES), LANES))

    now = lax.rem(j, 2)
    wg = wgu[now, 0]
    wu = wgu[now, 1]
    wd = wd_ref[...]
    part_rows(wn_ref, 1 - now, slice(None))
    for i in range(rows // FFN_ROWS):
        sl = slice(i * FFN_ROWS, (i + 1) * FFN_ROWS)
        xn = xn_ref[sl, :]
        gate = dot_nn(xn, wg)
        up = dot_nn(xn, wu)
        gh = dot_nt(ct_ref[sl, :], wd)
        sig = jax.nn.sigmoid(gate)
        silu = gate * sig
        hidden = (silu * up).astype(BF)
        dgate = (gh * up * sig * (1.0 + gate * (1.0 - sig))).astype(BF)
        dup = (gh * silu).astype(BF)
        hid[sl, :] = hidden
        dg[sl, :] = dgate
        du[sl, :] = dup
        acc_o[sl, :] += dot_nn(hidden, wd)
        acc_g[sl, :] += dot_nt(dgate, wg) + dot_nt(dup, wu)

    @pl.when(j >= SLOTS)
    def _():
        wide_do(j - SLOTS, sent)
        down_do(j - SLOTS, sent)

    away_d[slot] = dot_tn(hid[...], ct_ref[...]).astype(BF)
    down_do(j, lambda copy: copy.start())
    for k, (part, keep, bit) in enumerate(((dg, gk_ref, x), (du, uk_ref, y))):
        rows_at = lambda half: pl.ds(pl.multiple_of(half * HALF_ROWS, HALF_ROWS), HALF_ROWS)
        away_w[k, slot] = dot_nn(xt[rows_at(1 - bit), :], part[...]).astype(BF)
        keep[0] = dot_nn(xt[rows_at(bit), :], part[...]).astype(BF)
    wide_do(j, lambda copy: copy.start())

    @pl.when(j == steps - 1)
    def _():
        out_ref[...] = acc_o[...].astype(BF)
        gx_ref[...] = acc_g[...].astype(BF)
        for back in range(SLOTS, 0, -1):
            wide_do(steps - back, sent)
            down_do(steps - back, sent)
        for k in range(2):
            part = arrays[k][0].at[:, pl.ds(0, early * blk)]
            remote(part, part, ws.at[k, 0], wr.at[k], near[k]).wait_recv()
        for g in range(2):
            part = rd.at[g, pl.ds(0, early * PART)]
            remote(part, part, ds.at[g, 0], dr.at[g], near[g]).wait_recv()


def ffn_call(xn, ct, w_pairs, wd):
    rows, dim = xn.shape
    hidden = wd.shape[0]
    blk = FFN_COLS
    per = WIDE // blk
    full = pl.BlockSpec((rows, dim), lambda j: (0, 0))
    steps = hidden // blk
    tiles = 2 * blk // LANES
    first_w = pl.BlockSpec((dim, tiles, LANES), lambda j: (0, 0, 0))
    next_w = pl.BlockSpec((dim, tiles, LANES), lambda j: (0, jnp.minimum(j + 1, steps - 1), 0))
    roww = pl.BlockSpec((blk, dim), lambda j: (j, 0))
    grad = pl.BlockSpec((1, HALF_ROWS, blk), lambda j: (j // per, 0, lax.rem(j, per)))
    any_spec = pl.BlockSpec(memory_space=pl.ANY)
    wide = jax.ShapeDtypeStruct((2, HALF_ROWS, dim), BF)
    early = hidden // blk - LATE
    come = jax.ShapeDtypeStruct((HALF_ROWS, early * blk), BF)
    late = jax.ShapeDtypeStruct((HALF_ROWS + LATE * PART, LATE * blk), BF)
    dma = pltpu.SemaphoreType.DMA
    return pl.pallas_call(
        ffn_body,
        grid=(hidden // blk,),
        in_specs=[full, full, first_w, next_w, roww],
        out_specs=[full, full, grad, grad] + [any_spec] * 6,
        out_shape=[jax.ShapeDtypeStruct((rows, dim), BF)] * 2
        + [wide, wide, come, come, wide, jax.ShapeDtypeStruct((2, early * PART, dim), BF), late, late],
        scratch_shapes=[pltpu.VMEM((rows, dim), F32)] * 2
        + [pltpu.VMEM((rows, blk), BF)] * 3
        + [
            pltpu.VMEM((dim, rows), BF),
            pltpu.VMEM((2, 2, dim, blk), BF),
            pltpu.VMEM((2, SLOTS, HALF_ROWS, blk), BF),
            pltpu.VMEM((SLOTS, blk, dim), BF),
            dma((2, SLOTS)), dma((2,)), dma((4, SLOTS)), dma((2,)),
        ],
        compiler_params=pltpu.CompilerParams(collective_id=5, has_side_effects=True, vmem_limit_bytes=VMEM_LIMIT),
        name="ffn",
    )(xn, ct, w_pairs, w_pairs, wd)


def pair_rows(w):
    dim, two, width = w.shape
    tiled = jnp.transpose(w.reshape(dim, two, width // LANES, LANES), (0, 2, 1, 3))
    return tiled.reshape(dim, two * width // LANES, LANES)


def widen_body(
    ga_ref, gb_ref, da_ref, db_ref, aa_ref, v_ref, o_ref, small_ref, rows_ref, ig_ref,
    gu_ref, down_ref, qkv_ref, out_ref, g1_ref, g2_ref, gbias_ref, rows_out, ig_out,
):
    tiles = WIDE // LANES
    for f in range(2):
        for q in range(tiles // 4):
            parts = []
            for k in range(8):
                s = q * 4 + k // 2
                parts.append((ga_ref, gb_ref)[k % 2][0, f, :, s * LANES : (s + 1) * LANES].astype(F32))
            at = (f * tiles + q * 4) * 2
            gu_ref[:, at : at + 8, :] = jnp.swapaxes(jnp.stack(parts), 0, 1)
    down_ref[:, 0, 0] = da_ref[0, 0].astype(F32).reshape(down_ref.shape[0], PART, WIDE)
    down_ref[:, 1, 0] = db_ref[0, 0].astype(F32).reshape(down_ref.shape[0], PART, WIDE)
    width = qkv_ref.shape[2]
    qkv_ref[0] = aa_ref[0, 0, :, :width].astype(F32)
    qkv_ref[1] = aa_ref[0, 0, :, width:].astype(F32)
    qkv_ref[2] = v_ref[0, 0].astype(F32)
    out_ref[...] = o_ref[0, 0].astype(F32)
    rows_out[...] = rows_ref[...]
    ig_out[...] = ig_ref[...]

    @pl.when(pl.program_id(0) == 0)
    def _():
        g1_ref[...] = small_ref[0:1, :]
        g2_ref[...] = small_ref[1:2, :]
        row = lax.broadcasted_iota(jnp.int32, gbias_ref.shape, 0)
        col = lax.broadcasted_iota(jnp.int32, gbias_ref.shape, 1)
        total = jnp.zeros(gbias_ref.shape, F32)
        for h in range(gbias_ref.shape[1]):
            for s in range(2):
                at = (h % 2 * 2 + s) * QBLK
                one = jnp.sum(small_ref[2 + h // 2 : 3 + h // 2, at : at + QBLK], axis=1, keepdims=True)
                total = jnp.where((row == s) & (col == h), one, total)
        gbias_ref[...] = total


def widen_call(a, b, small, heads, block_output, input_grad):
    blk = 256
    half = HALF_ROWS // blk
    tiles = 4 * WIDE // LANES
    width = WIDE // 2
    gate = pl.BlockSpec((1, 2, blk, WIDE), lambda i: (i // half, 0, lax.rem(i, half), 0))
    block = lambda n: pl.BlockSpec((1, 1, blk, WIDE), lambda i: (i // half, n, lax.rem(i, half), 0))
    fixed = lambda shape: pl.BlockSpec(shape, lambda i: (0, 0))
    rows = block_output.shape[0]
    steps = 2 * half
    share = pl.BlockSpec((rows // steps, WIDE), lambda i: (i, 0))
    gu, down, qkv, out, g1, g2, gbias, block_output, input_grad = pl.pallas_call(
        widen_body,
        grid=(2 * half,),
        out_shape=[
            jax.ShapeDtypeStruct((2 * HALF_ROWS, tiles, LANES), F32),
            jax.ShapeDtypeStruct((HALF_ROWS // PART, 2, 2, PART, WIDE), F32),
            jax.ShapeDtypeStruct((3, 2 * HALF_ROWS, width), F32),
            jax.ShapeDtypeStruct((HALF_ROWS, WIDE), F32),
            jax.ShapeDtypeStruct((1, WIDE), F32),
            jax.ShapeDtypeStruct((1, WIDE), F32),
            jax.ShapeDtypeStruct((2, heads), F32),
            jax.ShapeDtypeStruct(block_output.shape, BF),
            jax.ShapeDtypeStruct(input_grad.shape, F32),
        ],
        in_specs=[
            gate, gate, block(2), block(2), block(3),
            pl.BlockSpec((1, 1, blk, width), lambda i: (0, 3, lax.rem(i, half), i // half)),
            pl.BlockSpec((1, 1, blk // 2, WIDE), lambda i: (1, 3, i, 0)),
            fixed((SMALL, WIDE)),
            share,
            share,
        ],
        out_specs=[
            pl.BlockSpec((blk, tiles, LANES), lambda i: (i, 0, 0)),
            pl.BlockSpec((blk // PART, 2, 1, PART, WIDE), lambda i: (lax.rem(i, half), 0, i // half, 0, 0)),
            pl.BlockSpec((3, blk, width), lambda i: (0, i, 0)),
            pl.BlockSpec((blk // 2, WIDE), lambda i: (i, 0)),
            fixed((1, WIDE)),
            fixed((1, WIDE)),
            fixed((2, heads)),
            share,
            share,
        ],
        compiler_params=pltpu.CompilerParams(vmem_limit_bytes=VMEM_LIMIT),
        name="widen",
    )(a, b, a, b, a, b, b, small, block_output, input_grad)
    gu = jnp.transpose(gu.reshape(2 * HALF_ROWS, tiles // 2, 2, LANES), (0, 2, 1, 3)).reshape(2 * HALF_ROWS, 2, 2 * WIDE)
    return gu, down.reshape(4 * HALF_ROWS, WIDE), qkv, out, g1, g2, gbias, block_output, input_grad


def norm_back(rows_now, gain, grads):
    inv = lax.rsqrt(jnp.mean(rows_now * rows_now, axis=-1, keepdims=True) + EPSILON)
    scaled = grads * gain
    gain_grad = jnp.sum(grads * rows_now * inv, axis=0, keepdims=True)
    back = inv * scaled - rows_now * (inv * inv * inv) * jnp.mean(scaled * rows_now, axis=-1, keepdims=True)
    return back, gain_grad


def ffn_back_body(
    gain_ref, w_ref, at_ref, gx, fo, mid, ct,
    do_ref, gw_ref, gg_ref, out, gm,
    gx_in, fo_in, gx_v, fo_v, mid_v, ct_v, gm_v, out_v, gb, ssem, rsem, lsem, osem,
):
    rows = mid.shape[0]
    blk = rows // CHUNKS

    def rows_of(c):
        return pl.ds(pl.multiple_of(c * blk, blk), blk)

    def load(k, c):
        src, dst = ((gx, gx_v), (mid, mid_v), (ct, ct_v), (fo, fo_v))[k]
        return pltpu.make_async_copy(src.at[rows_of(c)], dst.at[rows_of(c)], lsem.at[k, c])

    def store(k, c):
        src, dst = ((gm_v, gm), (out_v, out))[k]
        return pltpu.make_async_copy(src.at[rows_of(c)], dst.at[rows_of(c)], osem.at[k, c])

    for c in range(CHUNKS):
        for k in range(4):
            load(k, c).start()
    peer = partner_barrier()

    def core_copy(n, c):
        src, dst = ((gx, gx_in), (fo, fo_in))[n]
        return send_rows(src, dst, rows_of(c), ssem.at[n * CHUNKS + c], rsem.at[n * CHUNKS + c], peer)

    for n in range(2):
        for c in range(CHUNKS):
            core_copy(n, c).start()
    gg_ref[...] = jnp.zeros_like(gg_ref)

    @pl.loop(0, CHUNKS)
    def _(c):
        r = rows_of(c)
        for k in range(3):
            load(k, c).wait()
        core_copy(0, c).wait_recv()
        grads = gx_v[r, :].astype(F32) + gx_in[r, :].astype(F32)
        back, gain_grad = norm_back(mid_v[r, :], gain_ref[...], grads)
        gg_ref[...] += gain_grad
        grad_mid = ct_v[r, :].astype(F32) + back
        gm_v[r, :] = grad_mid
        store(0, c).start()
        low = grad_mid.astype(BF)
        gb[r, :] = low
        do_ref[r, :] = dot_nt(low, w_ref[...]).astype(BF)

    @pl.loop(0, CHUNKS)
    def _(c):
        r = rows_of(c)
        load(3, c).wait()
        core_copy(1, c).wait_recv()
        out_v[r, :] = (mid_v[r, :] + (fo_v[r, :].astype(F32) + fo_in[r, :].astype(F32))).astype(BF)
        store(1, c).start()

    gw_ref[...] = dot_tn(at_ref[...], gb[...]).astype(BF)
    for c in range(CHUNKS):
        for k in range(2):
            core_copy(k, c).wait_send()
            store(k, c).wait()


def ffn_back_call(gx, fo, mid, ct, gain, w, at):
    rows, dim = mid.shape
    width = w.shape[0]
    any_spec = pl.BlockSpec(memory_space=pl.ANY)
    low = pltpu.VMEM((rows, dim), BF)
    wide = pltpu.VMEM((rows, dim), F32)
    dma = pltpu.SemaphoreType.DMA
    do, gw, gg, out, gm = pl.pallas_call(
        ffn_back_body,
        out_shape=[
            jax.ShapeDtypeStruct((rows, width), BF),
            jax.ShapeDtypeStruct((width, dim), BF),
            jax.ShapeDtypeStruct((1, dim), F32),
            jax.ShapeDtypeStruct((rows, dim), BF),
            jax.ShapeDtypeStruct((rows, dim), F32),
        ],
        in_specs=[whole_spec()] * 3 + [any_spec] * 4,
        out_specs=[whole_spec()] * 3 + [any_spec] * 2,
        scratch_shapes=[
            low, low, low, low, wide, low, wide, low, low,
            dma((2 * CHUNKS,)), dma((2 * CHUNKS,)), dma((4, CHUNKS)), dma((2, CHUNKS)),
        ],
        compiler_params=pltpu.CompilerParams(collective_id=2, has_side_effects=True, vmem_limit_bytes=VMEM_MOST),
        name="ffn_back",
    )(gain, w, at, gx, fo, mid, ct)
    return out, gm, do, gw, gg


def peers_of(dp):
    z = dp // 4
    y = (dp // 2) % 2
    x = dp % 2
    at = lambda zz, yy, xx: zz * 4 + yy * 2 + xx
    return z, y, x, at(z, y, 1 - x), at(z, 1 - y, x), at(z + 1 - 2 * (z % 2), y, x), at(3 - z, y, x)


def sum_body(
    gk, rg, uk, ru, late_x, late_y, dk, rd, go, dqkv, w3, xn, xin, gmid, gain_ref, gain2_ref, bias_ref, out_a, out_b, ig, small_out,
    L, S, Z, R, Y, DL, DS, DA, G, sb, st, dl, wb, xb, mine_rows, their_rows, away_rows, xc, gc, ic,
    loc, s1s, s1r, sends, zr, rr, yr, ar, xr, lo, ss, sr, ld, cs, cr, xg, io, s2s, s2r, gs, gr,
):
    dp = lax.axis_index("dp")
    t = lax.axis_index("tensor")
    z, y, x, px, py, zn, mm = peers_of(dp)
    is_mid = (z == 1) | (z == 2)
    is_end = (z == 0) | (z == 3)
    mine = jnp.where(z == 2, WIDE // 2, 0)
    others = WIDE // 2 - mine
    n = KEPT_ROWS // ROWS
    cut_at = 2 * HALF_ROWS // ROWS
    tail_at = (2 * HALF_ROWS + QUARTER_ROWS) // ROWS
    starts = (0, HALF_ROWS // ROWS, cut_at, tail_at)
    first = (px, py)
    last = (py, px)
    outs = (out_a, out_b)
    owner = (x, y)
    bit = (y, x)
    F = S

    def remote(src, dst, ssem, rsem, peer, core=t):
        return pltpu.make_async_remote_copy(
            src_ref=src, dst_ref=dst, send_sem=ssem, recv_sem=rsem, device_id=(peer, core), device_id_type=MESH
        )

    def loads(g, b):
        rows = pl.ds(b * HALF_ROWS, HALF_ROWS)
        near = (rg, ru)[g]
        late = (late_x, late_y)[g]
        top = pl.ds(0, HALF_ROWS)
        if b < 2:
            copies = [((gk, uk)[g].at[b], L.at[g, rows])]
        else:
            copies = [(dk.at[g], DL.at[g])]
        if b == 0:
            copies.append((near.at[:, pl.ds(0, WIDE)], S.at[g, rows]))
        elif b == 1:
            cut = near.shape[1] - WIDE
            if cut:
                copies.append((near.at[:, pl.ds(WIDE, cut)], S.at[g, rows, pl.ds(0, cut)]))
            copies.append((late.at[top], S.at[g, rows, pl.ds(cut, WIDE - cut)]))
        else:
            cut = rd.shape[1]
            copies.append((rd.at[g], DS.at[g, pl.ds(0, cut)]))
            copies.append((late.at[pl.ds(HALF_ROWS, HALF_ROWS - cut)], DS.at[g, pl.ds(cut, HALF_ROWS - cut)]))
        return [pltpu.make_async_copy(src, dst, loc.at[g, b, k]) for k, (src, dst) in enumerate(copies)]

    own_loads = [pltpu.make_async_copy(src, dst, ld.at[k]) for k, (src, dst) in enumerate(((dqkv, dl), (w3, wb), (xn, xb)))]
    for g in range(2):
        for copy in loads(g, 0):
            copy.start()

    tail = pl.ds(2 * HALF_ROWS + QUARTER_ROWS, HALF_ROWS)

    def out_load(kept):
        return pltpu.make_async_copy(go, L.at[1, tail] if kept else away_rows.at[1], loc.at[1, 3, 0])

    def out_load_do(act):
        @pl.when(y == 1)
        def _():
            act(out_load(True))

        @pl.when(y == 0)
        def _():
            act(out_load(False))

    barrier = pltpu.get_barrier_semaphore()
    others_z = [lax.rem(z + k, 4) * 4 + y * 2 + x for k in range(1, 4)]
    for peer in [px, py] + others_z:
        pl.semaphore_signal(barrier, inc=1, device_id=(peer, t), device_id_type=MESH)
    pl.semaphore_signal(barrier, inc=1, device_id=(dp, 1 - t), device_id_type=MESH)
    pl.semaphore_wait(barrier, 6)
    for b in (2, 1):
        for g in range(2):
            for copy in loads(g, b):
                copy.start()
    for copy in own_loads:
        copy.start()
    out_load_do(lambda copy: copy.start())

    def first_exchange(g):
        return remote(away_rows.at[g], S.at[g, tail], s1s.at[g], s1r.at[g], first[g])

    def first_part(g, c):
        at = pl.multiple_of(c * SWAP_ROWS, SWAP_ROWS)
        dst = S.at[g, pl.ds(2 * HALF_ROWS + QUARTER_ROWS + at, SWAP_ROWS)]
        return remote(away_rows.at[g, pl.ds(at, SWAP_ROWS)], dst, s1s.at[g], s1r.at[g], first[g])

    quarter = pl.ds(2 * HALF_ROWS, QUARTER_ROWS)

    def second_exchange(g):
        return remote(DA.at[g], S.at[g, quarter], s2s.at[g], s2r.at[g], last[g])

    def second_part(g, c):
        at = pl.multiple_of(c * SWAP_ROWS, SWAP_ROWS)
        rows = pl.ds(at, SWAP_ROWS)
        dst = S.at[g, pl.ds(2 * HALF_ROWS + at, SWAP_ROWS)]
        return remote(DA.at[g, rows], dst, s2s.at[g], s2r.at[g], last[g])

    def down_quarter(half):
        return pl.ds(pl.multiple_of(half * QUARTER_ROWS, QUARTER_ROWS), QUARTER_ROWS)

    def piece_down(g):
        for copy in loads(g, 2):
            copy.wait()
        keep = down_quarter(bit[g])
        away = down_quarter(1 - bit[g])
        L[g, quarter, :] = (DL[g, keep, :].astype(F32) + DS[g, keep, :].astype(F32)).astype(BF)
        DA[g] = (DL[g, away, :].astype(F32) + DS[g, away, :].astype(F32)).astype(BF)

    def piece_swap(c):
        for g in range(2):
            first_part(g, c).start()

    def piece_second(c):
        for g in range(2):
            second_part(g, c).start()

    small_x = remote(st.at[2], sb.at[0], ss.at[0], sr.at[0], px)
    small_y = remote(st.at[0], sb.at[1], ss.at[1], sr.at[1], py)
    small_z = [remote(st.at[1], sb.at[2 + z], ss.at[2 + k], sr.at[2 + z], others_z[k]) for k in range(3)]

    def rows_of(i):
        return pl.ds(pl.multiple_of(i * ROWS, ROWS), ROWS)

    def cols_of(at):
        return pl.ds(pl.multiple_of(at, WIDE // 2), WIDE // 2)

    def z_copy(g, i):
        return remote(L.at[g, rows_of(i)], Z.at[g, rows_of(i)], sends.at[g, 0], zr.at[g, i], zn)

    def r_copy(g, i):
        return remote(L.at[g, rows_of(i), cols_of(others)], R.at[g, rows_of(i)], sends.at[g, 1], rr.at[g, i], mm)

    def y_copy(g, i):
        return remote(R.at[g, rows_of(i)], Y.at[g, rows_of(i)], sends.at[g, 2], yr.at[g, i], last[g])

    def a_copy(g, i, at):
        return remote(F.at[g, rows_of(i), cols_of(at)], F.at[g, rows_of(i), cols_of(at)], sends.at[g, 3], ar.at[g, i], mm)

    def o_copy(g, i):
        return remote(F.at[g, rows_of(i)], F.at[g, rows_of(i)], sends.at[g, 4], zr.at[g, i], zn)

    def out_rows(g, i):
        shift = jnp.where(i < cut_at, 0, jnp.where(i < tail_at, bit[g] * QUARTER_ROWS, QUARTER_ROWS))
        return pl.ds(pl.multiple_of(i * ROWS + shift, ROWS), ROWS)

    def x_copy(g, i):
        return remote(F.at[g, rows_of(i)], outs[g].at[owner[g], out_rows(g, i)], sends.at[g, 5], xr.at[g], first[g])

    def l_copy(g, i):
        return pltpu.make_async_copy(F.at[g, rows_of(i)], outs[g].at[owner[g], out_rows(g, i)], lo.at[g])

    def quarter_rows(i):
        return pl.ds(pl.multiple_of((i - cut_at) * ROWS, ROWS), ROWS)

    def g_copy(g, i):
        return remote(F.at[g, rows_of(i)], G.at[g, quarter_rows(i)], gs.at[g], gr.at[g, i - cut_at], last[g])

    def pass_on(g, i):
        rows = pl.ds(pl.multiple_of(i * ROWS + (1 - bit[g]) * QUARTER_ROWS, ROWS), ROWS)
        src = G.at[g, quarter_rows(i)]
        g_copy(g, i).wait_recv()
        remote(src, outs[g].at[owner[g], rows], sends.at[g, 5], xr.at[g], first[g]).start()
        pltpu.make_async_copy(src, outs[g].at[owner[g], rows], lo.at[g]).start()

    def is_cut(i):
        return (i >= cut_at) & (i < tail_at)

    def finish(g, i):
        x_copy(g, i).start()
        l_copy(g, i).start()

        @pl.when(is_cut(i))
        def _():
            g_copy(g, i).start()

    def end_in(g, j):
        r = rows_of(j)
        L[g, r, :] = (L[g, r, :].astype(F32) + S[g, r, :].astype(F32)).astype(BF)
        z_copy(g, j).start()

    def end_out(g, j):
        o_copy(g, j).wait_recv()
        finish(g, j)

    def mid_out(g, j):
        a_copy(g, j, others).wait_recv()
        o_copy(g, j).start()
        finish(g, j)

    def mid_join(g, j):
        @pl.when(jnp.logical_not(is_cut(j)))
        def _():
            y_copy(g, j).wait_recv()
            r = rows_of(j)
            F[g, r, cols_of(mine)] = (R[g, r, :].astype(F32) + Y[g, r, :].astype(F32)).astype(BF)
            a_copy(g, j, mine).start()

    def mid_half(g, j):
        r_copy(g, j).wait_recv()
        r = rows_of(j)
        total = (R[g, r, :].astype(F32) + L[g, r, cols_of(mine)].astype(F32)).astype(BF)

        @pl.when(is_cut(j))
        def _():
            F[g, r, cols_of(mine)] = total
            a_copy(g, j, mine).start()

        @pl.when(jnp.logical_not(is_cut(j)))
        def _():
            R[g, r, :] = total
            y_copy(g, j).start()

    def mid_in(g, j):
        z_copy(g, j).wait_recv()
        r = rows_of(j)
        L[g, r, :] = (L[g, r, :].astype(F32) + S[g, r, :].astype(F32) + Z[g, r, :].astype(F32)).astype(BF)
        r_copy(g, j).start()

    def stage(act, g, j):
        @pl.when((j >= 0) & (j < n))
        def _():
            act(g, j)

    seq = xin.shape[0]
    blk = seq // CHUNKS
    width = dl.shape[2]

    def piece_rows(c):
        return pl.ds(pl.multiple_of(c * blk, blk), blk)

    def core_copy(c):
        return remote(mine_rows.at[piece_rows(c)], their_rows.at[piece_rows(c)], cs.at[c], cr.at[c], dp, 1 - t)

    def norm_loads(c):
        return [
            pltpu.make_async_copy(xin.at[piece_rows(c)], xc.at[lax.rem(c, 2)], xg.at[lax.rem(c, 2), 0]),
            pltpu.make_async_copy(gmid.at[piece_rows(c)], gc.at[lax.rem(c, 2)], xg.at[lax.rem(c, 2), 1]),
        ]

    def ig_copy(c):
        return pltpu.make_async_copy(ic.at[lax.rem(c, 2)], ig.at[piece_rows(c)], io.at[lax.rem(c, 2)])

    def piece_start():
        for copy in own_loads:
            copy.wait()

    def piece_part(c):
        r = piece_rows(c)
        total = dot_nt(dl[0, r, :], wb[0]) + dot_nt(dl[1, r, :], wb[1]) + dot_nt(dl[2, r, :], wb[2])
        mine_rows[r, :] = total.astype(BF)
        core_copy(c).start()

    def row_half(half):
        return pl.ds(pl.multiple_of(half * HALF_ROWS, HALF_ROWS), HALF_ROWS)

    def piece_qk(k):
        cols = pl.ds(pl.multiple_of(k * width, width), width)
        L[0, tail, cols] = dot_tn(xb[:, row_half(x)], dl[k]).astype(BF)
        away_rows[0, :, cols] = dot_tn(xb[:, row_half(1 - x)], dl[k]).astype(BF)

    def piece_v():
        for k in range(2):
            cols = pl.ds(k * width, width)
            grad = dot_tn(xb[:, k * HALF_ROWS : (k + 1) * HALF_ROWS], dl[2]).astype(BF)

            @pl.when(y == 0)
            def _():
                L[1, tail, cols] = grad

            @pl.when(y == 1)
            def _():
                away_rows[1, :, cols] = grad

    def piece_send():
        out_load_do(lambda copy: copy.wait())
        for copy in norm_loads(0):
            copy.start()
        st[2] = jnp.zeros((SMALL, WIDE), F32)
        st[2, 1:2, :] = gain2_ref[...]
        for p in range(bias_ref.shape[0]):
            sums = [jnp.sum(bias_ref[p, h, s], axis=0, keepdims=True) for h in range(2) for s in range(2)]
            st[2, 2 + p : 3 + p, :] = jnp.concatenate(sums, axis=1)

    def piece_norm(c):
        @pl.when(c + 1 < CHUNKS)
        def _():
            for copy in norm_loads(c + 1):
                copy.start()

        for copy in norm_loads(c):
            copy.wait()
        core_copy(c).wait_recv()

        @pl.when(c >= 2)
        def _():
            ig_copy(c - 2).wait()

        r = piece_rows(c)
        grads = mine_rows[r, :].astype(F32) + their_rows[r, :].astype(F32)
        s = lax.rem(c, 2)
        back, gain_grad = norm_back(xc[s].astype(F32), gain_ref[...], grads)
        st[2, 0:1, :] = st[2, 0:1, :] + gain_grad
        ic[s] = gc[s] + back
        ig_copy(c).start()

    def small_first():
        small_x.start()

    def small_second():
        small_x.wait_recv()
        st[0] = st[2] + sb[0]
        small_y.start()

    def small_third():
        small_y.wait_recv()
        st[1] = st[0] + sb[1]
        for copy in small_z:
            copy.start()

    pieces = [
        (1, 1, lambda c: piece_down(0)),
        (2, 1, lambda c: piece_down(1)),
        (3, QUARTER_ROWS // SWAP_ROWS, piece_second),
        (3, 1, lambda c: piece_start()),
        (4, CHUNKS, piece_part),
        (4 + CHUNKS, 2, piece_qk),
        (6 + CHUNKS, 1, lambda c: piece_v()),
        (7 + CHUNKS, 1, lambda c: piece_send()),
        (8 + CHUNKS, HALF_ROWS // SWAP_ROWS, piece_swap),
        (9 + CHUNKS, CHUNKS, piece_norm),
        (10 + 2 * CHUNKS, 1, lambda c: small_first()),
        (14 + 2 * CHUNKS, 1, lambda c: small_second()),
        (18 + 2 * CHUNKS, 1, lambda c: small_third()),
    ]

    def body(i, carry):
        for b in range(4):

            @pl.when(i == starts[b])
            def _():
                for g in range(2):
                    if b < 2:
                        for copy in loads(g, b):
                            copy.wait()
                    elif b == 2:
                        second_exchange(g).wait_recv()
                    else:
                        first_exchange(g).wait_recv()

        @pl.when(is_end)
        def _():
            for g in range(2):
                stage(end_in, g, i)
                stage(end_out, g, i - LAGS[4])

        @pl.when(is_mid)
        def _():
            for g in range(2):
                stage(mid_out, g, i - LAGS[3])
                stage(mid_join, g, i - LAGS[2])
                stage(mid_half, g, i - LAGS[1])
                stage(mid_in, g, i - LAGS[0])

        for g in range(2):
            j = i - LAGS[4] - 2

            @pl.when(is_cut(j))
            def _():
                pass_on(g, j)

        for begin, steps, piece in pieces:

            @pl.when((i >= begin) & (i < begin + steps))
            def _():
                piece(i - begin)

        return carry

    lax.fori_loop(0, n + LAGS[4], body, 0)

    for k in range(3):
        zz = lax.rem(z + k + 1, 4)
        remote(st.at[1], sb.at[2 + zz], ss.at[2 + k], sr.at[2 + zz], others_z[k]).wait_recv()
    sb[2 + z] = st[1]
    small_out[...] = (sb[2] + sb[3]) + (sb[4] + sb[5])

    small_x.wait_send()
    small_y.wait_send()
    for copy in small_z:
        copy.wait_send()
    for c in range(CHUNKS):
        core_copy(c).wait_send()
    for c in (CHUNKS - 2, CHUNKS - 1):
        ig_copy(c).wait()
    for g in range(2):
        first_exchange(g).wait_send()
        away = 1 - owner[g]

        @pl.when(is_end)
        def _():
            remote(L.at[g], Z.at[g], sends.at[g, 0], zr.at[g, 0], zn).wait_send()

        @pl.when(is_mid)
        def _():
            remote(R.at[g], Y.at[g], sends.at[g, 1], rr.at[g, 0], mm).wait_send()
            some = pl.ds(0, KEPT_ROWS - QUARTER_ROWS)
            remote(R.at[g, some], Y.at[g, some], sends.at[g, 2], yr.at[g, 0], last[g]).wait_send()
            remote(R.at[g], Y.at[g], sends.at[g, 3], ar.at[g, 0], mm).wait_send()
            remote(F.at[g], F.at[g], sends.at[g, 4], zr.at[g, 0], zn).wait_send()

        second_exchange(g).wait_send()
        remote(G.at[g], G.at[g], gs.at[g], gr.at[g, 0], last[g]).wait_send()
        whole = remote(outs[g].at[away], outs[g].at[away], sends.at[g, 5], xr.at[g], first[g])
        whole.wait_send()
        whole.wait_recv()
        pltpu.make_async_copy(outs[g].at[owner[g]], outs[g].at[owner[g]], lo.at[g]).wait()


def sum_call(gk, rg, uk, ru, late_x, late_y, dk, rd, go, dqkv, w3, xn, xin, gmid, gain, gain2, bias):
    any_spec = pl.BlockSpec(memory_space=pl.ANY)
    n = KEPT_ROWS // ROWS
    rows, dim = xin.shape
    blk = rows // CHUNKS
    full = pltpu.VMEM((2, KEPT_ROWS, WIDE), BF)
    half = pltpu.VMEM((2, KEPT_ROWS, WIDE // 2), BF)
    quarter = pltpu.VMEM((2, QUARTER_ROWS, WIDE), BF)
    down = pltpu.VMEM((2, HALF_ROWS, WIDE), BF)
    dma = pltpu.SemaphoreType.DMA
    return pl.pallas_call(
        sum_body,
        out_shape=[jax.ShapeDtypeStruct((2, GROUP_ROWS, WIDE), BF)] * 2
        + [jax.ShapeDtypeStruct((rows, dim), F32), jax.ShapeDtypeStruct((SMALL, WIDE), F32)],
        in_specs=[any_spec] * 14 + [whole_spec()] * 3,
        out_specs=[any_spec] * 3 + [whole_spec()],
        scratch_shapes=[
            full, full, full, half, half, down, down, quarter, quarter,
            pltpu.VMEM((6, SMALL, WIDE), F32),
            pltpu.VMEM((3, SMALL, WIDE), F32),
            pltpu.VMEM(dqkv.shape, BF),
            pltpu.VMEM(w3.shape, BF),
            pltpu.VMEM((rows, dim), BF),
            pltpu.VMEM((rows, dim), BF),
            pltpu.VMEM((rows, dim), BF),
            pltpu.VMEM((2, HALF_ROWS, WIDE), BF),
            pltpu.VMEM((2, blk, dim), BF),
            pltpu.VMEM((2, blk, dim), F32),
            pltpu.VMEM((2, blk, dim), F32),
            dma((2, 4, 8)), dma((2,)), dma((2,)), dma((2, 6)),
            dma((2, n)), dma((2, n)), dma((2, n)), dma((2, n)),
            dma((2,)), dma((2,)), dma((5,)), dma((6,)),
            dma((3,)), dma((CHUNKS,)), dma((CHUNKS,)), dma((2, 2)), dma((2,)),
            dma((2,)), dma((2,)), dma((2,)), dma((2, QUARTER_ROWS // ROWS)),
        ],
        compiler_params=pltpu.CompilerParams(collective_id=4, has_side_effects=True, vmem_limit_bytes=VMEM_LIMIT),
        name="grad_sum",
    )(gk, rg, uk, ru, late_x, late_y, dk, rd, go, dqkv, w3, xn, xin, gmid, gain, gain2, bias)


def tables(time_ids):
    half = HEAD // 2
    freqs = jnp.exp(jnp.arange(half, dtype=F32) * (-2.0 * math.log(10000.0) / HEAD))
    angles = freqs[:, None] * time_ids.astype(F32)[None, :]
    return jnp.cos(angles), jnp.sin(angles)


def mask_tables(segments, variates):
    lane = jnp.arange(LANES)[None, :]
    var_here = (lane % VAR_COLS == variates[:, None]) & (lane < 3 * VAR_COLS)
    seg_here = (lane - SEG_COL == segments[:, None]) & (lane >= SEG_COL) & (lane < ONE_COL)
    seg_cols = (lane >= SEG_COL) & (lane < ONE_COL)
    ones = (lane >= ONE_COL) & (lane < ONE_COL + 3)
    base = jnp.where(var_here, 1.0, 0.0)
    segq = jnp.where(seg_cols & ~seg_here, MASKED, 0.0)
    extk = jnp.where(var_here | seg_here | ones, 1.0, 0.0).astype(BF)
    return base, segq, extk


def fast_local(
    block_input, segments, variates, time_ids, attn_gain, w_qkv, head_bias, w_out, ffn_gain, w_gate_up, w_down, cotangent
):
    w3 = jnp.transpose(w_qkv, (1, 0, 2))
    cosine, sine = tables(time_ids)
    base, segq, extk = mask_tables(segments, variates)
    gain1 = attn_gain[None, :]
    gain2 = ffn_gain[None, :]
    xn, q, k, v, cosine, sine = qkv_call(block_input, gain1, w3, cosine, sine)
    attended, o32, extq = attn_fwd_call(q, k, v, base, segq, extk, head_bias)
    mid, xn2 = attn_out_call(block_input, attended, w_out, gain2)
    ffn_part, gx_part, gk, uk, rg, ru, dk, rd, late_x, late_y = ffn_call(xn2, cotangent, pair_rows(w_gate_up), w_down)
    late_x = lax.ppermute(late_x, "dp", [(d, d ^ 1) for d in range(16)])
    late_y = lax.ppermute(late_y, "dp", [(d, d ^ 2) for d in range(16)])
    block_output, grad_mid, do, g_out, g_gain2 = ffn_back_call(
        gx_part, ffn_part, mid, cotangent, gain2, w_out, attended
    )
    dqkv, g_bias = attn_bwd_call(q, k, v, do, o32, extq, extk, variates[None, :], cosine, sine)
    sum_a, sum_b, input_grad, small = sum_call(
        gk, rg, uk, ru, late_x, late_y, dk, rd, g_out, dqkv, w3, xn, block_input, grad_mid, gain1, g_gain2, g_bias
    )
    sum_a = sum_a.reshape(2, 4, HALF_ROWS, WIDE)
    sum_b = sum_b.reshape(2, 4, HALF_ROWS, WIDE)
    heads = head_bias.shape[1]
    g_gate_up, g_down, g_qkv, g_out, g_gain1, g_gain2, g_bias, block_output, input_grad = widen_call(
        sum_a, sum_b, small, heads, block_output, input_grad
    )
    return (
        block_output, input_grad, g_gain1[0], jnp.transpose(g_qkv, (1, 0, 2)), g_bias, g_out, g_gain2[0], g_gate_up, g_down,
    )


def rope_tables(time_ids, head_dim):
    half_dim = head_dim // 2
    freqs = jnp.exp(jnp.arange(half_dim, dtype=jnp.float32) * (-2.0 * math.log(10000.0) / head_dim))
    angles = time_ids.astype(jnp.float32)[:, None] * freqs[None, :]
    return (jnp.cos(angles)[:, None, :], jnp.sin(angles)[:, None, :])


def rotate(vectors, cosine, sine_part):
    half_dim = vectors.shape[-1] // 2
    first_half = vectors[..., :half_dim]
    second_half = vectors[..., half_dim:]
    return jnp.concatenate(
        [
            first_half * cosine - second_half * sine_part,
            second_half * cosine + first_half * sine_part,
        ],
        axis=-1,
    )


def rotate_back(grads, cosine, sine_part):
    half_dim = grads.shape[-1] // 2
    first_half = grads[..., :half_dim]
    second_half = grads[..., half_dim:]
    return jnp.concatenate(
        [
            first_half * cosine + second_half * sine_part,
            second_half * cosine - first_half * sine_part,
        ],
        axis=-1,
    )


def norm_rows(rows_now, gain):
    inverse = lax.rsqrt(jnp.mean(rows_now * rows_now, axis=-1, keepdims=True) + EPSILON)
    return (rows_now * inverse * gain, inverse)


def plain_norm_back(rows_now, inverse, gain, grads):
    scaled = grads * gain
    gain_grad = jnp.sum(grads * rows_now * inverse, axis=0)
    rows_grad = inverse * scaled - rows_now * (inverse * inverse * inverse) * jnp.mean(
        scaled * rows_now, axis=-1, keepdims=True
    )
    return (rows_grad, gain_grad)


def scores_of(queries, keys_rot, same_var, allowed, head_bias, score_scale):
    raw_scores = (
        jnp.einsum("sqhd,skhd->shqk", queries, keys_rot, preferred_element_type=jnp.float32)
        * score_scale
    )
    biased = raw_scores + jnp.where(
        same_var[:, None], head_bias[0][None, :, None, None], head_bias[1][None, :, None, None]
    )
    return jnp.where(allowed[:, None], biased, MASKED)


def plain_local(
    block_input,
    segments,
    variates,
    time_ids,
    attn_gain,
    w_qkv,
    head_bias,
    w_out,
    ffn_gain,
    w_gate_up,
    w_down,
    cotangent,
):
    row_count = block_input.shape[0]
    heads_here = head_bias.shape[1]
    head_dim = w_qkv.shape[2] // heads_here
    seq_count = row_count // LEN
    score_scale = head_dim ** (-0.5)
    input_rows = block_input.astype(jnp.float32)
    attn_normed, attn_inverse = norm_rows(input_rows, attn_gain)
    attn_normed_low = attn_normed.astype(jnp.bfloat16)
    projected = jnp.einsum(
        "td,dck->tck", attn_normed_low, w_qkv, preferred_element_type=jnp.float32
    )
    cosine, sine_part = rope_tables(time_ids, head_dim)
    head_shape = (row_count, heads_here, head_dim)
    seq_shape = (seq_count, LEN, heads_here, head_dim)
    queries = (
        rotate(projected[:, 0].reshape(head_shape), cosine, sine_part)
        .astype(jnp.bfloat16)
        .reshape(seq_shape)
    )
    keys_rot = (
        rotate(projected[:, 1].reshape(head_shape), cosine, sine_part)
        .astype(jnp.bfloat16)
        .reshape(seq_shape)
    )
    values = projected[:, 2].astype(jnp.bfloat16).reshape(seq_shape)
    seg_ids = segments.reshape(seq_count, LEN)
    var_ids = variates.reshape(seq_count, LEN)
    allowed = seg_ids[:, :, None] == seg_ids[:, None, :]
    same_var = var_ids[:, :, None] == var_ids[:, None, :]
    scores = scores_of(queries, keys_rot, same_var, allowed, head_bias, score_scale)
    row_max = jnp.max(scores, axis=-1, keepdims=True)
    exp_total = jnp.sum(jnp.exp(scores - row_max), axis=-1, keepdims=True)
    log_total = row_max + jnp.log(exp_total)
    probs_low = jnp.exp(scores - log_total).astype(jnp.bfloat16)
    attended = jnp.einsum("shqk,skhd->sqhd", probs_low, values, preferred_element_type=jnp.float32)
    attended = attended.reshape(row_count, heads_here * head_dim).astype(jnp.bfloat16)
    attn_branch = lax.psum(
        jnp.dot(attended, w_out, preferred_element_type=jnp.float32).astype(jnp.bfloat16), "tensor"
    ).astype(jnp.float32)
    mid_rows = input_rows + attn_branch
    ffn_normed, ffn_inverse = norm_rows(mid_rows, ffn_gain)
    ffn_normed_low = ffn_normed.astype(jnp.bfloat16)
    gate_up = jnp.einsum(
        "td,dcf->tcf", ffn_normed_low, w_gate_up, preferred_element_type=jnp.float32
    )
    gate_vals = gate_up[:, 0]
    up_vals = gate_up[:, 1]
    sigmoid_gate = jax.nn.sigmoid(gate_vals)
    silu_gate = gate_vals * sigmoid_gate
    hidden_low = (silu_gate * up_vals).astype(jnp.bfloat16)
    ffn_branch = lax.psum(
        jnp.dot(hidden_low, w_down, preferred_element_type=jnp.float32).astype(jnp.bfloat16),
        "tensor",
    ).astype(jnp.float32)
    block_output = (mid_rows + ffn_branch).astype(jnp.bfloat16)
    grad_down = jnp.einsum("tf,td->fd", hidden_low, cotangent, preferred_element_type=jnp.float32)
    grad_hidden = jnp.einsum("td,fd->tf", cotangent, w_down, preferred_element_type=jnp.float32)
    grad_gate = grad_hidden * up_vals * sigmoid_gate * (1.0 + gate_vals * (1.0 - sigmoid_gate))
    grad_up = grad_hidden * silu_gate
    grad_gate_up = jnp.stack([grad_gate, grad_up], axis=1).astype(jnp.bfloat16)
    grad_w_gate_up = jnp.einsum(
        "td,tcf->dcf", ffn_normed_low, grad_gate_up, preferred_element_type=jnp.float32
    )
    grad_ffn_normed = lax.psum(
        jnp.einsum(
            "tcf,dcf->td", grad_gate_up, w_gate_up, preferred_element_type=jnp.float32
        ).astype(jnp.bfloat16),
        "tensor",
    ).astype(jnp.float32)
    norm_grad_mid, grad_ffn_gain = plain_norm_back(mid_rows, ffn_inverse, ffn_gain, grad_ffn_normed)
    grad_mid = cotangent.astype(jnp.float32) + norm_grad_mid
    grad_branch = grad_mid.astype(jnp.bfloat16)
    grad_w_out = jnp.einsum("tk,td->kd", attended, grad_branch, preferred_element_type=jnp.float32)
    grad_attended = jnp.einsum("td,kd->tk", grad_branch, w_out, preferred_element_type=jnp.float32)
    grad_attended = grad_attended.astype(jnp.bfloat16).reshape(seq_shape)
    scores_again = scores_of(queries, keys_rot, same_var, allowed, head_bias, score_scale)
    probs_again = jnp.exp(scores_again - log_total)
    probs_again_low = probs_again.astype(jnp.bfloat16)
    grad_probs = jnp.einsum(
        "sqhd,skhd->shqk", grad_attended, values, preferred_element_type=jnp.float32
    )
    grad_values = jnp.einsum(
        "shqk,sqhd->skhd", probs_again_low, grad_attended, preferred_element_type=jnp.float32
    )
    grad_scores = probs_again * (
        grad_probs - jnp.sum(probs_again * grad_probs, axis=-1, keepdims=True)
    )
    grad_scores_low = grad_scores.astype(jnp.bfloat16)
    same_low = same_var.astype(jnp.bfloat16)
    other_low = jnp.logical_not(same_var).astype(jnp.bfloat16)
    grad_bias = jnp.stack(
        [
            jnp.einsum(
                "shqk,sqk->h", grad_scores_low, same_low, preferred_element_type=jnp.float32
            ),
            jnp.einsum(
                "shqk,sqk->h", grad_scores_low, other_low, preferred_element_type=jnp.float32
            ),
        ],
        axis=0,
    )
    grad_queries = (
        jnp.einsum("shqk,skhd->sqhd", grad_scores_low, keys_rot, preferred_element_type=jnp.float32)
        * score_scale
    )
    grad_keys = (
        jnp.einsum("shqk,sqhd->skhd", grad_scores_low, queries, preferred_element_type=jnp.float32)
        * score_scale
    )
    grad_query_lin = rotate_back(grad_queries.reshape(head_shape), cosine, sine_part).reshape(
        row_count, heads_here * head_dim
    )
    grad_key_lin = rotate_back(grad_keys.reshape(head_shape), cosine, sine_part).reshape(
        row_count, heads_here * head_dim
    )
    grad_value_lin = grad_values.reshape(row_count, heads_here * head_dim)
    grad_projected = jnp.stack([grad_query_lin, grad_key_lin, grad_value_lin], axis=1).astype(
        jnp.bfloat16
    )
    grad_w_qkv = jnp.einsum(
        "td,tck->dck", attn_normed_low, grad_projected, preferred_element_type=jnp.float32
    )
    grad_attn_normed = lax.psum(
        jnp.einsum("tck,dck->td", grad_projected, w_qkv, preferred_element_type=jnp.float32).astype(
            jnp.bfloat16
        ),
        "tensor",
    ).astype(jnp.float32)
    norm_grad_input, grad_attn_gain = plain_norm_back(
        input_rows, attn_inverse, attn_gain, grad_attn_normed
    )
    input_grad = grad_mid + norm_grad_input
    grad_attn_gain, grad_w_qkv, grad_bias, grad_w_out, grad_ffn_gain, grad_w_gate_up, grad_down = (
        lax.psum(
            (
                grad_attn_gain,
                grad_w_qkv,
                grad_bias,
                grad_w_out,
                grad_ffn_gain,
                grad_w_gate_up,
                grad_down,
            ),
            "dp",
        )
    )
    return (
        block_output,
        input_grad,
        grad_attn_gain,
        grad_w_qkv,
        grad_bias,
        grad_w_out,
        grad_ffn_gain,
        grad_w_gate_up,
        grad_down,
    )


def solution(mesh):
    placed = (
        P("dp", None), P("dp"), P("dp"), P("dp"), P(), P(None, None, "tensor"), P(None, "tensor"),
        P("tensor", None), P(), P(None, None, "tensor"), P("tensor", None), P("dp", None),
    )
    fast = (mesh.shape["dp"], mesh.shape["tensor"]) == (16, 2)
    return jax.shard_map(
        fast_local if fast else plain_local,
        mesh=mesh,
        in_specs=placed,
        out_specs=(
            P("dp", None), P("dp", None), P(), P(None, None, "tensor"), P(None, "tensor"), P("tensor", None), P(),
            P(None, None, "tensor"), P("tensor", None),
        ),
        check_vma=False,
    )
```

```python
import functools
import math

import jax
import jax.numpy as jnp
from jax import lax
from jax.experimental import pallas as pl
from jax.experimental.pallas import tpu as pltpu
from jax.sharding import PartitionSpec as P

LEN = 1024
EPSILON = 1e-05
MASKED = -1000000000.0
BF = jnp.bfloat16
F32 = jnp.float32
MESH = pl.DeviceIdType.MESH
VMEM_LIMIT = 60 * 1024 * 1024
VMEM_MOST = 67043328 - 512 * 1024
LANES = 128
HEAD = 64
VAR_COLS = 4
SEG_COL = 12
ONE_COL = 20
ROWS = 32
LAGS = (2, 4, 6, 8, 10)
SWAP_ROWS = 32
HALF_ROWS = 512
QUARTER_ROWS = HALF_ROWS // 2
GROUP_ROWS = 4 * HALF_ROWS
KEPT_ROWS = GROUP_ROWS - QUARTER_ROWS
WIDE = 1024
SMALL = 8
QBLK = 256
FFN_ROWS = 1024
FFN_COLS = 512


def dot_nn(a, b):
    return lax.dot_general(a, b, (((1,), (0,)), ((), ())), preferred_element_type=F32)


def dot_nt(a, b):
    return lax.dot_general(a, b, (((1,), (1,)), ((), ())), preferred_element_type=F32)


def dot_tn(a, b):
    return lax.dot_general(a, b, (((0,), (0,)), ((), ())), preferred_element_type=F32)


def whole_spec():
    return pl.BlockSpec(memory_space=pltpu.VMEM)


def split3(v):
    hi = v.astype(BF).astype(F32)
    mid = (v - hi).astype(BF).astype(F32)
    return hi, mid, v - hi - mid


def half_swap(u):
    lane = lax.broadcasted_iota(jnp.int32, u.shape, 1) % HEAD
    return jnp.where(lane < HEAD // 2, pltpu.roll(u, LANES - HEAD // 2, 1), pltpu.roll(u, HEAD // 2, 1))


def qkv_body(x_ref, gain_ref, w_ref, cos_ref, sin_ref, xn_ref, q_ref, k_ref, v_ref, cos_out, sin_out):
    x = x_ref[...].astype(F32)
    inv = lax.rsqrt(jnp.mean(x * x, axis=-1, keepdims=True) + EPSILON)
    xn = (x * inv * gain_ref[...]).astype(BF)
    xn_ref[...] = xn
    half = cos_ref[...].T
    cosine = jnp.concatenate([half] * 4, axis=1)
    half = sin_ref[...].T
    sine = jnp.concatenate([-half, half] * 2, axis=1)
    cos_out[...] = cosine
    sin_out[...] = sine
    for part, out, factor in ((0, q_ref, HEAD**-0.5), (1, k_ref, 1.0)):
        lin = dot_nn(xn, w_ref[part])
        for s in range(lin.shape[1] // LANES):
            u = lin[:, s * LANES : (s + 1) * LANES]
            rot = (u * cosine + half_swap(u) * sine).astype(BF)
            if factor != 1.0:
                rot = (rot.astype(F32) * factor).astype(BF)
            out[:, s * LANES : (s + 1) * LANES] = rot
    v_ref[...] = dot_nn(xn, w_ref[2]).astype(BF)


def qkv_call(x, gain, w, cosine, sine):
    rows, dim = x.shape
    width = w.shape[2]
    blk = min(256, rows)
    row = lambda cols: pl.BlockSpec((blk, cols), lambda i: (i, 0))
    return pl.pallas_call(
        qkv_body,
        grid=(rows // blk,),
        out_shape=[jax.ShapeDtypeStruct((rows, dim), BF)]
        + [jax.ShapeDtypeStruct((rows, width), BF)] * 3
        + [jax.ShapeDtypeStruct((rows, LANES), F32)] * 2,
        in_specs=[
            row(dim),
            pl.BlockSpec((1, dim), lambda i: (0, 0)),
            pl.BlockSpec(w.shape, lambda i: (0, 0, 0)),
            pl.BlockSpec((HEAD // 2, blk), lambda i: (0, i)),
            pl.BlockSpec((HEAD // 2, blk), lambda i: (0, i)),
        ],
        out_specs=[row(dim), row(width), row(width), row(width), row(LANES), row(LANES)],
        compiler_params=pltpu.CompilerParams(vmem_limit_bytes=VMEM_LIMIT),
        name="qkv",
    )(x, gain, w, cosine, sine)


def attn_fwd_body(
    q_ref, k_ref, v_ref, base_ref, segq_ref, extk_ref, bias_ref, o_ref, o32_ref, extq_ref
):
    rows = q_ref.shape[0]
    blk = 256
    lane = lax.broadcasted_iota(jnp.int32, (blk, LANES), 1)
    kind = lax.broadcasted_iota(jnp.int32, (1, LANES), 1) // VAR_COLS
    bias_rows = []
    for h in range(2):
        head = pl.program_id(0) * 2 + h
        hi, mid, low = split3(jnp.full((1, LANES), bias_ref[0, head] - bias_ref[1, head], F32))
        bias_rows.append(jnp.where(kind == 0, hi, jnp.where(kind == 1, mid, jnp.where(kind == 2, low, 0.0))))
    kx = jnp.concatenate([k_ref[...], extk_ref[...]], axis=1)
    ones = jnp.ones((rows, LANES), BF)
    vx = jnp.concatenate([v_ref[...], ones], axis=1)
    for i in range(rows // blk):
        sl = slice(i * blk, (i + 1) * blk)
        q = q_ref[sl, :].astype(F32)
        base = base_ref[sl, :]
        segq = segq_ref[sl, :]
        outs = []
        for h in range(2):
            ext = base * bias_rows[h] + segq
            mine = (lane >= HEAD) if h else (lane < HEAD)
            qx = jnp.concatenate([jnp.where(mine, q, 0.0), ext], axis=1).astype(BF)
            s = dot_nt(qx, kx)
            top = jnp.max(s, axis=-1, keepdims=True)
            p = jnp.exp(s - top).astype(BF)
            ox = dot_nn(p, vx)
            total = ox[:, LANES:]
            outs.append(ox[:, :LANES] / total)
            lse = top + jnp.log(total)
            hi, mid, low = split3(lse)
            ext = jnp.where(
                lane == ONE_COL, -hi, jnp.where(lane == ONE_COL + 1, -mid, jnp.where(lane == ONE_COL + 2, -low, ext))
            )
            extq_ref[0, h, sl, :] = ext.astype(BF)
        o = jnp.where(lane < HEAD, outs[0], outs[1])
        o32_ref[sl, :] = o
        o_ref[sl, :] = o.astype(BF)


def attn_fwd_call(q, k, v, base, segq, extk, head_bias):
    rows, width = q.shape
    pairs = width // LANES
    col = pl.BlockSpec((rows, LANES), lambda p: (0, p))
    full = pl.BlockSpec((rows, LANES), lambda p: (0, 0))
    return pl.pallas_call(
        attn_fwd_body,
        grid=(pairs,),
        out_shape=[
            jax.ShapeDtypeStruct((rows, width), BF),
            jax.ShapeDtypeStruct((rows, width), F32),
            jax.ShapeDtypeStruct((pairs, 2, rows, LANES), BF),
        ],
        in_specs=[
            col, col, col, full, full, full,
            pl.BlockSpec(memory_space=pltpu.SMEM),
        ],
        out_specs=[col, col, pl.BlockSpec((1, 2, rows, LANES), lambda p: (p, 0, 0, 0))],
        compiler_params=pltpu.CompilerParams(vmem_limit_bytes=VMEM_LIMIT),
        name="attn_fwd",
    )(q, k, v, base, segq, extk, head_bias)


def attn_bwd_body(
    q_ref, k_ref, v_ref, do_ref, o32_ref, extq_ref, extk_ref, var_ref, cos_ref, sin_ref, d_ref, gb_ref, dqt_ref
):
    rows = q_ref.shape[0]
    blk = 256
    lane = lax.broadcasted_iota(jnp.int32, (blk, LANES), 1)
    kinds = lax.broadcasted_iota(jnp.int32, (8, blk), 0)
    kx = jnp.concatenate([k_ref[...], extk_ref[...]], axis=1)
    kxt = kx.T
    lane_all = lax.broadcasted_iota(jnp.int32, (rows, LANES), 1)
    vx = jnp.concatenate([v_ref[...], jnp.where(lane_all < 3, 1.0, 0.0).astype(BF)], axis=1)
    dv = jnp.zeros((rows, LANES), F32)
    dk = jnp.zeros((rows, LANES), F32)
    for h in range(2):
        same = jnp.zeros((8, blk), F32)
        other = jnp.zeros((8, blk), F32)
        for i in range(rows // blk):
            sl = slice(i * blk, (i + 1) * blk)
            mine = (lane >= HEAD) if h else (lane < HEAD)
            q = jnp.where(mine, q_ref[sl, :].astype(F32), 0.0).astype(BF)
            do32 = jnp.where(mine, do_ref[sl, :].astype(F32), 0.0)
            do = do32.astype(BF)
            delta = jnp.sum(do32 * o32_ref[sl, :], axis=-1, keepdims=True)
            hi, mid, low = split3(delta)
            dext = jnp.where(lane == 0, -hi, jnp.where(lane == 1, -mid, jnp.where(lane == 2, -low, 0.0))).astype(BF)
            st = dot_nt(kx, jnp.concatenate([q, extq_ref[0, h, sl, :]], axis=1))
            pt = jnp.exp(st)
            dpt = dot_nt(vx, jnp.concatenate([do, dext], axis=1))
            dst = (pt * dpt).astype(BF)
            dv = dv + dot_nn(pt.astype(BF), do)
            dk = dk + dot_nn(dst, q)
            dqt = dot_nn(kxt, dst)
            dqt_ref[h * HEAD : (h + 1) * HEAD, sl] = dqt[h * HEAD : (h + 1) * HEAD, :]
            g = dqt[LANES : LANES + 8, :]
            match = kinds == var_ref[:, sl]
            same = same + jnp.where(match, g, 0.0)
            other = other + jnp.where(match | (kinds >= VAR_COLS), 0.0, g)
        gb_ref[0, h, 0] = same
        gb_ref[0, h, 1] = other
    cosine = cos_ref[...]
    sine = sin_ref[...]
    dq = dqt_ref[...].T * HEAD**-0.5
    d_ref[0] = (dq * cosine - half_swap(dq) * sine).astype(BF)
    d_ref[1] = (dk * cosine - half_swap(dk) * sine).astype(BF)
    d_ref[2] = dv.astype(BF)


def attn_bwd_call(q, k, v, do, o32, extq, extk, variates, cosine, sine):
    rows, width = q.shape
    pairs = width // LANES
    col = pl.BlockSpec((rows, LANES), lambda p: (0, p))
    full = pl.BlockSpec((rows, LANES), lambda p: (0, 0))
    blk = 256
    return pl.pallas_call(
        attn_bwd_body,
        grid=(pairs,),
        out_shape=[jax.ShapeDtypeStruct((3, rows, width), BF), jax.ShapeDtypeStruct((pairs, 2, 2, 8, blk), F32)],
        in_specs=[
            col, col, col, col, col,
            pl.BlockSpec((1, 2, rows, LANES), lambda p: (p, 0, 0, 0)),
            full,
            pl.BlockSpec((1, rows), lambda p: (0, 0)),
            full, full,
        ],
        out_specs=[pl.BlockSpec((3, rows, LANES), lambda p: (0, 0, p)), pl.BlockSpec((1, 2, 2, 8, blk), lambda p: (p, 0, 0, 0, 0))],
        scratch_shapes=[pltpu.VMEM((LANES, rows), F32)],
        compiler_params=pltpu.CompilerParams(vmem_limit_bytes=VMEM_MOST),
        name="attn_bwd",
    )(q, k, v, do, o32, extq, extk, variates, cosine, sine)


def partner_barrier():
    dp = lax.axis_index("dp")
    other = 1 - lax.axis_index("tensor")
    barrier = pltpu.get_barrier_semaphore()
    pl.semaphore_signal(barrier, inc=1, device_id=(dp, other), device_id_type=MESH)
    pl.semaphore_wait(barrier, 1)
    return (dp, other)


def send_rows(src, dst, sl, ssem, rsem, peer):
    return pltpu.make_async_remote_copy(
        src_ref=src.at[sl], dst_ref=dst.at[sl], send_sem=ssem, recv_sem=rsem, device_id=peer, device_id_type=MESH
    )


CHUNKS = 4


def attn_out_body(o_ref, w_ref, gain_ref, x, mid, xn, x_v, mid_v, xn_v, mine, theirs, ssem, rsem, lsem, osem):
    rows = x.shape[0]
    blk = rows // CHUNKS

    def rows_of(c):
        return pl.ds(pl.multiple_of(c * blk, blk), blk)

    def load(c):
        return pltpu.make_async_copy(x.at[rows_of(c)], x_v.at[rows_of(c)], lsem.at[c])

    def stores(c):
        return [
            pltpu.make_async_copy(mid_v.at[rows_of(c)], mid.at[rows_of(c)], osem.at[0, c]),
            pltpu.make_async_copy(xn_v.at[rows_of(c)], xn.at[rows_of(c)], osem.at[1, c]),
        ]

    for c in range(CHUNKS):
        load(c).start()
    peer = partner_barrier()

    def core_copy(c):
        return send_rows(mine, theirs, rows_of(c), ssem.at[c], rsem.at[c], peer)

    @pl.loop(0, CHUNKS)
    def _(c):
        mine[rows_of(c), :] = dot_nn(o_ref[rows_of(c), :], w_ref[...]).astype(BF)
        core_copy(c).start()

    @pl.loop(0, CHUNKS)
    def _(c):
        r = rows_of(c)
        load(c).wait()
        core_copy(c).wait_recv()
        total = x_v[r, :].astype(F32) + (mine[r, :].astype(F32) + theirs[r, :].astype(F32))
        inv = lax.rsqrt(jnp.mean(total * total, axis=-1, keepdims=True) + EPSILON)
        mid_v[r, :] = total
        xn_v[r, :] = (total * inv * gain_ref[...]).astype(BF)
        for copy in stores(c):
            copy.start()

    for c in range(CHUNKS):
        core_copy(c).wait_send()
        for copy in stores(c):
            copy.wait()


def attn_out_call(x, o, w, gain):
    rows, dim = x.shape
    any_spec = pl.BlockSpec(memory_space=pl.ANY)
    low = pltpu.VMEM((rows, dim), BF)
    dma = pltpu.SemaphoreType.DMA
    return pl.pallas_call(
        attn_out_body,
        out_shape=[jax.ShapeDtypeStruct((rows, dim), F32), jax.ShapeDtypeStruct((rows, dim), BF)],
        in_specs=[whole_spec()] * 3 + [any_spec],
        out_specs=[any_spec] * 2,
        scratch_shapes=[
            low, pltpu.VMEM((rows, dim), F32), low, low, low,
            dma((CHUNKS,)), dma((CHUNKS,)), dma((CHUNKS,)), dma((2, CHUNKS)),
        ],
        compiler_params=pltpu.CompilerParams(collective_id=1, has_side_effects=True, vmem_limit_bytes=VMEM_LIMIT),
        name="attn_out",
    )(o, w, gain, x)


LATE = 2
SLOTS = 2
PART = FFN_COLS // 4


def sent(copy):
    copy.wait_send() if copy.is_remote else copy.wait()


def grid_bits():
    dp = lax.axis_index("dp")
    return dp, dp % 2, (dp // 2) % 2, peers_of(dp)[3], peers_of(dp)[4]


def ffn_body(
    xn_ref, ct_ref, w0_ref, wn_ref, wd_ref,
    out_ref, gx_ref, gk_ref, uk_ref, rg, ru, dk, rd, late_x, late_y,
    acc_o, acc_g, hid, dg, du, xt, wgu, away_w, away_d, ws, wr, ds, dr,
):
    j = pl.program_id(0)
    t = lax.axis_index("tensor")
    dp, x, y, px, py = grid_bits()
    steps = pl.num_programs(0)
    rows = xn_ref.shape[0]
    blk = wd_ref.shape[0]
    per = WIDE // blk
    early = 2 * per - LATE
    slot = lax.rem(j, SLOTS)
    near = (px, py)
    bits = (x, y)
    arrays = ((rg, late_x), (ru, late_y))

    def remote(src, dst, ssem, rsem, peer):
        return pltpu.make_async_remote_copy(
            src_ref=src, dst_ref=dst, send_sem=ssem, recv_sem=rsem, device_id=(peer, t), device_id_type=MESH
        )

    def wide_early(k, at):
        cols = pl.ds(pl.multiple_of(lax.rem(at, per) * blk, blk), blk)
        s = lax.rem(at, SLOTS)
        return remote(away_w.at[k, s], arrays[k][0].at[:, cols], ws.at[k, s], wr.at[k], near[k])

    def wide_late(k, at):
        cols = pl.ds(pl.multiple_of((at - early) * blk, blk), blk)
        s = lax.rem(at, SLOTS)
        return pltpu.make_async_copy(away_w.at[k, s], arrays[k][1].at[pl.ds(0, HALF_ROWS), cols], ws.at[k, s])

    def wide_do(at, act):
        for k in range(2):

            @pl.when(at < early)
            def _():
                act(wide_early(k, at))

            @pl.when(at >= early)
            def _():
                act(wide_late(k, at))

    def down_rows(g, half):
        return pl.ds(pl.multiple_of(g * 2 * PART + half * PART, PART), PART)

    def down_keep(g, at):
        s = lax.rem(at, SLOTS)
        return pltpu.make_async_copy(
            away_d.at[s, down_rows(g, bits[g])], dk.at[g, pl.ds(pl.multiple_of(at * PART, PART), PART)], ds.at[g, s]
        )

    def down_send(g, at):
        s = lax.rem(at, SLOTS)
        rows_at = pl.ds(pl.multiple_of(at * PART, PART), PART)
        return remote(away_d.at[s, down_rows(g, 1 - bits[g])], rd.at[g, rows_at], ds.at[2 + g, s], dr.at[g], near[g])

    def down_late(g, at):
        s = lax.rem(at, SLOTS)
        rows_at = pl.ds(pl.multiple_of(HALF_ROWS + (at - early) * PART, PART), PART)
        return pltpu.make_async_copy(
            away_d.at[s, down_rows(g, 1 - bits[g])], arrays[g][1].at[rows_at], ds.at[2 + g, s]
        )

    def down_do(at, act):
        for g in range(2):
            act(down_keep(g, at))

            @pl.when(at < early)
            def _():
                act(down_send(g, at))

            @pl.when(at >= early)
            def _():
                act(down_late(g, at))

    def part_rows(src, to, r):
        turned = jnp.swapaxes(src[r].astype(F32), 0, 1)
        for k in range(8):
            s = k // 2
            wgu[to, k % 2, r, s * LANES : (s + 1) * LANES] = turned[k].astype(BF)

    @pl.when(j == 0)
    def _():
        barrier = pltpu.get_barrier_semaphore()
        for peer in near:
            pl.semaphore_signal(barrier, inc=1, device_id=(peer, t), device_id_type=MESH)
        pl.semaphore_wait(barrier, 2)
        acc_o[...] = jnp.zeros_like(acc_o)
        acc_g[...] = jnp.zeros_like(acc_g)
        xt[...] = xn_ref[...].T

        @pl.loop(0, rows // LANES)
        def _(c):
            part_rows(w0_ref, 0, pl.ds(pl.multiple_of(c * LANES, LANES), LANES))

    now = lax.rem(j, 2)
    wg = wgu[now, 0]
    wu = wgu[now, 1]
    wd = wd_ref[...]
    part_rows(wn_ref, 1 - now, slice(None))
    for i in range(rows // FFN_ROWS):
        sl = slice(i * FFN_ROWS, (i + 1) * FFN_ROWS)
        xn = xn_ref[sl, :]
        gate = dot_nn(xn, wg)
        up = dot_nn(xn, wu)
        gh = dot_nt(ct_ref[sl, :], wd)
        sig = jax.nn.sigmoid(gate)
        silu = gate * sig
        hidden = (silu * up).astype(BF)
        dgate = (gh * up * sig * (1.0 + gate * (1.0 - sig))).astype(BF)
        dup = (gh * silu).astype(BF)
        hid[sl, :] = hidden
        dg[sl, :] = dgate
        du[sl, :] = dup
        acc_o[sl, :] += dot_nn(hidden, wd)
        acc_g[sl, :] += dot_nt(dgate, wg) + dot_nt(dup, wu)

    @pl.when(j >= SLOTS)
    def _():
        wide_do(j - SLOTS, sent)
        down_do(j - SLOTS, sent)

    away_d[slot] = dot_tn(hid[...], ct_ref[...]).astype(BF)
    down_do(j, lambda copy: copy.start())
    for k, (part, keep, bit) in enumerate(((dg, gk_ref, x), (du, uk_ref, y))):
        rows_at = lambda half: pl.ds(pl.multiple_of(half * HALF_ROWS, HALF_ROWS), HALF_ROWS)
        away_w[k, slot] = dot_nn(xt[rows_at(1 - bit), :], part[...]).astype(BF)
        keep[0] = dot_nn(xt[rows_at(bit), :], part[...]).astype(BF)
    wide_do(j, lambda copy: copy.start())

    @pl.when(j == steps - 1)
    def _():
        out_ref[...] = acc_o[...].astype(BF)
        gx_ref[...] = acc_g[...].astype(BF)
        for back in range(SLOTS, 0, -1):
            wide_do(steps - back, sent)
            down_do(steps - back, sent)
        for k in range(2):
            part = arrays[k][0].at[:, pl.ds(0, early * blk)]
            remote(part, part, ws.at[k, 0], wr.at[k], near[k]).wait_recv()
        for g in range(2):
            part = rd.at[g, pl.ds(0, early * PART)]
            remote(part, part, ds.at[g, 0], dr.at[g], near[g]).wait_recv()


def ffn_call(xn, ct, w_pairs, wd):
    rows, dim = xn.shape
    hidden = wd.shape[0]
    blk = FFN_COLS
    per = WIDE // blk
    full = pl.BlockSpec((rows, dim), lambda j: (0, 0))
    steps = hidden // blk
    tiles = 2 * blk // LANES
    first_w = pl.BlockSpec((dim, tiles, LANES), lambda j: (0, 0, 0))
    next_w = pl.BlockSpec((dim, tiles, LANES), lambda j: (0, jnp.minimum(j + 1, steps - 1), 0))
    roww = pl.BlockSpec((blk, dim), lambda j: (j, 0))
    grad = pl.BlockSpec((1, HALF_ROWS, blk), lambda j: (j // per, 0, lax.rem(j, per)))
    any_spec = pl.BlockSpec(memory_space=pl.ANY)
    wide = jax.ShapeDtypeStruct((2, HALF_ROWS, dim), BF)
    early = hidden // blk - LATE
    come = jax.ShapeDtypeStruct((HALF_ROWS, early * blk), BF)
    late = jax.ShapeDtypeStruct((HALF_ROWS + LATE * PART, LATE * blk), BF)
    dma = pltpu.SemaphoreType.DMA
    return pl.pallas_call(
        ffn_body,
        grid=(hidden // blk,),
        in_specs=[full, full, first_w, next_w, roww],
        out_specs=[full, full, grad, grad] + [any_spec] * 6,
        out_shape=[jax.ShapeDtypeStruct((rows, dim), BF)] * 2
        + [wide, wide, come, come, wide, jax.ShapeDtypeStruct((2, early * PART, dim), BF), late, late],
        scratch_shapes=[pltpu.VMEM((rows, dim), F32)] * 2
        + [pltpu.VMEM((rows, blk), BF)] * 3
        + [
            pltpu.VMEM((dim, rows), BF),
            pltpu.VMEM((2, 2, dim, blk), BF),
            pltpu.VMEM((2, SLOTS, HALF_ROWS, blk), BF),
            pltpu.VMEM((SLOTS, blk, dim), BF),
            dma((2, SLOTS)), dma((2,)), dma((4, SLOTS)), dma((2,)),
        ],
        compiler_params=pltpu.CompilerParams(collective_id=5, has_side_effects=True, vmem_limit_bytes=VMEM_LIMIT),
        name="ffn",
    )(xn, ct, w_pairs, w_pairs, wd)


def pair_rows(w):
    dim, two, width = w.shape
    tiled = jnp.transpose(w.reshape(dim, two, width // LANES, LANES), (0, 2, 1, 3))
    return tiled.reshape(dim, two * width // LANES, LANES)


def widen_body(
    ga_ref, gb_ref, da_ref, db_ref, aa_ref, v_ref, o_ref, small_ref, rows_ref, ig_ref,
    gu_ref, down_ref, qkv_ref, out_ref, g1_ref, g2_ref, gbias_ref, rows_out, ig_out,
):
    tiles = WIDE // LANES
    for f in range(2):
        for q in range(tiles // 4):
            parts = []
            for k in range(8):
                s = q * 4 + k // 2
                parts.append((ga_ref, gb_ref)[k % 2][0, f, :, s * LANES : (s + 1) * LANES].astype(F32))
            at = (f * tiles + q * 4) * 2
            gu_ref[:, at : at + 8, :] = jnp.swapaxes(jnp.stack(parts), 0, 1)
    down_ref[:, 0, 0] = da_ref[0, 0].astype(F32).reshape(down_ref.shape[0], PART, WIDE)
    down_ref[:, 1, 0] = db_ref[0, 0].astype(F32).reshape(down_ref.shape[0], PART, WIDE)
    width = qkv_ref.shape[2]
    qkv_ref[0] = aa_ref[0, 0, :, :width].astype(F32)
    qkv_ref[1] = aa_ref[0, 0, :, width:].astype(F32)
    qkv_ref[2] = v_ref[0, 0].astype(F32)
    out_ref[...] = o_ref[0, 0].astype(F32)
    rows_out[...] = rows_ref[...]
    ig_out[...] = ig_ref[...]

    @pl.when(pl.program_id(0) == 0)
    def _():
        g1_ref[...] = small_ref[0:1, :]
        g2_ref[...] = small_ref[1:2, :]
        row = lax.broadcasted_iota(jnp.int32, gbias_ref.shape, 0)
        col = lax.broadcasted_iota(jnp.int32, gbias_ref.shape, 1)
        total = jnp.zeros(gbias_ref.shape, F32)
        for h in range(gbias_ref.shape[1]):
            for s in range(2):
                at = (h % 2 * 2 + s) * QBLK
                one = jnp.sum(small_ref[2 + h // 2 : 3 + h // 2, at : at + QBLK], axis=1, keepdims=True)
                total = jnp.where((row == s) & (col == h), one, total)
        gbias_ref[...] = total


def widen_call(a, b, small, heads, block_output, input_grad):
    blk = 256
    half = HALF_ROWS // blk
    tiles = 4 * WIDE // LANES
    width = WIDE // 2
    gate = pl.BlockSpec((1, 2, blk, WIDE), lambda i: (i // half, 0, lax.rem(i, half), 0))
    block = lambda n: pl.BlockSpec((1, 1, blk, WIDE), lambda i: (i // half, n, lax.rem(i, half), 0))
    fixed = lambda shape: pl.BlockSpec(shape, lambda i: (0, 0))
    rows = block_output.shape[0]
    steps = 2 * half
    share = pl.BlockSpec((rows // steps, WIDE), lambda i: (i, 0))
    gu, down, qkv, out, g1, g2, gbias, block_output, input_grad = pl.pallas_call(
        widen_body,
        grid=(2 * half,),
        out_shape=[
            jax.ShapeDtypeStruct((2 * HALF_ROWS, tiles, LANES), F32),
            jax.ShapeDtypeStruct((HALF_ROWS // PART, 2, 2, PART, WIDE), F32),
            jax.ShapeDtypeStruct((3, 2 * HALF_ROWS, width), F32),
            jax.ShapeDtypeStruct((HALF_ROWS, WIDE), F32),
            jax.ShapeDtypeStruct((1, WIDE), F32),
            jax.ShapeDtypeStruct((1, WIDE), F32),
            jax.ShapeDtypeStruct((2, heads), F32),
            jax.ShapeDtypeStruct(block_output.shape, BF),
            jax.ShapeDtypeStruct(input_grad.shape, F32),
        ],
        in_specs=[
            gate, gate, block(2), block(2), block(3),
            pl.BlockSpec((1, 1, blk, width), lambda i: (0, 3, lax.rem(i, half), i // half)),
            pl.BlockSpec((1, 1, blk // 2, WIDE), lambda i: (1, 3, i, 0)),
            fixed((SMALL, WIDE)),
            share,
            share,
        ],
        out_specs=[
            pl.BlockSpec((blk, tiles, LANES), lambda i: (i, 0, 0)),
            pl.BlockSpec((blk // PART, 2, 1, PART, WIDE), lambda i: (lax.rem(i, half), 0, i // half, 0, 0)),
            pl.BlockSpec((3, blk, width), lambda i: (0, i, 0)),
            pl.BlockSpec((blk // 2, WIDE), lambda i: (i, 0)),
            fixed((1, WIDE)),
            fixed((1, WIDE)),
            fixed((2, heads)),
            share,
            share,
        ],
        compiler_params=pltpu.CompilerParams(vmem_limit_bytes=VMEM_LIMIT),
        name="widen",
    )(a, b, a, b, a, b, b, small, block_output, input_grad)
    gu = jnp.transpose(gu.reshape(2 * HALF_ROWS, tiles // 2, 2, LANES), (0, 2, 1, 3)).reshape(2 * HALF_ROWS, 2, 2 * WIDE)
    return gu, down.reshape(4 * HALF_ROWS, WIDE), qkv, out, g1, g2, gbias, block_output, input_grad


def norm_back(rows_now, gain, grads):
    inv = lax.rsqrt(jnp.mean(rows_now * rows_now, axis=-1, keepdims=True) + EPSILON)
    scaled = grads * gain
    gain_grad = jnp.sum(grads * rows_now * inv, axis=0, keepdims=True)
    back = inv * scaled - rows_now * (inv * inv * inv) * jnp.mean(scaled * rows_now, axis=-1, keepdims=True)
    return back, gain_grad


def ffn_back_body(
    gain_ref, w_ref, at_ref, gx, fo, mid, ct,
    do_ref, gw_ref, gg_ref, out, gm,
    gx_in, fo_in, gx_v, fo_v, mid_v, ct_v, gm_v, out_v, gb, ssem, rsem, lsem, osem,
):
    rows = mid.shape[0]
    blk = rows // CHUNKS

    def rows_of(c):
        return pl.ds(pl.multiple_of(c * blk, blk), blk)

    def load(k, c):
        src, dst = ((gx, gx_v), (mid, mid_v), (ct, ct_v), (fo, fo_v))[k]
        return pltpu.make_async_copy(src.at[rows_of(c)], dst.at[rows_of(c)], lsem.at[k, c])

    def store(k, c):
        src, dst = ((gm_v, gm), (out_v, out))[k]
        return pltpu.make_async_copy(src.at[rows_of(c)], dst.at[rows_of(c)], osem.at[k, c])

    for c in range(CHUNKS):
        for k in range(4):
            load(k, c).start()
    peer = partner_barrier()

    def core_copy(n, c):
        src, dst = ((gx, gx_in), (fo, fo_in))[n]
        return send_rows(src, dst, rows_of(c), ssem.at[n * CHUNKS + c], rsem.at[n * CHUNKS + c], peer)

    for n in range(2):
        for c in range(CHUNKS):
            core_copy(n, c).start()
    gg_ref[...] = jnp.zeros_like(gg_ref)

    @pl.loop(0, CHUNKS)
    def _(c):
        r = rows_of(c)
        for k in range(3):
            load(k, c).wait()
        core_copy(0, c).wait_recv()
        grads = gx_v[r, :].astype(F32) + gx_in[r, :].astype(F32)
        back, gain_grad = norm_back(mid_v[r, :], gain_ref[...], grads)
        gg_ref[...] += gain_grad
        grad_mid = ct_v[r, :].astype(F32) + back
        gm_v[r, :] = grad_mid
        store(0, c).start()
        low = grad_mid.astype(BF)
        gb[r, :] = low
        do_ref[r, :] = dot_nt(low, w_ref[...]).astype(BF)

    @pl.loop(0, CHUNKS)
    def _(c):
        r = rows_of(c)
        load(3, c).wait()
        core_copy(1, c).wait_recv()
        out_v[r, :] = (mid_v[r, :] + (fo_v[r, :].astype(F32) + fo_in[r, :].astype(F32))).astype(BF)
        store(1, c).start()

    gw_ref[...] = dot_tn(at_ref[...], gb[...]).astype(BF)
    for c in range(CHUNKS):
        for k in range(2):
            core_copy(k, c).wait_send()
            store(k, c).wait()


def ffn_back_call(gx, fo, mid, ct, gain, w, at):
    rows, dim = mid.shape
    width = w.shape[0]
    any_spec = pl.BlockSpec(memory_space=pl.ANY)
    low = pltpu.VMEM((rows, dim), BF)
    wide = pltpu.VMEM((rows, dim), F32)
    dma = pltpu.SemaphoreType.DMA
    do, gw, gg, out, gm = pl.pallas_call(
        ffn_back_body,
        out_shape=[
            jax.ShapeDtypeStruct((rows, width), BF),
            jax.ShapeDtypeStruct((width, dim), BF),
            jax.ShapeDtypeStruct((1, dim), F32),
            jax.ShapeDtypeStruct((rows, dim), BF),
            jax.ShapeDtypeStruct((rows, dim), F32),
        ],
        in_specs=[whole_spec()] * 3 + [any_spec] * 4,
        out_specs=[whole_spec()] * 3 + [any_spec] * 2,
        scratch_shapes=[
            low, low, low, low, wide, low, wide, low, low,
            dma((2 * CHUNKS,)), dma((2 * CHUNKS,)), dma((4, CHUNKS)), dma((2, CHUNKS)),
        ],
        compiler_params=pltpu.CompilerParams(collective_id=2, has_side_effects=True, vmem_limit_bytes=VMEM_MOST),
        name="ffn_back",
    )(gain, w, at, gx, fo, mid, ct)
    return out, gm, do, gw, gg


def peers_of(dp):
    z = dp // 4
    y = (dp // 2) % 2
    x = dp % 2
    at = lambda zz, yy, xx: zz * 4 + yy * 2 + xx
    return z, y, x, at(z, y, 1 - x), at(z, 1 - y, x), at(z + 1 - 2 * (z % 2), y, x), at(3 - z, y, x)


def sum_body(
    gk, rg, uk, ru, late_x, late_y, dk, rd, go, dqkv, w3, xn, xin, gmid, gain_ref, gain2_ref, bias_ref, out_a, out_b, ig, small_out,
    L, S, Z, R, Y, DL, DS, DA, G, sb, st, dl, wb, xb, mine_rows, their_rows, away_rows, xc, gc, ic,
    loc, s1s, s1r, sends, zr, rr, yr, ar, xr, lo, ss, sr, ld, cs, cr, xg, io, s2s, s2r, gs, gr,
):
    dp = lax.axis_index("dp")
    t = lax.axis_index("tensor")
    z, y, x, px, py, zn, mm = peers_of(dp)
    is_mid = (z == 1) | (z == 2)
    is_end = (z == 0) | (z == 3)
    mine = jnp.where(z == 2, WIDE // 2, 0)
    others = WIDE // 2 - mine
    n = KEPT_ROWS // ROWS
    cut_at = 2 * HALF_ROWS // ROWS
    tail_at = (2 * HALF_ROWS + QUARTER_ROWS) // ROWS
    starts = (0, HALF_ROWS // ROWS, cut_at, tail_at)
    first = (px, py)
    last = (py, px)
    outs = (out_a, out_b)
    owner = (x, y)
    bit = (y, x)
    F = S

    def remote(src, dst, ssem, rsem, peer, core=t):
        return pltpu.make_async_remote_copy(
            src_ref=src, dst_ref=dst, send_sem=ssem, recv_sem=rsem, device_id=(peer, core), device_id_type=MESH
        )

    def loads(g, b):
        rows = pl.ds(b * HALF_ROWS, HALF_ROWS)
        near = (rg, ru)[g]
        late = (late_x, late_y)[g]
        top = pl.ds(0, HALF_ROWS)
        if b < 2:
            copies = [((gk, uk)[g].at[b], L.at[g, rows])]
        else:
            copies = [(dk.at[g], DL.at[g])]
        if b == 0:
            copies.append((near.at[:, pl.ds(0, WIDE)], S.at[g, rows]))
        elif b == 1:
            cut = near.shape[1] - WIDE
            if cut:
                copies.append((near.at[:, pl.ds(WIDE, cut)], S.at[g, rows, pl.ds(0, cut)]))
            copies.append((late.at[top], S.at[g, rows, pl.ds(cut, WIDE - cut)]))
        else:
            cut = rd.shape[1]
            copies.append((rd.at[g], DS.at[g, pl.ds(0, cut)]))
            copies.append((late.at[pl.ds(HALF_ROWS, HALF_ROWS - cut)], DS.at[g, pl.ds(cut, HALF_ROWS - cut)]))
        return [pltpu.make_async_copy(src, dst, loc.at[g, b, k]) for k, (src, dst) in enumerate(copies)]

    own_loads = [pltpu.make_async_copy(src, dst, ld.at[k]) for k, (src, dst) in enumerate(((dqkv, dl), (w3, wb), (xn, xb)))]
    for g in range(2):
        for copy in loads(g, 0):
            copy.start()

    tail = pl.ds(2 * HALF_ROWS + QUARTER_ROWS, HALF_ROWS)

    def out_load(kept):
        return pltpu.make_async_copy(go, L.at[1, tail] if kept else away_rows.at[1], loc.at[1, 3, 0])

    def out_load_do(act):
        @pl.when(y == 1)
        def _():
            act(out_load(True))

        @pl.when(y == 0)
        def _():
            act(out_load(False))

    barrier = pltpu.get_barrier_semaphore()
    others_z = [lax.rem(z + k, 4) * 4 + y * 2 + x for k in range(1, 4)]
    for peer in [px, py] + others_z:
        pl.semaphore_signal(barrier, inc=1, device_id=(peer, t), device_id_type=MESH)
    pl.semaphore_signal(barrier, inc=1, device_id=(dp, 1 - t), device_id_type=MESH)
    pl.semaphore_wait(barrier, 6)
    for b in (2, 1):
        for g in range(2):
            for copy in loads(g, b):
                copy.start()
    for copy in own_loads:
        copy.start()
    out_load_do(lambda copy: copy.start())

    def first_exchange(g):
        return remote(away_rows.at[g], S.at[g, tail], s1s.at[g], s1r.at[g], first[g])

    def first_part(g, c):
        at = pl.multiple_of(c * SWAP_ROWS, SWAP_ROWS)
        dst = S.at[g, pl.ds(2 * HALF_ROWS + QUARTER_ROWS + at, SWAP_ROWS)]
        return remote(away_rows.at[g, pl.ds(at, SWAP_ROWS)], dst, s1s.at[g], s1r.at[g], first[g])

    quarter = pl.ds(2 * HALF_ROWS, QUARTER_ROWS)

    def second_exchange(g):
        return remote(DA.at[g], S.at[g, quarter], s2s.at[g], s2r.at[g], last[g])

    def second_part(g, c):
        at = pl.multiple_of(c * SWAP_ROWS, SWAP_ROWS)
        rows = pl.ds(at, SWAP_ROWS)
        dst = S.at[g, pl.ds(2 * HALF_ROWS + at, SWAP_ROWS)]
        return remote(DA.at[g, rows], dst, s2s.at[g], s2r.at[g], last[g])

    def down_quarter(half):
        return pl.ds(pl.multiple_of(half * QUARTER_ROWS, QUARTER_ROWS), QUARTER_ROWS)

    def piece_down(g):
        for copy in loads(g, 2):
            copy.wait()
        keep = down_quarter(bit[g])
        away = down_quarter(1 - bit[g])
        L[g, quarter, :] = (DL[g, keep, :].astype(F32) + DS[g, keep, :].astype(F32)).astype(BF)
        DA[g] = (DL[g, away, :].astype(F32) + DS[g, away, :].astype(F32)).astype(BF)

    def piece_swap(c):
        for g in range(2):
            first_part(g, c).start()

    def piece_second(c):
        for g in range(2):
            second_part(g, c).start()

    small_x = remote(st.at[2], sb.at[0], ss.at[0], sr.at[0], px)
    small_y = remote(st.at[0], sb.at[1], ss.at[1], sr.at[1], py)
    small_z = [remote(st.at[1], sb.at[2 + z], ss.at[2 + k], sr.at[2 + z], others_z[k]) for k in range(3)]

    def rows_of(i):
        return pl.ds(pl.multiple_of(i * ROWS, ROWS), ROWS)

    def cols_of(at):
        return pl.ds(pl.multiple_of(at, WIDE // 2), WIDE // 2)

    def z_copy(g, i):
        return remote(L.at[g, rows_of(i)], Z.at[g, rows_of(i)], sends.at[g, 0], zr.at[g, i], zn)

    def r_copy(g, i):
        return remote(L.at[g, rows_of(i), cols_of(others)], R.at[g, rows_of(i)], sends.at[g, 1], rr.at[g, i], mm)

    def y_copy(g, i):
        return remote(R.at[g, rows_of(i)], Y.at[g, rows_of(i)], sends.at[g, 2], yr.at[g, i], last[g])

    def a_copy(g, i, at):
        return remote(F.at[g, rows_of(i), cols_of(at)], F.at[g, rows_of(i), cols_of(at)], sends.at[g, 3], ar.at[g, i], mm)

    def o_copy(g, i):
        return remote(F.at[g, rows_of(i)], F.at[g, rows_of(i)], sends.at[g, 4], zr.at[g, i], zn)

    def out_rows(g, i):
        shift = jnp.where(i < cut_at, 0, jnp.where(i < tail_at, bit[g] * QUARTER_ROWS, QUARTER_ROWS))
        return pl.ds(pl.multiple_of(i * ROWS + shift, ROWS), ROWS)

    def x_copy(g, i):
        return remote(F.at[g, rows_of(i)], outs[g].at[owner[g], out_rows(g, i)], sends.at[g, 5], xr.at[g], first[g])

    def l_copy(g, i):
        return pltpu.make_async_copy(F.at[g, rows_of(i)], outs[g].at[owner[g], out_rows(g, i)], lo.at[g])

    def quarter_rows(i):
        return pl.ds(pl.multiple_of((i - cut_at) * ROWS, ROWS), ROWS)

    def g_copy(g, i):
        return remote(F.at[g, rows_of(i)], G.at[g, quarter_rows(i)], gs.at[g], gr.at[g, i - cut_at], last[g])

    def pass_on(g, i):
        rows = pl.ds(pl.multiple_of(i * ROWS + (1 - bit[g]) * QUARTER_ROWS, ROWS), ROWS)
        src = G.at[g, quarter_rows(i)]
        g_copy(g, i).wait_recv()
        remote(src, outs[g].at[owner[g], rows], sends.at[g, 5], xr.at[g], first[g]).start()
        pltpu.make_async_copy(src, outs[g].at[owner[g], rows], lo.at[g]).start()

    def is_cut(i):
        return (i >= cut_at) & (i < tail_at)

    def finish(g, i):
        x_copy(g, i).start()
        l_copy(g, i).start()

        @pl.when(is_cut(i))
        def _():
            g_copy(g, i).start()

    def end_in(g, j):
        r = rows_of(j)
        L[g, r, :] = (L[g, r, :].astype(F32) + S[g, r, :].astype(F32)).astype(BF)
        z_copy(g, j).start()

    def end_out(g, j):
        o_copy(g, j).wait_recv()
        finish(g, j)

    def mid_out(g, j):
        a_copy(g, j, others).wait_recv()
        o_copy(g, j).start()
        finish(g, j)

    def mid_join(g, j):
        @pl.when(jnp.logical_not(is_cut(j)))
        def _():
            y_copy(g, j).wait_recv()
            r = rows_of(j)
            F[g, r, cols_of(mine)] = (R[g, r, :].astype(F32) + Y[g, r, :].astype(F32)).astype(BF)
            a_copy(g, j, mine).start()

    def mid_half(g, j):
        r_copy(g, j).wait_recv()
        r = rows_of(j)
        total = (R[g, r, :].astype(F32) + L[g, r, cols_of(mine)].astype(F32)).astype(BF)

        @pl.when(is_cut(j))
        def _():
            F[g, r, cols_of(mine)] = total
            a_copy(g, j, mine).start()

        @pl.when(jnp.logical_not(is_cut(j)))
        def _():
            R[g, r, :] = total
            y_copy(g, j).start()

    def mid_in(g, j):
        z_copy(g, j).wait_recv()
        r = rows_of(j)
        L[g, r, :] = (L[g, r, :].astype(F32) + S[g, r, :].astype(F32) + Z[g, r, :].astype(F32)).astype(BF)
        r_copy(g, j).start()

    def stage(act, g, j):
        @pl.when((j >= 0) & (j < n))
        def _():
            act(g, j)

    seq = xin.shape[0]
    blk = seq // CHUNKS
    width = dl.shape[2]

    def piece_rows(c):
        return pl.ds(pl.multiple_of(c * blk, blk), blk)

    def core_copy(c):
        return remote(mine_rows.at[piece_rows(c)], their_rows.at[piece_rows(c)], cs.at[c], cr.at[c], dp, 1 - t)

    def norm_loads(c):
        return [
            pltpu.make_async_copy(xin.at[piece_rows(c)], xc.at[lax.rem(c, 2)], xg.at[lax.rem(c, 2), 0]),
            pltpu.make_async_copy(gmid.at[piece_rows(c)], gc.at[lax.rem(c, 2)], xg.at[lax.rem(c, 2), 1]),
        ]

    def ig_copy(c):
        return pltpu.make_async_copy(ic.at[lax.rem(c, 2)], ig.at[piece_rows(c)], io.at[lax.rem(c, 2)])

    def piece_start():
        for copy in own_loads:
            copy.wait()

    def piece_part(c):
        r = piece_rows(c)
        total = dot_nt(dl[0, r, :], wb[0]) + dot_nt(dl[1, r, :], wb[1]) + dot_nt(dl[2, r, :], wb[2])
        mine_rows[r, :] = total.astype(BF)
        core_copy(c).start()

    def row_half(half):
        return pl.ds(pl.multiple_of(half * HALF_ROWS, HALF_ROWS), HALF_ROWS)

    def piece_qk(k):
        cols = pl.ds(pl.multiple_of(k * width, width), width)
        L[0, tail, cols] = dot_tn(xb[:, row_half(x)], dl[k]).astype(BF)
        away_rows[0, :, cols] = dot_tn(xb[:, row_half(1 - x)], dl[k]).astype(BF)

    def piece_v():
        for k in range(2):
            cols = pl.ds(k * width, width)
            grad = dot_tn(xb[:, k * HALF_ROWS : (k + 1) * HALF_ROWS], dl[2]).astype(BF)

            @pl.when(y == 0)
            def _():
                L[1, tail, cols] = grad

            @pl.when(y == 1)
            def _():
                away_rows[1, :, cols] = grad

    def piece_send():
        out_load_do(lambda copy: copy.wait())
        for copy in norm_loads(0):
            copy.start()
        st[2] = jnp.zeros((SMALL, WIDE), F32)
        st[2, 1:2, :] = gain2_ref[...]
        for p in range(bias_ref.shape[0]):
            sums = [jnp.sum(bias_ref[p, h, s], axis=0, keepdims=True) for h in range(2) for s in range(2)]
            st[2, 2 + p : 3 + p, :] = jnp.concatenate(sums, axis=1)

    def piece_norm(c):
        @pl.when(c + 1 < CHUNKS)
        def _():
            for copy in norm_loads(c + 1):
                copy.start()

        for copy in norm_loads(c):
            copy.wait()
        core_copy(c).wait_recv()

        @pl.when(c >= 2)
        def _():
            ig_copy(c - 2).wait()

        r = piece_rows(c)
        grads = mine_rows[r, :].astype(F32) + their_rows[r, :].astype(F32)
        s = lax.rem(c, 2)
        back, gain_grad = norm_back(xc[s].astype(F32), gain_ref[...], grads)
        st[2, 0:1, :] = st[2, 0:1, :] + gain_grad
        ic[s] = gc[s] + back
        ig_copy(c).start()

    def small_first():
        small_x.start()

    def small_second():
        small_x.wait_recv()
        st[0] = st[2] + sb[0]
        small_y.start()

    def small_third():
        small_y.wait_recv()
        st[1] = st[0] + sb[1]
        for copy in small_z:
            copy.start()

    pieces = [
        (1, 1, lambda c: piece_down(0)),
        (2, 1, lambda c: piece_down(1)),
        (3, QUARTER_ROWS // SWAP_ROWS, piece_second),
        (3, 1, lambda c: piece_start()),
        (4, CHUNKS, piece_part),
        (4 + CHUNKS, 2, piece_qk),
        (6 + CHUNKS, 1, lambda c: piece_v()),
        (7 + CHUNKS, 1, lambda c: piece_send()),
        (8 + CHUNKS, HALF_ROWS // SWAP_ROWS, piece_swap),
        (9 + CHUNKS, CHUNKS, piece_norm),
        (10 + 2 * CHUNKS, 1, lambda c: small_first()),
        (14 + 2 * CHUNKS, 1, lambda c: small_second()),
        (18 + 2 * CHUNKS, 1, lambda c: small_third()),
    ]

    def body(i, carry):
        for b in range(4):

            @pl.when(i == starts[b])
            def _():
                for g in range(2):
                    if b < 2:
                        for copy in loads(g, b):
                            copy.wait()
                    elif b == 2:
                        second_exchange(g).wait_recv()
                    else:
                        first_exchange(g).wait_recv()

        @pl.when(is_end)
        def _():
            for g in range(2):
                stage(end_in, g, i)
                stage(end_out, g, i - LAGS[4])

        @pl.when(is_mid)
        def _():
            for g in range(2):
                stage(mid_out, g, i - LAGS[3])
                stage(mid_join, g, i - LAGS[2])
                stage(mid_half, g, i - LAGS[1])
                stage(mid_in, g, i - LAGS[0])

        for g in range(2):
            j = i - LAGS[4] - 2

            @pl.when(is_cut(j))
            def _():
                pass_on(g, j)

        for begin, steps, piece in pieces:

            @pl.when((i >= begin) & (i < begin + steps))
            def _():
                piece(i - begin)

        return carry

    lax.fori_loop(0, n + LAGS[4], body, 0)

    for k in range(3):
        zz = lax.rem(z + k + 1, 4)
        remote(st.at[1], sb.at[2 + zz], ss.at[2 + k], sr.at[2 + zz], others_z[k]).wait_recv()
    sb[2 + z] = st[1]
    small_out[...] = (sb[2] + sb[3]) + (sb[4] + sb[5])

    small_x.wait_send()
    small_y.wait_send()
    for copy in small_z:
        copy.wait_send()
    for c in range(CHUNKS):
        core_copy(c).wait_send()
    for c in (CHUNKS - 2, CHUNKS - 1):
        ig_copy(c).wait()
    for g in range(2):
        first_exchange(g).wait_send()
        away = 1 - owner[g]

        @pl.when(is_end)
        def _():
            remote(L.at[g], Z.at[g], sends.at[g, 0], zr.at[g, 0], zn).wait_send()

        @pl.when(is_mid)
        def _():
            remote(R.at[g], Y.at[g], sends.at[g, 1], rr.at[g, 0], mm).wait_send()
            some = pl.ds(0, KEPT_ROWS - QUARTER_ROWS)
            remote(R.at[g, some], Y.at[g, some], sends.at[g, 2], yr.at[g, 0], last[g]).wait_send()
            remote(R.at[g], Y.at[g], sends.at[g, 3], ar.at[g, 0], mm).wait_send()
            remote(F.at[g], F.at[g], sends.at[g, 4], zr.at[g, 0], zn).wait_send()

        second_exchange(g).wait_send()
        remote(G.at[g], G.at[g], gs.at[g], gr.at[g, 0], last[g]).wait_send()
        whole = remote(outs[g].at[away], outs[g].at[away], sends.at[g, 5], xr.at[g], first[g])
        whole.wait_send()
        whole.wait_recv()
        pltpu.make_async_copy(outs[g].at[owner[g]], outs[g].at[owner[g]], lo.at[g]).wait()


def sum_call(gk, rg, uk, ru, late_x, late_y, dk, rd, go, dqkv, w3, xn, xin, gmid, gain, gain2, bias):
    any_spec = pl.BlockSpec(memory_space=pl.ANY)
    n = KEPT_ROWS // ROWS
    rows, dim = xin.shape
    blk = rows // CHUNKS
    full = pltpu.VMEM((2, KEPT_ROWS, WIDE), BF)
    half = pltpu.VMEM((2, KEPT_ROWS, WIDE // 2), BF)
    quarter = pltpu.VMEM((2, QUARTER_ROWS, WIDE), BF)
    down = pltpu.VMEM((2, HALF_ROWS, WIDE), BF)
    dma = pltpu.SemaphoreType.DMA
    return pl.pallas_call(
        sum_body,
        out_shape=[jax.ShapeDtypeStruct((2, GROUP_ROWS, WIDE), BF)] * 2
        + [jax.ShapeDtypeStruct((rows, dim), F32), jax.ShapeDtypeStruct((SMALL, WIDE), F32)],
        in_specs=[any_spec] * 14 + [whole_spec()] * 3,
        out_specs=[any_spec] * 3 + [whole_spec()],
        scratch_shapes=[
            full, full, full, half, half, down, down, quarter, quarter,
            pltpu.VMEM((6, SMALL, WIDE), F32),
            pltpu.VMEM((3, SMALL, WIDE), F32),
            pltpu.VMEM(dqkv.shape, BF),
            pltpu.VMEM(w3.shape, BF),
            pltpu.VMEM((rows, dim), BF),
            pltpu.VMEM((rows, dim), BF),
            pltpu.VMEM((rows, dim), BF),
            pltpu.VMEM((2, HALF_ROWS, WIDE), BF),
            pltpu.VMEM((2, blk, dim), BF),
            pltpu.VMEM((2, blk, dim), F32),
            pltpu.VMEM((2, blk, dim), F32),
            dma((2, 4, 8)), dma((2,)), dma((2,)), dma((2, 6)),
            dma((2, n)), dma((2, n)), dma((2, n)), dma((2, n)),
            dma((2,)), dma((2,)), dma((5,)), dma((6,)),
            dma((3,)), dma((CHUNKS,)), dma((CHUNKS,)), dma((2, 2)), dma((2,)),
            dma((2,)), dma((2,)), dma((2,)), dma((2, QUARTER_ROWS // ROWS)),
        ],
        compiler_params=pltpu.CompilerParams(collective_id=4, has_side_effects=True, vmem_limit_bytes=VMEM_LIMIT),
        name="grad_sum",
    )(gk, rg, uk, ru, late_x, late_y, dk, rd, go, dqkv, w3, xn, xin, gmid, gain, gain2, bias)


def tables(time_ids):
    half = HEAD // 2
    freqs = jnp.exp(jnp.arange(half, dtype=F32) * (-2.0 * math.log(10000.0) / HEAD))
    angles = freqs[:, None] * time_ids.astype(F32)[None, :]
    return jnp.cos(angles), jnp.sin(angles)


def mask_tables(segments, variates):
    lane = jnp.arange(LANES)[None, :]
    var_here = (lane % VAR_COLS == variates[:, None]) & (lane < 3 * VAR_COLS)
    seg_here = (lane - SEG_COL == segments[:, None]) & (lane >= SEG_COL) & (lane < ONE_COL)
    seg_cols = (lane >= SEG_COL) & (lane < ONE_COL)
    ones = (lane >= ONE_COL) & (lane < ONE_COL + 3)
    base = jnp.where(var_here, 1.0, 0.0)
    segq = jnp.where(seg_cols & ~seg_here, MASKED, 0.0)
    extk = jnp.where(var_here | seg_here | ones, 1.0, 0.0).astype(BF)
    return base, segq, extk


def fast_local(
    block_input, segments, variates, time_ids, attn_gain, w_qkv, head_bias, w_out, ffn_gain, w_gate_up, w_down, cotangent
):
    w3 = jnp.transpose(w_qkv, (1, 0, 2))
    cosine, sine = tables(time_ids)
    base, segq, extk = mask_tables(segments, variates)
    gain1 = attn_gain[None, :]
    gain2 = ffn_gain[None, :]
    xn, q, k, v, cosine, sine = qkv_call(block_input, gain1, w3, cosine, sine)
    attended, o32, extq = attn_fwd_call(q, k, v, base, segq, extk, head_bias)
    mid, xn2 = attn_out_call(block_input, attended, w_out, gain2)
    ffn_part, gx_part, gk, uk, rg, ru, dk, rd, late_x, late_y = ffn_call(xn2, cotangent, pair_rows(w_gate_up), w_down)
    late_x = lax.ppermute(late_x, "dp", [(d, d ^ 1) for d in range(16)])
    late_y = lax.ppermute(late_y, "dp", [(d, d ^ 2) for d in range(16)])
    block_output, grad_mid, do, g_out, g_gain2 = ffn_back_call(
        gx_part, ffn_part, mid, cotangent, gain2, w_out, attended
    )
    dqkv, g_bias = attn_bwd_call(q, k, v, do, o32, extq, extk, variates[None, :], cosine, sine)
    sum_a, sum_b, input_grad, small = sum_call(
        gk, rg, uk, ru, late_x, late_y, dk, rd, g_out, dqkv, w3, xn, block_input, grad_mid, gain1, g_gain2, g_bias
    )
    sum_a = sum_a.reshape(2, 4, HALF_ROWS, WIDE)
    sum_b = sum_b.reshape(2, 4, HALF_ROWS, WIDE)
    heads = head_bias.shape[1]
    g_gate_up, g_down, g_qkv, g_out, g_gain1, g_gain2, g_bias, block_output, input_grad = widen_call(
        sum_a, sum_b, small, heads, block_output, input_grad
    )
    return (
        block_output, input_grad, g_gain1[0], jnp.transpose(g_qkv, (1, 0, 2)), g_bias, g_out, g_gain2[0], g_gate_up, g_down,
    )


def rope_tables(time_ids, head_dim):
    half_dim = head_dim // 2
    freqs = jnp.exp(jnp.arange(half_dim, dtype=jnp.float32) * (-2.0 * math.log(10000.0) / head_dim))
    angles = time_ids.astype(jnp.float32)[:, None] * freqs[None, :]
    return (jnp.cos(angles)[:, None, :], jnp.sin(angles)[:, None, :])


def rotate(vectors, cosine, sine_part):
    half_dim = vectors.shape[-1] // 2
    first_half = vectors[..., :half_dim]
    second_half = vectors[..., half_dim:]
    return jnp.concatenate(
        [
            first_half * cosine - second_half * sine_part,
            second_half * cosine + first_half * sine_part,
        ],
        axis=-1,
    )


def rotate_back(grads, cosine, sine_part):
    half_dim = grads.shape[-1] // 2
    first_half = grads[..., :half_dim]
    second_half = grads[..., half_dim:]
    return jnp.concatenate(
        [
            first_half * cosine + second_half * sine_part,
            second_half * cosine - first_half * sine_part,
        ],
        axis=-1,
    )


def norm_rows(rows_now, gain):
    inverse = lax.rsqrt(jnp.mean(rows_now * rows_now, axis=-1, keepdims=True) + EPSILON)
    return (rows_now * inverse * gain, inverse)


def plain_norm_back(rows_now, inverse, gain, grads):
    scaled = grads * gain
    gain_grad = jnp.sum(grads * rows_now * inverse, axis=0)
    rows_grad = inverse * scaled - rows_now * (inverse * inverse * inverse) * jnp.mean(
        scaled * rows_now, axis=-1, keepdims=True
    )
    return (rows_grad, gain_grad)


def scores_of(queries, keys_rot, same_var, allowed, head_bias, score_scale):
    raw_scores = (
        jnp.einsum("sqhd,skhd->shqk", queries, keys_rot, preferred_element_type=jnp.float32)
        * score_scale
    )
    biased = raw_scores + jnp.where(
        same_var[:, None], head_bias[0][None, :, None, None], head_bias[1][None, :, None, None]
    )
    return jnp.where(allowed[:, None], biased, MASKED)


def plain_local(
    block_input,
    segments,
    variates,
    time_ids,
    attn_gain,
    w_qkv,
    head_bias,
    w_out,
    ffn_gain,
    w_gate_up,
    w_down,
    cotangent,
):
    row_count = block_input.shape[0]
    heads_here = head_bias.shape[1]
    head_dim = w_qkv.shape[2] // heads_here
    seq_count = row_count // LEN
    score_scale = head_dim ** (-0.5)
    input_rows = block_input.astype(jnp.float32)
    attn_normed, attn_inverse = norm_rows(input_rows, attn_gain)
    attn_normed_low = attn_normed.astype(jnp.bfloat16)
    projected = jnp.einsum(
        "td,dck->tck", attn_normed_low, w_qkv, preferred_element_type=jnp.float32
    )
    cosine, sine_part = rope_tables(time_ids, head_dim)
    head_shape = (row_count, heads_here, head_dim)
    seq_shape = (seq_count, LEN, heads_here, head_dim)
    queries = (
        rotate(projected[:, 0].reshape(head_shape), cosine, sine_part)
        .astype(jnp.bfloat16)
        .reshape(seq_shape)
    )
    keys_rot = (
        rotate(projected[:, 1].reshape(head_shape), cosine, sine_part)
        .astype(jnp.bfloat16)
        .reshape(seq_shape)
    )
    values = projected[:, 2].astype(jnp.bfloat16).reshape(seq_shape)
    seg_ids = segments.reshape(seq_count, LEN)
    var_ids = variates.reshape(seq_count, LEN)
    allowed = seg_ids[:, :, None] == seg_ids[:, None, :]
    same_var = var_ids[:, :, None] == var_ids[:, None, :]
    scores = scores_of(queries, keys_rot, same_var, allowed, head_bias, score_scale)
    row_max = jnp.max(scores, axis=-1, keepdims=True)
    exp_total = jnp.sum(jnp.exp(scores - row_max), axis=-1, keepdims=True)
    log_total = row_max + jnp.log(exp_total)
    probs_low = jnp.exp(scores - log_total).astype(jnp.bfloat16)
    attended = jnp.einsum("shqk,skhd->sqhd", probs_low, values, preferred_element_type=jnp.float32)
    attended = attended.reshape(row_count, heads_here * head_dim).astype(jnp.bfloat16)
    attn_branch = lax.psum(
        jnp.dot(attended, w_out, preferred_element_type=jnp.float32).astype(jnp.bfloat16), "tensor"
    ).astype(jnp.float32)
    mid_rows = input_rows + attn_branch
    ffn_normed, ffn_inverse = norm_rows(mid_rows, ffn_gain)
    ffn_normed_low = ffn_normed.astype(jnp.bfloat16)
    gate_up = jnp.einsum(
        "td,dcf->tcf", ffn_normed_low, w_gate_up, preferred_element_type=jnp.float32
    )
    gate_vals = gate_up[:, 0]
    up_vals = gate_up[:, 1]
    sigmoid_gate = jax.nn.sigmoid(gate_vals)
    silu_gate = gate_vals * sigmoid_gate
    hidden_low = (silu_gate * up_vals).astype(jnp.bfloat16)
    ffn_branch = lax.psum(
        jnp.dot(hidden_low, w_down, preferred_element_type=jnp.float32).astype(jnp.bfloat16),
        "tensor",
    ).astype(jnp.float32)
    block_output = (mid_rows + ffn_branch).astype(jnp.bfloat16)
    grad_down = jnp.einsum("tf,td->fd", hidden_low, cotangent, preferred_element_type=jnp.float32)
    grad_hidden = jnp.einsum("td,fd->tf", cotangent, w_down, preferred_element_type=jnp.float32)
    grad_gate = grad_hidden * up_vals * sigmoid_gate * (1.0 + gate_vals * (1.0 - sigmoid_gate))
    grad_up = grad_hidden * silu_gate
    grad_gate_up = jnp.stack([grad_gate, grad_up], axis=1).astype(jnp.bfloat16)
    grad_w_gate_up = jnp.einsum(
        "td,tcf->dcf", ffn_normed_low, grad_gate_up, preferred_element_type=jnp.float32
    )
    grad_ffn_normed = lax.psum(
        jnp.einsum(
            "tcf,dcf->td", grad_gate_up, w_gate_up, preferred_element_type=jnp.float32
        ).astype(jnp.bfloat16),
        "tensor",
    ).astype(jnp.float32)
    norm_grad_mid, grad_ffn_gain = plain_norm_back(mid_rows, ffn_inverse, ffn_gain, grad_ffn_normed)
    grad_mid = cotangent.astype(jnp.float32) + norm_grad_mid
    grad_branch = grad_mid.astype(jnp.bfloat16)
    grad_w_out = jnp.einsum("tk,td->kd", attended, grad_branch, preferred_element_type=jnp.float32)
    grad_attended = jnp.einsum("td,kd->tk", grad_branch, w_out, preferred_element_type=jnp.float32)
    grad_attended = grad_attended.astype(jnp.bfloat16).reshape(seq_shape)
    scores_again = scores_of(queries, keys_rot, same_var, allowed, head_bias, score_scale)
    probs_again = jnp.exp(scores_again - log_total)
    probs_again_low = probs_again.astype(jnp.bfloat16)
    grad_probs = jnp.einsum(
        "sqhd,skhd->shqk", grad_attended, values, preferred_element_type=jnp.float32
    )
    grad_values = jnp.einsum(
        "shqk,sqhd->skhd", probs_again_low, grad_attended, preferred_element_type=jnp.float32
    )
    grad_scores = probs_again * (
        grad_probs - jnp.sum(probs_again * grad_probs, axis=-1, keepdims=True)
    )
    grad_scores_low = grad_scores.astype(jnp.bfloat16)
    same_low = same_var.astype(jnp.bfloat16)
    other_low = jnp.logical_not(same_var).astype(jnp.bfloat16)
    grad_bias = jnp.stack(
        [
            jnp.einsum(
                "shqk,sqk->h", grad_scores_low, same_low, preferred_element_type=jnp.float32
            ),
            jnp.einsum(
                "shqk,sqk->h", grad_scores_low, other_low, preferred_element_type=jnp.float32
            ),
        ],
        axis=0,
    )
    grad_queries = (
        jnp.einsum("shqk,skhd->sqhd", grad_scores_low, keys_rot, preferred_element_type=jnp.float32)
        * score_scale
    )
    grad_keys = (
        jnp.einsum("shqk,sqhd->skhd", grad_scores_low, queries, preferred_element_type=jnp.float32)
        * score_scale
    )
    grad_query_lin = rotate_back(grad_queries.reshape(head_shape), cosine, sine_part).reshape(
        row_count, heads_here * head_dim
    )
    grad_key_lin = rotate_back(grad_keys.reshape(head_shape), cosine, sine_part).reshape(
        row_count, heads_here * head_dim
    )
    grad_value_lin = grad_values.reshape(row_count, heads_here * head_dim)
    grad_projected = jnp.stack([grad_query_lin, grad_key_lin, grad_value_lin], axis=1).astype(
        jnp.bfloat16
    )
    grad_w_qkv = jnp.einsum(
        "td,tck->dck", attn_normed_low, grad_projected, preferred_element_type=jnp.float32
    )
    grad_attn_normed = lax.psum(
        jnp.einsum("tck,dck->td", grad_projected, w_qkv, preferred_element_type=jnp.float32).astype(
            jnp.bfloat16
        ),
        "tensor",
    ).astype(jnp.float32)
    norm_grad_input, grad_attn_gain = plain_norm_back(
        input_rows, attn_inverse, attn_gain, grad_attn_normed
    )
    input_grad = grad_mid + norm_grad_input
    grad_attn_gain, grad_w_qkv, grad_bias, grad_w_out, grad_ffn_gain, grad_w_gate_up, grad_down = (
        lax.psum(
            (
                grad_attn_gain,
                grad_w_qkv,
                grad_bias,
                grad_w_out,
                grad_ffn_gain,
                grad_w_gate_up,
                grad_down,
            ),
            "dp",
        )
    )
    return (
        block_output,
        input_grad,
        grad_attn_gain,
        grad_w_qkv,
        grad_bias,
        grad_w_out,
        grad_ffn_gain,
        grad_w_gate_up,
        grad_down,
    )


def solution(mesh):
    placed = (
        P("dp", None), P("dp"), P("dp"), P("dp"), P(), P(None, None, "tensor"), P(None, "tensor"),
        P("tensor", None), P(), P(None, None, "tensor"), P("tensor", None), P("dp", None),
    )
    fast = (mesh.shape["dp"], mesh.shape["tensor"]) == (16, 2)
    return jax.shard_map(
        fast_local if fast else plain_local,
        mesh=mesh,
        in_specs=placed,
        out_specs=(
            P("dp", None), P("dp", None), P(), P(None, None, "tensor"), P(None, "tensor"), P("tensor", None), P(),
            P(None, None, "tensor"), P("tensor", None),
        ),
        check_vma=False,
    )
```
